32 devices in a mesh: expert: 8 (over z, y), narrow: 4 (over x, core).
Axes of the slice: x: 2, y: 2, z: 4, core: 2. Of those that a mesh axis runs over, the one named last changes fastest.
Arguments:
- tokens: bfloat16 [32768, 768], P(('expert', 'narrow')), may hold values from -6 to 6
- segments: int32 [32, 1024], P(('expert', 'narrow')), may hold values from 0 to 3, never falling along the last dimension, each value on 1 to 512 neighbouring positions
- routes: int32 [32768, 1], P(('expert', 'narrow')), may hold values from 0 to 7; in each aligned block of 1024 rows (0 to 1023, 1024 to 2047, ...) at most 256 rows name the same one
- gate_logit: float32 [32768], P(('expert', 'narrow')), may hold values from -3 to 3
- w_qkv: bfloat16 [768, 2304], P(('expert', 'narrow')), may hold values from -0.21875 to 0.21875
- w_out: bfloat16 [768, 768], P(('expert', 'narrow')), may hold values from -1.5 to 1.5
- norm_gains: bfloat16 [2, 768], P(None, ('expert', 'narrow')), may hold values from 0.5 to 1.5
- w_in: bfloat16 [8, 768, 3072], P('expert', None, 'narrow'), may hold values from -0.21875 to 0.21875
- w_hid: bfloat16 [8, 3072, 768], P('expert', 'narrow'), may hold values from -0.3125 to 0.3125
- cotangent: bfloat16 [32768, 768], P(('expert', 'narrow')), may hold values from -6 to 6
Outputs:
- block_out: bfloat16 [32768, 768], P(('expert', 'narrow'))
- grad_tokens: float32 [32768, 768], P(('expert', 'narrow'))
- grad_qkv: float32 [768, 2304], P(('expert', 'narrow'))
- grad_out: float32 [768, 768], P(('expert', 'narrow'))
- grad_gains: float32 [2, 768], P(None, ('expert', 'narrow'))
- grad_w_in: float32 [8, 768, 3072], P('expert', None, 'narrow')
- grad_w_hid: float32 [8, 3072, 768], P('expert', 'narrow')
The draws below stay inside these ranges and needn't reach their ends.
Inputs may be any that keep to these rules, and one draw needn't show every extreme that they name: `routes`: within the 1024 tokens of one device at most 256 go to one expert. `segments`: within a packed row ids never fall; a document holds at most 512 tokens.
All inputs are finite; a program needn't handle non-finite values.
Results may differ from the reference program's by a relative error of at most 0.013.
Values may be sent and summed in bfloat16 or wider, within the bound.
A program may use at most 448 MiB of HBM per device.

```python
import math
import jax
import jax.numpy as jnp
import numpy as np
from jax import lax

D = 768
HEADS = 12
HEAD_DIM = 64
FF = 3072
SEQ = 1024
EXPERTS = 8
TOK_DEV = 1024
SEQS = 32
TOKENS = 32768
CAP = 256
N_EXPERT = 8
N_NARROW = 4


def strengthened(drawn, key, source, target, blocks, factor):
    owner, partner = [(jnp.arange(drawn.shape[axis_at]) // (drawn.shape[axis_at] // blocks)).reshape([-1 if axis == axis_at else 1 for axis in range(drawn.ndim)]) for axis_at in (source, target)]
    chosen = jax.random.permutation(key, blocks)[partner]
    strong = (owner == chosen) | (owner == (partner + blocks // 2) % blocks)
    return jnp.where(strong, factor * drawn, drawn)


def block_levels(stream_key, extent, split, low, top_value):
    factor_of = 1.0
    for dim, parts in split:
        heights = jax.random.uniform(jax.random.fold_in(jax.random.fold_in(stream_key, 6), dim), (parts,), jnp.float32, low / len(split), top_value / len(split))
        factor_of = factor_of * jnp.repeat(jnp.exp(heights), extent[dim] // parts).reshape((-1,) + (1,) * (len(extent) - 1 - dim))
    return factor_of


def length_profile(amount, total, bound, skew):
    loads = [(1 << 20) // math.isqrt(standing ** skew) + 1 for standing in range(2, amount + 1)]
    rest, counts = total - bound - (amount - 1), [1] * (amount - 1)
    while rest > 0:
        free = [i for i in range(amount - 1) if counts[i] < bound]
        pool, budget = sum([loads[i] for i in free]), rest
        for i in free:
            addition = min(bound - counts[i], max(1, budget * loads[i] // pool), rest)
            counts[i] = counts[i] + addition
            rest = rest - addition
    return np.array([bound] + counts)


def ragged_sizes(own_key, number_of, total, limit, slope):
    if number_of == 2:
        one = jax.random.randint(own_key, (), max(1, total - limit), min(limit, total - 1) + 1)
        return jnp.stack([one, total - one])
    sizes = jnp.asarray(length_profile(number_of, total, limit, slope), jnp.int32)
    twos = (number_of - 1) // 2
    source_of, taker = sizes[1:1 + 2 * twos:2], sizes[2:2 + 2 * twos:2]
    margin = jnp.minimum(source_of - 1, limit - taker)
    moved = jax.random.randint(jax.random.fold_in(own_key, 1), (twos,), 0, 1 << 20) % (margin + 1)
    sizes = sizes.at[1:1 + 2 * twos:2].set(source_of - moved).at[2:2 + 2 * twos:2].set(taker + moved)
    return sizes[jax.random.permutation(jax.random.fold_in(own_key, 2), number_of)]


def assign_block(own_key, own, number, rows, amount, top, bound, skew):
    ranking = jax.random.permutation(own_key, amount)
    crowded, usual = portions_of(amount, rows * top, bound, skew, True), portions_of(amount, rows * top, bound, skew, False)
    places = jnp.arange(amount)

    def named(lengths, rotation):
        used = int((lengths > 0).sum())
        fixed = max(1, used // 4)
        passed = fixed + (places - fixed + rotation * (used - fixed)) % max(1, amount - fixed)
        return jnp.zeros((amount,), jnp.int32).at[ranking[jnp.where(places < fixed, places, passed)]].set(jnp.asarray(lengths, jnp.int32))

    lengths = jnp.where(number % 4 == 0, named(crowded, number // 4), named(usual, number - number // 4 - 1))
    mixed = jax.random.permutation(jax.random.fold_in(own, 3), amount)
    donor, receiver = mixed[0:amount // 2 * 2:2], mixed[1:amount // 2 * 2:2]
    room = jnp.minimum(lengths[donor] - 1, bound - lengths[receiver]) // 2
    room = jnp.where((donor == ranking[0]) | (receiver == ranking[0]) | (lengths[receiver] == 0), 0, jnp.maximum(room, 0))
    passed = jax.random.randint(jax.random.fold_in(own, 4), (amount // 2,), 0, 1 << 20) % (room + 1)
    lengths = lengths.at[donor].add(-passed).at[receiver].add(passed)
    members = jnp.searchsorted(jnp.cumsum(lengths), jnp.arange(rows * top), side="right").astype(jnp.int32)
    grid = members.reshape(top, rows).T
    grid = grid[jax.random.permutation(jax.random.fold_in(own, 1), rows)]
    rotation = jax.random.randint(jax.random.fold_in(own, 2), (rows, 1), 0, top)
    return jnp.take_along_axis(grid, (jnp.arange(top)[None, :] + rotation) % top, axis=1)


def portions_of(count, total, bound, lean, full):
    loads = [(1 << 20) // math.isqrt(rank ** lean) + 1 for rank in range(1, count + 1)]
    largest = bound if full else min(bound, max(-(-total // count), total * loads[0] // sum(loads)))
    least = 1 if total - largest >= count - 1 else 0
    holding, surplus = [largest] + [least] * (count - 1), total - largest - least * (count - 1)
    while surplus > 0:
        candidates = [i for i in range(1, count) if holding[i] < largest] or [i for i in range(1, count) if holding[i] < bound]
        mass, left = sum([loads[i] for i in candidates]), surplus
        for i in candidates:
            extra = min(bound - holding[i], max(1, left * loads[i] // mass), surplus)
            holding[i] = holding[i] + extra
            surplus = surplus - extra
    return np.array(holding)


def scatter_about(stream_key, dims, deviation, bound, cuts=(), held_as=jnp.bfloat16):
    drawn = jax.random.normal(stream_key, dims, jnp.float32) * deviation
    if len(cuts) > 0:
        drawn = block_levels(stream_key, dims, cuts, -0.22, 0.18) * drawn
    return jnp.clip(drawn, min=-bound, max=bound).astype(held_as)


def heavy_noise(own_key, shape, spread, most, cuts, heavy, kind=jnp.bfloat16):
    drawn = spread * jax.random.normal(own_key, shape, jnp.float32)
    if cuts:
        drawn = drawn * block_levels(own_key, shape, cuts, -0.22, 0.18)
    return jnp.clip(strengthened(drawn, jax.random.fold_in(own_key, 3), *heavy), -most, most).astype(kind)


def setup_inputs(seed: int = 0) -> dict:
    seeds = jax.random.split(jax.random.key(seed), 11)
    tokens = heavy_noise(seeds[0], (TOKENS, D), 1.0, 6.0, ((0, 32),), (0, 1, 32, 2.75))
    segments = jax.vmap(lambda own: jnp.searchsorted(jnp.cumsum(ragged_sizes(own, 4, SEQ, SEQ // 2, 0)), jnp.arange(SEQ), side="right"))(jax.random.split(seeds[1], SEQS)).reshape((SEQS, SEQ)).astype(jnp.int32)
    routes_keys = jax.random.split(jax.random.fold_in(seeds[2], 1), TOKENS // TOK_DEV)
    routes_turns = jax.random.permutation(jax.random.fold_in(seeds[2], 3), TOKENS // TOK_DEV)
    routes = jax.vmap(lambda own, number: assign_block(jax.random.fold_in(seeds[2], 2), own, number, TOK_DEV, EXPERTS, 1, CAP, 1))(routes_keys, routes_turns).reshape((TOKENS, 1))
    gate_logit = scatter_about(seeds[3], (TOKENS,), 1.0, 3.0, ((0, 32),), jnp.float32)
    w_qkv = scatter_about(seeds[4], (D, 3 * D), D ** -0.5, 0.21875, ((0, 32),))
    w_out = scatter_about(seeds[5], (D, D), (D // 48) ** -0.5, 1.5, ((0, 32),))
    norm_gains = jnp.clip(1.0 + 0.1 * jax.random.normal(seeds[6], (2, D), jnp.float32), 0.5, 1.5).astype(jnp.bfloat16)
    w_in = scatter_about(seeds[7], (EXPERTS, D, FF), D ** -0.5, 0.21875, ((0, 8), (2, 4)))
    w_hid = scatter_about(seeds[8], (EXPERTS, FF, D), (FF // 8) ** -0.5, 0.3125, ((0, 8), (1, 4)))
    cotangent = scatter_about(seeds[9], (TOKENS, D), 1.0, 6.0, ((0, 32),))
    return {"tokens": tokens, "segments": segments, "routes": routes, "gate_logit": gate_logit, "w_qkv": w_qkv, "w_out": w_out, "norm_gains": norm_gains, "w_in": w_in, "w_hid": w_hid, "cotangent": cotangent}


@jax.custom_vjp
def low(v):
    return lax.optimization_barrier(v.astype(jnp.bfloat16)).astype(jnp.float32)

@jax.custom_vjp
def low_back(v):
    return v

def low_keep(v):
    return (low(v), None)

def low_pass(kept, grad):
    return (grad,)

def back_keep(v):
    return (v, None)

def back_low(kept, grad):
    return (low(grad),)
low.defvjp(low_keep, low_pass)
low_back.defvjp(back_keep, back_low)
epsilon = 1e-05
big_negative = -1e+30
highest = lax.Precision.HIGHEST

def normalize(values):
    centre = lax.optimization_barrier(jnp.mean(values, axis=-1, keepdims=True))
    shifted = values - centre
    return shifted * lax.rsqrt(lax.optimization_barrier(jnp.mean(shifted * shifted, axis=-1, keepdims=True)) + epsilon)

def slot_tables(routes):
    chosen = routes[:, 0].astype(jnp.int32)
    onehot = (chosen.reshape(N_EXPERT * N_NARROW, TOK_DEV)[:, :, None] == jnp.arange(EXPERTS, dtype=jnp.int32)[None, None, :]).astype(jnp.int32)
    rank_index = lax.optimization_barrier(jnp.sum((jnp.cumsum(onehot, axis=1) - 1) * onehot, axis=2)).reshape(TOKENS)
    device_index = jnp.arange(TOKENS, dtype=jnp.int32) // TOK_DEV
    per_expert = N_EXPERT * N_NARROW * CAP
    slot_pos = (chosen * per_expert + device_index * CAP + rank_index).astype(jnp.int32)
    slot_token = jnp.zeros((EXPERTS * per_expert,), jnp.int32).at[slot_pos].set(jnp.arange(TOKENS, dtype=jnp.int32))
    slot_valid = jnp.zeros((EXPERTS * per_expert,), jnp.float32).at[slot_pos].set(1.0)
    return (slot_pos, slot_token.reshape(EXPERTS, per_expert), slot_valid.reshape(EXPERTS, per_expert))

def attend(pieces):
    queries, key_rows, value_rows, seg_row = pieces
    positions = jnp.arange(SEQ, dtype=jnp.int32)
    allowed = (positions[:, None] >= positions[None, :]) & (seg_row[:, None] == seg_row[None, :])
    scores = low_back(jnp.einsum('qhd,khd->hqk', queries, key_rows, precision=highest) * HEAD_DIM ** (-0.5))
    scores = jnp.where(allowed[None], scores, big_negative)
    largest = lax.optimization_barrier(jnp.max(scores, axis=-1, keepdims=True))
    raised = jnp.exp(scores - largest)
    weights = raised / lax.optimization_barrier(jnp.sum(raised, axis=-1, keepdims=True))
    return jnp.einsum('hqk,khd->qhd', low(weights), value_rows, precision=highest)

def forward(resid_in, qkv_weight, out_weight, gains, in_weight, hid_weight, segments, gating, slot_pos, slot_token, slot_valid):
    act_one = low(normalize(resid_in) * gains[0])
    packed = jnp.dot(act_one, qkv_weight, precision=highest)
    queries = low_back(low(packed[:, :D])).reshape(SEQS, SEQ, HEADS, HEAD_DIM)
    key_rows = low_back(low(packed[:, D:2 * D])).reshape(SEQS, SEQ, HEADS, HEAD_DIM)
    value_rows = low_back(low(packed[:, 2 * D:])).reshape(SEQS, SEQ, HEADS, HEAD_DIM)
    context = lax.map(jax.checkpoint(attend), (queries, key_rows, value_rows, segments))
    context = low_back(low(context.reshape(TOKENS, D)))
    hidden_state = resid_in + low_back(jnp.dot(context, out_weight, precision=highest))
    act_two = low_back(low(normalize(hidden_state) * gains[1]))

    def expert_rows(pieces):
        weight_first, weight_second, token_ids, valid_rows = pieces
        token_rows = act_two[token_ids] * valid_rows[:, None]
        pre_act = low_back(jnp.dot(token_rows, weight_first, precision=highest))
        activated = low(jax.nn.gelu(pre_act, approximate=False))
        return low_back(low(jnp.dot(activated, weight_second, precision=highest)))
    outputs = lax.map(jax.checkpoint(expert_rows), (in_weight, hid_weight, slot_token, slot_valid))
    expert_out = outputs.reshape(-1, D)[slot_pos]
    return hidden_state + gating[:, None] * expert_out

def reference(tokens, segments, routes, gate_logit, w_qkv, w_out, norm_gains, w_in, w_hid, cotangent):
    slot_pos, slot_token, slot_valid = slot_tables(routes)
    gating = jax.nn.sigmoid(gate_logit)

    def wrapped(resid_in, qkv_weight, out_weight, gains, in_weight, hid_weight):
        return forward(resid_in, qkv_weight, out_weight, gains, in_weight, hid_weight, segments, gating, slot_pos, slot_token, slot_valid)
    block_out, pull_back = jax.vjp(wrapped, tokens.astype(jnp.float32), w_qkv.astype(jnp.float32), w_out.astype(jnp.float32), norm_gains.astype(jnp.float32), w_in.astype(jnp.float32), w_hid.astype(jnp.float32))
    grads = pull_back(cotangent.astype(jnp.float32))
    return (block_out.astype(jnp.bfloat16), grads[0], grads[1], grads[2], grads[3], grads[4], grads[5])
```

```python
import functools

import jax
import jax.numpy as jnp
from jax import lax
from jax.experimental import pallas as pl
from jax.experimental.pallas import tpu as pltpu
from jax.sharding import PartitionSpec as P

HEAD_DIM = 64
SEQ = 1024
BLOCK = 256
LOOKBACK = 2
EPSILON = 1e-05
BIG_NEGATIVE = -1e30
F32 = jnp.float32
BF16 = jnp.bfloat16

TAIL_P = 0.3
TAIL_C = (
    0.11962923306946524,
    0.12075497050525577,
    0.0999071263144056,
    0.12858273368127124,
    -0.053723704944995426,
    0.20639718480180155,
    -0.1572285075725372,
    0.03568089149479804,
)


def dot(a, b):
    return lax.dot_general(a, b, (((1,), (0,)), ((), ())), preferred_element_type=F32)


def dot_t(a, b):
    return lax.dot_general(a, b, (((1,), (1,)), ((), ())), preferred_element_type=F32)


def t_dot(a, b):
    return lax.dot_general(a, b, (((0,), (0,)), ((), ())), preferred_element_type=F32)


def normalize(values):
    centre = jnp.mean(values, axis=-1, keepdims=True)
    shifted = values - centre
    factor = lax.rsqrt(jnp.mean(shifted * shifted, axis=-1, keepdims=True) + EPSILON)
    return shifted * factor, factor


def norm_back(grad_normed, normed, factor):
    return factor * (
        grad_normed
        - jnp.mean(grad_normed, axis=-1, keepdims=True)
        - normed * jnp.mean(grad_normed * normed, axis=-1, keepdims=True)
    )


def gelu_pair(u):
    size = jnp.abs(u)
    t = 1.0 / (1.0 + TAIL_P * size)
    poly = jnp.full_like(t, TAIL_C[-1])
    for c in TAIL_C[-2::-1]:
        poly = poly * t + c
    bell = jnp.exp(-0.5 * (u * u))
    tail = poly * t * bell
    phi = jnp.where(u >= 0, 1.0 - tail, tail)
    return u * phi, phi + u * (bell * 0.3989422804014327)


def iota(shape, dim):
    return lax.broadcasted_iota(jnp.int32, shape, dim)


def prep_kernel(capacity, experts, rrow_ref, rcol_ref, gate_ref, ct_ref, srow_ref, scol_ref, send_ref):
    tokens = ct_ref.shape[0]
    wide = max(8, experts)
    hot = (iota((wide, tokens), 0) == rrow_ref[...]).astype(F32)
    before = (iota((tokens, tokens), 0) < iota((tokens, tokens), 1)).astype(BF16)
    rank = dot(hot.astype(BF16), before)
    base = (iota((wide, tokens), 0) * capacity).astype(F32)
    srow = jnp.sum(hot * (rank + base), axis=0, keepdims=True)
    srow_ref[...] = jnp.broadcast_to(srow, srow_ref.shape)
    hot_c = (iota((tokens, 128), 1) == rcol_ref[...]).astype(F32)
    after = (iota((tokens, tokens), 1) < iota((tokens, tokens), 0)).astype(BF16)
    rank_c = dot(after, hot_c.astype(BF16))
    base_c = (iota((tokens, 128), 1) * capacity).astype(F32)
    scol_ref[...] = jnp.sum(hot_c * (rank_c + base_c), axis=1, keepdims=True)
    gated = (jax.nn.sigmoid(gate_ref[...]) * ct_ref[...].astype(F32)).astype(BF16)
    fill_slots(srow, gated, send_ref)


def fill_slots(srow, values, send_ref):
    rows = send_ref.shape[0]
    tokens = values.shape[0]

    @pl.loop(0, rows // BLOCK)
    def _(i):
        first = i * BLOCK
        ids = (iota((BLOCK, tokens), 0) + first).astype(F32)
        pick = (ids == srow).astype(BF16)
        send_ref[pl.ds(pl.multiple_of(first, BLOCK), BLOCK), :] = dot(pick, values).astype(BF16)


def prep(routes, gate_logit, cotangent, experts, capacity):
    tokens, width = cotangent.shape
    return pl.pallas_call(
        functools.partial(prep_kernel, capacity, experts),
        out_shape=(
            jax.ShapeDtypeStruct((8, tokens), F32),
            jax.ShapeDtypeStruct((tokens, 1), F32),
            jax.ShapeDtypeStruct((experts * capacity, width), BF16),
        ),
        compiler_params=pltpu.CompilerParams(vmem_limit_bytes=56 << 20),
        cost_estimate=pl.CostEstimate(flops=8 << 30, bytes_accessed=8 << 20, transcendentals=0),
    )(routes.reshape(1, tokens), routes, gate_logit.reshape(tokens, 1), cotangent)


def fwd_kernel(
    x_ref, w_ref, gain_ref, segr_ref, segc_ref, srow_ref, qkv_ref, c_ref, stat_ref, h_ref, send_ref, act_scr, bias_scr, col_scr
):
    tokens, width = x_ref.shape
    blocks = tokens // BLOCK
    pairs = width // 128
    gain_one = gain_ref[0:1, :]
    gain_two = gain_ref[1:2, :]

    @pl.loop(0, blocks)
    def _(i):
        rows = pl.ds(pl.multiple_of(i * BLOCK, BLOCK), BLOCK)
        normed, _f = normalize(x_ref[rows, :].astype(F32))
        act = (normed * gain_one).astype(BF16)
        qkv_ref[rows, :] = dot(act, w_ref[:, : 3 * width]).astype(BF16)

    col_scr[...] = jnp.zeros_like(col_scr)
    low = iota((BLOCK, 128), 1) < HEAD_DIM
    for qb in range(blocks):
        kb = max(0, qb - LOOKBACK)
        span = (qb - kb + 1) * BLOCK
        rows = pl.ds(qb * BLOCK, BLOCK)
        keys = pl.ds(kb * BLOCK, span)
        q_pos = iota((BLOCK, span), 0) + qb * BLOCK
        k_pos = iota((BLOCK, span), 1) + kb * BLOCK
        ok = (k_pos <= q_pos) & (segc_ref[rows, :] == segr_ref[0:1, keys])
        bias_scr[:, :span] = jnp.where(ok, 0.0, BIG_NEGATIVE)

        @pl.loop(0, pairs)
        def _(hp):
            at = pl.multiple_of(hp * 128, 128)
            q = qkv_ref[rows, pl.ds(at, 128)] * jnp.asarray(HEAD_DIM**-0.5, BF16)
            k = qkv_ref[keys, pl.ds(width + at, 128)]
            v = qkv_ref[keys, pl.ds(2 * width + at, 128)]
            outs = []
            col = col_scr[rows, :]
            for half in range(2):
                mine = low if half == 0 else ~low
                s = dot_t(jnp.where(mine, q, 0), k) + bias_scr[:, :span]
                top = jnp.max(s, axis=1, keepdims=True)
                raised = jnp.exp(s - top)
                total = jnp.sum(raised, axis=1, keepdims=True)
                outs.append(dot((raised * (1.0 / total)).astype(BF16), v))
                col = jnp.where(iota((BLOCK, 128), 1) == 2 * hp + half, top + jnp.log(total), col)
            col_scr[rows, :] = col
            c_ref[rows, pl.ds(at, 128)] = jnp.where(low, outs[0], outs[1]).astype(BF16)

    stat_ref[...] = col_scr[...].T

    @pl.loop(0, blocks)
    def _(i):
        rows = pl.ds(pl.multiple_of(i * BLOCK, BLOCK), BLOCK)
        hidden = x_ref[rows, :].astype(F32) + dot(c_ref[rows, :], w_ref[:, 3 * width : 4 * width])
        h_ref[rows, :] = hidden
        normed, _f = normalize(hidden)
        act_scr[rows, :] = (normed * gain_two).astype(BF16)

    fill_slots(srow_ref[0:1, :], act_scr[...], send_ref)


def attend_fwd(tokens_in, w_all, gains, segr, segc, srow, slot_rows):
    tokens, width = tokens_in.shape
    return pl.pallas_call(
        fwd_kernel,
        out_shape=(
            jax.ShapeDtypeStruct((tokens, 3 * width), BF16),
            jax.ShapeDtypeStruct((tokens, width), BF16),
            jax.ShapeDtypeStruct((128, tokens), F32),
            jax.ShapeDtypeStruct((tokens, width), F32),
            jax.ShapeDtypeStruct((slot_rows, width), BF16),
        ),
        scratch_shapes=[
            pltpu.VMEM((tokens, width), BF16),
            pltpu.VMEM((BLOCK, (LOOKBACK + 1) * BLOCK), F32),
            pltpu.VMEM((tokens, 128), F32),
        ],
        compiler_params=pltpu.CompilerParams(vmem_limit_bytes=56 << 20),
        cost_estimate=pl.CostEstimate(flops=40 << 30, bytes_accessed=24 << 20, transcendentals=0),
    )(tokens_in, w_all, gains, segr, segc, srow)


def expert_kernel(a_ref, dy_ref, win_ref, whid_ref, g_ref, du_ref, da_ref, acc_scr):
    a = a_ref[...]
    dy = dy_ref[...]
    parts = win_ref.shape[0]
    wide = win_ref.shape[2]
    acc_scr[...] = jnp.zeros_like(acc_scr)

    @pl.loop(0, parts)
    def _(j):
        cols = pl.ds(pl.multiple_of(j * wide, wide), wide)
        u = dot(a, win_ref[j])
        grad = dot_t(dy, whid_ref[j])
        g, slope = gelu_pair(u)
        g_ref[:, cols] = g.astype(BF16)
        du = (grad * slope).astype(BF16)
        du_ref[:, cols] = du
        acc_scr[...] += dot_t(du, win_ref[j])

    da_ref[...] = acc_scr[...].astype(BF16)


def experts(acts, grads, w_in, w_hid):
    rows, width = acts.shape
    parts, _, wide = w_in.shape
    hidden = parts * wide
    row_spec = pl.BlockSpec((BLOCK, width), lambda i: (i, 0))
    wide_spec = pl.BlockSpec((BLOCK, hidden), lambda i: (i, 0))
    return pl.pallas_call(
        expert_kernel,
        grid=(rows // BLOCK,),
        out_shape=(
            jax.ShapeDtypeStruct((rows, hidden), BF16),
            jax.ShapeDtypeStruct((rows, hidden), BF16),
            jax.ShapeDtypeStruct((rows, width), BF16),
        ),
        in_specs=[
            row_spec,
            row_spec,
            pl.BlockSpec(w_in.shape, lambda i: (0, 0, 0), pipeline_mode=pl.Buffered(1)),
            pl.BlockSpec(w_hid.shape, lambda i: (0, 0, 0), pipeline_mode=pl.Buffered(1)),
        ],
        out_specs=(wide_spec, wide_spec, row_spec),
        scratch_shapes=[pltpu.VMEM((BLOCK, width), F32)],
        compiler_params=pltpu.CompilerParams(vmem_limit_bytes=56 << 20),
        cost_estimate=pl.CostEstimate(flops=60 << 30, bytes_accessed=40 << 20, transcendentals=0),
    )(acts, grads, w_in, w_hid)


def out_kernel(ret_ref, scol_ref, h_ref, gate_ref, out_ref):
    tokens, rows = out_ref.shape[0], ret_ref.shape[0]
    pick = (iota((tokens, rows), 1).astype(F32) == scol_ref[...]).astype(BF16)
    y = dot(pick, ret_ref[...])
    out_ref[...] = (h_ref[...] + jax.nn.sigmoid(gate_ref[...]) * y).astype(BF16)


def block_output(returned, scol, hidden, gate_logit):
    rows, width = returned.shape
    tokens = hidden.shape[0]
    tile = pl.BlockSpec((BLOCK, width), lambda i: (i, 0))
    column = pl.BlockSpec((BLOCK, 1), lambda i: (i, 0))
    return pl.pallas_call(
        out_kernel,
        grid=(tokens // BLOCK,),
        out_shape=jax.ShapeDtypeStruct((tokens, width), BF16),
        in_specs=[pl.BlockSpec((rows, width), lambda i: (0, 0)), column, tile, column],
        out_specs=tile,
        compiler_params=pltpu.CompilerParams(vmem_limit_bytes=40 << 20),
        cost_estimate=pl.CostEstimate(flops=4 << 30, bytes_accessed=10 << 20, transcendentals=0),
    )(returned, scol, hidden, gate_logit.reshape(tokens, 1))


def bwd_kernel(
    ret_ref,
    scol_ref,
    x_ref,
    ct_ref,
    h_ref,
    qkv_ref,
    c_ref,
    stat_ref,
    w_ref,
    gain_ref,
    segr_ref,
    segc_ref,
    gt_ref,
    gw_ref,
    gg_ref,
    dc_scr,
    dhb_scr,
    dqkv_scr,
    act_scr,
    d_scr,
    dk_scr,
    dv_scr,
):
    tokens, width = x_ref.shape
    slots = ret_ref.shape[0]
    blocks = tokens // BLOCK
    pairs = width // 128
    gain_one = gain_ref[0:1, :]
    gain_two = gain_ref[1:2, :]
    gg_ref[...] = jnp.zeros_like(gg_ref)
    member = (iota((16, width), 1) // HEAD_DIM == iota((16, width), 0)).astype(F32)

    for i in range(blocks):
        rows = pl.ds(i * BLOCK, BLOCK)
        pick = (iota((BLOCK, slots), 1).astype(F32) == scol_ref[rows, :]).astype(BF16)
        da = dot(pick, ret_ref[...])
        normed, factor = normalize(h_ref[rows, :])
        gg_ref[1:2, :] += jnp.sum(da * normed, axis=0, keepdims=True)
        dh = ct_ref[rows, :].astype(F32) + norm_back(da * gain_two, normed, factor)
        gt_ref[rows, :] = dh
        dhb = dh.astype(BF16)
        dhb_scr[rows, :] = dhb
        dc = dot_t(dhb, w_ref[:, 3 * width : 4 * width]).astype(BF16)
        dc_scr[rows, :] = dc
        d_scr[:, rows] = lax.dot_general(
            member,
            dc.astype(F32) * c_ref[rows, :].astype(F32),
            (((1,), (1,)), ((), ())),
            precision=lax.Precision.HIGHEST,
            preferred_element_type=F32,
        )

    gw_ref[:, 3 * width : 4 * width] = t_dot(c_ref[...], dhb_scr[...])
    low = iota((BLOCK, 128), 1) < HEAD_DIM
    scale = HEAD_DIM**-0.5

    @pl.loop(0, pairs)
    def _(hp):
        at = pl.multiple_of(hp * 128, 128)
        dk_scr[...] = jnp.zeros_like(dk_scr)
        dv_scr[...] = jnp.zeros_like(dv_scr)
        for qb in range(blocks):
            rows = pl.ds(qb * BLOCK, BLOCK)
            q = qkv_ref[rows, pl.ds(at, 128)] * jnp.asarray(scale, BF16)
            dc = dc_scr[rows, pl.ds(at, 128)]
            q_half = [jnp.where(low, q, 0), jnp.where(low, 0, q)]
            dc_half = [jnp.where(low, dc, 0), jnp.where(low, 0, dc)]
            dq = jnp.zeros((BLOCK, 128), F32)
            for kb in range(max(0, qb - LOOKBACK), qb + 1):
                keys = pl.ds(kb * BLOCK, BLOCK)
                k = qkv_ref[keys, pl.ds(width + at, 128)]
                v = qkv_ref[keys, pl.ds(2 * width + at, 128)]
                ok = segc_ref[keys, :] == segr_ref[0:1, rows]
                if kb == qb:
                    ok = ok & (iota((BLOCK, BLOCK), 0) <= iota((BLOCK, BLOCK), 1))
                ps, dss = [], []
                for half in range(2):
                    s = dot_t(k, q_half[half])
                    p = jnp.where(ok, jnp.exp(s - stat_ref[pl.ds(2 * hp + half, 1), rows]), 0.0)
                    dp = dot_t(v, dc_half[half])
                    dss.append((p * (dp - d_scr[pl.ds(2 * hp + half, 1), rows])).astype(BF16))
                    ps.append(p.astype(BF16))
                dv_scr[keys, :] += dot(jnp.concatenate(ps, 1), jnp.concatenate(dc_half, 0))
                dk_scr[keys, :] += dot(jnp.concatenate(dss, 1), jnp.concatenate(q_half, 0))
                dq += jnp.where(low, t_dot(dss[0], k), t_dot(dss[1], k))
            dqkv_scr[rows, pl.ds(at, 128)] = (dq * scale).astype(BF16)
        dqkv_scr[:, pl.ds(width + at, 128)] = dk_scr[...].astype(BF16)
        dqkv_scr[:, pl.ds(2 * width + at, 128)] = dv_scr[...].astype(BF16)

    @pl.loop(0, blocks)
    def _(i):
        rows = pl.ds(pl.multiple_of(i * BLOCK, BLOCK), BLOCK)
        normed, factor = normalize(x_ref[rows, :].astype(F32))
        act_scr[rows, :] = (normed * gain_one).astype(BF16)
        dn = dot_t(dqkv_scr[rows, :], w_ref[:, : 3 * width])
        gg_ref[0:1, :] += jnp.sum(dn * normed, axis=0, keepdims=True)
        gt_ref[rows, :] += norm_back(dn * gain_one, normed, factor)

    gw_ref[:, : 3 * width] = t_dot(act_scr[...], dqkv_scr[...])


def attend_bwd(returned, scol, tokens_in, cotangent, hidden, qkv, context, stats, w_all, gains, segr, segc):
    tokens, width = tokens_in.shape
    return pl.pallas_call(
        bwd_kernel,
        out_shape=(
            jax.ShapeDtypeStruct((tokens, width), F32),
            jax.ShapeDtypeStruct((width, 4 * width), F32),
            jax.ShapeDtypeStruct((8, width), F32),
        ),
        scratch_shapes=[
            pltpu.VMEM((tokens, width), BF16),
            pltpu.VMEM((tokens, width), BF16),
            pltpu.VMEM((tokens, 3 * width), BF16),
            pltpu.VMEM((tokens, width), BF16),
            pltpu.VMEM((16, tokens), F32),
            pltpu.VMEM((tokens, 128), F32),
            pltpu.VMEM((tokens, 128), F32),
        ],
        compiler_params=pltpu.CompilerParams(vmem_limit_bytes=60 << 20),
        cost_estimate=pl.CostEstimate(flops=80 << 30, bytes_accessed=40 << 20, transcendentals=0),
    )(returned, scol, tokens_in, cotangent, hidden, qkv, context, stats, w_all, gains, segr, segc)


def local(tokens, segments, routes, gate_logit, w_qkv, w_out, norm_gains, w_in, w_hid, cotangent):
    tok_count, width = tokens.shape
    n_expert = lax.axis_size("expert")
    n_narrow = lax.axis_size("narrow")
    capacity = 2 * tok_count // n_expert
    slot_rows = n_expert * capacity
    everyone = ("expert", "narrow")

    gain_cols = jnp.pad(norm_gains.T, ((0, 0), (0, 126)))
    w_all = lax.all_gather(
        jnp.concatenate((w_qkv, w_out, gain_cols), axis=1), everyone, axis=0, tiled=True
    )
    gains = w_all[:, 4 * width : 4 * width + 2].T.astype(F32)
    w_in_all = lax.all_gather(w_in[0], "narrow", axis=0, tiled=False)
    w_hid_all = lax.all_gather(w_hid[0], "narrow", axis=0, tiled=False)

    def exchange(values):
        return lax.all_to_all(
            values.reshape(n_expert, capacity, width), "expert", split_axis=0, concat_axis=0, tiled=True
        ).reshape(slot_rows, width)

    segr = segments.reshape(1, tok_count)
    segc = segments.reshape(tok_count, 1)
    srow, scol, dy_slots = prep(routes, gate_logit, cotangent, n_expert, capacity)
    dy_rows = exchange(dy_slots)
    qkv, context, stats, hidden, act_slots = attend_fwd(tokens, w_all, gains, segr, segc, srow, slot_rows)
    act_rows = exchange(act_slots)
    activated, grad_pre, da_rows = experts(act_rows, dy_rows, w_in_all, w_hid_all)
    da_back = exchange(da_rows)
    hidden_units = activated.shape[1]
    y_rows = dot(activated, w_hid_all.reshape(hidden_units, width)).astype(BF16)
    y_back = exchange(y_rows)
    grad_hid = t_dot(activated, dy_rows).astype(BF16)
    grad_in = lax.dot_general(
        act_rows, grad_pre.reshape(slot_rows, n_narrow, -1), (((0,), (0,)), ((), ())), preferred_element_type=F32
    ).astype(BF16)
    grad_tokens, grad_w, grad_gains = attend_bwd(
        da_back, scol, tokens, cotangent, hidden, qkv, context, stats, w_all, gains, segr, segc
    )
    block_out = block_output(y_back, scol, hidden, gate_logit)
    grad_hid_w = lax.psum_scatter(grad_hid, "narrow", scatter_dimension=0, tiled=True).astype(F32)[None]
    grad_in_w = lax.psum_scatter(grad_in, "narrow", scatter_dimension=1, tiled=True).astype(F32)
    grad_in_w = grad_in_w.reshape(1, width, -1)
    packed = jnp.concatenate((grad_w, jnp.pad(grad_gains[:2].T, ((0, 0), (0, 126)))), axis=1)
    own = lax.psum_scatter(packed, everyone, scatter_dimension=0, tiled=True)
    return (
        block_out,
        grad_tokens,
        own[:, : 3 * width],
        own[:, 3 * width : 4 * width],
        own[:, 4 * width : 4 * width + 2].T,
        grad_in_w,
        grad_hid_w,
    )


def solution(mesh):
    placed = (
        P(("expert", "narrow"), None),
        P(("expert", "narrow"), None),
        P(("expert", "narrow"), None),
        P(("expert", "narrow")),
        P(("expert", "narrow"), None),
        P(("expert", "narrow"), None),
        P(None, ("expert", "narrow")),
        P("expert", None, "narrow"),
        P("expert", "narrow", None),
        P(("expert", "narrow"), None),
    )
    return jax.shard_map(
        local,
        mesh=mesh,
        in_specs=placed,
        out_specs=(
            P(("expert", "narrow"), None),
            P(("expert", "narrow"), None),
            P(("expert", "narrow"), None),
            P(("expert", "narrow"), None),
            P(None, ("expert", "narrow")),
            P("expert", None, "narrow"),
            P("expert", "narrow", None),
        ),
        check_vma=False,
    )
```

```python
import functools

import jax
import jax.numpy as jnp
from jax import lax
from jax.experimental import pallas as pl
from jax.experimental.pallas import tpu as pltpu
from jax.sharding import PartitionSpec as P

HEAD_DIM = 64
SEQ = 1024
BLOCK = 256
LOOKBACK = 2
EPSILON = 1e-05
BIG_NEGATIVE = -1e30
F32 = jnp.float32
BF16 = jnp.bfloat16

TAIL_P = 0.3
TAIL_C = (
    0.11962923306946524,
    0.12075497050525577,
    0.0999071263144056,
    0.12858273368127124,
    -0.053723704944995426,
    0.20639718480180155,
    -0.1572285075725372,
    0.03568089149479804,
)


def dot(a, b):
    return lax.dot_general(a, b, (((1,), (0,)), ((), ())), preferred_element_type=F32)


def dot_t(a, b):
    return lax.dot_general(a, b, (((1,), (1,)), ((), ())), preferred_element_type=F32)


def t_dot(a, b):
    return lax.dot_general(a, b, (((0,), (0,)), ((), ())), preferred_element_type=F32)


def normalize(values):
    centre = jnp.mean(values, axis=-1, keepdims=True)
    shifted = values - centre
    factor = lax.rsqrt(jnp.mean(shifted * shifted, axis=-1, keepdims=True) + EPSILON)
    return shifted * factor, factor


def norm_back(grad_normed, normed, factor):
    return factor * (
        grad_normed
        - jnp.mean(grad_normed, axis=-1, keepdims=True)
        - normed * jnp.mean(grad_normed * normed, axis=-1, keepdims=True)
    )


def gelu_pair(u):
    size = jnp.abs(u)
    t = 1.0 / (1.0 + TAIL_P * size)
    poly = jnp.full_like(t, TAIL_C[-1])
    for c in TAIL_C[-2::-1]:
        poly = poly * t + c
    bell = jnp.exp(-0.5 * (u * u))
    tail = poly * t * bell
    phi = jnp.where(u >= 0, 1.0 - tail, tail)
    return u * phi, phi + u * (bell * 0.3989422804014327)


def iota(shape, dim):
    return lax.broadcasted_iota(jnp.int32, shape, dim)


def prep_kernel(capacity, experts, rrow_ref, rcol_ref, gate_ref, ct_ref, srow_ref, scol_ref, send_ref):
    tokens = ct_ref.shape[0]
    wide = max(8, experts)
    hot = (iota((wide, tokens), 0) == rrow_ref[...]).astype(F32)
    before = (iota((tokens, tokens), 0) < iota((tokens, tokens), 1)).astype(BF16)
    rank = dot(hot.astype(BF16), before)
    base = (iota((wide, tokens), 0) * capacity).astype(F32)
    srow = jnp.sum(hot * (rank + base), axis=0, keepdims=True)
    srow_ref[...] = jnp.broadcast_to(srow, srow_ref.shape)
    hot_c = (iota((tokens, 128), 1) == rcol_ref[...]).astype(F32)
    after = (iota((tokens, tokens), 1) < iota((tokens, tokens), 0)).astype(BF16)
    rank_c = dot(after, hot_c.astype(BF16))
    base_c = (iota((tokens, 128), 1) * capacity).astype(F32)
    scol_ref[...] = jnp.sum(hot_c * (rank_c + base_c), axis=1, keepdims=True)
    gated = (jax.nn.sigmoid(gate_ref[...]) * ct_ref[...].astype(F32)).astype(BF16)
    fill_slots(srow, gated, send_ref)


def fill_slots(srow, values, send_ref):
    rows = send_ref.shape[0]
    tokens = values.shape[0]

    @pl.loop(0, rows // BLOCK)
    def _(i):
        first = i * BLOCK
        ids = (iota((BLOCK, tokens), 0) + first).astype(F32)
        pick = (ids == srow).astype(BF16)
        send_ref[pl.ds(pl.multiple_of(first, BLOCK), BLOCK), :] = dot(pick, values).astype(BF16)


def prep(routes, gate_logit, cotangent, experts, capacity):
    tokens, width = cotangent.shape
    return pl.pallas_call(
        functools.partial(prep_kernel, capacity, experts),
        out_shape=(
            jax.ShapeDtypeStruct((8, tokens), F32),
            jax.ShapeDtypeStruct((tokens, 1), F32),
            jax.ShapeDtypeStruct((experts * capacity, width), BF16),
        ),
        compiler_params=pltpu.CompilerParams(vmem_limit_bytes=56 << 20),
        cost_estimate=pl.CostEstimate(flops=8 << 30, bytes_accessed=8 << 20, transcendentals=0),
    )(routes.reshape(1, tokens), routes, gate_logit.reshape(tokens, 1), cotangent)


def fwd_kernel(
    x_ref, w_ref, gain_ref, segr_ref, segc_ref, srow_ref, qkv_ref, c_ref, stat_ref, h_ref, send_ref, act_scr, bias_scr, col_scr
):
    tokens, width = x_ref.shape
    blocks = tokens // BLOCK
    pairs = width // 128
    gain_one = gain_ref[0:1, :]
    gain_two = gain_ref[1:2, :]

    @pl.loop(0, blocks)
    def _(i):
        rows = pl.ds(pl.multiple_of(i * BLOCK, BLOCK), BLOCK)
        normed, _f = normalize(x_ref[rows, :].astype(F32))
        act = (normed * gain_one).astype(BF16)
        qkv_ref[rows, :] = dot(act, w_ref[:, : 3 * width]).astype(BF16)

    col_scr[...] = jnp.zeros_like(col_scr)
    low = iota((BLOCK, 128), 1) < HEAD_DIM
    for qb in range(blocks):
        kb = max(0, qb - LOOKBACK)
        span = (qb - kb + 1) * BLOCK
        rows = pl.ds(qb * BLOCK, BLOCK)
        keys = pl.ds(kb * BLOCK, span)
        q_pos = iota((BLOCK, span), 0) + qb * BLOCK
        k_pos = iota((BLOCK, span), 1) + kb * BLOCK
        ok = (k_pos <= q_pos) & (segc_ref[rows, :] == segr_ref[0:1, keys])
        bias_scr[:, :span] = jnp.where(ok, 0.0, BIG_NEGATIVE)

        @pl.loop(0, pairs)
        def _(hp):
            at = pl.multiple_of(hp * 128, 128)
            q = qkv_ref[rows, pl.ds(at, 128)] * jnp.asarray(HEAD_DIM**-0.5, BF16)
            k = qkv_ref[keys, pl.ds(width + at, 128)]
            v = qkv_ref[keys, pl.ds(2 * width + at, 128)]
            outs = []
            col = col_scr[rows, :]
            for half in range(2):
                mine = low if half == 0 else ~low
                s = dot_t(jnp.where(mine, q, 0), k) + bias_scr[:, :span]
                top = jnp.max(s, axis=1, keepdims=True)
                raised = jnp.exp(s - top)
                total = jnp.sum(raised, axis=1, keepdims=True)
                outs.append(dot((raised * (1.0 / total)).astype(BF16), v))
                col = jnp.where(iota((BLOCK, 128), 1) == 2 * hp + half, top + jnp.log(total), col)
            col_scr[rows, :] = col
            c_ref[rows, pl.ds(at, 128)] = jnp.where(low, outs[0], outs[1]).astype(BF16)

    stat_ref[...] = col_scr[...].T

    @pl.loop(0, blocks)
    def _(i):
        rows = pl.ds(pl.multiple_of(i * BLOCK, BLOCK), BLOCK)
        hidden = x_ref[rows, :].astype(F32) + dot(c_ref[rows, :], w_ref[:, 3 * width : 4 * width])
        h_ref[rows, :] = hidden
        normed, _f = normalize(hidden)
        act_scr[rows, :] = (normed * gain_two).astype(BF16)

    fill_slots(srow_ref[0:1, :], act_scr[...], send_ref)


def attend_fwd(tokens_in, w_all, gains, segr, segc, srow, slot_rows):
    tokens, width = tokens_in.shape
    return pl.pallas_call(
        fwd_kernel,
        out_shape=(
            jax.ShapeDtypeStruct((tokens, 3 * width), BF16),
            jax.ShapeDtypeStruct((tokens, width), BF16),
            jax.ShapeDtypeStruct((128, tokens), F32),
            jax.ShapeDtypeStruct((tokens, width), F32),
            jax.ShapeDtypeStruct((slot_rows, width), BF16),
        ),
        scratch_shapes=[
            pltpu.VMEM((tokens, width), BF16),
            pltpu.VMEM((BLOCK, (LOOKBACK + 1) * BLOCK), F32),
            pltpu.VMEM((tokens, 128), F32),
        ],
        compiler_params=pltpu.CompilerParams(vmem_limit_bytes=56 << 20),
        cost_estimate=pl.CostEstimate(flops=40 << 30, bytes_accessed=24 << 20, transcendentals=0),
    )(tokens_in, w_all, gains, segr, segc, srow)


def expert_kernel(a_ref, dy_ref, win_ref, whid_ref, g_ref, du_ref, da_ref, acc_scr):
    a = a_ref[...]
    dy = dy_ref[...]
    parts = win_ref.shape[0]
    wide = win_ref.shape[2]
    acc_scr[...] = jnp.zeros_like(acc_scr)

    @pl.loop(0, parts)
    def _(j):
        cols = pl.ds(pl.multiple_of(j * wide, wide), wide)
        u = dot(a, win_ref[j])
        grad = dot_t(dy, whid_ref[j])
        g, slope = gelu_pair(u)
        g_ref[:, cols] = g.astype(BF16)
        du = (grad * slope).astype(BF16)
        du_ref[:, cols] = du
        acc_scr[...] += dot_t(du, win_ref[j])

    da_ref[...] = acc_scr[...].astype(BF16)


def experts(acts, grads, w_in, w_hid):
    rows, width = acts.shape
    parts, _, wide = w_in.shape
    hidden = parts * wide
    row_spec = pl.BlockSpec((BLOCK, width), lambda i: (i, 0))
    wide_spec = pl.BlockSpec((BLOCK, hidden), lambda i: (i, 0))
    return pl.pallas_call(
        expert_kernel,
        grid=(rows // BLOCK,),
        out_shape=(
            jax.ShapeDtypeStruct((rows, hidden), BF16),
            jax.ShapeDtypeStruct((rows, hidden), BF16),
            jax.ShapeDtypeStruct((rows, width), BF16),
        ),
        in_specs=[
            row_spec,
            row_spec,
            pl.BlockSpec(w_in.shape, lambda i: (0, 0, 0), pipeline_mode=pl.Buffered(1)),
            pl.BlockSpec(w_hid.shape, lambda i: (0, 0, 0), pipeline_mode=pl.Buffered(1)),
        ],
        out_specs=(wide_spec, wide_spec, row_spec),
        scratch_shapes=[pltpu.VMEM((BLOCK, width), F32)],
        compiler_params=pltpu.CompilerParams(vmem_limit_bytes=56 << 20),
        cost_estimate=pl.CostEstimate(flops=60 << 30, bytes_accessed=40 << 20, transcendentals=0),
    )(acts, grads, w_in, w_hid)


def out_kernel(ret_ref, scol_ref, h_ref, gate_ref, out_ref):
    tokens, rows = out_ref.shape[0], ret_ref.shape[0]
    pick = (iota((tokens, rows), 1).astype(F32) == scol_ref[...]).astype(BF16)
    y = dot(pick, ret_ref[...])
    out_ref[...] = (h_ref[...] + jax.nn.sigmoid(gate_ref[...]) * y).astype(BF16)


def block_output(returned, scol, hidden, gate_logit):
    rows, width = returned.shape
    tokens = hidden.shape[0]
    tile = pl.BlockSpec((BLOCK, width), lambda i: (i, 0))
    column = pl.BlockSpec((BLOCK, 1), lambda i: (i, 0))
    return pl.pallas_call(
        out_kernel,
        grid=(tokens // BLOCK,),
        out_shape=jax.ShapeDtypeStruct((tokens, width), BF16),
        in_specs=[pl.BlockSpec((rows, width), lambda i: (0, 0)), column, tile, column],
        out_specs=tile,
        compiler_params=pltpu.CompilerParams(vmem_limit_bytes=40 << 20),
        cost_estimate=pl.CostEstimate(flops=4 << 30, bytes_accessed=10 << 20, transcendentals=0),
    )(returned, scol, hidden, gate_logit.reshape(tokens, 1))


def bwd_kernel(
    ret_ref,
    scol_ref,
    x_ref,
    ct_ref,
    h_ref,
    qkv_ref,
    c_ref,
    stat_ref,
    w_ref,
    gain_ref,
    segr_ref,
    segc_ref,
    gt_ref,
    gw_ref,
    gg_ref,
    dc_scr,
    dhb_scr,
    dqkv_scr,
    act_scr,
    d_scr,
    dk_scr,
    dv_scr,
):
    tokens, width = x_ref.shape
    slots = ret_ref.shape[0]
    blocks = tokens // BLOCK
    pairs = width // 128
    gain_one = gain_ref[0:1, :]
    gain_two = gain_ref[1:2, :]
    gg_ref[...] = jnp.zeros_like(gg_ref)
    member = (iota((16, width), 1) // HEAD_DIM == iota((16, width), 0)).astype(F32)

    for i in range(blocks):
        rows = pl.ds(i * BLOCK, BLOCK)
        pick = (iota((BLOCK, slots), 1).astype(F32) == scol_ref[rows, :]).astype(BF16)
        da = dot(pick, ret_ref[...])
        normed, factor = normalize(h_ref[rows, :])
        gg_ref[1:2, :] += jnp.sum(da * normed, axis=0, keepdims=True)
        dh = ct_ref[rows, :].astype(F32) + norm_back(da * gain_two, normed, factor)
        gt_ref[rows, :] = dh
        dhb = dh.astype(BF16)
        dhb_scr[rows, :] = dhb
        dc = dot_t(dhb, w_ref[:, 3 * width : 4 * width]).astype(BF16)
        dc_scr[rows, :] = dc
        d_scr[:, rows] = lax.dot_general(
            member,
            dc.astype(F32) * c_ref[rows, :].astype(F32),
            (((1,), (1,)), ((), ())),
            precision=lax.Precision.HIGHEST,
            preferred_element_type=F32,
        )

    gw_ref[:, 3 * width : 4 * width] = t_dot(c_ref[...], dhb_scr[...])
    low = iota((BLOCK, 128), 1) < HEAD_DIM
    scale = HEAD_DIM**-0.5

    @pl.loop(0, pairs)
    def _(hp):
        at = pl.multiple_of(hp * 128, 128)
        dk_scr[...] = jnp.zeros_like(dk_scr)
        dv_scr[...] = jnp.zeros_like(dv_scr)
        for qb in range(blocks):
            rows = pl.ds(qb * BLOCK, BLOCK)
            q = qkv_ref[rows, pl.ds(at, 128)] * jnp.asarray(scale, BF16)
            dc = dc_scr[rows, pl.ds(at, 128)]
            q_half = [jnp.where(low, q, 0), jnp.where(low, 0, q)]
            dc_half = [jnp.where(low, dc, 0), jnp.where(low, 0, dc)]
            dq = jnp.zeros((BLOCK, 128), F32)
            for kb in range(max(0, qb - LOOKBACK), qb + 1):
                keys = pl.ds(kb * BLOCK, BLOCK)
                k = qkv_ref[keys, pl.ds(width + at, 128)]
                v = qkv_ref[keys, pl.ds(2 * width + at, 128)]
                ok = segc_ref[keys, :] == segr_ref[0:1, rows]
                if kb == qb:
                    ok = ok & (iota((BLOCK, BLOCK), 0) <= iota((BLOCK, BLOCK), 1))
                ps, dss = [], []
                for half in range(2):
                    s = dot_t(k, q_half[half])
                    p = jnp.where(ok, jnp.exp(s - stat_ref[pl.ds(2 * hp + half, 1), rows]), 0.0)
                    dp = dot_t(v, dc_half[half])
                    dss.append((p * (dp - d_scr[pl.ds(2 * hp + half, 1), rows])).astype(BF16))
                    ps.append(p.astype(BF16))
                dv_scr[keys, :] += dot(jnp.concatenate(ps, 1), jnp.concatenate(dc_half, 0))
                dk_scr[keys, :] += dot(jnp.concatenate(dss, 1), jnp.concatenate(q_half, 0))
                dq += jnp.where(low, t_dot(dss[0], k), t_dot(dss[1], k))
            dqkv_scr[rows, pl.ds(at, 128)] = (dq * scale).astype(BF16)
        dqkv_scr[:, pl.ds(width + at, 128)] = dk_scr[...].astype(BF16)
        dqkv_scr[:, pl.ds(2 * width + at, 128)] = dv_scr[...].astype(BF16)

    @pl.loop(0, blocks)
    def _(i):
        rows = pl.ds(pl.multiple_of(i * BLOCK, BLOCK), BLOCK)
        normed, factor = normalize(x_ref[rows, :].astype(F32))
        act_scr[rows, :] = (normed * gain_one).astype(BF16)
        dn = dot_t(dqkv_scr[rows, :], w_ref[:, : 3 * width])
        gg_ref[0:1, :] += jnp.sum(dn * normed, axis=0, keepdims=True)
        gt_ref[rows, :] += norm_back(dn * gain_one, normed, factor)

    gw_ref[:, : 3 * width] = t_dot(act_scr[...], dqkv_scr[...])


def attend_bwd(returned, scol, tokens_in, cotangent, hidden, qkv, context, stats, w_all, gains, segr, segc):
    tokens, width = tokens_in.shape
    return pl.pallas_call(
        bwd_kernel,
        out_shape=(
            jax.ShapeDtypeStruct((tokens, width), F32),
            jax.ShapeDtypeStruct((width, 4 * width), F32),
            jax.ShapeDtypeStruct((8, width), F32),
        ),
        scratch_shapes=[
            pltpu.VMEM((tokens, width), BF16),
            pltpu.VMEM((tokens, width), BF16),
            pltpu.VMEM((tokens, 3 * width), BF16),
            pltpu.VMEM((tokens, width), BF16),
            pltpu.VMEM((16, tokens), F32),
            pltpu.VMEM((tokens, 128), F32),
            pltpu.VMEM((tokens, 128), F32),
        ],
        compiler_params=pltpu.CompilerParams(vmem_limit_bytes=60 << 20),
        cost_estimate=pl.CostEstimate(flops=80 << 30, bytes_accessed=40 << 20, transcendentals=0),
    )(returned, scol, tokens_in, cotangent, hidden, qkv, context, stats, w_all, gains, segr, segc)


MESH = pl.DeviceIdType.MESH


def place():
    e, n = lax.axis_index("expert"), lax.axis_index("narrow")
    return e // 2, lax.rem(e, 2), n // 2, lax.rem(n, 2)


def device(z, y, x, c):
    return (z * 2 + y, x * 2 + c)


def across(z, k):
    hi, lo = z // 2, lax.rem(z, 2)
    hi = 1 - hi if k & 2 else hi
    lo = 1 - lo if k & 1 else lo
    return hi * 2 + lo


class Links:
    def __init__(self, send, recv):
        self.send, self.recv, self.used = send, recv, 0

    def make(self, src, dst, to):
        i = self.used
        self.used += 1
        return pltpu.make_async_remote_copy(
            src_ref=src, dst_ref=dst, send_sem=self.send.at[i], recv_sem=self.recv.at[i], device_id=to, device_id_type=MESH
        )

    def push(self, src, dst, to):
        copy = self.make(src, dst, to)
        copy.start()
        return copy


class Loads:
    def __init__(self, sems):
        self.sems, self.used = sems, 0

    def start(self, src, dst):
        copy = pltpu.make_async_copy(src, dst, self.sems.at[self.used])
        self.used += 1
        copy.start()
        return copy


def greet(peers):
    barrier = pltpu.get_barrier_semaphore()
    for peer in peers:
        pl.semaphore_signal(barrier, inc=1, device_id=peer, device_id_type=MESH)
    pl.semaphore_wait(barrier, len(peers))


FLIPS = (6, 7, 4, 5, 2, 3, 1)


def peers_of(z, y, x, c):
    return [device(across(z, k >> 1), 1 - y if k & 1 else y, x, c) for k in FLIPS]


def tail_kernel(
    ret_hbm,
    x_hbm,
    ct_hbm,
    h_hbm,
    qkv_hbm,
    c_hbm,
    w_hbm,
    yrow_hbm,
    gin_hbm,
    ghid_hbm,
    scol_ref,
    stat_ref,
    gain_ref,
    segr_ref,
    segc_ref,
    gt_hbm,
    yback_hbm,
    r1_hbm,
    r2_hbm,
    gin_out,
    ghid_out,
    own_ref,
    gg_ref,
    ret_ref,
    x_ref,
    ct_ref,
    h_ref,
    qkv_ref,
    c_ref,
    w_ref,
    gt_ref,
    dc_scr,
    dhb_scr,
    dqkv_scr,
    act_scr,
    d_scr,
    dk_scr,
    dv_scr,
    gq,
    rc,
    r1a,
    r1b,
    r2a,
    r2b,
    r3,
    fin,
    r4,
    ggs,
    rg,
    na,
    nb,
    nsum,
    nout,
    send_sems,
    recv_sems,
    load_sems,
):
    z, y, x, c = place()
    me_e = z * 2 + y
    tokens, width = x_ref.shape
    slots = ret_ref.shape[0]
    blocks = tokens // BLOCK
    pairs = width // 128
    core, xpeer, ypeer = device(z, y, x, 1 - c), device(z, y, 1 - x, c), device(z, 1 - y, x, c)
    far = peers_of(z, y, x, c)
    links = Links(send_sems, recv_sems)
    loads = Loads(load_sems)

    first = [
        loads.start(a, b)
        for a, b in ((ret_hbm, ret_ref), (h_hbm, h_ref), (ct_hbm, ct_ref), (c_hbm, c_ref), (w_hbm, w_ref))
    ]
    second = [loads.start(a, b) for a, b in ((qkv_hbm, qkv_ref), (x_hbm, x_ref))]
    own_y = loads.start(yrow_hbm.at[me_e], yback_hbm.at[me_e])

    greet(far + [core, xpeer])

    y_copies = [links.push(yrow_hbm.at[to[0]], yback_hbm.at[me_e], to) for to in far]
    w_copies = []
    for a, src in enumerate((gin_hbm, ghid_hbm)):
        for xx in range(2):
            w_copies.append(links.push(src.at[xx * 2 + 1 - c], r1_hbm.at[a, xx], core))

    gain_one = gain_ref[0:1, :]
    gain_two = gain_ref[1:2, :]
    member = (iota((16, width), 1) // HEAD_DIM == iota((16, width), 0)).astype(F32)
    for copy in first:
        copy.wait()
    ggs[...] = jnp.zeros_like(ggs)

    @pl.loop(0, blocks)
    def _(i):
        rows = pl.ds(pl.multiple_of(i * BLOCK, BLOCK), BLOCK)
        pick = (iota((BLOCK, slots), 1).astype(F32) == scol_ref[rows, :]).astype(BF16)
        da = dot(pick, ret_ref[...])
        normed, factor = normalize(h_ref[rows, :])
        ggs[0, 1:2, :] += jnp.sum(da * normed, axis=0, keepdims=True)
        dh = ct_ref[rows, :].astype(F32) + norm_back(da * gain_two, normed, factor)
        gt_ref[rows, :] = dh
        dhb = dh.astype(BF16)
        dhb_scr[rows, :] = dhb
        dc = dot_t(dhb, w_ref[:, 3 * width : 4 * width]).astype(BF16)
        dc_scr[rows, :] = dc
        d_scr[:, rows] = lax.dot_general(
            member,
            dc.astype(F32) * c_ref[rows, :].astype(F32),
            (((1,), (1,)), ((), ())),
            precision=lax.Precision.HIGHEST,
            preferred_element_type=F32,
        )

    for copy in w_copies:
        copy.wait()
    x_copies = []
    for a, src in enumerate((gin_hbm, ghid_hbm)):
        for step in range(2):
            xx = 1 - x if step == 0 else x
            la = loads.start(src.at[xx * 2 + c], na)
            lb = loads.start(r1_hbm.at[a, xx], nb)
            la.wait()
            lb.wait()
            nsum[step, a] = (na[...].astype(F32) + nb[...].astype(F32)).astype(BF16)
            if step == 0:
                x_copies.append(links.push(nsum.at[0, a], r2_hbm.at[a], xpeer))

    def put_quarter(j, value):
        for chip in range(16):
            gq[j, chip // 4, chip // 2 % 2, chip % 2] = value[chip * 48 : chip * 48 + 48, :].astype(BF16)

    put_quarter(3, t_dot(c_ref[...], dhb_scr[...]))
    for copy in second:
        copy.wait()
    low = iota((BLOCK, 128), 1) < HEAD_DIM
    scale = HEAD_DIM**-0.5

    @pl.loop(0, pairs)
    def _(hp):
        at = pl.multiple_of(hp * 128, 128)
        dk_scr[...] = jnp.zeros_like(dk_scr)
        dv_scr[...] = jnp.zeros_like(dv_scr)
        for qb in range(blocks):
            rows = pl.ds(qb * BLOCK, BLOCK)
            q = qkv_ref[rows, pl.ds(at, 128)] * jnp.asarray(scale, BF16)
            dc = dc_scr[rows, pl.ds(at, 128)]
            q_half = [jnp.where(low, q, 0), jnp.where(low, 0, q)]
            dc_half = [jnp.where(low, dc, 0), jnp.where(low, 0, dc)]
            dq = jnp.zeros((BLOCK, 128), F32)
            for kb in range(max(0, qb - LOOKBACK), qb + 1):
                keys = pl.ds(kb * BLOCK, BLOCK)
                k = qkv_ref[keys, pl.ds(width + at, 128)]
                v = qkv_ref[keys, pl.ds(2 * width + at, 128)]
                ok = segc_ref[keys, :] == segr_ref[0:1, rows]
                if kb == qb:
                    ok = ok & (iota((BLOCK, BLOCK), 0) <= iota((BLOCK, BLOCK), 1))
                ps, dss = [], []
                for half in range(2):
                    s = dot_t(k, q_half[half])
                    p = jnp.where(ok, jnp.exp(s - stat_ref[pl.ds(2 * hp + half, 1), rows]), 0.0)
                    dp = dot_t(v, dc_half[half])
                    dss.append((p * (dp - d_scr[pl.ds(2 * hp + half, 1), rows])).astype(BF16))
                    ps.append(p.astype(BF16))
                dv_scr[keys, :] += dot(jnp.concatenate(ps, 1), jnp.concatenate(dc_half, 0))
                dk_scr[keys, :] += dot(jnp.concatenate(dss, 1), jnp.concatenate(q_half, 0))
                dq += jnp.where(low, t_dot(dss[0], k), t_dot(dss[1], k))
            dqkv_scr[rows, pl.ds(at, 128)] = (dq * scale).astype(BF16)
        dqkv_scr[:, pl.ds(width + at, 128)] = dk_scr[...].astype(BF16)
        dqkv_scr[:, pl.ds(2 * width + at, 128)] = dv_scr[...].astype(BF16)

    @pl.loop(0, blocks)
    def _(i):
        rows = pl.ds(pl.multiple_of(i * BLOCK, BLOCK), BLOCK)
        normed, _f = normalize(x_ref[rows, :].astype(F32))
        act_scr[rows, :] = (normed * gain_one).astype(BF16)

    for j in range(3):
        put_quarter(j, t_dot(act_scr[...], dqkv_scr[:, j * width : (j + 1) * width]))
    core_copies = [links.push(gq.at[2 * (1 - c) + p], rc.at[p], core) for p in range(2)]

    @pl.loop(0, blocks)
    def _(i):
        rows = pl.ds(pl.multiple_of(i * BLOCK, BLOCK), BLOCK)
        normed, factor = normalize(x_ref[rows, :].astype(F32))
        dn = dot_t(dqkv_scr[rows, :], w_ref[:, : 3 * width])
        ggs[0, 0:1, :] += jnp.sum(dn * normed, axis=0, keepdims=True)
        gt_ref[rows, :] += norm_back(dn * gain_one, normed, factor)

    store_gt = loads.start(gt_ref, gt_hbm)
    gains_copy = links.push(ggs.at[0], rg.at[0], core)
    for copy in core_copies:
        copy.wait()
    qa, qb_ = 2 * c, 2 * c + 1

    @pl.loop(0, 4)
    def _(k):
        for p in range(2):
            gq[2 * c + p, k] = (gq[2 * c + p, k].astype(F32) + rc[p, k].astype(F32)).astype(BF16)

    copies = [
        links.push(gq.at[qa, :, :, 1 - x], r1a, xpeer),
        links.push(gq.at[qb_, :, 1 - y], r1b, ypeer),
    ]
    gains_copy.wait()
    ggs[1] = ggs[0] + rg[0]
    gains_copy = links.push(ggs.at[1], rg.at[1], xpeer)
    for copy in copies:
        copy.wait()

    @pl.loop(0, 4)
    def _(k):
        for i in range(2):
            gq[qa, k, i, x] = (gq[qa, k, i, x].astype(F32) + r1a[k, i].astype(F32)).astype(BF16)
            gq[qb_, k, y, i] = (gq[qb_, k, y, i].astype(F32) + r1b[k, i].astype(F32)).astype(BF16)

    copies = [
        links.push(gq.at[qa, :, 1 - y, x], r2a, ypeer),
        links.push(gq.at[qb_, :, y, 1 - x], r2b, xpeer),
    ]
    gains_copy.wait()
    ggs[2] = ggs[1] + rg[1]
    gains_copy = links.push(ggs.at[2], rg.at[2], ypeer)
    for copy in copies:
        copy.wait()

    @pl.loop(0, 4)
    def _(k):
        gq[qa, k, y, x] = (gq[qa, k, y, x].astype(F32) + r2a[k].astype(F32)).astype(BF16)
        gq[qb_, k, y, x] = (gq[qb_, k, y, x].astype(F32) + r2b[k].astype(F32)).astype(BF16)

    copies = []
    for k in (2, 3, 1):
        zz = across(z, k)
        for p in range(2):
            copies.append(links.push(gq.at[2 * c + p, zz, y, x], r3.at[p, k - 1], device(zz, y, x, c)))
    gains_copy.wait()
    ggs[3] = ggs[2] + rg[2]
    for k in (2, 3, 1):
        copies.append(links.push(ggs.at[3], rg.at[2 + k], device(across(z, k), y, x, c)))

    for copy in x_copies:
        copy.wait()
    stores = []
    for a, out in enumerate((gin_out, ghid_out)):
        lb = loads.start(r2_hbm.at[a], nb)
        lb.wait()
        nout[a] = nsum[1, a].astype(F32) + nb[...].astype(F32)
        stores.append(loads.start(nout.at[a], out))

    for copy in copies:
        copy.wait()
    for p in range(2):
        total = gq[2 * c + p, z, y, x].astype(F32)
        for k in range(3):
            total = total + r3[p, k].astype(F32)
        fin[p] = total
    last = links.push(fin.at[:, pl.ds(pl.multiple_of((1 - c) * 24, 8), 24)], r4, core)
    gg_ref[...] = ggs[3] + rg[3] + rg[4] + rg[5]
    for p in range(2):
        own_ref[2 * c + p] = fin[p, pl.ds(pl.multiple_of(c * 24, 8), 24), :]
    last.wait()
    for p in range(2):
        own_ref[2 * (1 - c) + p] = r4[p]
    for copy in stores + y_copies:
        copy.wait()
    own_y.wait()
    store_gt.wait()


def tail(returned, scol, tokens_in, cotangent, hidden, qkv, context, stats, w_all, gains, segr, segc, y_rows, gin, ghid):
    tokens, width = tokens_in.shape
    slots = returned.shape[0]
    any_spec = pl.BlockSpec(memory_space=pl.ANY)
    vmem = pl.BlockSpec(memory_space=pltpu.VMEM)
    return pl.pallas_call(
        tail_kernel,
        out_shape=(
            jax.ShapeDtypeStruct((tokens, width), F32),
            jax.ShapeDtypeStruct(y_rows.shape, BF16),
            jax.ShapeDtypeStruct((2, 2) + gin.shape[1:], BF16),
            jax.ShapeDtypeStruct((2,) + gin.shape[1:], BF16),
            jax.ShapeDtypeStruct(gin.shape[1:], F32),
            jax.ShapeDtypeStruct(ghid.shape[1:], F32),
            jax.ShapeDtypeStruct((4, 24, width), F32),
            jax.ShapeDtypeStruct((8, width), F32),
        ),
        in_specs=[any_spec] * 10 + [vmem] * 5,
        out_specs=(any_spec,) * 6 + (vmem,) * 2,
        scratch_shapes=[
            pltpu.VMEM((slots, width), BF16),
            pltpu.VMEM((tokens, width), BF16),
            pltpu.VMEM((tokens, width), BF16),
            pltpu.VMEM((tokens, width), F32),
            pltpu.VMEM((tokens, 3 * width), BF16),
            pltpu.VMEM((tokens, width), BF16),
            pltpu.VMEM(w_all.shape, BF16),
            pltpu.VMEM((tokens, width), F32),
            pltpu.VMEM((tokens, width), BF16),
            pltpu.VMEM((tokens, width), BF16),
            pltpu.VMEM((tokens, 3 * width), BF16),
            pltpu.VMEM((tokens, width), BF16),
            pltpu.VMEM((16, tokens), F32),
            pltpu.VMEM((tokens, 128), F32),
            pltpu.VMEM((tokens, 128), F32),
            pltpu.VMEM((4, 4, 2, 2, 48, width), BF16),
            pltpu.VMEM((2, 4, 2, 2, 48, width), BF16),
            pltpu.VMEM((4, 2, 48, width), BF16),
            pltpu.VMEM((4, 2, 48, width), BF16),
            pltpu.VMEM((4, 48, width), BF16),
            pltpu.VMEM((4, 48, width), BF16),
            pltpu.VMEM((2, 3, 48, width), BF16),
            pltpu.VMEM((2, 48, width), F32),
            pltpu.VMEM((2, 24, width), F32),
            pltpu.VMEM((4, 8, width), F32),
            pltpu.VMEM((6, 8, width), F32),
            pltpu.VMEM(gin.shape[1:], BF16),
            pltpu.VMEM(gin.shape[1:], BF16),
            pltpu.VMEM((2, 2) + gin.shape[1:], BF16),
            pltpu.VMEM((2,) + gin.shape[1:], F32),
            pltpu.SemaphoreType.DMA((40,)),
            pltpu.SemaphoreType.DMA((40,)),
            pltpu.SemaphoreType.DMA((24,)),
        ],
        compiler_params=pltpu.CompilerParams(vmem_limit_bytes=62 << 20, collective_id=2, has_side_effects=True),
        cost_estimate=pl.CostEstimate(flops=80 << 30, bytes_accessed=40 << 20, transcendentals=0),
    )(returned, tokens_in, cotangent, hidden, qkv, context, w_all, y_rows, gin, ghid, scol, stats, gains, segr, segc)


def local(tokens, segments, routes, gate_logit, w_qkv, w_out, norm_gains, w_in, w_hid, cotangent):
    tok_count, width = tokens.shape
    n_expert = lax.axis_size("expert")
    n_narrow = lax.axis_size("narrow")
    capacity = 2 * tok_count // n_expert
    slot_rows = n_expert * capacity
    everyone = ("expert", "narrow")

    gain_cols = jnp.pad(norm_gains.T, ((0, 0), (0, 126)))
    w_all = lax.all_gather(
        jnp.concatenate((w_qkv, w_out, gain_cols), axis=1), everyone, axis=0, tiled=True
    )
    gains = w_all[:, 4 * width : 4 * width + 2].T.astype(F32)
    w_in_all = lax.all_gather(w_in[0], "narrow", axis=0, tiled=False)
    w_hid_all = lax.all_gather(w_hid[0], "narrow", axis=0, tiled=False)

    def exchange(values):
        return lax.all_to_all(
            values.reshape(n_expert, capacity, width), "expert", split_axis=0, concat_axis=0, tiled=True
        ).reshape(slot_rows, width)

    segr = segments.reshape(1, tok_count)
    segc = segments.reshape(tok_count, 1)
    srow, scol, dy_slots = prep(routes, gate_logit, cotangent, n_expert, capacity)
    dy_rows = exchange(dy_slots)
    qkv, context, stats, hidden, act_slots = attend_fwd(tokens, w_all, gains, segr, segc, srow, slot_rows)
    act_rows = exchange(act_slots)
    activated, grad_pre, da_rows = experts(act_rows, dy_rows, w_in_all, w_hid_all)
    da_back = exchange(da_rows)
    hidden_units = activated.shape[1]
    y_rows = dot(activated, w_hid_all.reshape(hidden_units, width)).astype(BF16)
    grad_hid = t_dot(activated, dy_rows).astype(BF16)
    grad_in = lax.dot_general(
        act_rows, grad_pre.reshape(slot_rows, n_narrow, -1), (((0,), (0,)), ((), ())), preferred_element_type=F32
    ).astype(BF16)
    if n_expert == 8 and n_narrow == 4:
        gin = grad_in.transpose(1, 0, 2)
        ghid = grad_hid.reshape(n_narrow, -1, width)
        grad_tokens, y_back, _r1, _r2, gin_own, ghid_own, own, gg = tail(
            da_back,
            scol,
            tokens,
            cotangent,
            hidden,
            qkv,
            context,
            stats,
            w_all,
            gains,
            segr,
            segc,
            y_rows.reshape(n_expert, capacity, width),
            gin,
            ghid,
        )
        block_out = block_output(y_back.reshape(slot_rows, width), scol, hidden, gate_logit)
        me = lax.axis_index("expert") * n_narrow + lax.axis_index("narrow")
        share = width // (n_expert * n_narrow)
        return (
            block_out,
            grad_tokens,
            own[:3].transpose(1, 0, 2).reshape(share, 3 * width),
            own[3],
            lax.dynamic_slice_in_dim(gg[:2], me * share, share, axis=1),
            gin_own[None],
            ghid_own[None],
        )
    y_back = exchange(y_rows)
    grad_tokens, grad_w, grad_gains = attend_bwd(
        da_back, scol, tokens, cotangent, hidden, qkv, context, stats, w_all, gains, segr, segc
    )
    block_out = block_output(y_back, scol, hidden, gate_logit)
    grad_hid_w = lax.psum_scatter(grad_hid, "narrow", scatter_dimension=0, tiled=True).astype(F32)[None]
    grad_in_w = lax.psum_scatter(grad_in, "narrow", scatter_dimension=1, tiled=True).astype(F32)
    grad_in_w = grad_in_w.reshape(1, width, -1)
    packed = jnp.concatenate((grad_w, jnp.pad(grad_gains[:2].T, ((0, 0), (0, 126)))), axis=1)
    own = lax.psum_scatter(packed, everyone, scatter_dimension=0, tiled=True)
    return (
        block_out,
        grad_tokens,
        own[:, : 3 * width],
        own[:, 3 * width : 4 * width],
        own[:, 4 * width : 4 * width + 2].T,
        grad_in_w,
        grad_hid_w,
    )


def solution(mesh):
    placed = (
        P(("expert", "narrow"), None),
        P(("expert", "narrow"), None),
        P(("expert", "narrow"), None),
        P(("expert", "narrow")),
        P(("expert", "narrow"), None),
        P(("expert", "narrow"), None),
        P(None, ("expert", "narrow")),
        P("expert", None, "narrow"),
        P("expert", "narrow", None),
        P(("expert", "narrow"), None),
    )
    return jax.shard_map(
        local,
        mesh=mesh,
        in_specs=placed,
        out_specs=(
            P(("expert", "narrow"), None),
            P(("expert", "narrow"), None),
            P(("expert", "narrow"), None),
            P(("expert", "narrow"), None),
            P(None, ("expert", "narrow")),
            P("expert", None, "narrow"),
            P("expert", "narrow", None),
        ),
        check_vma=False,
    )
```

```python
import functools

import jax
import jax.numpy as jnp
from jax import lax
from jax.experimental import pallas as pl
from jax.experimental.pallas import tpu as pltpu
from jax.sharding import PartitionSpec as P

HEAD_DIM = 64
SEQ = 1024
BLOCK = 256
LOOKBACK = 2
EPSILON = 1e-05
BIG_NEGATIVE = -1e30
F32 = jnp.float32
BF16 = jnp.bfloat16

TAIL_P = 0.3
TAIL_C = (
    0.11962923306946524,
    0.12075497050525577,
    0.0999071263144056,
    0.12858273368127124,
    -0.053723704944995426,
    0.20639718480180155,
    -0.1572285075725372,
    0.03568089149479804,
)


def dot(a, b):
    return lax.dot_general(a, b, (((1,), (0,)), ((), ())), preferred_element_type=F32)


def dot_t(a, b):
    return lax.dot_general(a, b, (((1,), (1,)), ((), ())), preferred_element_type=F32)


def t_dot(a, b):
    return lax.dot_general(a, b, (((0,), (0,)), ((), ())), preferred_element_type=F32)


def normalize(values):
    centre = jnp.mean(values, axis=-1, keepdims=True)
    shifted = values - centre
    factor = lax.rsqrt(jnp.mean(shifted * shifted, axis=-1, keepdims=True) + EPSILON)
    return shifted * factor, factor


def norm_back(grad_normed, normed, factor):
    return factor * (
        grad_normed
        - jnp.mean(grad_normed, axis=-1, keepdims=True)
        - normed * jnp.mean(grad_normed * normed, axis=-1, keepdims=True)
    )


def gelu_pair(u):
    size = jnp.abs(u)
    t = 1.0 / (1.0 + TAIL_P * size)
    poly = jnp.full_like(t, TAIL_C[-1])
    for c in TAIL_C[-2::-1]:
        poly = poly * t + c
    bell = jnp.exp(-0.5 * (u * u))
    tail = poly * t * bell
    phi = jnp.where(u >= 0, 1.0 - tail, tail)
    return u * phi, phi + u * (bell * 0.3989422804014327)


def iota(shape, dim):
    return lax.broadcasted_iota(jnp.int32, shape, dim)


def prep_kernel(capacity, experts, rrow_ref, rcol_ref, gate_ref, ct_ref, srow_ref, scol_ref, send_ref):
    tokens = ct_ref.shape[0]
    wide = max(8, experts)
    hot = (iota((wide, tokens), 0) == rrow_ref[...]).astype(F32)
    before = (iota((tokens, tokens), 0) < iota((tokens, tokens), 1)).astype(BF16)
    rank = dot(hot.astype(BF16), before)
    base = (iota((wide, tokens), 0) * capacity).astype(F32)
    srow = jnp.sum(hot * (rank + base), axis=0, keepdims=True)
    srow_ref[...] = jnp.broadcast_to(srow, srow_ref.shape)
    hot_c = (iota((tokens, 128), 1) == rcol_ref[...]).astype(F32)
    after = (iota((tokens, tokens), 1) < iota((tokens, tokens), 0)).astype(BF16)
    rank_c = dot(after, hot_c.astype(BF16))
    base_c = (iota((tokens, 128), 1) * capacity).astype(F32)
    scol_ref[...] = jnp.sum(hot_c * (rank_c + base_c), axis=1, keepdims=True)
    gated = (jax.nn.sigmoid(gate_ref[...]) * ct_ref[...].astype(F32)).astype(BF16)
    fill_slots(srow, gated, send_ref)


def fill_slots(srow, values, send_ref):
    rows = send_ref.shape[0]
    tokens = values.shape[0]

    @pl.loop(0, rows // BLOCK)
    def _(i):
        first = i * BLOCK
        ids = (iota((BLOCK, tokens), 0) + first).astype(F32)
        pick = (ids == srow).astype(BF16)
        send_ref[pl.ds(pl.multiple_of(first, BLOCK), BLOCK), :] = dot(pick, values).astype(BF16)


def prep(routes, gate_logit, cotangent, experts, capacity):
    tokens, width = cotangent.shape
    return pl.pallas_call(
        functools.partial(prep_kernel, capacity, experts),
        out_shape=(
            jax.ShapeDtypeStruct((8, tokens), F32),
            jax.ShapeDtypeStruct((tokens, 1), F32),
            jax.ShapeDtypeStruct((experts * capacity, width), BF16),
        ),
        compiler_params=pltpu.CompilerParams(vmem_limit_bytes=56 << 20),
        cost_estimate=pl.CostEstimate(flops=8 << 30, bytes_accessed=8 << 20, transcendentals=0),
    )(routes.reshape(1, tokens), routes, gate_logit.reshape(tokens, 1), cotangent)


def fwd_kernel(
    x_ref, w_ref, gain_ref, segr_ref, segc_ref, srow_ref, qkv_ref, c_ref, stat_ref, h_ref, send_ref, act_scr, bias_scr, col_scr
):
    tokens, width = x_ref.shape
    blocks = tokens // BLOCK
    pairs = width // 128
    gain_one = gain_ref[0:1, :]
    gain_two = gain_ref[1:2, :]

    @pl.loop(0, blocks)
    def _(i):
        rows = pl.ds(pl.multiple_of(i * BLOCK, BLOCK), BLOCK)
        normed, _f = normalize(x_ref[rows, :].astype(F32))
        act = (normed * gain_one).astype(BF16)
        qkv_ref[rows, :] = dot(act, w_ref[:, : 3 * width]).astype(BF16)

    col_scr[...] = jnp.zeros_like(col_scr)
    low = iota((BLOCK, 128), 1) < HEAD_DIM
    for qb in range(blocks):
        kb = max(0, qb - LOOKBACK)
        span = (qb - kb + 1) * BLOCK
        rows = pl.ds(qb * BLOCK, BLOCK)
        keys = pl.ds(kb * BLOCK, span)
        q_pos = iota((BLOCK, span), 0) + qb * BLOCK
        k_pos = iota((BLOCK, span), 1) + kb * BLOCK
        ok = (k_pos <= q_pos) & (segc_ref[rows, :] == segr_ref[0:1, keys])
        bias_scr[:, :span] = jnp.where(ok, 0.0, BIG_NEGATIVE)

        @pl.loop(0, pairs)
        def _(hp):
            at = pl.multiple_of(hp * 128, 128)
            q = qkv_ref[rows, pl.ds(at, 128)] * jnp.asarray(HEAD_DIM**-0.5, BF16)
            k = qkv_ref[keys, pl.ds(width + at, 128)]
            v = qkv_ref[keys, pl.ds(2 * width + at, 128)]
            outs = []
            col = col_scr[rows, :]
            for half in range(2):
                mine = low if half == 0 else ~low
                s = dot_t(jnp.where(mine, q, 0), k) + bias_scr[:, :span]
                top = jnp.max(s, axis=1, keepdims=True)
                raised = jnp.exp(s - top)
                total = jnp.sum(raised, axis=1, keepdims=True)
                outs.append(dot((raised * (1.0 / total)).astype(BF16), v))
                col = jnp.where(iota((BLOCK, 128), 1) == 2 * hp + half, top + jnp.log(total), col)
            col_scr[rows, :] = col
            c_ref[rows, pl.ds(at, 128)] = jnp.where(low, outs[0], outs[1]).astype(BF16)

    stat_ref[...] = col_scr[...].T

    @pl.loop(0, blocks)
    def _(i):
        rows = pl.ds(pl.multiple_of(i * BLOCK, BLOCK), BLOCK)
        hidden = x_ref[rows, :].astype(F32) + dot(c_ref[rows, :], w_ref[:, 3 * width : 4 * width])
        h_ref[rows, :] = hidden
        normed, _f = normalize(hidden)
        act_scr[rows, :] = (normed * gain_two).astype(BF16)

    fill_slots(srow_ref[0:1, :], act_scr[...], send_ref)


def attend_fwd(tokens_in, w_all, gains, segr, segc, srow, slot_rows):
    tokens, width = tokens_in.shape
    return pl.pallas_call(
        fwd_kernel,
        out_shape=(
            jax.ShapeDtypeStruct((tokens, 3 * width), BF16),
            jax.ShapeDtypeStruct((tokens, width), BF16),
            jax.ShapeDtypeStruct((128, tokens), F32),
            jax.ShapeDtypeStruct((tokens, width), F32),
            jax.ShapeDtypeStruct((slot_rows, width), BF16),
        ),
        scratch_shapes=[
            pltpu.VMEM((tokens, width), BF16),
            pltpu.VMEM((BLOCK, (LOOKBACK + 1) * BLOCK), F32),
            pltpu.VMEM((tokens, 128), F32),
        ],
        compiler_params=pltpu.CompilerParams(vmem_limit_bytes=56 << 20),
        cost_estimate=pl.CostEstimate(flops=40 << 30, bytes_accessed=24 << 20, transcendentals=0),
    )(tokens_in, w_all, gains, segr, segc, srow)


def expert_kernel(a_ref, dy_ref, win_ref, whid_ref, g_ref, du_ref, da_ref, acc_scr):
    a = a_ref[...]
    dy = dy_ref[...]
    parts = win_ref.shape[0]
    wide = win_ref.shape[2]
    acc_scr[...] = jnp.zeros_like(acc_scr)

    @pl.loop(0, parts)
    def _(j):
        cols = pl.ds(pl.multiple_of(j * wide, wide), wide)
        u = dot(a, win_ref[j])
        grad = dot_t(dy, whid_ref[j])
        g, slope = gelu_pair(u)
        g_ref[:, cols] = g.astype(BF16)
        du = (grad * slope).astype(BF16)
        du_ref[:, cols] = du
        acc_scr[...] += dot_t(du, win_ref[j])

    da_ref[...] = acc_scr[...].astype(BF16)


def experts(acts, grads, w_in, w_hid):
    rows, width = acts.shape
    parts, _, wide = w_in.shape
    hidden = parts * wide
    row_spec = pl.BlockSpec((BLOCK, width), lambda i: (i, 0))
    wide_spec = pl.BlockSpec((BLOCK, hidden), lambda i: (i, 0))
    return pl.pallas_call(
        expert_kernel,
        grid=(rows // BLOCK,),
        out_shape=(
            jax.ShapeDtypeStruct((rows, hidden), BF16),
            jax.ShapeDtypeStruct((rows, hidden), BF16),
            jax.ShapeDtypeStruct((rows, width), BF16),
        ),
        in_specs=[
            row_spec,
            row_spec,
            pl.BlockSpec(w_in.shape, lambda i: (0, 0, 0), pipeline_mode=pl.Buffered(1)),
            pl.BlockSpec(w_hid.shape, lambda i: (0, 0, 0), pipeline_mode=pl.Buffered(1)),
        ],
        out_specs=(wide_spec, wide_spec, row_spec),
        scratch_shapes=[pltpu.VMEM((BLOCK, width), F32)],
        compiler_params=pltpu.CompilerParams(vmem_limit_bytes=56 << 20),
        cost_estimate=pl.CostEstimate(flops=60 << 30, bytes_accessed=40 << 20, transcendentals=0),
    )(acts, grads, w_in, w_hid)


def out_kernel(ret_ref, scol_ref, h_ref, gate_ref, out_ref):
    tokens, rows = out_ref.shape[0], ret_ref.shape[0]
    pick = (iota((tokens, rows), 1).astype(F32) == scol_ref[...]).astype(BF16)
    y = dot(pick, ret_ref[...])
    out_ref[...] = (h_ref[...] + jax.nn.sigmoid(gate_ref[...]) * y).astype(BF16)


def block_output(returned, scol, hidden, gate_logit):
    rows, width = returned.shape
    tokens = hidden.shape[0]
    tile = pl.BlockSpec((BLOCK, width), lambda i: (i, 0))
    column = pl.BlockSpec((BLOCK, 1), lambda i: (i, 0))
    return pl.pallas_call(
        out_kernel,
        grid=(tokens // BLOCK,),
        out_shape=jax.ShapeDtypeStruct((tokens, width), BF16),
        in_specs=[pl.BlockSpec((rows, width), lambda i: (0, 0)), column, tile, column],
        out_specs=tile,
        compiler_params=pltpu.CompilerParams(vmem_limit_bytes=40 << 20),
        cost_estimate=pl.CostEstimate(flops=4 << 30, bytes_accessed=10 << 20, transcendentals=0),
    )(returned, scol, hidden, gate_logit.reshape(tokens, 1))


def bwd_kernel(
    ret_ref,
    scol_ref,
    x_ref,
    ct_ref,
    h_ref,
    qkv_ref,
    c_ref,
    stat_ref,
    w_ref,
    gain_ref,
    segr_ref,
    segc_ref,
    gt_ref,
    gw_ref,
    gg_ref,
    dc_scr,
    dhb_scr,
    dqkv_scr,
    act_scr,
    d_scr,
    dk_scr,
    dv_scr,
):
    tokens, width = x_ref.shape
    slots = ret_ref.shape[0]
    blocks = tokens // BLOCK
    pairs = width // 128
    gain_one = gain_ref[0:1, :]
    gain_two = gain_ref[1:2, :]
    gg_ref[...] = jnp.zeros_like(gg_ref)
    member = (iota((16, width), 1) // HEAD_DIM == iota((16, width), 0)).astype(F32)

    for i in range(blocks):
        rows = pl.ds(i * BLOCK, BLOCK)
        pick = (iota((BLOCK, slots), 1).astype(F32) == scol_ref[rows, :]).astype(BF16)
        da = dot(pick, ret_ref[...])
        normed, factor = normalize(h_ref[rows, :])
        gg_ref[1:2, :] += jnp.sum(da * normed, axis=0, keepdims=True)
        dh = ct_ref[rows, :].astype(F32) + norm_back(da * gain_two, normed, factor)
        gt_ref[rows, :] = dh
        dhb = dh.astype(BF16)
        dhb_scr[rows, :] = dhb
        dc = dot_t(dhb, w_ref[:, 3 * width : 4 * width]).astype(BF16)
        dc_scr[rows, :] = dc
        d_scr[:, rows] = lax.dot_general(
            member,
            dc.astype(F32) * c_ref[rows, :].astype(F32),
            (((1,), (1,)), ((), ())),
            precision=lax.Precision.HIGHEST,
            preferred_element_type=F32,
        )

    gw_ref[:, 3 * width : 4 * width] = t_dot(c_ref[...], dhb_scr[...])
    low = iota((BLOCK, 128), 1) < HEAD_DIM
    scale = HEAD_DIM**-0.5

    @pl.loop(0, pairs)
    def _(hp):
        at = pl.multiple_of(hp * 128, 128)
        dk_scr[...] = jnp.zeros_like(dk_scr)
        dv_scr[...] = jnp.zeros_like(dv_scr)
        for qb in range(blocks):
            rows = pl.ds(qb * BLOCK, BLOCK)
            q = qkv_ref[rows, pl.ds(at, 128)] * jnp.asarray(scale, BF16)
            dc = dc_scr[rows, pl.ds(at, 128)]
            q_half = [jnp.where(low, q, 0), jnp.where(low, 0, q)]
            dc_half = [jnp.where(low, dc, 0), jnp.where(low, 0, dc)]
            dq = jnp.zeros((BLOCK, 128), F32)
            for kb in range(max(0, qb - LOOKBACK), qb + 1):
                keys = pl.ds(kb * BLOCK, BLOCK)
                k = qkv_ref[keys, pl.ds(width + at, 128)]
                v = qkv_ref[keys, pl.ds(2 * width + at, 128)]
                ok = segc_ref[keys, :] == segr_ref[0:1, rows]
                if kb == qb:
                    ok = ok & (iota((BLOCK, BLOCK), 0) <= iota((BLOCK, BLOCK), 1))
                ps, dss = [], []
                for half in range(2):
                    s = dot_t(k, q_half[half])
                    p = jnp.where(ok, jnp.exp(s - stat_ref[pl.ds(2 * hp + half, 1), rows]), 0.0)
                    dp = dot_t(v, dc_half[half])
                    dss.append((p * (dp - d_scr[pl.ds(2 * hp + half, 1), rows])).astype(BF16))
                    ps.append(p.astype(BF16))
                dv_scr[keys, :] += dot(jnp.concatenate(ps, 1), jnp.concatenate(dc_half, 0))
                dk_scr[keys, :] += dot(jnp.concatenate(dss, 1), jnp.concatenate(q_half, 0))
                dq += jnp.where(low, t_dot(dss[0], k), t_dot(dss[1], k))
            dqkv_scr[rows, pl.ds(at, 128)] = (dq * scale).astype(BF16)
        dqkv_scr[:, pl.ds(width + at, 128)] = dk_scr[...].astype(BF16)
        dqkv_scr[:, pl.ds(2 * width + at, 128)] = dv_scr[...].astype(BF16)

    @pl.loop(0, blocks)
    def _(i):
        rows = pl.ds(pl.multiple_of(i * BLOCK, BLOCK), BLOCK)
        normed, factor = normalize(x_ref[rows, :].astype(F32))
        act_scr[rows, :] = (normed * gain_one).astype(BF16)
        dn = dot_t(dqkv_scr[rows, :], w_ref[:, : 3 * width])
        gg_ref[0:1, :] += jnp.sum(dn * normed, axis=0, keepdims=True)
        gt_ref[rows, :] += norm_back(dn * gain_one, normed, factor)

    gw_ref[:, : 3 * width] = t_dot(act_scr[...], dqkv_scr[...])


def attend_bwd(returned, scol, tokens_in, cotangent, hidden, qkv, context, stats, w_all, gains, segr, segc):
    tokens, width = tokens_in.shape
    return pl.pallas_call(
        bwd_kernel,
        out_shape=(
            jax.ShapeDtypeStruct((tokens, width), F32),
            jax.ShapeDtypeStruct((width, 4 * width), F32),
            jax.ShapeDtypeStruct((8, width), F32),
        ),
        scratch_shapes=[
            pltpu.VMEM((tokens, width), BF16),
            pltpu.VMEM((tokens, width), BF16),
            pltpu.VMEM((tokens, 3 * width), BF16),
            pltpu.VMEM((tokens, width), BF16),
            pltpu.VMEM((16, tokens), F32),
            pltpu.VMEM((tokens, 128), F32),
            pltpu.VMEM((tokens, 128), F32),
        ],
        compiler_params=pltpu.CompilerParams(vmem_limit_bytes=60 << 20),
        cost_estimate=pl.CostEstimate(flops=80 << 30, bytes_accessed=40 << 20, transcendentals=0),
    )(returned, scol, tokens_in, cotangent, hidden, qkv, context, stats, w_all, gains, segr, segc)


MESH = pl.DeviceIdType.MESH


def place():
    e, n = lax.axis_index("expert"), lax.axis_index("narrow")
    return e // 2, lax.rem(e, 2), n // 2, lax.rem(n, 2)


def device(z, y, x, c):
    return (z * 2 + y, x * 2 + c)


def across(z, k):
    hi, lo = z // 2, lax.rem(z, 2)
    hi = 1 - hi if k & 2 else hi
    lo = 1 - lo if k & 1 else lo
    return hi * 2 + lo


class Links:
    def __init__(self, send, recv):
        self.send, self.recv, self.used = send, recv, 0

    def make(self, src, dst, to):
        i = self.used
        self.used += 1
        return pltpu.make_async_remote_copy(
            src_ref=src, dst_ref=dst, send_sem=self.send.at[i], recv_sem=self.recv.at[i], device_id=to, device_id_type=MESH
        )

    def push(self, src, dst, to):
        copy = self.make(src, dst, to)
        copy.start()
        return copy


class Loads:
    def __init__(self, sems):
        self.sems, self.used = sems, 0

    def start(self, src, dst):
        copy = pltpu.make_async_copy(src, dst, self.sems.at[self.used])
        self.used += 1
        copy.start()
        return copy


def greet(peers):
    barrier = pltpu.get_barrier_semaphore()
    for peer in peers:
        pl.semaphore_signal(barrier, inc=1, device_id=peer, device_id_type=MESH)
    pl.semaphore_wait(barrier, len(peers))


FLIPS = (1, 2, 3, 4, 5, 6, 7)


def peers_of(z, y, x, c):
    return [device(across(z, k >> 1), 1 - y if k & 1 else y, x, c) for k in FLIPS]


def weight(blocks, first, count):
    half = blocks.shape[-1]
    rows = blocks.shape[1] * blocks.shape[2] * blocks.shape[3] * blocks.shape[4]
    return jnp.concatenate([blocks[b].reshape(rows, half) for b in range(first, first + count)], axis=1)


def head_kernel(
    capacity,
    experts,
    x_hbm,
    ct_hbm,
    shard_hbm,
    win_hbm,
    whid_hbm,
    rrow_ref,
    rcol_ref,
    gate_ref,
    segr_ref,
    segc_ref,
    qkv_hbm,
    c_hbm,
    h_hbm,
    act_hbm,
    w_hbm,
    dyrow_hbm,
    win4_hbm,
    whid4_hbm,
    stat_ref,
    scol_ref,
    gain_ref,
    x_ref,
    ct_ref,
    st,
    wq,
    wg,
    qkv_ref,
    c_ref,
    h_ref,
    a_scr,
    act_ref,
    dy_ref,
    bias_scr,
    col_scr,
    send_sems,
    recv_sems,
    load_sems,
):
    z, y, x, c = place()
    me_e = z * 2 + y
    me_n = x * 2 + c
    tokens, width = x_ref.shape
    blocks = tokens // BLOCK
    pairs = width // 128
    half = width // 2
    core, xpeer, ypeer = device(z, y, x, 1 - c), device(z, y, 1 - x, c), device(z, 1 - y, x, c)
    links = Links(send_sems, recv_sems)
    loads = Loads(load_sems)
    loading_ct = loads.start(ct_hbm, ct_ref)
    loading_x = loads.start(x_hbm, x_ref)
    own_shard = loads.start(shard_hbm.at[c], st.at[c])
    own_in = loads.start(win_hbm, win4_hbm.at[me_n])
    own_hid = loads.start(whid_hbm, whid4_hbm.at[me_n])

    greet(peers_of(z, y, x, c) + [core, xpeer])
    zero = links.push(shard_hbm.at[1 - c], st.at[c], core)

    wide = max(8, experts)
    hot = (iota((wide, tokens), 0) == rrow_ref[...]).astype(F32)
    before = (iota((tokens, tokens), 0) < iota((tokens, tokens), 1)).astype(BF16)
    rank = dot(hot.astype(BF16), before)
    base = (iota((wide, tokens), 0) * capacity).astype(F32)
    srow = jnp.sum(hot * (rank + base), axis=0, keepdims=True)

    zero.wait()
    own_shard.wait()
    rows48 = jnp.concatenate((st[0], st[1]), axis=0)
    for j in range(4):
        wq[2 * j + c, z, y, x] = rows48[:, j * half : (j + 1) * half].astype(BF16)
    wg[z, y, x] = rows48[:, 4 * half :].astype(BF16)
    ring_z = []
    for piece in range(2):
        group = []
        for k in (1, 2, 3):
            to = device(across(z, k), y, x, c)
            for j in (2 * piece, 2 * piece + 1):
                part = wq.at[2 * j + c, z, y, x]
                group.append(links.push(part, part, to))
            if piece == 0:
                group.append(links.push(wg.at[z, y, x], wg.at[z, y, x], to))
        ring_z.append(group)

    hot_c = (iota((tokens, 128), 1) == rcol_ref[...]).astype(F32)
    after = (iota((tokens, tokens), 1) < iota((tokens, tokens), 0)).astype(BF16)
    rank_c = dot(after, hot_c.astype(BF16))
    base_c = (iota((tokens, 128), 1) * capacity).astype(F32)
    scol_ref[...] = jnp.sum(hot_c * (rank_c + base_c), axis=1, keepdims=True)

    def fill(values, out):
        @pl.loop(0, out.shape[0])
        def _(i):
            ids = (iota((capacity, tokens), 0) + i * capacity).astype(F32)
            out[i] = dot((ids == srow).astype(BF16), values).astype(BF16)

    loading_ct.wait()
    fill((jax.nn.sigmoid(gate_ref[...]) * ct_ref[...].astype(F32)).astype(BF16), dy_ref)

    ring_2 = []
    for piece in range(2):
        for copy in ring_z[piece]:
            copy.wait()
        ja, jb = 2 * (2 * piece) + c, 2 * (2 * piece + 1) + c
        group = [
            links.push(wq.at[ja, :, y, x], wq.at[ja, :, y, x], ypeer),
            links.push(wq.at[jb, :, y, x], wq.at[jb, :, y, x], xpeer),
        ]
        if piece == 0:
            group.append(links.push(wg.at[:, y, x], wg.at[:, y, x], ypeer))
        ring_2.append(group)
    dy_copies = []
    for k in FLIPS:
        zz, yy = across(z, k >> 1), (1 - y if k & 1 else y)
        dy_copies.append(links.push(dy_ref.at[zz * 2 + yy], dyrow_hbm.at[me_e], device(zz, yy, x, c)))
    own_dy = loads.start(dy_ref.at[me_e], dyrow_hbm.at[me_e])
    ring_3 = []
    for piece in range(2):
        for copy in ring_2[piece]:
            copy.wait()
        ja, jb = 2 * (2 * piece) + c, 2 * (2 * piece + 1) + c
        group = [
            links.push(wq.at[ja, :, :, x], wq.at[ja, :, :, x], xpeer),
            links.push(wq.at[jb, :, y], wq.at[jb, :, y], ypeer),
        ]
        if piece == 0:
            group.append(links.push(wg.at[:, :, x], wg.at[:, :, x], xpeer))
        ring_3.append(group)
    ring_4 = []
    for piece in range(2):
        for copy in ring_3[piece]:
            copy.wait()
        ring_4.append([links.push(wq.at[2 * j + c], wq.at[2 * j + c], core) for j in (2 * piece, 2 * piece + 1)])

    slices = []
    for src, dst in ((win_hbm, win4_hbm), (whid_hbm, whid4_hbm)):
        slices.append((links.push(src, dst.at[me_n], xpeer), dst))
    core_slices = [links.push(src, dst.at[me_n], core) for src, dst in ((win_hbm, win4_hbm), (whid_hbm, whid4_hbm))]

    gains = jnp.transpose(wg[...].reshape(width, 128).astype(F32))[0:8, :]
    gain_ref[...] = gains
    gain_one = gains[0:1, :]
    gain_two = gains[1:2, :]
    loading_x.wait()
    for piece in range(2):
        for copy in ring_4[piece]:
            copy.wait()
    storing = [loads.start(wq, w_hbm)]

    @pl.loop(0, blocks)
    def _(i):
        rows = pl.ds(pl.multiple_of(i * BLOCK, BLOCK), BLOCK)
        normed, _f = normalize(x_ref[rows, :].astype(F32))
        act = (normed * gain_one).astype(BF16)
        qkv_ref[rows, :] = dot(act, weight(wq, 0, 6)).astype(BF16)

    storing.append(loads.start(qkv_ref, qkv_hbm))
    col_scr[...] = jnp.zeros_like(col_scr)
    low = iota((BLOCK, 128), 1) < HEAD_DIM
    for qb in range(blocks):
        kb = max(0, qb - LOOKBACK)
        span = (qb - kb + 1) * BLOCK
        rows = pl.ds(qb * BLOCK, BLOCK)
        keys = pl.ds(kb * BLOCK, span)
        q_pos = iota((BLOCK, span), 0) + qb * BLOCK
        k_pos = iota((BLOCK, span), 1) + kb * BLOCK
        ok = (k_pos <= q_pos) & (segc_ref[rows, :] == segr_ref[0:1, keys])
        bias_scr[:, :span] = jnp.where(ok, 0.0, BIG_NEGATIVE)

        @pl.loop(0, pairs)
        def _(hp):
            at = pl.multiple_of(hp * 128, 128)
            q = qkv_ref[rows, pl.ds(at, 128)] * jnp.asarray(HEAD_DIM**-0.5, BF16)
            k = qkv_ref[keys, pl.ds(width + at, 128)]
            v = qkv_ref[keys, pl.ds(2 * width + at, 128)]
            outs = []
            col = col_scr[rows, :]
            for side in range(2):
                mine = low if side == 0 else ~low
                s = dot_t(jnp.where(mine, q, 0), k) + bias_scr[:, :span]
                top = jnp.max(s, axis=1, keepdims=True)
                raised = jnp.exp(s - top)
                total = jnp.sum(raised, axis=1, keepdims=True)
                outs.append(dot((raised * (1.0 / total)).astype(BF16), v))
                col = jnp.where(iota((BLOCK, 128), 1) == 2 * hp + side, top + jnp.log(total), col)
            col_scr[rows, :] = col
            c_ref[rows, pl.ds(at, 128)] = jnp.where(low, outs[0], outs[1]).astype(BF16)

        if qb == 0:
            for copy, dst in slices:
                copy.wait()
                core_slices.append(links.push(dst.at[(1 - x) * 2 + c], dst.at[(1 - x) * 2 + c], core))

    storing.append(loads.start(c_ref, c_hbm))
    stat_ref[...] = col_scr[...].T

    @pl.loop(0, blocks)
    def _(i):
        rows = pl.ds(pl.multiple_of(i * BLOCK, BLOCK), BLOCK)
        hidden = x_ref[rows, :].astype(F32) + dot(c_ref[rows, :], weight(wq, 6, 2))
        h_ref[rows, :] = hidden
        normed, _f = normalize(hidden)
        a_scr[rows, :] = (normed * gain_two).astype(BF16)

    storing.append(loads.start(h_ref, h_hbm))
    fill(a_scr[...], act_ref)
    storing.append(loads.start(act_ref, act_hbm))
    for copy in storing + [own_in, own_hid, own_dy] + core_slices + dy_copies:
        copy.wait()


def head(tokens_in, cotangent, shard, w_in, w_hid, routes, gate_logit, segr, segc, experts, capacity):
    tokens, width = tokens_in.shape
    any_spec = pl.BlockSpec(memory_space=pl.ANY)
    vmem = pl.BlockSpec(memory_space=pltpu.VMEM)
    slots = (experts, capacity, width)
    blocks = (8, 4, 2, 2, 48, width // 2)
    return pl.pallas_call(
        functools.partial(head_kernel, capacity, experts),
        out_shape=(
            jax.ShapeDtypeStruct((tokens, 3 * width), BF16),
            jax.ShapeDtypeStruct((tokens, width), BF16),
            jax.ShapeDtypeStruct((tokens, width), F32),
            jax.ShapeDtypeStruct(slots, BF16),
            jax.ShapeDtypeStruct(blocks, BF16),
            jax.ShapeDtypeStruct(slots, BF16),
            jax.ShapeDtypeStruct((4,) + w_in.shape, BF16),
            jax.ShapeDtypeStruct((4,) + w_hid.shape, BF16),
            jax.ShapeDtypeStruct((128, tokens), F32),
            jax.ShapeDtypeStruct((tokens, 1), F32),
            jax.ShapeDtypeStruct((8, width), F32),
        ),
        in_specs=[any_spec] * 5 + [vmem] * 5,
        out_specs=(any_spec,) * 8 + (vmem,) * 3,
        scratch_shapes=[
            pltpu.VMEM((tokens, width), BF16),
            pltpu.VMEM((tokens, width), BF16),
            pltpu.VMEM(shard.shape, F32),
            pltpu.VMEM(blocks, BF16),
            pltpu.VMEM((4, 2, 2, 48, 128), BF16),
            pltpu.VMEM((tokens, 3 * width), BF16),
            pltpu.VMEM((tokens, width), BF16),
            pltpu.VMEM((tokens, width), F32),
            pltpu.VMEM((tokens, width), BF16),
            pltpu.VMEM(slots, BF16),
            pltpu.VMEM(slots, BF16),
            pltpu.VMEM((BLOCK, (LOOKBACK + 1) * BLOCK), F32),
            pltpu.VMEM((tokens, 128), F32),
            pltpu.SemaphoreType.DMA((48,)),
            pltpu.SemaphoreType.DMA((48,)),
            pltpu.SemaphoreType.DMA((16,)),
        ],
        compiler_params=pltpu.CompilerParams(vmem_limit_bytes=62 << 20, collective_id=0, has_side_effects=True),
        cost_estimate=pl.CostEstimate(flops=60 << 30, bytes_accessed=40 << 20, transcendentals=0),
    )(
        tokens_in,
        cotangent,
        shard,
        w_in,
        w_hid,
        routes.reshape(1, tokens),
        routes,
        gate_logit.reshape(tokens, 1),
        segr,
        segc,
    )


def tail_kernel(
    ret_hbm,
    x_hbm,
    ct_hbm,
    h_hbm,
    qkv_hbm,
    c_hbm,
    w_hbm,
    yrow_hbm,
    gin_hbm,
    ghid_hbm,
    scol_ref,
    stat_ref,
    gain_ref,
    segr_ref,
    segc_ref,
    gt_hbm,
    yback_hbm,
    r1_hbm,
    r2_hbm,
    gin_out,
    ghid_out,
    own_ref,
    gg_ref,
    ret_ref,
    x_ref,
    ct_ref,
    h_ref,
    qkv_ref,
    c_ref,
    w_ref,
    gt_ref,
    dc_scr,
    dhb_scr,
    dqkv_scr,
    act_scr,
    d_scr,
    dk_scr,
    dv_scr,
    gq,
    rc,
    r1a,
    r1b,
    r2a,
    r2b,
    r3,
    fin,
    r4,
    ggs,
    rg,
    na,
    nb,
    nsum,
    nout,
    send_sems,
    recv_sems,
    load_sems,
):
    z, y, x, c = place()
    me_e = z * 2 + y
    tokens, width = x_ref.shape
    slots = ret_ref.shape[0]
    blocks = tokens // BLOCK
    pairs = width // 128
    core, xpeer, ypeer = device(z, y, x, 1 - c), device(z, y, 1 - x, c), device(z, 1 - y, x, c)
    far = peers_of(z, y, x, c)
    links = Links(send_sems, recv_sems)
    loads = Loads(load_sems)

    first = [
        loads.start(a, b)
        for a, b in ((ret_hbm, ret_ref), (h_hbm, h_ref), (ct_hbm, ct_ref), (c_hbm, c_ref), (w_hbm, w_ref))
    ]
    second = [loads.start(a, b) for a, b in ((qkv_hbm, qkv_ref), (x_hbm, x_ref))]
    own_y = loads.start(yrow_hbm.at[me_e], yback_hbm.at[me_e])

    greet(far + [core, xpeer])

    y_copies = [links.push(yrow_hbm.at[to[0]], yback_hbm.at[me_e], to) for to in far]
    w_copies = []
    for a, src in enumerate((gin_hbm, ghid_hbm)):
        for xx in range(2):
            w_copies.append(links.push(src.at[xx * 2 + 1 - c], r1_hbm.at[a, xx], core))

    gain_one = gain_ref[0:1, :]
    gain_two = gain_ref[1:2, :]
    member = (iota((16, width), 1) // HEAD_DIM == iota((16, width), 0)).astype(F32)
    for copy in first:
        copy.wait()
    ggs[...] = jnp.zeros_like(ggs)

    @pl.loop(0, blocks)
    def _(i):
        rows = pl.ds(pl.multiple_of(i * BLOCK, BLOCK), BLOCK)
        pick = (iota((BLOCK, slots), 1).astype(F32) == scol_ref[rows, :]).astype(BF16)
        da = dot(pick, ret_ref[...])
        normed, factor = normalize(h_ref[rows, :])
        ggs[0, 1:2, :] += jnp.sum(da * normed, axis=0, keepdims=True)
        dh = ct_ref[rows, :].astype(F32) + norm_back(da * gain_two, normed, factor)
        gt_ref[rows, :] = dh
        dhb = dh.astype(BF16)
        dhb_scr[rows, :] = dhb
        dc = dot_t(dhb, weight(w_ref, 6, 2)).astype(BF16)
        dc_scr[rows, :] = dc
        d_scr[:, rows] = lax.dot_general(
            member,
            dc.astype(F32) * c_ref[rows, :].astype(F32),
            (((1,), (1,)), ((), ())),
            precision=lax.Precision.HIGHEST,
            preferred_element_type=F32,
        )

    for copy in w_copies:
        copy.wait()
    x_copies = []
    for a, src in enumerate((gin_hbm, ghid_hbm)):
        for step in range(2):
            xx = 1 - x if step == 0 else x
            la = loads.start(src.at[xx * 2 + c], na)
            lb = loads.start(r1_hbm.at[a, xx], nb)
            la.wait()
            lb.wait()
            nsum[step, a] = (na[...].astype(F32) + nb[...].astype(F32)).astype(BF16)
            if step == 0:
                x_copies.append(links.push(nsum.at[0, a], r2_hbm.at[a], xpeer))

    def put_quarter(j, value):
        for chip in range(16):
            gq[j, chip // 4, chip // 2 % 2, chip % 2] = value[chip * 48 : chip * 48 + 48, :].astype(BF16)

    put_quarter(3, t_dot(c_ref[...], dhb_scr[...]))
    for copy in second:
        copy.wait()
    low = iota((BLOCK, 128), 1) < HEAD_DIM
    scale = HEAD_DIM**-0.5

    @pl.loop(0, pairs)
    def _(hp):
        at = pl.multiple_of(hp * 128, 128)
        dk_scr[...] = jnp.zeros_like(dk_scr)
        dv_scr[...] = jnp.zeros_like(dv_scr)
        for qb in range(blocks):
            rows = pl.ds(qb * BLOCK, BLOCK)
            q = qkv_ref[rows, pl.ds(at, 128)] * jnp.asarray(scale, BF16)
            dc = dc_scr[rows, pl.ds(at, 128)]
            q_half = [jnp.where(low, q, 0), jnp.where(low, 0, q)]
            dc_half = [jnp.where(low, dc, 0), jnp.where(low, 0, dc)]
            dq = jnp.zeros((BLOCK, 128), F32)
            for kb in range(max(0, qb - LOOKBACK), qb + 1):
                keys = pl.ds(kb * BLOCK, BLOCK)
                k = qkv_ref[keys, pl.ds(width + at, 128)]
                v = qkv_ref[keys, pl.ds(2 * width + at, 128)]
                ok = segc_ref[keys, :] == segr_ref[0:1, rows]
                if kb == qb:
                    ok = ok & (iota((BLOCK, BLOCK), 0) <= iota((BLOCK, BLOCK), 1))
                ps, dss = [], []
                for half in range(2):
                    s = dot_t(k, q_half[half])
                    p = jnp.where(ok, jnp.exp(s - stat_ref[pl.ds(2 * hp + half, 1), rows]), 0.0)
                    dp = dot_t(v, dc_half[half])
                    dss.append((p * (dp - d_scr[pl.ds(2 * hp + half, 1), rows])).astype(BF16))
                    ps.append(p.astype(BF16))
                dv_scr[keys, :] += dot(jnp.concatenate(ps, 1), jnp.concatenate(dc_half, 0))
                dk_scr[keys, :] += dot(jnp.concatenate(dss, 1), jnp.concatenate(q_half, 0))
                dq += jnp.where(low, t_dot(dss[0], k), t_dot(dss[1], k))
            dqkv_scr[rows, pl.ds(at, 128)] = (dq * scale).astype(BF16)
        dqkv_scr[:, pl.ds(width + at, 128)] = dk_scr[...].astype(BF16)
        dqkv_scr[:, pl.ds(2 * width + at, 128)] = dv_scr[...].astype(BF16)

    @pl.loop(0, blocks)
    def _(i):
        rows = pl.ds(pl.multiple_of(i * BLOCK, BLOCK), BLOCK)
        normed, _f = normalize(x_ref[rows, :].astype(F32))
        act_scr[rows, :] = (normed * gain_one).astype(BF16)

    for j in range(3):
        put_quarter(j, t_dot(act_scr[...], dqkv_scr[:, j * width : (j + 1) * width]))
    core_copies = [links.push(gq.at[2 * (1 - c) + p], rc.at[p], core) for p in range(2)]

    @pl.loop(0, blocks)
    def _(i):
        rows = pl.ds(pl.multiple_of(i * BLOCK, BLOCK), BLOCK)
        normed, factor = normalize(x_ref[rows, :].astype(F32))
        dn = dot_t(dqkv_scr[rows, :], weight(w_ref, 0, 6))
        ggs[0, 0:1, :] += jnp.sum(dn * normed, axis=0, keepdims=True)
        gt_ref[rows, :] += norm_back(dn * gain_one, normed, factor)

    store_gt = loads.start(gt_ref, gt_hbm)
    gains_copy = links.push(ggs.at[0], rg.at[0], core)
    for copy in core_copies:
        copy.wait()
    qa, qb_ = 2 * c, 2 * c + 1

    @pl.loop(0, 4)
    def _(k):
        for p in range(2):
            gq[2 * c + p, k] = (gq[2 * c + p, k].astype(F32) + rc[p, k].astype(F32)).astype(BF16)

    copies = [
        links.push(gq.at[qa, :, :, 1 - x], r1a, xpeer),
        links.push(gq.at[qb_, :, 1 - y], r1b, ypeer),
    ]
    gains_copy.wait()
    ggs[1] = ggs[0] + rg[0]
    gains_copy = links.push(ggs.at[1], rg.at[1], xpeer)
    for copy in copies:
        copy.wait()

    @pl.loop(0, 4)
    def _(k):
        for i in range(2):
            gq[qa, k, i, x] = (gq[qa, k, i, x].astype(F32) + r1a[k, i].astype(F32)).astype(BF16)
            gq[qb_, k, y, i] = (gq[qb_, k, y, i].astype(F32) + r1b[k, i].astype(F32)).astype(BF16)

    copies = [
        links.push(gq.at[qa, :, 1 - y, x], r2a, ypeer),
        links.push(gq.at[qb_, :, y, 1 - x], r2b, xpeer),
    ]
    gains_copy.wait()
    ggs[2] = ggs[1] + rg[1]
    gains_copy = links.push(ggs.at[2], rg.at[2], ypeer)
    for copy in copies:
        copy.wait()

    @pl.loop(0, 4)
    def _(k):
        gq[qa, k, y, x] = (gq[qa, k, y, x].astype(F32) + r2a[k].astype(F32)).astype(BF16)
        gq[qb_, k, y, x] = (gq[qb_, k, y, x].astype(F32) + r2b[k].astype(F32)).astype(BF16)

    copies = []
    for k in (2, 3, 1):
        zz = across(z, k)
        for p in range(2):
            copies.append(links.push(gq.at[2 * c + p, zz, y, x], r3.at[p, k - 1], device(zz, y, x, c)))
    gains_copy.wait()
    ggs[3] = ggs[2] + rg[2]
    for k in (2, 3, 1):
        copies.append(links.push(ggs.at[3], rg.at[2 + k], device(across(z, k), y, x, c)))

    for copy in x_copies:
        copy.wait()
    stores = []
    for a, out in enumerate((gin_out, ghid_out)):
        lb = loads.start(r2_hbm.at[a], nb)
        lb.wait()
        nout[a] = nsum[1, a].astype(F32) + nb[...].astype(F32)
        stores.append(loads.start(nout.at[a], out))

    for copy in copies:
        copy.wait()
    for p in range(2):
        total = gq[2 * c + p, z, y, x].astype(F32)
        for k in range(3):
            total = total + r3[p, k].astype(F32)
        fin[p] = total
    last = links.push(fin.at[:, pl.ds(pl.multiple_of((1 - c) * 24, 8), 24)], r4, core)
    gg_ref[...] = ggs[3] + rg[3] + rg[4] + rg[5]
    for p in range(2):
        own_ref[2 * c + p] = fin[p, pl.ds(pl.multiple_of(c * 24, 8), 24), :]
    last.wait()
    for p in range(2):
        own_ref[2 * (1 - c) + p] = r4[p]
    for copy in stores + y_copies:
        copy.wait()
    own_y.wait()
    store_gt.wait()


def tail(returned, scol, tokens_in, cotangent, hidden, qkv, context, stats, w_all, gains, segr, segc, y_rows, gin, ghid):
    tokens, width = tokens_in.shape
    slots = returned.shape[0]
    any_spec = pl.BlockSpec(memory_space=pl.ANY)
    vmem = pl.BlockSpec(memory_space=pltpu.VMEM)
    return pl.pallas_call(
        tail_kernel,
        out_shape=(
            jax.ShapeDtypeStruct((tokens, width), F32),
            jax.ShapeDtypeStruct(y_rows.shape, BF16),
            jax.ShapeDtypeStruct((2, 2) + gin.shape[1:], BF16),
            jax.ShapeDtypeStruct((2,) + gin.shape[1:], BF16),
            jax.ShapeDtypeStruct(gin.shape[1:], F32),
            jax.ShapeDtypeStruct(ghid.shape[1:], F32),
            jax.ShapeDtypeStruct((4, 24, width), F32),
            jax.ShapeDtypeStruct((8, width), F32),
        ),
        in_specs=[any_spec] * 10 + [vmem] * 5,
        out_specs=(any_spec,) * 6 + (vmem,) * 2,
        scratch_shapes=[
            pltpu.VMEM((slots, width), BF16),
            pltpu.VMEM((tokens, width), BF16),
            pltpu.VMEM((tokens, width), BF16),
            pltpu.VMEM((tokens, width), F32),
            pltpu.VMEM((tokens, 3 * width), BF16),
            pltpu.VMEM((tokens, width), BF16),
            pltpu.VMEM(w_all.shape, BF16),
            pltpu.VMEM((tokens, width), F32),
            pltpu.VMEM((tokens, width), BF16),
            pltpu.VMEM((tokens, width), BF16),
            pltpu.VMEM((tokens, 3 * width), BF16),
            pltpu.VMEM((tokens, width), BF16),
            pltpu.VMEM((16, tokens), F32),
            pltpu.VMEM((tokens, 128), F32),
            pltpu.VMEM((tokens, 128), F32),
            pltpu.VMEM((4, 4, 2, 2, 48, width), BF16),
            pltpu.VMEM((2, 4, 2, 2, 48, width), BF16),
            pltpu.VMEM((4, 2, 48, width), BF16),
            pltpu.VMEM((4, 2, 48, width), BF16),
            pltpu.VMEM((4, 48, width), BF16),
            pltpu.VMEM((4, 48, width), BF16),
            pltpu.VMEM((2, 3, 48, width), BF16),
            pltpu.VMEM((2, 48, width), F32),
            pltpu.VMEM((2, 24, width), F32),
            pltpu.VMEM((4, 8, width), F32),
            pltpu.VMEM((6, 8, width), F32),
            pltpu.VMEM(gin.shape[1:], BF16),
            pltpu.VMEM(gin.shape[1:], BF16),
            pltpu.VMEM((2, 2) + gin.shape[1:], BF16),
            pltpu.VMEM((2,) + gin.shape[1:], F32),
            pltpu.SemaphoreType.DMA((40,)),
            pltpu.SemaphoreType.DMA((40,)),
            pltpu.SemaphoreType.DMA((24,)),
        ],
        compiler_params=pltpu.CompilerParams(vmem_limit_bytes=62 << 20, collective_id=2, has_side_effects=True),
        cost_estimate=pl.CostEstimate(flops=80 << 30, bytes_accessed=40 << 20, transcendentals=0),
    )(returned, tokens_in, cotangent, hidden, qkv, context, w_all, y_rows, gin, ghid, scol, stats, gains, segr, segc)


def flipped(z, y, k):
    hi, lo = z // 2, lax.rem(z, 2)
    zz = lax.rem(hi + k // 4, 2) * 2 + lax.rem(lo + lax.rem(k // 2, 2), 2)
    return zz, lax.rem(y + lax.rem(k, 2), 2)


def swap_kernel(
    act_hbm,
    dy_hbm,
    win_hbm,
    whid_hbm,
    ret_hbm,
    y_hbm,
    gin_hbm,
    ghid_hbm,
    a_ref,
    dy_ref,
    win_ref,
    whid_ref,
    g_ref,
    du_ref,
    da_ref,
    us,
    gs,
    stage,
    send_sems,
    recv_sems,
    load_sems,
):
    z, y, x, c = place()
    me = z * 2 + y
    count, cap, width = a_ref.shape
    parts = win_ref.shape[0]
    wide = win_ref.shape[2]
    loads = Loads(load_sems)
    first = [
        loads.start(a, b)
        for a, b in (
            (act_hbm.at[me], a_ref.at[me]),
            (win_hbm, win_ref),
            (whid_hbm, whid_ref),
            (dy_hbm, dy_ref),
        )
    ]

    def partner(k):
        zz, yy = flipped(z, y, k)
        return zz * 2 + yy, device(zz, yy, x, c)

    def outward(k):
        e, to = partner(k)
        return pltpu.make_async_remote_copy(
            src_ref=act_hbm.at[e],
            dst_ref=a_ref.at[me],
            send_sem=send_sems.at[k],
            recv_sem=recv_sems.at[k],
            device_id=to,
            device_id_type=MESH,
        )

    def homeward(k):
        e, to = partner(k)
        return pltpu.make_async_remote_copy(
            src_ref=da_ref.at[e],
            dst_ref=ret_hbm.at[me],
            send_sem=send_sems.at[8 + k],
            recv_sem=recv_sems.at[8 + k],
            device_id=to,
            device_id_type=MESH,
        )

    greet([partner(k)[1] for k in range(1, 8)])
    for k in FLIPS:
        outward(k).start()
    for copy in first:
        copy.wait()

    @pl.loop(0, count)
    def _(k):
        @pl.when(k > 0)
        def _():
            outward(k).wait_recv()

        e, _to = partner(k)
        a = a_ref[e]
        dy = dy_ref[e]
        rows = pl.ds(pl.multiple_of(e * cap, cap), cap)

        def enter(j):
            us[j % 2] = dot(a, win_ref[j])
            gs[j % 2] = dot_t(dy, whid_ref[j])

        def bend(j):
            g, slope = gelu_pair(us[j % 2])
            g_ref[rows, j * wide : (j + 1) * wide] = g.astype(BF16)
            du_ref[rows, j * wide : (j + 1) * wide] = (gs[j % 2] * slope).astype(BF16)

        def leave(j):
            return dot_t(du_ref[rows, j * wide : (j + 1) * wide], win_ref[j])

        enter(0)
        total = None
        for j in range(parts):
            if j + 1 < parts:
                enter(j + 1)
            bend(j)
            if j > 0:
                term = leave(j - 1)
                total = term if total is None else total + term
        da_ref[e] = (total + leave(parts - 1)).astype(BF16)

        @pl.when(k > 0)
        def _():
            homeward(k).start()

    own = loads.start(da_ref.at[me], ret_hbm.at[me])

    def put(i, out):
        return pltpu.make_async_copy(stage.at[lax.rem(i, 2)], out, load_sems.at[8 + lax.rem(i, 2)])

    acts = a_ref[...].reshape(count * cap, width)
    dys = dy_ref[...].reshape(count * cap, width)

    @pl.loop(0, parts)
    def _(j):
        cols = pl.ds(pl.multiple_of(j * wide, wide), wide)

        @pl.when(j >= 1)
        def _():
            put(0, gin_hbm.at[j - 1]).wait()
            put(1, ghid_hbm.at[j - 1]).wait()

        stage[0] = t_dot(acts, du_ref[:, cols]).astype(BF16)
        put(0, gin_hbm.at[j]).start()
        stage[1] = t_dot(g_ref[:, cols], dys).astype(BF16)
        put(1, ghid_hbm.at[j]).start()

    @pl.loop(0, count)
    def _(i):
        rows = pl.ds(pl.multiple_of(i * cap, cap), cap)
        a_ref[i] = dot(g_ref[rows, :], whid_ref[...].reshape(parts * wide, width)).astype(BF16)

    out = loads.start(a_ref, y_hbm)
    put(0, gin_hbm.at[parts - 1]).wait()
    put(1, ghid_hbm.at[parts - 1]).wait()
    for k in range(1, 8):
        outward(k).wait_send()
        homeward(k).wait()
    own.wait()
    out.wait()


def swap(act_slots, dy_rows, w_in, w_hid):
    count, cap, width = act_slots.shape
    parts, _, wide = w_in.shape
    hidden = parts * wide
    any_spec = pl.BlockSpec(memory_space=pl.ANY)
    return pl.pallas_call(
        swap_kernel,
        out_shape=(
            jax.ShapeDtypeStruct((count, cap, width), BF16),
            jax.ShapeDtypeStruct((count, cap, width), BF16),
            jax.ShapeDtypeStruct((parts, width, wide), BF16),
            jax.ShapeDtypeStruct((parts, wide, width), BF16),
        ),
        in_specs=[any_spec] * 4,
        out_specs=(any_spec,) * 4,
        scratch_shapes=[
            pltpu.VMEM((count, cap, width), BF16),
            pltpu.VMEM((count, cap, width), BF16),
            pltpu.VMEM(w_in.shape, BF16),
            pltpu.VMEM(w_hid.shape, BF16),
            pltpu.VMEM((count * cap, hidden), BF16),
            pltpu.VMEM((count * cap, hidden), BF16),
            pltpu.VMEM((count, cap, width), BF16),
            pltpu.VMEM((2, cap, wide), F32),
            pltpu.VMEM((2, cap, wide), F32),
            pltpu.VMEM((2, width, wide), BF16),
            pltpu.SemaphoreType.DMA((16,)),
            pltpu.SemaphoreType.DMA((16,)),
            pltpu.SemaphoreType.DMA((10,)),
        ],
        compiler_params=pltpu.CompilerParams(vmem_limit_bytes=62 << 20, collective_id=1, has_side_effects=True),
        cost_estimate=pl.CostEstimate(flops=100 << 30, bytes_accessed=60 << 20, transcendentals=0),
    )(act_slots, dy_rows, w_in, w_hid)


def local(tokens, segments, routes, gate_logit, w_qkv, w_out, norm_gains, w_in, w_hid, cotangent):
    tok_count, width = tokens.shape
    n_expert = lax.axis_size("expert")
    n_narrow = lax.axis_size("narrow")
    capacity = 2 * tok_count // n_expert
    slot_rows = n_expert * capacity
    everyone = ("expert", "narrow")

    if n_expert == 8 and n_narrow == 4:
        share = w_qkv.shape[0]
        halves = jnp.concatenate((w_qkv, w_out), axis=1).reshape(share, 4, 2, width // 2)
        halves = halves.transpose(2, 0, 1, 3).reshape(2, share, 2 * width)
        gain_cols = jnp.broadcast_to(jnp.pad(norm_gains.T, ((0, 0), (0, 126))), (2, share, 128))
        shard = jnp.concatenate((halves, gain_cols), axis=2).astype(F32)
        segr = segments.reshape(1, tok_count)
        segc = segments.reshape(tok_count, 1)
        qkv, context, hidden, act_slots, w_blocks, dy_rows, w_in_all, w_hid_all, stats, scol, gains = head(
            tokens, cotangent, shard, w_in[0], w_hid[0], routes, gate_logit, segr, segc, n_expert, capacity
        )
        da_back, y_rows, gin, ghid = swap(act_slots, dy_rows, w_in_all, w_hid_all)
        grad_tokens, y_back, _r1, _r2, gin_own, ghid_own, own, gg = tail(
            da_back.reshape(slot_rows, width),
            scol,
            tokens,
            cotangent,
            hidden,
            qkv,
            context,
            stats,
            w_blocks,
            gains,
            segr,
            segc,
            y_rows,
            gin,
            ghid,
        )
        block_out = block_output(y_back.reshape(slot_rows, width), scol, hidden, gate_logit)
        me = lax.axis_index("expert") * n_narrow + lax.axis_index("narrow")
        return (
            block_out,
            grad_tokens,
            own[:3].transpose(1, 0, 2).reshape(share, 3 * width),
            own[3],
            lax.dynamic_slice_in_dim(gg[:2], me * share, share, axis=1),
            gin_own[None],
            ghid_own[None],
        )
    gain_cols = jnp.pad(norm_gains.T, ((0, 0), (0, 126)))
    w_all = lax.all_gather(
        jnp.concatenate((w_qkv, w_out, gain_cols), axis=1), everyone, axis=0, tiled=True
    )
    gains = w_all[:, 4 * width : 4 * width + 2].T.astype(F32)
    w_in_all = lax.all_gather(w_in[0], "narrow", axis=0, tiled=False)
    w_hid_all = lax.all_gather(w_hid[0], "narrow", axis=0, tiled=False)

    def exchange(values):
        return lax.all_to_all(
            values.reshape(n_expert, capacity, width), "expert", split_axis=0, concat_axis=0, tiled=True
        ).reshape(slot_rows, width)

    segr = segments.reshape(1, tok_count)
    segc = segments.reshape(tok_count, 1)
    srow, scol, dy_slots = prep(routes, gate_logit, cotangent, n_expert, capacity)
    dy_rows = exchange(dy_slots)
    qkv, context, stats, hidden, act_slots = attend_fwd(tokens, w_all, gains, segr, segc, srow, slot_rows)
    act_rows = exchange(act_slots)
    activated, grad_pre, da_rows = experts(act_rows, dy_rows, w_in_all, w_hid_all)
    da_back = exchange(da_rows)
    hidden_units = activated.shape[1]
    y_rows = dot(activated, w_hid_all.reshape(hidden_units, width)).astype(BF16)
    grad_hid = t_dot(activated, dy_rows).astype(BF16)
    grad_in = lax.dot_general(
        act_rows, grad_pre.reshape(slot_rows, n_narrow, -1), (((0,), (0,)), ((), ())), preferred_element_type=F32
    ).astype(BF16)
    y_back = exchange(y_rows)
    grad_tokens, grad_w, grad_gains = attend_bwd(
        da_back, scol, tokens, cotangent, hidden, qkv, context, stats, w_all, gains, segr, segc
    )
    block_out = block_output(y_back, scol, hidden, gate_logit)
    grad_hid_w = lax.psum_scatter(grad_hid, "narrow", scatter_dimension=0, tiled=True).astype(F32)[None]
    grad_in_w = lax.psum_scatter(grad_in, "narrow", scatter_dimension=1, tiled=True).astype(F32)
    grad_in_w = grad_in_w.reshape(1, width, -1)
    packed = jnp.concatenate((grad_w, jnp.pad(grad_gains[:2].T, ((0, 0), (0, 126)))), axis=1)
    own = lax.psum_scatter(packed, everyone, scatter_dimension=0, tiled=True)
    return (
        block_out,
        grad_tokens,
        own[:, : 3 * width],
        own[:, 3 * width : 4 * width],
        own[:, 4 * width : 4 * width + 2].T,
        grad_in_w,
        grad_hid_w,
    )


def solution(mesh):
    placed = (
        P(("expert", "narrow"), None),
        P(("expert", "narrow"), None),
        P(("expert", "narrow"), None),
        P(("expert", "narrow")),
        P(("expert", "narrow"), None),
        P(("expert", "narrow"), None),
        P(None, ("expert", "narrow")),
        P("expert", None, "narrow"),
        P("expert", "narrow", None),
        P(("expert", "narrow"), None),
    )
    return jax.shard_map(
        local,
        mesh=mesh,
        in_specs=placed,
        out_specs=(
            P(("expert", "narrow"), None),
            P(("expert", "narrow"), None),
            P(("expert", "narrow"), None),
            P(("expert", "narrow"), None),
            P(None, ("expert", "narrow")),
            P("expert", None, "narrow"),
            P("expert", "narrow", None),
        ),
        check_vma=False,
    )
```

```python
import functools

import jax
import jax.numpy as jnp
from jax import lax
from jax.experimental import pallas as pl
from jax.experimental.pallas import tpu as pltpu
from jax.sharding import PartitionSpec as P

HEAD_DIM = 64
SEQ = 1024
BLOCK = 256
LOOKBACK = 2
EPSILON = 1e-05
BIG_NEGATIVE = -1e30
F32 = jnp.float32
BF16 = jnp.bfloat16

TAIL_P = 0.3
TAIL_C = (
    0.11962923306946524,
    0.12075497050525577,
    0.0999071263144056,
    0.12858273368127124,
    -0.053723704944995426,
    0.20639718480180155,
    -0.1572285075725372,
    0.03568089149479804,
)


def dot(a, b):
    return lax.dot_general(a, b, (((1,), (0,)), ((), ())), preferred_element_type=F32)


def dot_t(a, b):
    return lax.dot_general(a, b, (((1,), (1,)), ((), ())), preferred_element_type=F32)


def t_dot(a, b):
    return lax.dot_general(a, b, (((0,), (0,)), ((), ())), preferred_element_type=F32)


def normalize(values):
    centre = jnp.mean(values, axis=-1, keepdims=True)
    shifted = values - centre
    factor = lax.rsqrt(jnp.mean(shifted * shifted, axis=-1, keepdims=True) + EPSILON)
    return shifted * factor, factor


def norm_back(grad_normed, normed, factor):
    return factor * (
        grad_normed
        - jnp.mean(grad_normed, axis=-1, keepdims=True)
        - normed * jnp.mean(grad_normed * normed, axis=-1, keepdims=True)
    )


def gelu_pair(u):
    size = jnp.abs(u)
    t = 1.0 / (1.0 + TAIL_P * size)
    poly = jnp.full_like(t, TAIL_C[-1])
    for c in TAIL_C[-2::-1]:
        poly = poly * t + c
    bell = jnp.exp(-0.5 * (u * u))
    tail = poly * t * bell
    phi = jnp.where(u >= 0, 1.0 - tail, tail)
    return u * phi, phi + u * (bell * 0.3989422804014327)


def iota(shape, dim):
    return lax.broadcasted_iota(jnp.int32, shape, dim)


def prep_kernel(capacity, experts, rrow_ref, rcol_ref, gate_ref, ct_ref, srow_ref, scol_ref, send_ref):
    tokens = ct_ref.shape[0]
    wide = max(8, experts)
    hot = (iota((wide, tokens), 0) == rrow_ref[...]).astype(F32)
    before = (iota((tokens, tokens), 0) < iota((tokens, tokens), 1)).astype(BF16)
    rank = dot(hot.astype(BF16), before)
    base = (iota((wide, tokens), 0) * capacity).astype(F32)
    srow = jnp.sum(hot * (rank + base), axis=0, keepdims=True)
    srow_ref[...] = jnp.broadcast_to(srow, srow_ref.shape)
    hot_c = (iota((tokens, 128), 1) == rcol_ref[...]).astype(F32)
    after = (iota((tokens, tokens), 1) < iota((tokens, tokens), 0)).astype(BF16)
    rank_c = dot(after, hot_c.astype(BF16))
    base_c = (iota((tokens, 128), 1) * capacity).astype(F32)
    scol_ref[...] = jnp.sum(hot_c * (rank_c + base_c), axis=1, keepdims=True)
    gated = (jax.nn.sigmoid(gate_ref[...]) * ct_ref[...].astype(F32)).astype(BF16)
    fill_slots(srow, gated, send_ref)


def fill_slots(srow, values, send_ref):
    rows = send_ref.shape[0]
    tokens = values.shape[0]

    @pl.loop(0, rows // BLOCK)
    def _(i):
        first = i * BLOCK
        ids = (iota((BLOCK, tokens), 0) + first).astype(F32)
        pick = (ids == srow).astype(BF16)
        send_ref[pl.ds(pl.multiple_of(first, BLOCK), BLOCK), :] = dot(pick, values).astype(BF16)


def prep(routes, gate_logit, cotangent, experts, capacity):
    tokens, width = cotangent.shape
    return pl.pallas_call(
        functools.partial(prep_kernel, capacity, experts),
        out_shape=(
            jax.ShapeDtypeStruct((8, tokens), F32),
            jax.ShapeDtypeStruct((tokens, 1), F32),
            jax.ShapeDtypeStruct((experts * capacity, width), BF16),
        ),
        compiler_params=pltpu.CompilerParams(vmem_limit_bytes=56 << 20),
        cost_estimate=pl.CostEstimate(flops=8 << 30, bytes_accessed=8 << 20, transcendentals=0),
    )(routes.reshape(1, tokens), routes, gate_logit.reshape(tokens, 1), cotangent)


def fwd_kernel(
    x_ref, w_ref, gain_ref, segr_ref, segc_ref, srow_ref, qkv_ref, c_ref, stat_ref, h_ref, send_ref, act_scr, bias_scr, col_scr
):
    tokens, width = x_ref.shape
    blocks = tokens // BLOCK
    pairs = width // 128
    gain_one = gain_ref[0:1, :]
    gain_two = gain_ref[1:2, :]

    @pl.loop(0, blocks)
    def _(i):
        rows = pl.ds(pl.multiple_of(i * BLOCK, BLOCK), BLOCK)
        normed, _f = normalize(x_ref[rows, :].astype(F32))
        act = (normed * gain_one).astype(BF16)
        qkv_ref[rows, :] = dot(act, w_ref[:, : 3 * width]).astype(BF16)

    col_scr[...] = jnp.zeros_like(col_scr)
    low = iota((BLOCK, 128), 1) < HEAD_DIM
    for qb in range(blocks):
        kb = max(0, qb - LOOKBACK)
        span = (qb - kb + 1) * BLOCK
        rows = pl.ds(qb * BLOCK, BLOCK)
        keys = pl.ds(kb * BLOCK, span)
        q_pos = iota((BLOCK, span), 0) + qb * BLOCK
        k_pos = iota((BLOCK, span), 1) + kb * BLOCK
        ok = (k_pos <= q_pos) & (segc_ref[rows, :] == segr_ref[0:1, keys])
        bias_scr[:, :span] = jnp.where(ok, 0.0, BIG_NEGATIVE)

        @pl.loop(0, pairs)
        def _(hp):
            at = pl.multiple_of(hp * 128, 128)
            q = qkv_ref[rows, pl.ds(at, 128)] * jnp.asarray(HEAD_DIM**-0.5, BF16)
            k = qkv_ref[keys, pl.ds(width + at, 128)]
            v = qkv_ref[keys, pl.ds(2 * width + at, 128)]
            outs = []
            col = col_scr[rows, :]
            for half in range(2):
                mine = low if half == 0 else ~low
                s = dot_t(jnp.where(mine, q, 0), k) + bias_scr[:, :span]
                top = jnp.max(s, axis=1, keepdims=True)
                raised = jnp.exp(s - top)
                total = jnp.sum(raised, axis=1, keepdims=True)
                outs.append(dot((raised * (1.0 / total)).astype(BF16), v))
                col = jnp.where(iota((BLOCK, 128), 1) == 2 * hp + half, top + jnp.log(total), col)
            col_scr[rows, :] = col
            c_ref[rows, pl.ds(at, 128)] = jnp.where(low, outs[0], outs[1]).astype(BF16)

    stat_ref[...] = col_scr[...].T

    @pl.loop(0, blocks)
    def _(i):
        rows = pl.ds(pl.multiple_of(i * BLOCK, BLOCK), BLOCK)
        hidden = x_ref[rows, :].astype(F32) + dot(c_ref[rows, :], w_ref[:, 3 * width : 4 * width])
        h_ref[rows, :] = hidden
        normed, _f = normalize(hidden)
        act_scr[rows, :] = (normed * gain_two).astype(BF16)

    fill_slots(srow_ref[0:1, :], act_scr[...], send_ref)


def attend_fwd(tokens_in, w_all, gains, segr, segc, srow, slot_rows):
    tokens, width = tokens_in.shape
    return pl.pallas_call(
        fwd_kernel,
        out_shape=(
            jax.ShapeDtypeStruct((tokens, 3 * width), BF16),
            jax.ShapeDtypeStruct((tokens, width), BF16),
            jax.ShapeDtypeStruct((128, tokens), F32),
            jax.ShapeDtypeStruct((tokens, width), F32),
            jax.ShapeDtypeStruct((slot_rows, width), BF16),
        ),
        scratch_shapes=[
            pltpu.VMEM((tokens, width), BF16),
            pltpu.VMEM((BLOCK, (LOOKBACK + 1) * BLOCK), F32),
            pltpu.VMEM((tokens, 128), F32),
        ],
        compiler_params=pltpu.CompilerParams(vmem_limit_bytes=56 << 20),
        cost_estimate=pl.CostEstimate(flops=40 << 30, bytes_accessed=24 << 20, transcendentals=0),
    )(tokens_in, w_all, gains, segr, segc, srow)


def expert_kernel(a_ref, dy_ref, win_ref, whid_ref, g_ref, du_ref, da_ref, acc_scr):
    a = a_ref[...]
    dy = dy_ref[...]
    parts = win_ref.shape[0]
    wide = win_ref.shape[2]
    acc_scr[...] = jnp.zeros_like(acc_scr)

    @pl.loop(0, parts)
    def _(j):
        cols = pl.ds(pl.multiple_of(j * wide, wide), wide)
        u = dot(a, win_ref[j])
        grad = dot_t(dy, whid_ref[j])
        g, slope = gelu_pair(u)
        g_ref[:, cols] = g.astype(BF16)
        du = (grad * slope).astype(BF16)
        du_ref[:, cols] = du
        acc_scr[...] += dot_t(du, win_ref[j])

    da_ref[...] = acc_scr[...].astype(BF16)


def experts(acts, grads, w_in, w_hid):
    rows, width = acts.shape
    parts, _, wide = w_in.shape
    hidden = parts * wide
    row_spec = pl.BlockSpec((BLOCK, width), lambda i: (i, 0))
    wide_spec = pl.BlockSpec((BLOCK, hidden), lambda i: (i, 0))
    return pl.pallas_call(
        expert_kernel,
        grid=(rows // BLOCK,),
        out_shape=(
            jax.ShapeDtypeStruct((rows, hidden), BF16),
            jax.ShapeDtypeStruct((rows, hidden), BF16),
            jax.ShapeDtypeStruct((rows, width), BF16),
        ),
        in_specs=[
            row_spec,
            row_spec,
            pl.BlockSpec(w_in.shape, lambda i: (0, 0, 0), pipeline_mode=pl.Buffered(1)),
            pl.BlockSpec(w_hid.shape, lambda i: (0, 0, 0), pipeline_mode=pl.Buffered(1)),
        ],
        out_specs=(wide_spec, wide_spec, row_spec),
        scratch_shapes=[pltpu.VMEM((BLOCK, width), F32)],
        compiler_params=pltpu.CompilerParams(vmem_limit_bytes=56 << 20),
        cost_estimate=pl.CostEstimate(flops=60 << 30, bytes_accessed=40 << 20, transcendentals=0),
    )(acts, grads, w_in, w_hid)


def out_kernel(ret_ref, scol_ref, h_ref, gate_ref, out_ref):
    tokens, rows = out_ref.shape[0], ret_ref.shape[0]
    pick = (iota((tokens, rows), 1).astype(F32) == scol_ref[...]).astype(BF16)
    y = dot(pick, ret_ref[...])
    out_ref[...] = (h_ref[...] + jax.nn.sigmoid(gate_ref[...]) * y).astype(BF16)


def block_output(returned, scol, hidden, gate_logit):
    rows, width = returned.shape
    tokens = hidden.shape[0]
    tile = pl.BlockSpec((BLOCK, width), lambda i: (i, 0))
    column = pl.BlockSpec((BLOCK, 1), lambda i: (i, 0))
    return pl.pallas_call(
        out_kernel,
        grid=(tokens // BLOCK,),
        out_shape=jax.ShapeDtypeStruct((tokens, width), BF16),
        in_specs=[pl.BlockSpec((rows, width), lambda i: (0, 0)), column, tile, column],
        out_specs=tile,
        compiler_params=pltpu.CompilerParams(vmem_limit_bytes=40 << 20),
        cost_estimate=pl.CostEstimate(flops=4 << 30, bytes_accessed=10 << 20, transcendentals=0),
    )(returned, scol, hidden, gate_logit.reshape(tokens, 1))


def bwd_kernel(
    ret_ref,
    scol_ref,
    x_ref,
    ct_ref,
    h_ref,
    qkv_ref,
    c_ref,
    stat_ref,
    w_ref,
    gain_ref,
    segr_ref,
    segc_ref,
    gt_ref,
    gw_ref,
    gg_ref,
    dc_scr,
    dhb_scr,
    dqkv_scr,
    act_scr,
    d_scr,
    dk_scr,
    dv_scr,
):
    tokens, width = x_ref.shape
    slots = ret_ref.shape[0]
    blocks = tokens // BLOCK
    pairs = width // 128
    gain_one = gain_ref[0:1, :]
    gain_two = gain_ref[1:2, :]
    gg_ref[...] = jnp.zeros_like(gg_ref)
    member = (iota((16, width), 1) // HEAD_DIM == iota((16, width), 0)).astype(F32)

    for i in range(blocks):
        rows = pl.ds(i * BLOCK, BLOCK)
        pick = (iota((BLOCK, slots), 1).astype(F32) == scol_ref[rows, :]).astype(BF16)
        da = dot(pick, ret_ref[...])
        normed, factor = normalize(h_ref[rows, :])
        gg_ref[1:2, :] += jnp.sum(da * normed, axis=0, keepdims=True)
        dh = ct_ref[rows, :].astype(F32) + norm_back(da * gain_two, normed, factor)
        gt_ref[rows, :] = dh
        dhb = dh.astype(BF16)
        dhb_scr[rows, :] = dhb
        dc = dot_t(dhb, w_ref[:, 3 * width : 4 * width]).astype(BF16)
        dc_scr[rows, :] = dc
        d_scr[:, rows] = lax.dot_general(
            member,
            dc.astype(F32) * c_ref[rows, :].astype(F32),
            (((1,), (1,)), ((), ())),
            precision=lax.Precision.HIGHEST,
            preferred_element_type=F32,
        )

    gw_ref[:, 3 * width : 4 * width] = t_dot(c_ref[...], dhb_scr[...])
    low = iota((BLOCK, 128), 1) < HEAD_DIM
    scale = HEAD_DIM**-0.5

    @pl.loop(0, pairs)
    def _(hp):
        at = pl.multiple_of(hp * 128, 128)
        dk_scr[...] = jnp.zeros_like(dk_scr)
        dv_scr[...] = jnp.zeros_like(dv_scr)
        for qb in range(blocks):
            rows = pl.ds(qb * BLOCK, BLOCK)
            q = qkv_ref[rows, pl.ds(at, 128)] * jnp.asarray(scale, BF16)
            dc = dc_scr[rows, pl.ds(at, 128)]
            q_half = [jnp.where(low, q, 0), jnp.where(low, 0, q)]
            dc_half = [jnp.where(low, dc, 0), jnp.where(low, 0, dc)]
            dq = jnp.zeros((BLOCK, 128), F32)
            for kb in range(max(0, qb - LOOKBACK), qb + 1):
                keys = pl.ds(kb * BLOCK, BLOCK)
                k = qkv_ref[keys, pl.ds(width + at, 128)]
                v = qkv_ref[keys, pl.ds(2 * width + at, 128)]
                ok = segc_ref[keys, :] == segr_ref[0:1, rows]
                if kb == qb:
                    ok = ok & (iota((BLOCK, BLOCK), 0) <= iota((BLOCK, BLOCK), 1))
                ps, dss = [], []
                for half in range(2):
                    s = dot_t(k, q_half[half])
                    p = jnp.where(ok, jnp.exp(s - stat_ref[pl.ds(2 * hp + half, 1), rows]), 0.0)
                    dp = dot_t(v, dc_half[half])
                    dss.append((p * (dp - d_scr[pl.ds(2 * hp + half, 1), rows])).astype(BF16))
                    ps.append(p.astype(BF16))
                dv_scr[keys, :] += dot(jnp.concatenate(ps, 1), jnp.concatenate(dc_half, 0))
                dk_scr[keys, :] += dot(jnp.concatenate(dss, 1), jnp.concatenate(q_half, 0))
                dq += jnp.where(low, t_dot(dss[0], k), t_dot(dss[1], k))
            dqkv_scr[rows, pl.ds(at, 128)] = (dq * scale).astype(BF16)
        dqkv_scr[:, pl.ds(width + at, 128)] = dk_scr[...].astype(BF16)
        dqkv_scr[:, pl.ds(2 * width + at, 128)] = dv_scr[...].astype(BF16)

    @pl.loop(0, blocks)
    def _(i):
        rows = pl.ds(pl.multiple_of(i * BLOCK, BLOCK), BLOCK)
        normed, factor = normalize(x_ref[rows, :].astype(F32))
        act_scr[rows, :] = (normed * gain_one).astype(BF16)
        dn = dot_t(dqkv_scr[rows, :], w_ref[:, : 3 * width])
        gg_ref[0:1, :] += jnp.sum(dn * normed, axis=0, keepdims=True)
        gt_ref[rows, :] += norm_back(dn * gain_one, normed, factor)

    gw_ref[:, : 3 * width] = t_dot(act_scr[...], dqkv_scr[...])


def attend_bwd(returned, scol, tokens_in, cotangent, hidden, qkv, context, stats, w_all, gains, segr, segc):
    tokens, width = tokens_in.shape
    return pl.pallas_call(
        bwd_kernel,
        out_shape=(
            jax.ShapeDtypeStruct((tokens, width), F32),
            jax.ShapeDtypeStruct((width, 4 * width), F32),
            jax.ShapeDtypeStruct((8, width), F32),
        ),
        scratch_shapes=[
            pltpu.VMEM((tokens, width), BF16),
            pltpu.VMEM((tokens, width), BF16),
            pltpu.VMEM((tokens, 3 * width), BF16),
            pltpu.VMEM((tokens, width), BF16),
            pltpu.VMEM((16, tokens), F32),
            pltpu.VMEM((tokens, 128), F32),
            pltpu.VMEM((tokens, 128), F32),
        ],
        compiler_params=pltpu.CompilerParams(vmem_limit_bytes=60 << 20),
        cost_estimate=pl.CostEstimate(flops=80 << 30, bytes_accessed=40 << 20, transcendentals=0),
    )(returned, scol, tokens_in, cotangent, hidden, qkv, context, stats, w_all, gains, segr, segc)


MESH = pl.DeviceIdType.MESH


def place():
    e, n = lax.axis_index("expert"), lax.axis_index("narrow")
    return e // 2, lax.rem(e, 2), n // 2, lax.rem(n, 2)


def device(z, y, x, c):
    return (z * 2 + y, x * 2 + c)


def across(z, k):
    hi, lo = z // 2, lax.rem(z, 2)
    hi = 1 - hi if k & 2 else hi
    lo = 1 - lo if k & 1 else lo
    return hi * 2 + lo


class Links:
    def __init__(self, send, recv):
        self.send, self.recv, self.used = send, recv, 0

    def make(self, src, dst, to):
        i = self.used
        self.used += 1
        return pltpu.make_async_remote_copy(
            src_ref=src, dst_ref=dst, send_sem=self.send.at[i], recv_sem=self.recv.at[i], device_id=to, device_id_type=MESH
        )

    def push(self, src, dst, to):
        copy = self.make(src, dst, to)
        copy.start()
        return copy


class Loads:
    def __init__(self, sems):
        self.sems, self.used = sems, 0

    def start(self, src, dst):
        copy = pltpu.make_async_copy(src, dst, self.sems.at[self.used])
        self.used += 1
        copy.start()
        return copy


def greet(peers):
    barrier = pltpu.get_barrier_semaphore()
    for peer in peers:
        pl.semaphore_signal(barrier, inc=1, device_id=peer, device_id_type=MESH)
    pl.semaphore_wait(barrier, len(peers))


FLIPS = (1, 2, 3, 4, 5, 6, 7)


def peers_of(z, y, x, c):
    return [device(across(z, k >> 1), 1 - y if k & 1 else y, x, c) for k in FLIPS]


def weight(blocks, first, count):
    half = blocks.shape[-1]
    rows = blocks.shape[1] * blocks.shape[2] * blocks.shape[3] * blocks.shape[4]
    return jnp.concatenate([blocks[b].reshape(rows, half) for b in range(first, first + count)], axis=1)


def head_kernel(
    capacity,
    experts,
    x_hbm,
    ct_hbm,
    shard_hbm,
    win_hbm,
    whid_hbm,
    row_ref,
    qkv_hbm,
    c_hbm,
    h_hbm,
    act_hbm,
    w_hbm,
    dyrow_hbm,
    win4_hbm,
    whid4_hbm,
    stat_ref,
    col_ref,
    gain_ref,
    x_ref,
    ct_ref,
    st,
    wq,
    wg,
    qkv_ref,
    c_ref,
    h_ref,
    a_scr,
    act_ref,
    dy_ref,
    bias_scr,
    col_scr,
    send_sems,
    recv_sems,
    load_sems,
):
    z, y, x, c = place()
    me_e = z * 2 + y
    me_n = x * 2 + c
    tokens, width = x_ref.shape
    blocks = tokens // BLOCK
    pairs = width // 128
    half = width // 2
    core, xpeer, ypeer = device(z, y, x, 1 - c), device(z, y, 1 - x, c), device(z, 1 - y, x, c)
    links = Links(send_sems, recv_sems)
    loads = Loads(load_sems)
    loading_ct = loads.start(ct_hbm, ct_ref)
    loading_x = loads.start(x_hbm, x_ref)
    own_shard = loads.start(shard_hbm.at[c], st.at[c])

    greet(peers_of(z, y, x, c) + [core, xpeer])
    zero = links.push(shard_hbm.at[1 - c], st.at[c], core)

    deep = width // 2
    upper, lower = pl.ds(0, deep), pl.ds(deep, deep)

    def hand(src, dst, rows):
        return links.push(src.at[rows], dst.at[me_n, rows], xpeer)

    def onward(dst, rows):
        part = dst.at[(1 - x) * 2 + c, rows]
        return links.push(part, part, core)

    parts = [(hand(win_hbm, win4_hbm, upper), win4_hbm, upper)]

    wide = max(8, experts)
    hot = (iota((wide, tokens), 0).astype(F32) == row_ref[0:1, :]).astype(F32)
    before = (iota((tokens, tokens), 0) < iota((tokens, tokens), 1)).astype(BF16)
    rank = dot(hot.astype(BF16), before)
    base = (iota((wide, tokens), 0) * capacity).astype(F32)
    srow = jnp.sum(hot * (rank + base), axis=0, keepdims=True)

    zero.wait()
    own_shard.wait()
    rows48 = jnp.concatenate((st[0], st[1]), axis=0)
    for j in range(4):
        wq[2 * j + c, z, y, x] = rows48[:, j * half : (j + 1) * half].astype(BF16)
    wg[z, y, x] = rows48[:, 4 * half :].astype(BF16)
    ring_z = []
    for piece in range(2):
        group = []
        for k in (1, 2, 3):
            to = device(across(z, k), y, x, c)
            for j in (2 * piece, 2 * piece + 1):
                part = wq.at[2 * j + c, z, y, x]
                group.append(links.push(part, part, to))
            if piece == 0:
                group.append(links.push(wg.at[z, y, x], wg.at[z, y, x], to))
        ring_z.append(group)

    listed = row_ref[...].T
    hot_c = (iota((tokens, 128), 1).astype(F32) == listed[:, 0:1]).astype(F32)
    after = (iota((tokens, tokens), 1) < iota((tokens, tokens), 0)).astype(BF16)
    rank_c = dot(after, hot_c.astype(BF16))
    base_c = (iota((tokens, 128), 1) * capacity).astype(F32)
    scol = jnp.sum(hot_c * (rank_c + base_c), axis=1, keepdims=True)
    col_ref[...] = jnp.where(iota(listed.shape, 1) == 0, scol, listed)

    def fill(values, out):
        @pl.loop(0, out.shape[0])
        def _(i):
            ids = (iota((capacity, tokens), 0) + i * capacity).astype(F32)
            out[i] = dot((ids == srow).astype(BF16), values).astype(BF16)

    loading_ct.wait()
    fill((jax.nn.sigmoid(listed[:, 1:2]) * ct_ref[...].astype(F32)).astype(BF16), dy_ref)

    dy_copies = []
    for k in FLIPS:
        zz, yy = across(z, k >> 1), (1 - y if k & 1 else y)
        dy_copies.append(links.push(dy_ref.at[zz * 2 + yy], dyrow_hbm.at[me_e], device(zz, yy, x, c)))
    own_dy = loads.start(dy_ref.at[me_e], dyrow_hbm.at[me_e])
    ring_2 = []
    for piece in range(2):
        for copy in ring_z[piece]:
            copy.wait()
        ja, jb = 2 * (2 * piece) + c, 2 * (2 * piece + 1) + c
        group = [
            links.push(wq.at[ja, :, y, x], wq.at[ja, :, y, x], ypeer),
            links.push(wq.at[jb, :, y, x], wq.at[jb, :, y, x], xpeer),
        ]
        if piece == 0:
            group.append(links.push(wg.at[:, y, x], wg.at[:, y, x], ypeer))
        ring_2.append(group)
    ring_3 = []
    for piece in range(2):
        for copy in ring_2[piece]:
            copy.wait()
        ja, jb = 2 * (2 * piece) + c, 2 * (2 * piece + 1) + c
        group = [
            links.push(wq.at[ja, :, :, x], wq.at[ja, :, :, x], xpeer),
            links.push(wq.at[jb, :, y], wq.at[jb, :, y], ypeer),
        ]
        if piece == 0:
            group.append(links.push(wg.at[:, :, x], wg.at[:, :, x], xpeer))
        ring_3.append(group)
    for src, dst, rows in ((win_hbm, win4_hbm, lower), (whid_hbm, whid4_hbm, upper), (whid_hbm, whid4_hbm, lower)):
        parts.append((hand(src, dst, rows), dst, rows))
    ring_4 = []
    for piece in range(2):
        for copy in ring_3[piece]:
            copy.wait()
        ring_4.append([links.push(wq.at[2 * j + c], wq.at[2 * j + c], core) for j in (2 * piece, 2 * piece + 1)])

    gains = jnp.transpose(wg[...].reshape(width, 128).astype(F32))[0:8, :]
    gain_ref[...] = gains
    gain_one = gains[0:1, :]
    gain_two = gains[1:2, :]
    loading_x.wait()
    for piece in range(2):
        for copy in ring_4[piece]:
            copy.wait()
    storing = [loads.start(wq, w_hbm)]
    core_slices = [links.push(src, dst.at[me_n], core) for src, dst in ((win_hbm, win4_hbm), (whid_hbm, whid4_hbm))]

    def pass_on(i):
        copy, dst, rows = parts[i]
        copy.wait()
        core_slices.append(onward(dst, rows))

    pass_on(0)

    @pl.loop(0, blocks)
    def _(i):
        rows = pl.ds(pl.multiple_of(i * BLOCK, BLOCK), BLOCK)
        normed, _f = normalize(x_ref[rows, :].astype(F32))
        act = (normed * gain_one).astype(BF16)
        qkv_ref[rows, :] = dot(act, weight(wq, 0, 6)).astype(BF16)

    storing.append(loads.start(qkv_ref, qkv_hbm))
    col_scr[...] = jnp.zeros_like(col_scr)
    low = iota((BLOCK, 128), 1) < HEAD_DIM
    for qb in range(blocks):
        kb = max(0, qb - LOOKBACK)
        span = (qb - kb + 1) * BLOCK
        rows = pl.ds(qb * BLOCK, BLOCK)
        keys = pl.ds(kb * BLOCK, span)
        q_pos = iota((BLOCK, span), 0) + qb * BLOCK
        k_pos = iota((BLOCK, span), 1) + kb * BLOCK
        ok = (k_pos <= q_pos) & (col_ref[rows, 2:3] == row_ref[2:3, keys])
        bias_scr[:, :span] = jnp.where(ok, 0.0, BIG_NEGATIVE)

        @pl.loop(0, pairs)
        def _(hp):
            at = pl.multiple_of(hp * 128, 128)
            q = qkv_ref[rows, pl.ds(at, 128)] * jnp.asarray(HEAD_DIM**-0.5, BF16)
            k = qkv_ref[keys, pl.ds(width + at, 128)]
            v = qkv_ref[keys, pl.ds(2 * width + at, 128)]
            outs = []
            col = col_scr[rows, :]
            for side in range(2):
                mine = low if side == 0 else ~low
                s = dot_t(jnp.where(mine, q, 0), k) + bias_scr[:, :span]
                top = jnp.max(s, axis=1, keepdims=True)
                raised = jnp.exp(s - top)
                total = jnp.sum(raised, axis=1, keepdims=True)
                outs.append(dot((raised * (1.0 / total)).astype(BF16), v))
                col = jnp.where(iota((BLOCK, 128), 1) == 2 * hp + side, top + jnp.log(total), col)
            col_scr[rows, :] = col
            c_ref[rows, pl.ds(at, 128)] = jnp.where(low, outs[0], outs[1]).astype(BF16)

    storing.append(loads.start(c_ref, c_hbm))
    stat_ref[...] = col_scr[...].T

    @pl.loop(0, blocks)
    def _(i):
        rows = pl.ds(pl.multiple_of(i * BLOCK, BLOCK), BLOCK)
        hidden = x_ref[rows, :].astype(F32) + dot(c_ref[rows, :], weight(wq, 6, 2))
        h_ref[rows, :] = hidden
        normed, _f = normalize(hidden)
        a_scr[rows, :] = (normed * gain_two).astype(BF16)

    storing.append(loads.start(h_ref, h_hbm))
    fill(a_scr[...], act_ref)
    storing.append(loads.start(act_ref, act_hbm))
    for i in range(1, 4):
        pass_on(i)
    for copy in storing + [own_dy] + core_slices + dy_copies:
        copy.wait()


def head(tokens_in, cotangent, shard, w_in, w_hid, listed, experts, capacity):
    tokens, width = tokens_in.shape
    any_spec = pl.BlockSpec(memory_space=pl.ANY)
    vmem = pl.BlockSpec(memory_space=pltpu.VMEM)
    slots = (experts, capacity, width)
    blocks = (8, 4, 2, 2, 48, width // 2)
    return pl.pallas_call(
        functools.partial(head_kernel, capacity, experts),
        out_shape=(
            jax.ShapeDtypeStruct((tokens, 3 * width), BF16),
            jax.ShapeDtypeStruct((tokens, width), BF16),
            jax.ShapeDtypeStruct((tokens, width), F32),
            jax.ShapeDtypeStruct(slots, BF16),
            jax.ShapeDtypeStruct(blocks, BF16),
            jax.ShapeDtypeStruct(slots, BF16),
            jax.ShapeDtypeStruct((4,) + w_in.shape, BF16),
            jax.ShapeDtypeStruct((4,) + w_hid.shape, BF16),
            jax.ShapeDtypeStruct((128, tokens), F32),
            jax.ShapeDtypeStruct((tokens, 8), F32),
            jax.ShapeDtypeStruct((8, width), F32),
        ),
        in_specs=[any_spec] * 5 + [vmem],
        out_specs=(any_spec,) * 8 + (vmem,) * 3,
        scratch_shapes=[
            pltpu.VMEM((tokens, width), BF16),
            pltpu.VMEM((tokens, width), BF16),
            pltpu.VMEM(shard.shape, F32),
            pltpu.VMEM(blocks, BF16),
            pltpu.VMEM((4, 2, 2, 48, 128), BF16),
            pltpu.VMEM((tokens, 3 * width), BF16),
            pltpu.VMEM((tokens, width), BF16),
            pltpu.VMEM((tokens, width), F32),
            pltpu.VMEM((tokens, width), BF16),
            pltpu.VMEM(slots, BF16),
            pltpu.VMEM(slots, BF16),
            pltpu.VMEM((BLOCK, (LOOKBACK + 1) * BLOCK), F32),
            pltpu.VMEM((tokens, 128), F32),
            pltpu.SemaphoreType.DMA((48,)),
            pltpu.SemaphoreType.DMA((48,)),
            pltpu.SemaphoreType.DMA((16,)),
        ],
        compiler_params=pltpu.CompilerParams(vmem_limit_bytes=62 << 20, collective_id=0, has_side_effects=True),
        cost_estimate=pl.CostEstimate(flops=60 << 30, bytes_accessed=40 << 20, transcendentals=0),
    )(tokens_in, cotangent, shard, w_in, w_hid, listed)


class Reduce:
    def __init__(self, spot, ph, gq, rc, r1, r2, r3, fin, r4, send_sems, recv_sems):
        self.z, self.y, self.x, self.c = spot
        self.gq, self.rc, self.r1, self.r2, self.r3, self.fin, self.r4 = (
            gq.at[ph],
            rc.at[ph],
            r1.at[ph],
            r2.at[ph],
            r3.at[ph],
            fin.at[ph],
            r4.at[ph],
        )
        self.base = ph * 7
        self.send, self.recv = send_sems, recv_sems

    def copy(self, i, src, dst, to):
        return pltpu.make_async_remote_copy(
            src_ref=src,
            dst_ref=dst,
            send_sem=self.send.at[self.base + i],
            recv_sem=self.recv.at[self.base + i],
            device_id=to,
            device_id_type=MESH,
        )

    def turn(self, i):
        return i * (1 - self.c) + self.y * self.c, self.x * (1 - self.c) + i * self.c

    def add(self, where, term):
        self.gq[where] = (self.gq[where].astype(F32) + term.astype(F32)).astype(BF16)

    def cores(self):
        z, y, x, c = self.z, self.y, self.x, self.c
        return self.copy(0, self.gq.at[1 - c], self.rc, device(z, y, x, 1 - c))

    def by_core(self, go, first, second):
        @pl.when(self.c == 0)
        def _():
            go(first)

        @pl.when(self.c == 1)
        def _():
            go(second)

    def one(self, go):
        z, y, x, c = self.z, self.y, self.x, self.c
        self.by_core(
            go,
            self.copy(1, self.gq.at[0, :, :, 1 - x], self.r1, device(z, y, 1 - x, c)),
            self.copy(1, self.gq.at[1, :, 1 - y], self.r1, device(z, 1 - y, x, c)),
        )

    def two(self, go):
        z, y, x, c = self.z, self.y, self.x, self.c
        self.by_core(
            go,
            self.copy(2, self.gq.at[0, :, 1 - y, x], self.r2, device(z, 1 - y, x, c)),
            self.copy(2, self.gq.at[1, :, y, 1 - x], self.r2, device(z, y, 1 - x, c)),
        )

    def three(self):
        z, y, x, c = self.z, self.y, self.x, self.c
        return [
            self.copy(2 + k, self.gq.at[c, across(z, k), y, x], self.r3.at[k - 1], device(across(z, k), y, x, c))
            for k in (1, 2, 3)
        ]

    def four(self):
        z, y, x, c = self.z, self.y, self.x, self.c
        rows = pl.ds(pl.multiple_of((1 - c) * 24, 8), 24)
        return self.copy(6, self.fin.at[rows], self.r4, device(z, y, x, 1 - c))

    def step(self, stage):
        z, y, x, c = self.z, self.y, self.x, self.c
        if stage == 0:
            self.cores().start()
        if stage == 1:
            self.cores().wait()

            @pl.loop(0, 4)
            def _(k):
                self.add((c, k), self.rc[k])

            self.one(lambda copy: copy.start())
        if stage == 2:
            self.one(lambda copy: copy.wait())

            @pl.loop(0, 4)
            def _(k):
                for i in range(2):
                    yy, xx = self.turn(i)
                    self.add((c, k, yy, xx), self.r1[k, i])

            self.two(lambda copy: copy.start())
        if stage == 3:
            self.two(lambda copy: copy.wait())

            @pl.loop(0, 4)
            def _(k):
                self.add((c, k, y, x), self.r2[k])

            for copy in self.three():
                copy.start()
        if stage == 4:
            for copy in self.three():
                copy.wait()
            total = self.gq[c, z, y, x].astype(F32)
            for k in range(3):
                total = total + self.r3[k].astype(F32)
            self.fin[...] = total
            self.four().start()


def tail_kernel(
    ret_hbm,
    x_hbm,
    ct_hbm,
    h_hbm,
    qkv_hbm,
    c_hbm,
    w_hbm,
    yrow_hbm,
    gw_hbm,
    col_ref,
    row_ref,
    stat_ref,
    gain_ref,
    gt_hbm,
    r1_hbm,
    r2_hbm,
    gw_out,
    out_hbm,
    own_ref,
    gg_ref,
    ret_ref,
    x_ref,
    ct_ref,
    h_ref,
    qkv_ref,
    c_ref,
    w_ref,
    gt_ref,
    dc_scr,
    dhb_scr,
    dqkv_scr,
    actt_scr,
    d_scr,
    dk_scr,
    dv_scr,
    gq,
    rc,
    q1,
    q2,
    q3,
    fin,
    q4,
    ggs,
    rg,
    na,
    nb,
    nsum,
    yback,
    send_sems,
    recv_sems,
    red_send,
    red_recv,
    load_sems,
):
    spot = place()
    z, y, x, c = spot
    me_e = z * 2 + y
    tokens, width = x_ref.shape
    slots, _w = ret_ref.shape
    blocks = tokens // BLOCK
    half = width // 2
    core, xpeer, ypeer = device(z, y, x, 1 - c), device(z, y, 1 - x, c), device(z, 1 - y, x, c)
    far = peers_of(z, y, x, c)
    links = Links(send_sems, recv_sems)
    loads = Loads(load_sems)

    def reduce(ph):
        return Reduce(spot, ph, gq, rc, q1, q2, q3, fin, q4, red_send, red_recv)

    first = [
        loads.start(a, b)
        for a, b in ((ret_hbm, ret_ref), (h_hbm, h_ref), (ct_hbm, ct_ref), (c_hbm, c_ref), (w_hbm, w_ref), (x_hbm, x_ref))
    ]
    second = [loads.start(qkv_hbm, qkv_ref), loads.start(yrow_hbm.at[me_e], yback.at[me_e])]
    greet(far + [core, xpeer])

    w_copies = [links.push(gw_hbm.at[xx * 2 + 1 - c], r1_hbm.at[xx], core) for xx in range(2)]
    y_copies = [links.push(yrow_hbm.at[to[0]], yback.at[me_e], to) for to in far]

    gain_one = gain_ref[0:1, :]
    gain_two = gain_ref[1:2, :]
    member = (iota((16, width), 1) // HEAD_DIM == iota((16, width), 0)).astype(F32)
    for copy in first:
        copy.wait()
    ggs[...] = jnp.zeros_like(ggs)

    def picks(rows):
        return (iota((BLOCK, slots), 1).astype(F32) == col_ref[rows, 0:1]).astype(BF16)

    @pl.loop(0, blocks)
    def _(i):
        rows = pl.ds(pl.multiple_of(i * BLOCK, BLOCK), BLOCK)
        da = dot(picks(rows), ret_ref[...])
        normed, factor = normalize(h_ref[rows, :])
        ggs[0, 1:2, :] += jnp.sum(da * normed, axis=0, keepdims=True)
        dh = ct_ref[rows, :].astype(F32) + norm_back(da * gain_two, normed, factor)
        gt_ref[rows, :] = dh
        dhb = dh.astype(BF16)
        dhb_scr[rows, :] = dhb
        dc = dot_t(dhb, weight(w_ref, 6, 2)).astype(BF16)
        dc_scr[rows, :] = dc
        d_scr[:, rows] = lax.dot_general(
            member,
            dc.astype(F32) * c_ref[rows, :].astype(F32),
            (((1,), (1,)), ((), ())),
            precision=lax.Precision.HIGHEST,
            preferred_element_type=F32,
        )

    def put(ph, value):
        for owner in range(2):
            for chip in range(16):
                gq[ph, owner, chip // 4, chip // 2 % 2, chip % 2] = value[
                    chip * 48 : chip * 48 + 48, owner * half : (owner + 1) * half
                ].astype(BF16)

    put(0, t_dot(c_ref[...], dhb_scr[...]))
    reduce(0).step(0)

    for copy in w_copies:
        copy.wait()
    x_copies = []
    for step in range(2):
        xx = 1 - x if step == 0 else x
        la = loads.start(gw_hbm.at[xx * 2 + c], na)
        lb = loads.start(r1_hbm.at[xx], nb)
        la.wait()
        lb.wait()
        nsum[step] = (na[...].astype(F32) + nb[...].astype(F32)).astype(BF16)
        if step == 0:
            x_copies.append(links.push(nsum.at[0], r2_hbm, xpeer))

    @pl.loop(0, blocks)
    def _(i):
        rows = pl.ds(pl.multiple_of(i * BLOCK, BLOCK), BLOCK)
        normed, _f = normalize(x_ref[rows, :].astype(F32))
        dhb_scr[rows, :] = (normed * gain_one).astype(BF16)

    actt_scr[...] = dhb_scr[...].T
    for copy in second:
        copy.wait()
    low = iota((BLOCK, 128), 1) < HEAD_DIM
    scale = HEAD_DIM**-0.5

    @pl.loop(0, 3)
    def _(t):
        @pl.loop(0, 2)
        def _(inner):
            hp = 2 * t + inner
            at = pl.multiple_of(hp * 128, 128)
            dk_scr[...] = jnp.zeros_like(dk_scr)
            dv_scr[...] = jnp.zeros_like(dv_scr)
            for qb in range(blocks):
                rows = pl.ds(qb * BLOCK, BLOCK)
                q = qkv_ref[rows, pl.ds(at, 128)] * jnp.asarray(scale, BF16)
                dc = dc_scr[rows, pl.ds(at, 128)]
                q_half = [jnp.where(low, q, 0), jnp.where(low, 0, q)]
                dc_half = [jnp.where(low, dc, 0), jnp.where(low, 0, dc)]
                dq = jnp.zeros((BLOCK, 128), F32)
                for kb in range(max(0, qb - LOOKBACK), qb + 1):
                    keys = pl.ds(kb * BLOCK, BLOCK)
                    k = qkv_ref[keys, pl.ds(width + at, 128)]
                    v = qkv_ref[keys, pl.ds(2 * width + at, 128)]
                    ok = col_ref[keys, 2:3] == row_ref[2:3, rows]
                    if kb == qb:
                        ok = ok & (iota((BLOCK, BLOCK), 0) <= iota((BLOCK, BLOCK), 1))
                    ps, dss = [], []
                    for side in range(2):
                        s = dot_t(k, q_half[side])
                        p = jnp.where(ok, jnp.exp(s - stat_ref[pl.ds(2 * hp + side, 1), rows]), 0.0)
                        dp = dot_t(v, dc_half[side])
                        dss.append((p * (dp - d_scr[pl.ds(2 * hp + side, 1), rows])).astype(BF16))
                        ps.append(p.astype(BF16))
                    dv_scr[keys, :] += dot(jnp.concatenate(ps, 1), jnp.concatenate(dc_half, 0))
                    dk_scr[keys, :] += dot(jnp.concatenate(dss, 1), jnp.concatenate(q_half, 0))
                    dq += jnp.where(low, t_dot(dss[0], k), t_dot(dss[1], k))
                dqkv_scr[rows, pl.ds(at, 128)] = (dq * scale).astype(BF16)
            dqkv_scr[:, pl.ds(width + at, 128)] = dk_scr[...].astype(BF16)
            dqkv_scr[:, pl.ds(2 * width + at, 128)] = dv_scr[...].astype(BF16)

        columns = []
        for inner in range(2):
            at = pl.multiple_of((2 * t + inner) * 128, 128)
            columns += [dqkv_scr[:, pl.ds(j * width + at, 128)] for j in range(3)]
        put(t + 1, dot(actt_scr[...], jnp.concatenate(columns, axis=1)))
        reduce(t + 1).step(0)
        reduce(t).step(1)

        @pl.when(t >= 1)
        def _():
            reduce(t - 1).step(2)

        @pl.when(t >= 2)
        def _():
            reduce(t - 2).step(3)

    @pl.loop(0, blocks)
    def _(i):
        rows = pl.ds(pl.multiple_of(i * BLOCK, BLOCK), BLOCK)
        normed, factor = normalize(x_ref[rows, :].astype(F32))
        dn = dot_t(dqkv_scr[rows, :], weight(w_ref, 0, 6))
        ggs[0, 0:1, :] += jnp.sum(dn * normed, axis=0, keepdims=True)
        gt_ref[rows, :] += norm_back(dn * gain_one, normed, factor)

    stores = [loads.start(gt_ref, gt_hbm)]
    gains_copy = links.push(ggs.at[0], rg.at[0], core)
    reduce(3).step(1)
    reduce(2).step(2)
    reduce(1).step(3)
    reduce(0).step(4)
    gains_copy.wait()
    ggs[1] = ggs[0] + rg[0]
    gains_copy = links.push(ggs.at[1], rg.at[1], xpeer)

    def finish(lo, hi):
        @pl.loop(lo, hi)
        def _(i):
            rows = pl.ds(pl.multiple_of(i * BLOCK, BLOCK), BLOCK)
            got = dot(picks(rows), yback[...].reshape(slots, width))
            ct_ref[rows, :] = (h_ref[rows, :] + jax.nn.sigmoid(col_ref[rows, 1:2]) * got).astype(BF16)

    for copy in y_copies:
        copy.wait()
    finish(0, 2)
    reduce(3).step(2)
    reduce(2).step(3)
    reduce(1).step(4)
    gains_copy.wait()
    ggs[2] = ggs[1] + rg[1]
    gains_copy = links.push(ggs.at[2], rg.at[2], ypeer)
    finish(2, blocks)
    stores.append(loads.start(ct_ref, out_hbm))
    reduce(3).step(3)
    reduce(2).step(4)
    gains_copy.wait()
    ggs[3] = ggs[2] + rg[2]
    gain_copies = [links.push(ggs.at[3], rg.at[2 + k], device(across(z, k), y, x, c)) for k in (1, 2, 3)]
    for copy in x_copies:
        copy.wait()
    lb = loads.start(r2_hbm, nb)
    lb.wait()
    gw_out[...] = nsum[1].astype(F32) + nb[...].astype(F32)
    reduce(3).step(4)
    for copy in gain_copies:
        copy.wait()
    gg_ref[...] = ggs[3] + rg[3] + rg[4] + rg[5]
    for ph in range(4):
        own_ref[ph, c] = fin[ph, pl.ds(pl.multiple_of(c * 24, 8), 24), :]
        reduce(ph).four().wait()
        own_ref[ph, 1 - c] = q4[ph]
    for copy in stores:
        copy.wait()


def tail(returned, cols, rows, tokens_in, cotangent, hidden, qkv, context, stats, w_blocks, gains, y_rows, gw):
    tokens, width = tokens_in.shape
    slots = returned.shape[0]
    half = width // 2
    any_spec = pl.BlockSpec(memory_space=pl.ANY)
    vmem = pl.BlockSpec(memory_space=pltpu.VMEM)
    return pl.pallas_call(
        tail_kernel,
        out_shape=(
            jax.ShapeDtypeStruct((tokens, width), F32),
            jax.ShapeDtypeStruct((2,) + gw.shape[1:], BF16),
            jax.ShapeDtypeStruct(gw.shape[1:], BF16),
            jax.ShapeDtypeStruct(gw.shape[1:], F32),
            jax.ShapeDtypeStruct((tokens, width), BF16),
            jax.ShapeDtypeStruct((4, 2, 24, half), F32),
            jax.ShapeDtypeStruct((8, width), F32),
        ),
        in_specs=[any_spec] * 9 + [vmem] * 4,
        out_specs=(any_spec, any_spec, any_spec, vmem, any_spec, vmem, vmem),
        scratch_shapes=[
            pltpu.VMEM((slots, width), BF16),
            pltpu.VMEM((tokens, width), BF16),
            pltpu.VMEM((tokens, width), BF16),
            pltpu.VMEM((tokens, width), F32),
            pltpu.VMEM((tokens, 3 * width), BF16),
            pltpu.VMEM((tokens, width), BF16),
            pltpu.VMEM(w_blocks.shape, BF16),
            pltpu.VMEM((tokens, width), F32),
            pltpu.VMEM((tokens, width), BF16),
            pltpu.VMEM((tokens, width), BF16),
            pltpu.VMEM((tokens, 3 * width), BF16),
            pltpu.VMEM((width, tokens), BF16),
            pltpu.VMEM((16, tokens), F32),
            pltpu.VMEM((tokens, 128), F32),
            pltpu.VMEM((tokens, 128), F32),
            pltpu.VMEM((4, 2, 4, 2, 2, 48, half), BF16),
            pltpu.VMEM((4, 4, 2, 2, 48, half), BF16),
            pltpu.VMEM((4, 4, 2, 48, half), BF16),
            pltpu.VMEM((4, 4, 48, half), BF16),
            pltpu.VMEM((4, 3, 48, half), BF16),
            pltpu.VMEM((4, 48, half), F32),
            pltpu.VMEM((4, 24, half), F32),
            pltpu.VMEM((4, 8, width), F32),
            pltpu.VMEM((6, 8, width), F32),
            pltpu.VMEM(gw.shape[1:], BF16),
            pltpu.VMEM(gw.shape[1:], BF16),
            pltpu.VMEM((2,) + gw.shape[1:], BF16),
            pltpu.VMEM(y_rows.shape, BF16),
            pltpu.SemaphoreType.DMA((20,)),
            pltpu.SemaphoreType.DMA((20,)),
            pltpu.SemaphoreType.DMA((28,)),
            pltpu.SemaphoreType.DMA((28,)),
            pltpu.SemaphoreType.DMA((16,)),
        ],
        compiler_params=pltpu.CompilerParams(vmem_limit_bytes=62 << 20, collective_id=2, has_side_effects=True),
        cost_estimate=pl.CostEstimate(flops=80 << 30, bytes_accessed=40 << 20, transcendentals=0),
    )(returned, tokens_in, cotangent, hidden, qkv, context, w_blocks, y_rows, gw, cols, rows, stats, gains)


def flipped(z, y, k):
    hi, lo = z // 2, lax.rem(z, 2)
    zz = lax.rem(hi + k // 4, 2) * 2 + lax.rem(lo + lax.rem(k // 2, 2), 2)
    return zz, lax.rem(y + lax.rem(k, 2), 2)


def swap_kernel(
    act_hbm,
    dy_hbm,
    win_hbm,
    whid_hbm,
    own_in_hbm,
    own_hid_hbm,
    ret_hbm,
    y_hbm,
    gin_hbm,
    ghid_hbm,
    a_ref,
    dy_ref,
    win_ref,
    whid_ref,
    g_ref,
    du_ref,
    da_ref,
    us,
    gs,
    stage,
    near,
    next_x,
    send_sems,
    recv_sems,
    load_sems,
):
    z, y, x, c = place()
    me = z * 2 + y
    me_n = x * 2 + c
    count, cap, width = a_ref.shape
    parts = win_ref.shape[0]
    wide = win_ref.shape[2]
    loads = Loads(load_sems)
    first = [
        loads.start(a, b)
        for a, b in (
            (act_hbm.at[me], a_ref.at[me]),
            (own_in_hbm, win_ref.at[me_n]),
            (own_hid_hbm, whid_ref.at[me_n]),
            (dy_hbm, dy_ref),
        )
    ]
    for i in range(1, parts):
        n = lax.rem(me_n + i, parts)
        first += [loads.start(win_hbm.at[n], win_ref.at[n]), loads.start(whid_hbm.at[n], whid_ref.at[n])]

    def partner(k):
        zz, yy = flipped(z, y, k)
        return zz * 2 + yy, device(zz, yy, x, c)

    def outward(k):
        e, to = partner(k)
        return pltpu.make_async_remote_copy(
            src_ref=act_hbm.at[e],
            dst_ref=a_ref.at[me],
            send_sem=send_sems.at[k],
            recv_sem=recv_sems.at[k],
            device_id=to,
            device_id_type=MESH,
        )

    def homeward(k):
        e, to = partner(k)
        return pltpu.make_async_remote_copy(
            src_ref=da_ref.at[e],
            dst_ref=ret_hbm.at[me],
            send_sem=send_sems.at[8 + k],
            recv_sem=recv_sems.at[8 + k],
            device_id=to,
            device_id_type=MESH,
        )

    core, xpeer = device(z, y, x, 1 - c), device(z, y, 1 - x, c)
    greet([partner(k)[1] for k in range(1, 8)] + [core, xpeer])
    for k in FLIPS:
        outward(k).start()
    for copy in first:
        copy.wait()

    @pl.loop(0, count)
    def _(k):
        @pl.when(k > 0)
        def _():
            outward(k).wait_recv()

        e, _to = partner(k)
        a = a_ref[e]
        dy = dy_ref[e]
        rows = pl.ds(pl.multiple_of(e * cap, cap), cap)

        def enter(j):
            us[j % 2] = dot(a, win_ref[j])
            gs[j % 2] = dot_t(dy, whid_ref[j])

        def bend(j):
            g, slope = gelu_pair(us[j % 2])
            g_ref[rows, j * wide : (j + 1) * wide] = g.astype(BF16)
            du_ref[rows, j * wide : (j + 1) * wide] = (gs[j % 2] * slope).astype(BF16)

        def leave(j):
            return dot_t(du_ref[rows, j * wide : (j + 1) * wide], win_ref[j])

        enter(0)
        total = None
        for j in range(parts):
            if j + 1 < parts:
                enter(j + 1)
            bend(j)
            if j > 0:
                term = leave(j - 1)
                total = term if total is None else total + term
        da_ref[e] = (total + leave(parts - 1)).astype(BF16)

        @pl.when(k > 0)
        def _():
            homeward(k).start()

    own = loads.start(da_ref.at[me], ret_hbm.at[me])

    def put(i, out):
        return pltpu.make_async_copy(stage.at[i], out, load_sems.at[16 + i])

    def third(i, src, dst, to):
        return pltpu.make_async_remote_copy(
            src_ref=src,
            dst_ref=dst,
            send_sem=send_sems.at[16 + i],
            recv_sem=recv_sems.at[16 + i],
            device_id=to,
            device_id_type=MESH,
        )

    acts = a_ref[...].reshape(count * cap, width)

    @pl.loop(0, parts)
    def _(j):
        cols = pl.ds(pl.multiple_of(j * wide, wide), wide)
        win_ref[j] = t_dot(acts, du_ref[:, cols]).astype(BF16)

    to_core = [third(xx, win_ref.at[xx * 2 + 1 - c], near.at[xx], core) for xx in range(2)]
    for copy in to_core:
        copy.start()

    @pl.loop(0, parts // 2)
    def _(jj):
        for i in range(2):
            j = 2 * jj + i
            cols = pl.ds(pl.multiple_of(j * wide, wide), wide)

            @pl.when(jj >= 1)
            def _():
                put(i, ghid_hbm.at[j - 2]).wait()

            stage[i] = t_dot(g_ref[:, cols], dy_ref[...].reshape(count * cap, width)).astype(BF16)
            put(i, ghid_hbm.at[j]).start()

    for copy in to_core:
        copy.wait()
    other = (1 - x) * 2 + c
    win_ref[other] = (win_ref[other].astype(F32) + near[1 - x].astype(F32)).astype(BF16)
    to_x = third(2, win_ref.at[other], next_x, xpeer)
    to_x.start()

    @pl.loop(0, count)
    def _(i):
        rows = pl.ds(pl.multiple_of(i * cap, cap), cap)
        a_ref[i] = dot(g_ref[rows, :], whid_ref[...].reshape(parts * wide, width)).astype(BF16)

    out = loads.start(a_ref, y_hbm)
    for i in range(2):
        put(i, ghid_hbm.at[parts - 2 + i]).wait()
    to_x.wait()
    tiles = []
    for i, tile in enumerate((us.at[0], us.at[1], gs.at[0])):
        rows = pl.ds(i * cap, cap)
        tile[...] = win_ref[me_n, rows].astype(F32) + near[x, rows].astype(F32) + next_x[rows].astype(F32)
        tiles.append(loads.start(tile, gin_hbm.at[rows]))
    for k in range(1, 8):
        outward(k).wait_send()
        homeward(k).wait()
    for copy in tiles + [own, out]:
        copy.wait()


def swap(act_slots, dy_rows, w_in, w_hid, own_in, own_hid):
    count, cap, width = act_slots.shape
    parts, _, wide = w_in.shape
    hidden = parts * wide
    any_spec = pl.BlockSpec(memory_space=pl.ANY)
    return pl.pallas_call(
        swap_kernel,
        out_shape=(
            jax.ShapeDtypeStruct((count, cap, width), BF16),
            jax.ShapeDtypeStruct((count, cap, width), BF16),
            jax.ShapeDtypeStruct((width, wide), F32),
            jax.ShapeDtypeStruct((parts, wide, width), BF16),
        ),
        in_specs=[any_spec] * 6,
        out_specs=(any_spec,) * 4,
        scratch_shapes=[
            pltpu.VMEM((count, cap, width), BF16),
            pltpu.VMEM((count, cap, width), BF16),
            pltpu.VMEM(w_in.shape, BF16),
            pltpu.VMEM(w_hid.shape, BF16),
            pltpu.VMEM((count * cap, hidden), BF16),
            pltpu.VMEM((count * cap, hidden), BF16),
            pltpu.VMEM((count, cap, width), BF16),
            pltpu.VMEM((2, cap, wide), F32),
            pltpu.VMEM((2, cap, wide), F32),
            pltpu.VMEM((2, width, wide), BF16),
            pltpu.VMEM((2, width, wide), BF16),
            pltpu.VMEM((width, wide), BF16),
            pltpu.SemaphoreType.DMA((20,)),
            pltpu.SemaphoreType.DMA((20,)),
            pltpu.SemaphoreType.DMA((18,)),
        ],
        compiler_params=pltpu.CompilerParams(vmem_limit_bytes=62 << 20, collective_id=1, has_side_effects=True),
        cost_estimate=pl.CostEstimate(flops=100 << 30, bytes_accessed=60 << 20, transcendentals=0),
    )(act_slots, dy_rows, w_in, w_hid, own_in, own_hid)


def local(tokens, segments, routes, gate_logit, w_qkv, w_out, norm_gains, w_in, w_hid, cotangent):
    tok_count, width = tokens.shape
    n_expert = lax.axis_size("expert")
    n_narrow = lax.axis_size("narrow")
    capacity = 2 * tok_count // n_expert
    slot_rows = n_expert * capacity
    everyone = ("expert", "narrow")

    if n_expert == 8 and n_narrow == 4:
        share = w_qkv.shape[0]
        halves = jnp.concatenate((w_qkv, w_out), axis=1).reshape(share, 4, 2, width // 2)
        halves = halves.transpose(2, 0, 1, 3).reshape(2, share, 2 * width)
        gain_cols = jnp.broadcast_to(jnp.pad(norm_gains.T, ((0, 0), (0, 126))), (2, share, 128))
        shard = jnp.concatenate((halves, gain_cols), axis=2).astype(F32)
        listed = jnp.concatenate(
            (
                routes.reshape(1, tok_count).astype(F32),
                gate_logit.reshape(1, tok_count),
                segments.reshape(1, tok_count).astype(F32),
                jnp.zeros((5, tok_count), F32),
            )
        )
        qkv, context, hidden, act_slots, w_blocks, dy_rows, w_in_all, w_hid_all, stats, cols, gains = head(
            tokens, cotangent, shard, w_in[0], w_hid[0], listed, n_expert, capacity
        )
        da_back, y_rows, gin_own, ghid = swap(act_slots, dy_rows, w_in_all, w_hid_all, w_in[0], w_hid[0])
        grad_tokens, _r1, _r2, ghid_own, block_out, own, gg = tail(
            da_back.reshape(slot_rows, width),
            cols,
            listed,
            tokens,
            cotangent,
            hidden,
            qkv,
            context,
            stats,
            w_blocks,
            gains,
            y_rows,
            ghid,
        )
        me = lax.axis_index("expert") * n_narrow + lax.axis_index("narrow")
        heads = own[1:].reshape(6, share, 3, 128).transpose(1, 2, 0, 3)
        return (
            block_out,
            grad_tokens,
            heads.reshape(share, 3 * width),
            own[0].transpose(1, 0, 2).reshape(share, width),
            lax.dynamic_slice_in_dim(gg[:2], me * share, share, axis=1),
            gin_own[None],
            ghid_own[None],
        )
    gain_cols = jnp.pad(norm_gains.T, ((0, 0), (0, 126)))
    w_all = lax.all_gather(
        jnp.concatenate((w_qkv, w_out, gain_cols), axis=1), everyone, axis=0, tiled=True
    )
    gains = w_all[:, 4 * width : 4 * width + 2].T.astype(F32)
    w_in_all = lax.all_gather(w_in[0], "narrow", axis=0, tiled=False)
    w_hid_all = lax.all_gather(w_hid[0], "narrow", axis=0, tiled=False)

    def exchange(values):
        return lax.all_to_all(
            values.reshape(n_expert, capacity, width), "expert", split_axis=0, concat_axis=0, tiled=True
        ).reshape(slot_rows, width)

    segr = segments.reshape(1, tok_count)
    segc = segments.reshape(tok_count, 1)
    srow, scol, dy_slots = prep(routes, gate_logit, cotangent, n_expert, capacity)
    dy_rows = exchange(dy_slots)
    qkv, context, stats, hidden, act_slots = attend_fwd(tokens, w_all, gains, segr, segc, srow, slot_rows)
    act_rows = exchange(act_slots)
    activated, grad_pre, da_rows = experts(act_rows, dy_rows, w_in_all, w_hid_all)
    da_back = exchange(da_rows)
    hidden_units = activated.shape[1]
    y_rows = dot(activated, w_hid_all.reshape(hidden_units, width)).astype(BF16)
    grad_hid = t_dot(activated, dy_rows).astype(BF16)
    grad_in = lax.dot_general(
        act_rows, grad_pre.reshape(slot_rows, n_narrow, -1), (((0,), (0,)), ((), ())), preferred_element_type=F32
    ).astype(BF16)
    y_back = exchange(y_rows)
    grad_tokens, grad_w, grad_gains = attend_bwd(
        da_back, scol, tokens, cotangent, hidden, qkv, context, stats, w_all, gains, segr, segc
    )
    block_out = block_output(y_back, scol, hidden, gate_logit)
    grad_hid_w = lax.psum_scatter(grad_hid, "narrow", scatter_dimension=0, tiled=True).astype(F32)[None]
    grad_in_w = lax.psum_scatter(grad_in, "narrow", scatter_dimension=1, tiled=True).astype(F32)
    grad_in_w = grad_in_w.reshape(1, width, -1)
    packed = jnp.concatenate((grad_w, jnp.pad(grad_gains[:2].T, ((0, 0), (0, 126)))), axis=1)
    own = lax.psum_scatter(packed, everyone, scatter_dimension=0, tiled=True)
    return (
        block_out,
        grad_tokens,
        own[:, : 3 * width],
        own[:, 3 * width : 4 * width],
        own[:, 4 * width : 4 * width + 2].T,
        grad_in_w,
        grad_hid_w,
    )


def solution(mesh):
    placed = (
        P(("expert", "narrow"), None),
        P(("expert", "narrow"), None),
        P(("expert", "narrow"), None),
        P(("expert", "narrow")),
        P(("expert", "narrow"), None),
        P(("expert", "narrow"), None),
        P(None, ("expert", "narrow")),
        P("expert", None, "narrow"),
        P("expert", "narrow", None),
        P(("expert", "narrow"), None),
    )
    return jax.shard_map(
        local,
        mesh=mesh,
        in_specs=placed,
        out_specs=(
            P(("expert", "narrow"), None),
            P(("expert", "narrow"), None),
            P(("expert", "narrow"), None),
            P(("expert", "narrow"), None),
            P(None, ("expert", "narrow")),
            P("expert", None, "narrow"),
            P("expert", "narrow", None),
        ),
        check_vma=False,
    )
```

```python
import functools

import jax
import jax.numpy as jnp
from jax import lax
from jax.experimental import pallas as pl
from jax.experimental.pallas import tpu as pltpu
from jax.sharding import PartitionSpec as P

HEAD_DIM = 64
SEQ = 1024
BLOCK = 256
LOOKBACK = 2
EPSILON = 1e-05
BIG_NEGATIVE = -1e30
F32 = jnp.float32
BF16 = jnp.bfloat16

TAIL_P = 0.3
TAIL_C = (
    0.11962923306946524,
    0.12075497050525577,
    0.0999071263144056,
    0.12858273368127124,
    -0.053723704944995426,
    0.20639718480180155,
    -0.1572285075725372,
    0.03568089149479804,
)


def dot(a, b):
    return lax.dot_general(a, b, (((1,), (0,)), ((), ())), preferred_element_type=F32)


def dot_t(a, b):
    return lax.dot_general(a, b, (((1,), (1,)), ((), ())), preferred_element_type=F32)


def t_dot(a, b):
    return lax.dot_general(a, b, (((0,), (0,)), ((), ())), preferred_element_type=F32)


def normalize(values):
    centre = jnp.mean(values, axis=-1, keepdims=True)
    shifted = values - centre
    factor = lax.rsqrt(jnp.mean(shifted * shifted, axis=-1, keepdims=True) + EPSILON)
    return shifted * factor, factor


def norm_back(grad_normed, normed, factor):
    return factor * (
        grad_normed
        - jnp.mean(grad_normed, axis=-1, keepdims=True)
        - normed * jnp.mean(grad_normed * normed, axis=-1, keepdims=True)
    )


def gelu_pair(u):
    size = jnp.abs(u)
    t = 1.0 / (1.0 + TAIL_P * size)
    poly = jnp.full_like(t, TAIL_C[-1])
    for c in TAIL_C[-2::-1]:
        poly = poly * t + c
    bell = jnp.exp(-0.5 * (u * u))
    tail = poly * t * bell
    phi = jnp.where(u >= 0, 1.0 - tail, tail)
    return u * phi, phi + u * (bell * 0.3989422804014327)


def iota(shape, dim):
    return lax.broadcasted_iota(jnp.int32, shape, dim)


def prep_kernel(capacity, experts, rrow_ref, rcol_ref, gate_ref, ct_ref, srow_ref, scol_ref, send_ref):
    tokens = ct_ref.shape[0]
    wide = max(8, experts)
    hot = (iota((wide, tokens), 0) == rrow_ref[...]).astype(F32)
    before = (iota((tokens, tokens), 0) < iota((tokens, tokens), 1)).astype(BF16)
    rank = dot(hot.astype(BF16), before)
    base = (iota((wide, tokens), 0) * capacity).astype(F32)
    srow = jnp.sum(hot * (rank + base), axis=0, keepdims=True)
    srow_ref[...] = jnp.broadcast_to(srow, srow_ref.shape)
    hot_c = (iota((tokens, 128), 1) == rcol_ref[...]).astype(F32)
    after = (iota((tokens, tokens), 1) < iota((tokens, tokens), 0)).astype(BF16)
    rank_c = dot(after, hot_c.astype(BF16))
    base_c = (iota((tokens, 128), 1) * capacity).astype(F32)
    scol_ref[...] = jnp.sum(hot_c * (rank_c + base_c), axis=1, keepdims=True)
    gated = (jax.nn.sigmoid(gate_ref[...]) * ct_ref[...].astype(F32)).astype(BF16)
    fill_slots(srow, gated, send_ref)


def fill_slots(srow, values, send_ref):
    rows = send_ref.shape[0]
    tokens = values.shape[0]

    @pl.loop(0, rows // BLOCK)
    def _(i):
        first = i * BLOCK
        ids = (iota((BLOCK, tokens), 0) + first).astype(F32)
        pick = (ids == srow).astype(BF16)
        send_ref[pl.ds(pl.multiple_of(first, BLOCK), BLOCK), :] = dot(pick, values).astype(BF16)


def prep(routes, gate_logit, cotangent, experts, capacity):
    tokens, width = cotangent.shape
    return pl.pallas_call(
        functools.partial(prep_kernel, capacity, experts),
        out_shape=(
            jax.ShapeDtypeStruct((8, tokens), F32),
            jax.ShapeDtypeStruct((tokens, 1), F32),
            jax.ShapeDtypeStruct((experts * capacity, width), BF16),
        ),
        compiler_params=pltpu.CompilerParams(vmem_limit_bytes=56 << 20),
        cost_estimate=pl.CostEstimate(flops=8 << 30, bytes_accessed=8 << 20, transcendentals=0),
    )(routes.reshape(1, tokens), routes, gate_logit.reshape(tokens, 1), cotangent)


def fwd_kernel(
    x_ref, w_ref, gain_ref, segr_ref, segc_ref, srow_ref, qkv_ref, c_ref, stat_ref, h_ref, send_ref, act_scr, bias_scr, col_scr
):
    tokens, width = x_ref.shape
    blocks = tokens // BLOCK
    pairs = width // 128
    gain_one = gain_ref[0:1, :]
    gain_two = gain_ref[1:2, :]

    @pl.loop(0, blocks)
    def _(i):
        rows = pl.ds(pl.multiple_of(i * BLOCK, BLOCK), BLOCK)
        normed, _f = normalize(x_ref[rows, :].astype(F32))
        act = (normed * gain_one).astype(BF16)
        qkv_ref[rows, :] = dot(act, w_ref[:, : 3 * width]).astype(BF16)

    col_scr[...] = jnp.zeros_like(col_scr)
    low = iota((BLOCK, 128), 1) < HEAD_DIM
    for qb in range(blocks):
        kb = max(0, qb - LOOKBACK)
        span = (qb - kb + 1) * BLOCK
        rows = pl.ds(qb * BLOCK, BLOCK)
        keys = pl.ds(kb * BLOCK, span)
        q_pos = iota((BLOCK, span), 0) + qb * BLOCK
        k_pos = iota((BLOCK, span), 1) + kb * BLOCK
        ok = (k_pos <= q_pos) & (segc_ref[rows, :] == segr_ref[0:1, keys])
        bias_scr[:, :span] = jnp.where(ok, 0.0, BIG_NEGATIVE)

        @pl.loop(0, pairs)
        def _(hp):
            at = pl.multiple_of(hp * 128, 128)
            q = qkv_ref[rows, pl.ds(at, 128)] * jnp.asarray(HEAD_DIM**-0.5, BF16)
            k = qkv_ref[keys, pl.ds(width + at, 128)]
            v = qkv_ref[keys, pl.ds(2 * width + at, 128)]
            outs = []
            col = col_scr[rows, :]
            for half in range(2):
                mine = low if half == 0 else ~low
                s = dot_t(jnp.where(mine, q, 0), k) + bias_scr[:, :span]
                top = jnp.max(s, axis=1, keepdims=True)
                raised = jnp.exp(s - top)
                total = jnp.sum(raised, axis=1, keepdims=True)
                outs.append(dot((raised * (1.0 / total)).astype(BF16), v))
                col = jnp.where(iota((BLOCK, 128), 1) == 2 * hp + half, top + jnp.log(total), col)
            col_scr[rows, :] = col
            c_ref[rows, pl.ds(at, 128)] = jnp.where(low, outs[0], outs[1]).astype(BF16)

    stat_ref[...] = col_scr[...].T

    @pl.loop(0, blocks)
    def _(i):
        rows = pl.ds(pl.multiple_of(i * BLOCK, BLOCK), BLOCK)
        hidden = x_ref[rows, :].astype(F32) + dot(c_ref[rows, :], w_ref[:, 3 * width : 4 * width])
        h_ref[rows, :] = hidden
        normed, _f = normalize(hidden)
        act_scr[rows, :] = (normed * gain_two).astype(BF16)

    fill_slots(srow_ref[0:1, :], act_scr[...], send_ref)


def attend_fwd(tokens_in, w_all, gains, segr, segc, srow, slot_rows):
    tokens, width = tokens_in.shape
    return pl.pallas_call(
        fwd_kernel,
        out_shape=(
            jax.ShapeDtypeStruct((tokens, 3 * width), BF16),
            jax.ShapeDtypeStruct((tokens, width), BF16),
            jax.ShapeDtypeStruct((128, tokens), F32),
            jax.ShapeDtypeStruct((tokens, width), F32),
            jax.ShapeDtypeStruct((slot_rows, width), BF16),
        ),
        scratch_shapes=[
            pltpu.VMEM((tokens, width), BF16),
            pltpu.VMEM((BLOCK, (LOOKBACK + 1) * BLOCK), F32),
            pltpu.VMEM((tokens, 128), F32),
        ],
        compiler_params=pltpu.CompilerParams(vmem_limit_bytes=56 << 20),
        cost_estimate=pl.CostEstimate(flops=40 << 30, bytes_accessed=24 << 20, transcendentals=0),
    )(tokens_in, w_all, gains, segr, segc, srow)


def expert_kernel(a_ref, dy_ref, win_ref, whid_ref, g_ref, du_ref, da_ref, acc_scr):
    a = a_ref[...]
    dy = dy_ref[...]
    parts = win_ref.shape[0]
    wide = win_ref.shape[2]
    acc_scr[...] = jnp.zeros_like(acc_scr)

    @pl.loop(0, parts)
    def _(j):
        cols = pl.ds(pl.multiple_of(j * wide, wide), wide)
        u = dot(a, win_ref[j])
        grad = dot_t(dy, whid_ref[j])
        g, slope = gelu_pair(u)
        g_ref[:, cols] = g.astype(BF16)
        du = (grad * slope).astype(BF16)
        du_ref[:, cols] = du
        acc_scr[...] += dot_t(du, win_ref[j])

    da_ref[...] = acc_scr[...].astype(BF16)


def experts(acts, grads, w_in, w_hid):
    rows, width = acts.shape
    parts, _, wide = w_in.shape
    hidden = parts * wide
    row_spec = pl.BlockSpec((BLOCK, width), lambda i: (i, 0))
    wide_spec = pl.BlockSpec((BLOCK, hidden), lambda i: (i, 0))
    return pl.pallas_call(
        expert_kernel,
        grid=(rows // BLOCK,),
        out_shape=(
            jax.ShapeDtypeStruct((rows, hidden), BF16),
            jax.ShapeDtypeStruct((rows, hidden), BF16),
            jax.ShapeDtypeStruct((rows, width), BF16),
        ),
        in_specs=[
            row_spec,
            row_spec,
            pl.BlockSpec(w_in.shape, lambda i: (0, 0, 0), pipeline_mode=pl.Buffered(1)),
            pl.BlockSpec(w_hid.shape, lambda i: (0, 0, 0), pipeline_mode=pl.Buffered(1)),
        ],
        out_specs=(wide_spec, wide_spec, row_spec),
        scratch_shapes=[pltpu.VMEM((BLOCK, width), F32)],
        compiler_params=pltpu.CompilerParams(vmem_limit_bytes=56 << 20),
        cost_estimate=pl.CostEstimate(flops=60 << 30, bytes_accessed=40 << 20, transcendentals=0),
    )(acts, grads, w_in, w_hid)


def out_kernel(ret_ref, scol_ref, h_ref, gate_ref, out_ref):
    tokens, rows = out_ref.shape[0], ret_ref.shape[0]
    pick = (iota((tokens, rows), 1).astype(F32) == scol_ref[...]).astype(BF16)
    y = dot(pick, ret_ref[...])
    out_ref[...] = (h_ref[...] + jax.nn.sigmoid(gate_ref[...]) * y).astype(BF16)


def block_output(returned, scol, hidden, gate_logit):
    rows, width = returned.shape
    tokens = hidden.shape[0]
    tile = pl.BlockSpec((BLOCK, width), lambda i: (i, 0))
    column = pl.BlockSpec((BLOCK, 1), lambda i: (i, 0))
    return pl.pallas_call(
        out_kernel,
        grid=(tokens // BLOCK,),
        out_shape=jax.ShapeDtypeStruct((tokens, width), BF16),
        in_specs=[pl.BlockSpec((rows, width), lambda i: (0, 0)), column, tile, column],
        out_specs=tile,
        compiler_params=pltpu.CompilerParams(vmem_limit_bytes=40 << 20),
        cost_estimate=pl.CostEstimate(flops=4 << 30, bytes_accessed=10 << 20, transcendentals=0),
    )(returned, scol, hidden, gate_logit.reshape(tokens, 1))


def bwd_kernel(
    ret_ref,
    scol_ref,
    x_ref,
    ct_ref,
    h_ref,
    qkv_ref,
    c_ref,
    stat_ref,
    w_ref,
    gain_ref,
    segr_ref,
    segc_ref,
    gt_ref,
    gw_ref,
    gg_ref,
    dc_scr,
    dhb_scr,
    dqkv_scr,
    act_scr,
    d_scr,
    dk_scr,
    dv_scr,
):
    tokens, width = x_ref.shape
    slots = ret_ref.shape[0]
    blocks = tokens // BLOCK
    pairs = width // 128
    gain_one = gain_ref[0:1, :]
    gain_two = gain_ref[1:2, :]
    gg_ref[...] = jnp.zeros_like(gg_ref)
    member = (iota((16, width), 1) // HEAD_DIM == iota((16, width), 0)).astype(F32)

    for i in range(blocks):
        rows = pl.ds(i * BLOCK, BLOCK)
        pick = (iota((BLOCK, slots), 1).astype(F32) == scol_ref[rows, :]).astype(BF16)
        da = dot(pick, ret_ref[...])
        normed, factor = normalize(h_ref[rows, :])
        gg_ref[1:2, :] += jnp.sum(da * normed, axis=0, keepdims=True)
        dh = ct_ref[rows, :].astype(F32) + norm_back(da * gain_two, normed, factor)
        gt_ref[rows, :] = dh
        dhb = dh.astype(BF16)
        dhb_scr[rows, :] = dhb
        dc = dot_t(dhb, w_ref[:, 3 * width : 4 * width]).astype(BF16)
        dc_scr[rows, :] = dc
        d_scr[:, rows] = lax.dot_general(
            member,
            dc.astype(F32) * c_ref[rows, :].astype(F32),
            (((1,), (1,)), ((), ())),
            precision=lax.Precision.HIGHEST,
            preferred_element_type=F32,
        )

    gw_ref[:, 3 * width : 4 * width] = t_dot(c_ref[...], dhb_scr[...])
    low = iota((BLOCK, 128), 1) < HEAD_DIM
    scale = HEAD_DIM**-0.5

    @pl.loop(0, pairs)
    def _(hp):
        at = pl.multiple_of(hp * 128, 128)
        dk_scr[...] = jnp.zeros_like(dk_scr)
        dv_scr[...] = jnp.zeros_like(dv_scr)
        for qb in range(blocks):
            rows = pl.ds(qb * BLOCK, BLOCK)
            q = qkv_ref[rows, pl.ds(at, 128)] * jnp.asarray(scale, BF16)
            dc = dc_scr[rows, pl.ds(at, 128)]
            q_half = [jnp.where(low, q, 0), jnp.where(low, 0, q)]
            dc_half = [jnp.where(low, dc, 0), jnp.where(low, 0, dc)]
            dq = jnp.zeros((BLOCK, 128), F32)
            for kb in range(max(0, qb - LOOKBACK), qb + 1):
                keys = pl.ds(kb * BLOCK, BLOCK)
                k = qkv_ref[keys, pl.ds(width + at, 128)]
                v = qkv_ref[keys, pl.ds(2 * width + at, 128)]
                ok = segc_ref[keys, :] == segr_ref[0:1, rows]
                if kb == qb:
                    ok = ok & (iota((BLOCK, BLOCK), 0) <= iota((BLOCK, BLOCK), 1))
                ps, dss = [], []
                for half in range(2):
                    s = dot_t(k, q_half[half])
                    p = jnp.where(ok, jnp.exp(s - stat_ref[pl.ds(2 * hp + half, 1), rows]), 0.0)
                    dp = dot_t(v, dc_half[half])
                    dss.append((p * (dp - d_scr[pl.ds(2 * hp + half, 1), rows])).astype(BF16))
                    ps.append(p.astype(BF16))
                dv_scr[keys, :] += dot(jnp.concatenate(ps, 1), jnp.concatenate(dc_half, 0))
                dk_scr[keys, :] += dot(jnp.concatenate(dss, 1), jnp.concatenate(q_half, 0))
                dq += jnp.where(low, t_dot(dss[0], k), t_dot(dss[1], k))
            dqkv_scr[rows, pl.ds(at, 128)] = (dq * scale).astype(BF16)
        dqkv_scr[:, pl.ds(width + at, 128)] = dk_scr[...].astype(BF16)
        dqkv_scr[:, pl.ds(2 * width + at, 128)] = dv_scr[...].astype(BF16)

    @pl.loop(0, blocks)
    def _(i):
        rows = pl.ds(pl.multiple_of(i * BLOCK, BLOCK), BLOCK)
        normed, factor = normalize(x_ref[rows, :].astype(F32))
        act_scr[rows, :] = (normed * gain_one).astype(BF16)
        dn = dot_t(dqkv_scr[rows, :], w_ref[:, : 3 * width])
        gg_ref[0:1, :] += jnp.sum(dn * normed, axis=0, keepdims=True)
        gt_ref[rows, :] += norm_back(dn * gain_one, normed, factor)

    gw_ref[:, : 3 * width] = t_dot(act_scr[...], dqkv_scr[...])


def attend_bwd(returned, scol, tokens_in, cotangent, hidden, qkv, context, stats, w_all, gains, segr, segc):
    tokens, width = tokens_in.shape
    return pl.pallas_call(
        bwd_kernel,
        out_shape=(
            jax.ShapeDtypeStruct((tokens, width), F32),
            jax.ShapeDtypeStruct((width, 4 * width), F32),
            jax.ShapeDtypeStruct((8, width), F32),
        ),
        scratch_shapes=[
            pltpu.VMEM((tokens, width), BF16),
            pltpu.VMEM((tokens, width), BF16),
            pltpu.VMEM((tokens, 3 * width), BF16),
            pltpu.VMEM((tokens, width), BF16),
            pltpu.VMEM((16, tokens), F32),
            pltpu.VMEM((tokens, 128), F32),
            pltpu.VMEM((tokens, 128), F32),
        ],
        compiler_params=pltpu.CompilerParams(vmem_limit_bytes=60 << 20),
        cost_estimate=pl.CostEstimate(flops=80 << 30, bytes_accessed=40 << 20, transcendentals=0),
    )(returned, scol, tokens_in, cotangent, hidden, qkv, context, stats, w_all, gains, segr, segc)


MESH = pl.DeviceIdType.MESH


def place():
    e, n = lax.axis_index("expert"), lax.axis_index("narrow")
    return e // 2, lax.rem(e, 2), n // 2, lax.rem(n, 2)


def device(z, y, x, c):
    return (z * 2 + y, x * 2 + c)


def across(z, k):
    hi, lo = z // 2, lax.rem(z, 2)
    hi = 1 - hi if k & 2 else hi
    lo = 1 - lo if k & 1 else lo
    return hi * 2 + lo


class Links:
    def __init__(self, send, recv):
        self.send, self.recv, self.used = send, recv, 0

    def make(self, src, dst, to):
        i = self.used
        self.used += 1
        return pltpu.make_async_remote_copy(
            src_ref=src, dst_ref=dst, send_sem=self.send.at[i], recv_sem=self.recv.at[i], device_id=to, device_id_type=MESH
        )

    def push(self, src, dst, to):
        copy = self.make(src, dst, to)
        copy.start()
        return copy


class Loads:
    def __init__(self, sems):
        self.sems, self.used = sems, 0

    def start(self, src, dst):
        copy = pltpu.make_async_copy(src, dst, self.sems.at[self.used])
        self.used += 1
        copy.start()
        return copy


def greet(peers):
    barrier = pltpu.get_barrier_semaphore()
    for peer in peers:
        pl.semaphore_signal(barrier, inc=1, device_id=peer, device_id_type=MESH)
    pl.semaphore_wait(barrier, len(peers))


FLIPS = (4, 2, 6, 1, 5, 3, 7)


def peers_of(z, y, x, c):
    return [device(across(z, k >> 1), 1 - y if k & 1 else y, x, c) for k in FLIPS]


def weight(ref, lo, hi):
    return ref[:, :, :, :, lo:hi].reshape(-1, hi - lo)


def head_kernel(
    capacity,
    experts,
    x_hbm,
    ct_hbm,
    win_hbm,
    whid_hbm,
    row_ref,
    wqkv_ref,
    wout_ref,
    gshard_ref,
    qkv_hbm,
    c_hbm,
    h_hbm,
    act_hbm,
    w_hbm,
    dyrow_hbm,
    win4_hbm,
    whid4_hbm,
    stat_ref,
    col_ref,
    gain_ref,
    x_ref,
    ct_ref,
    sh,
    st,
    square,
    wq,
    wg,
    qkv_ref,
    c_ref,
    h_ref,
    a_scr,
    act_ref,
    dy_ref,
    bias_scr,
    col_scr,
    send_sems,
    recv_sems,
    load_sems,
):
    z, y, x, c = place()
    me_e = z * 2 + y
    me_n = x * 2 + c
    tokens, width = x_ref.shape
    blocks = tokens // BLOCK
    pairs = width // 128
    half = width // 2
    core, xpeer, ypeer = device(z, y, x, 1 - c), device(z, y, 1 - x, c), device(z, 1 - y, x, c)
    links = Links(send_sems, recv_sems)
    loads = Loads(load_sems)
    loading_ct = loads.start(ct_hbm, ct_ref)
    loading_x = loads.start(x_hbm, x_ref)

    square[...] = jnp.zeros_like(square)
    square[0:2, 0 : gshard_ref.shape[1]] = gshard_ref[...].astype(F32)
    gain_cols = square[...].T
    for side in range(2):
        for j in range(4):
            src, at = (wqkv_ref, j * width) if j < 3 else (wout_ref, 0)
            sh[side, :, j * half : (j + 1) * half] = src[:, at + side * half : at + (side + 1) * half].astype(F32)
        sh[side, :, 4 * half :] = gain_cols[0 : gshard_ref.shape[1], :]
    st[c] = sh[c]

    greet(peers_of(z, y, x, c) + [core, xpeer])
    zero = links.push(sh.at[1 - c], st.at[c], core)

    deep = width // 2
    upper, lower = pl.ds(0, deep), pl.ds(deep, deep)

    def hand(src, dst, rows):
        return links.push(src.at[rows], dst.at[me_n, rows], xpeer)

    def onward(dst, rows):
        part = dst.at[(1 - x) * 2 + c, rows]
        return links.push(part, part, core)

    parts = [(hand(win_hbm, win4_hbm, upper), win4_hbm, upper)]

    wide = max(8, experts)
    hot = (iota((wide, tokens), 0).astype(F32) == row_ref[0:1, :]).astype(F32)
    before = (iota((tokens, tokens), 0) < iota((tokens, tokens), 1)).astype(BF16)
    rank = dot(hot.astype(BF16), before)
    base = (iota((wide, tokens), 0) * capacity).astype(F32)
    srow = jnp.sum(hot * (rank + base), axis=0, keepdims=True)

    def cols(j):
        return pl.ds(pl.multiple_of((2 * j + c) * half, 128), half)

    zero.wait()
    rows48 = jnp.concatenate((st[0], st[1]), axis=0)
    for j in range(4):
        wq[z, y, x, :, cols(j)] = rows48[:, j * half : (j + 1) * half].astype(BF16)
    wg[z, y, x] = rows48[:, 4 * half :].astype(BF16)
    ring_z = []
    for piece in range(2):
        group = []
        for k in (1, 2, 3):
            to = device(across(z, k), y, x, c)
            for j in (2 * piece, 2 * piece + 1):
                part = wq.at[z, y, x, :, cols(j)]
                group.append(links.push(part, part, to))
            if piece == 0:
                group.append(links.push(wg.at[z, y, x], wg.at[z, y, x], to))
        ring_z.append(group)

    listed = row_ref[...].T
    hot_c = (iota((tokens, 128), 1).astype(F32) == listed[:, 0:1]).astype(F32)
    after = (iota((tokens, tokens), 1) < iota((tokens, tokens), 0)).astype(BF16)
    rank_c = dot(after, hot_c.astype(BF16))
    base_c = (iota((tokens, 128), 1) * capacity).astype(F32)
    scol = jnp.sum(hot_c * (rank_c + base_c), axis=1, keepdims=True)
    col_ref[...] = jnp.where(iota(listed.shape, 1) == 0, scol, listed)

    def fill(values, out):
        @pl.loop(0, out.shape[0])
        def _(i):
            ids = (iota((capacity, tokens), 0) + i * capacity).astype(F32)
            out[i] = dot((ids == srow).astype(BF16), values).astype(BF16)

    loading_ct.wait()
    fill((jax.nn.sigmoid(listed[:, 1:2]) * ct_ref[...].astype(F32)).astype(BF16), dy_ref)

    ring_2 = []
    for piece in range(2):
        for copy in ring_z[piece]:
            copy.wait()
        ca, cb = cols(2 * piece), cols(2 * piece + 1)
        group = [
            links.push(wq.at[:, y, x, :, ca], wq.at[:, y, x, :, ca], ypeer),
            links.push(wq.at[:, y, x, :, cb], wq.at[:, y, x, :, cb], xpeer),
        ]
        if piece == 0:
            group.append(links.push(wg.at[:, y, x], wg.at[:, y, x], ypeer))
        ring_2.append(group)
    dy_copies = []
    for k in FLIPS:
        zz, yy = across(z, k >> 1), (1 - y if k & 1 else y)
        dy_copies.append(links.push(dy_ref.at[zz * 2 + yy], dyrow_hbm.at[me_e], device(zz, yy, x, c)))
    own_dy = loads.start(dy_ref.at[me_e], dyrow_hbm.at[me_e])
    ring_3 = []
    for piece in range(2):
        for copy in ring_2[piece]:
            copy.wait()
        ca, cb = cols(2 * piece), cols(2 * piece + 1)
        group = [
            links.push(wq.at[:, :, x, :, ca], wq.at[:, :, x, :, ca], xpeer),
            links.push(wq.at[:, y, :, :, cb], wq.at[:, y, :, :, cb], ypeer),
        ]
        if piece == 0:
            group.append(links.push(wg.at[:, :, x], wg.at[:, :, x], xpeer))
        ring_3.append(group)
    for src, dst, rows in ((win_hbm, win4_hbm, lower), (whid_hbm, whid4_hbm, upper), (whid_hbm, whid4_hbm, lower)):
        parts.append((hand(src, dst, rows), dst, rows))
    ring_4 = []
    for piece in range(2):
        for copy in ring_3[piece]:
            copy.wait()
        ring_4.append([links.push(wq.at[:, :, :, :, cols(j)], wq.at[:, :, :, :, cols(j)], core) for j in (2 * piece, 2 * piece + 1)])

    gains = jnp.transpose(wg[...].reshape(width, 128).astype(F32))[0:8, :]
    gain_ref[...] = gains
    gain_one = gains[0:1, :]
    gain_two = gains[1:2, :]
    loading_x.wait()
    for piece in range(2):
        for copy in ring_4[piece]:
            copy.wait()
    storing = [loads.start(wq, w_hbm)]
    core_slices = [links.push(src, dst.at[me_n], core) for src, dst in ((win_hbm, win4_hbm), (whid_hbm, whid4_hbm))]

    def pass_on(i):
        copy, dst, rows = parts[i]
        copy.wait()
        core_slices.append(onward(dst, rows))

    pass_on(0)

    @pl.loop(0, blocks)
    def _(i):
        rows = pl.ds(pl.multiple_of(i * BLOCK, BLOCK), BLOCK)
        normed, _f = normalize(x_ref[rows, :].astype(F32))
        act = (normed * gain_one).astype(BF16)
        qkv_ref[rows, :] = dot(act, weight(wq, 0, 3 * width)).astype(BF16)

    storing.append(loads.start(qkv_ref, qkv_hbm))
    col_scr[...] = jnp.zeros_like(col_scr)
    low = iota((BLOCK, 128), 1) < HEAD_DIM
    for qb in range(blocks):
        kb = max(0, qb - LOOKBACK)
        span = (qb - kb + 1) * BLOCK
        rows = pl.ds(qb * BLOCK, BLOCK)
        keys = pl.ds(kb * BLOCK, span)
        q_pos = iota((BLOCK, span), 0) + qb * BLOCK
        k_pos = iota((BLOCK, span), 1) + kb * BLOCK
        ok = (k_pos <= q_pos) & (col_ref[rows, 2:3] == row_ref[2:3, keys])
        bias_scr[:, :span] = jnp.where(ok, 0.0, BIG_NEGATIVE)

        @pl.loop(0, pairs)
        def _(hp):
            at = pl.multiple_of(hp * 128, 128)
            q = qkv_ref[rows, pl.ds(at, 128)] * jnp.asarray(HEAD_DIM**-0.5, BF16)
            k = qkv_ref[keys, pl.ds(width + at, 128)]
            v = qkv_ref[keys, pl.ds(2 * width + at, 128)]
            outs = []
            col = col_scr[rows, :]
            for side in range(2):
                mine = low if side == 0 else ~low
                s = dot_t(jnp.where(mine, q, 0), k) + bias_scr[:, :span]
                top = jnp.max(s, axis=1, keepdims=True)
                raised = jnp.exp(s - top)
                total = jnp.sum(raised, axis=1, keepdims=True)
                outs.append(dot((raised * (1.0 / total)).astype(BF16), v))
                col = jnp.where(iota((BLOCK, 128), 1) == 2 * hp + side, top + jnp.log(total), col)
            col_scr[rows, :] = col
            c_ref[rows, pl.ds(at, 128)] = jnp.where(low, outs[0], outs[1]).astype(BF16)

    storing.append(loads.start(c_ref, c_hbm))
    stat_ref[...] = col_scr[...].T

    @pl.loop(0, blocks)
    def _(i):
        rows = pl.ds(pl.multiple_of(i * BLOCK, BLOCK), BLOCK)
        hidden = x_ref[rows, :].astype(F32) + dot(c_ref[rows, :], weight(wq, 3 * width, 4 * width))
        h_ref[rows, :] = hidden
        normed, _f = normalize(hidden)
        a_scr[rows, :] = (normed * gain_two).astype(BF16)

    storing.append(loads.start(h_ref, h_hbm))
    fill(a_scr[...], act_ref)
    storing.append(loads.start(act_ref, act_hbm))
    for i in range(1, 4):
        pass_on(i)
    for copy in storing + [own_dy] + core_slices + dy_copies:
        copy.wait()


def head(tokens_in, cotangent, w_in, w_hid, listed, w_qkv, w_out, gain_shard, experts, capacity):
    tokens, width = tokens_in.shape
    any_spec = pl.BlockSpec(memory_space=pl.ANY)
    vmem = pl.BlockSpec(memory_space=pltpu.VMEM)
    slots = (experts, capacity, width)
    blocks = (4, 2, 2, 48, 4 * width)
    shard = (2, w_qkv.shape[0], 2 * width + 128)
    return pl.pallas_call(
        functools.partial(head_kernel, capacity, experts),
        out_shape=(
            jax.ShapeDtypeStruct((tokens, 3 * width), BF16),
            jax.ShapeDtypeStruct((tokens, width), BF16),
            jax.ShapeDtypeStruct((tokens, width), F32),
            jax.ShapeDtypeStruct(slots, BF16),
            jax.ShapeDtypeStruct(blocks, BF16),
            jax.ShapeDtypeStruct(slots, BF16),
            jax.ShapeDtypeStruct((4,) + w_in.shape, BF16),
            jax.ShapeDtypeStruct((4,) + w_hid.shape, BF16),
            jax.ShapeDtypeStruct((128, tokens), F32),
            jax.ShapeDtypeStruct((tokens, 8), F32),
            jax.ShapeDtypeStruct((8, width), F32),
        ),
        in_specs=[any_spec] * 4 + [vmem] * 4,
        out_specs=(any_spec,) * 8 + (vmem,) * 3,
        scratch_shapes=[
            pltpu.VMEM((tokens, width), BF16),
            pltpu.VMEM((tokens, width), BF16),
            pltpu.VMEM(shard, F32),
            pltpu.VMEM(shard, F32),
            pltpu.VMEM((128, 128), F32),
            pltpu.VMEM(blocks, BF16),
            pltpu.VMEM((4, 2, 2, 48, 128), BF16),
            pltpu.VMEM((tokens, 3 * width), BF16),
            pltpu.VMEM((tokens, width), BF16),
            pltpu.VMEM((tokens, width), F32),
            pltpu.VMEM((tokens, width), BF16),
            pltpu.VMEM(slots, BF16),
            pltpu.VMEM(slots, BF16),
            pltpu.VMEM((BLOCK, (LOOKBACK + 1) * BLOCK), F32),
            pltpu.VMEM((tokens, 128), F32),
            pltpu.SemaphoreType.DMA((48,)),
            pltpu.SemaphoreType.DMA((48,)),
            pltpu.SemaphoreType.DMA((16,)),
        ],
        compiler_params=pltpu.CompilerParams(vmem_limit_bytes=62 << 20, collective_id=0, has_side_effects=True),
        cost_estimate=pl.CostEstimate(flops=60 << 30, bytes_accessed=40 << 20, transcendentals=0),
    )(tokens_in, cotangent, w_in, w_hid, listed, w_qkv, w_out, gain_shard)


class Reduce:
    def __init__(self, spot, ph, gq, rc, r1, r2, r3, fin, r4, send_sems, recv_sems):
        self.z, self.y, self.x, self.c = spot
        self.gq, self.rc, self.r1, self.r2, self.r3, self.fin, self.r4 = (
            gq.at[ph],
            rc.at[ph],
            r1.at[ph],
            r2.at[ph],
            r3.at[ph],
            fin.at[ph],
            r4.at[ph],
        )
        self.base = ph * 7
        self.send, self.recv = send_sems, recv_sems

    def copy(self, i, src, dst, to):
        return pltpu.make_async_remote_copy(
            src_ref=src,
            dst_ref=dst,
            send_sem=self.send.at[self.base + i],
            recv_sem=self.recv.at[self.base + i],
            device_id=to,
            device_id_type=MESH,
        )

    def turn(self, i):
        return i * (1 - self.c) + self.y * self.c, self.x * (1 - self.c) + i * self.c

    def add(self, where, term):
        self.gq[where] = (self.gq[where].astype(F32) + term.astype(F32)).astype(BF16)

    def cores(self):
        z, y, x, c = self.z, self.y, self.x, self.c
        return self.copy(0, self.gq.at[1 - c], self.rc, device(z, y, x, 1 - c))

    def by_core(self, go, first, second):
        @pl.when(self.c == 0)
        def _():
            go(first)

        @pl.when(self.c == 1)
        def _():
            go(second)

    def one(self, go):
        z, y, x, c = self.z, self.y, self.x, self.c
        self.by_core(
            go,
            self.copy(1, self.gq.at[0, :, :, 1 - x], self.r1, device(z, y, 1 - x, c)),
            self.copy(1, self.gq.at[1, :, 1 - y], self.r1, device(z, 1 - y, x, c)),
        )

    def two(self, go):
        z, y, x, c = self.z, self.y, self.x, self.c
        self.by_core(
            go,
            self.copy(2, self.gq.at[0, :, 1 - y, x], self.r2, device(z, 1 - y, x, c)),
            self.copy(2, self.gq.at[1, :, y, 1 - x], self.r2, device(z, y, 1 - x, c)),
        )

    def three(self):
        z, y, x, c = self.z, self.y, self.x, self.c
        return [
            self.copy(2 + k, self.gq.at[c, across(z, k), y, x], self.r3.at[k - 1], device(across(z, k), y, x, c))
            for k in (1, 2, 3)
        ]

    def four(self):
        z, y, x, c = self.z, self.y, self.x, self.c
        rows = pl.ds(pl.multiple_of((1 - c) * 24, 8), 24)
        return self.copy(6, self.fin.at[rows], self.r4, device(z, y, x, 1 - c))

    def step(self, stage):
        z, y, x, c = self.z, self.y, self.x, self.c
        if stage == 0:
            self.cores().start()
        if stage == 1:
            self.cores().wait()

            @pl.loop(0, 4)
            def _(k):
                self.add((c, k), self.rc[k])

            self.one(lambda copy: copy.start())
        if stage == 2:
            self.one(lambda copy: copy.wait())

            @pl.loop(0, 4)
            def _(k):
                for i in range(2):
                    yy, xx = self.turn(i)
                    self.add((c, k, yy, xx), self.r1[k, i])

            self.two(lambda copy: copy.start())
        if stage == 3:
            self.two(lambda copy: copy.wait())

            @pl.loop(0, 4)
            def _(k):
                self.add((c, k, y, x), self.r2[k])

            for copy in self.three():
                copy.start()
        if stage == 4:
            for copy in self.three():
                copy.wait()
            total = self.gq[c, z, y, x].astype(F32)
            for k in range(3):
                total = total + self.r3[k].astype(F32)
            self.fin[...] = total
            self.four().start()


def tail_kernel(
    ret_hbm,
    x_hbm,
    ct_hbm,
    h_hbm,
    qkv_hbm,
    c_hbm,
    w_hbm,
    yrow_hbm,
    gw_hbm,
    col_ref,
    row_ref,
    stat_ref,
    gain_ref,
    gt_hbm,
    r1_hbm,
    r2_hbm,
    gw_out,
    out_hbm,
    ownq_ref,
    owno_ref,
    gg_ref,
    ret_ref,
    x_ref,
    ct_ref,
    h_ref,
    qkv_ref,
    c_ref,
    w_ref,
    gt_ref,
    dc_scr,
    dhb_scr,
    dqkv_scr,
    actt_scr,
    d_scr,
    dk_scr,
    dv_scr,
    gq,
    rc,
    q1,
    q2,
    q3,
    fin,
    q4,
    ggs,
    rg,
    na,
    nb,
    nsum,
    yback,
    send_sems,
    recv_sems,
    red_send,
    red_recv,
    load_sems,
):
    spot = place()
    z, y, x, c = spot
    me_e = z * 2 + y
    tokens, width = x_ref.shape
    slots, _w = ret_ref.shape
    blocks = tokens // BLOCK
    half = width // 2
    core, xpeer, ypeer = device(z, y, x, 1 - c), device(z, y, 1 - x, c), device(z, 1 - y, x, c)
    far = peers_of(z, y, x, c)
    links = Links(send_sems, recv_sems)
    loads = Loads(load_sems)

    def reduce(ph):
        return Reduce(spot, ph, gq, rc, q1, q2, q3, fin, q4, red_send, red_recv)

    first = [
        loads.start(a, b)
        for a, b in (
            (ret_hbm, ret_ref),
            (h_hbm, h_ref),
            (w_hbm.at[:, :, :, :, pl.ds(3 * width, width)], w_ref.at[:, :, :, :, pl.ds(3 * width, width)]),
            (ct_hbm, ct_ref),
            (c_hbm, c_ref),
        )
    ]
    second = [
        loads.start(a, b)
        for a, b in (
            (x_hbm, x_ref),
            (qkv_hbm, qkv_ref),
            (w_hbm.at[:, :, :, :, pl.ds(0, 3 * width)], w_ref.at[:, :, :, :, pl.ds(0, 3 * width)]),
            (yrow_hbm.at[me_e], yback.at[me_e]),
        )
    ]
    greet(far + [core, xpeer])

    w_copies = [links.push(gw_hbm.at[xx * 2 + 1 - c], r1_hbm.at[xx], core) for xx in range(2)]
    y_copies = [links.push(yrow_hbm.at[to[0]], yback.at[me_e], to) for to in far]

    gain_one = gain_ref[0:1, :]
    gain_two = gain_ref[1:2, :]
    member = (iota((16, width), 1) // HEAD_DIM == iota((16, width), 0)).astype(F32)
    for copy in first:
        copy.wait()
    ggs[...] = jnp.zeros_like(ggs)

    def picks(rows):
        return (iota((BLOCK, slots), 1).astype(F32) == col_ref[rows, 0:1]).astype(BF16)

    @pl.loop(0, blocks)
    def _(i):
        rows = pl.ds(pl.multiple_of(i * BLOCK, BLOCK), BLOCK)
        da = dot(picks(rows), ret_ref[...])
        normed, factor = normalize(h_ref[rows, :])
        ggs[0, 1:2, :] += jnp.sum(da * normed, axis=0, keepdims=True)
        dh = ct_ref[rows, :].astype(F32) + norm_back(da * gain_two, normed, factor)
        gt_ref[rows, :] = dh
        dhb = dh.astype(BF16)
        dhb_scr[rows, :] = dhb
        dc = dot_t(dhb, weight(w_ref, 3 * width, 4 * width)).astype(BF16)
        dc_scr[rows, :] = dc
        d_scr[:, rows] = lax.dot_general(
            member,
            dc.astype(F32) * c_ref[rows, :].astype(F32),
            (((1,), (1,)), ((), ())),
            precision=lax.Precision.HIGHEST,
            preferred_element_type=F32,
        )

    def put(ph, value):
        for owner in range(2):
            for chip in range(16):
                gq[ph, owner, chip // 4, chip // 2 % 2, chip % 2] = value[
                    chip * 48 : chip * 48 + 48, owner * half : (owner + 1) * half
                ].astype(BF16)

    put(0, t_dot(c_ref[...], dhb_scr[...]))
    reduce(0).step(0)

    for copy in w_copies:
        copy.wait()

    def to_x(i):
        rows = pl.ds(pl.multiple_of(i * (width // 4), width // 4), width // 4)
        return pltpu.make_async_remote_copy(
            src_ref=nsum.at[0, rows],
            dst_ref=r2_hbm.at[rows],
            send_sem=send_sems.at[16 + i],
            recv_sem=recv_sems.at[16 + i],
            device_id=xpeer,
            device_id_type=MESH,
        )

    for step in range(2):
        xx = 1 - x if step == 0 else x
        la = loads.start(gw_hbm.at[xx * 2 + c], na)
        lb = loads.start(r1_hbm.at[xx], nb)
        la.wait()
        lb.wait()
        nsum[step] = (na[...].astype(F32) + nb[...].astype(F32)).astype(BF16)
        if step == 0:
            to_x(0).start()

    for copy in second:
        copy.wait()

    @pl.loop(0, blocks)
    def _(i):
        rows = pl.ds(pl.multiple_of(i * BLOCK, BLOCK), BLOCK)
        normed, _f = normalize(x_ref[rows, :].astype(F32))
        dhb_scr[rows, :] = (normed * gain_one).astype(BF16)

    actt_scr[...] = dhb_scr[...].T
    low = iota((BLOCK, 128), 1) < HEAD_DIM
    scale = HEAD_DIM**-0.5

    @pl.loop(0, 3)
    def _(t):
        @pl.loop(0, 2)
        def _(inner):
            hp = 2 * t + inner
            at = pl.multiple_of(hp * 128, 128)
            dk_scr[...] = jnp.zeros_like(dk_scr)
            dv_scr[...] = jnp.zeros_like(dv_scr)
            for qb in range(blocks):
                rows = pl.ds(qb * BLOCK, BLOCK)
                q = qkv_ref[rows, pl.ds(at, 128)] * jnp.asarray(scale, BF16)
                dc = dc_scr[rows, pl.ds(at, 128)]
                q_half = [jnp.where(low, q, 0), jnp.where(low, 0, q)]
                dc_half = [jnp.where(low, dc, 0), jnp.where(low, 0, dc)]
                dq = jnp.zeros((BLOCK, 128), F32)
                for kb in range(max(0, qb - LOOKBACK), qb + 1):
                    keys = pl.ds(kb * BLOCK, BLOCK)
                    k = qkv_ref[keys, pl.ds(width + at, 128)]
                    v = qkv_ref[keys, pl.ds(2 * width + at, 128)]
                    ok = col_ref[keys, 2:3] == row_ref[2:3, rows]
                    if kb == qb:
                        ok = ok & (iota((BLOCK, BLOCK), 0) <= iota((BLOCK, BLOCK), 1))
                    ps, dss = [], []
                    for side in range(2):
                        s = dot_t(k, q_half[side])
                        p = jnp.where(ok, jnp.exp(s - stat_ref[pl.ds(2 * hp + side, 1), rows]), 0.0)
                        dp = dot_t(v, dc_half[side])
                        dss.append((p * (dp - d_scr[pl.ds(2 * hp + side, 1), rows])).astype(BF16))
                        ps.append(p.astype(BF16))
                    dv_scr[keys, :] += dot(jnp.concatenate(ps, 1), jnp.concatenate(dc_half, 0))
                    dk_scr[keys, :] += dot(jnp.concatenate(dss, 1), jnp.concatenate(q_half, 0))
                    dq += jnp.where(low, t_dot(dss[0], k), t_dot(dss[1], k))
                dqkv_scr[rows, pl.ds(at, 128)] = (dq * scale).astype(BF16)
            dqkv_scr[:, pl.ds(width + at, 128)] = dk_scr[...].astype(BF16)
            dqkv_scr[:, pl.ds(2 * width + at, 128)] = dv_scr[...].astype(BF16)

        columns = []
        for inner in range(2):
            at = pl.multiple_of((2 * t + inner) * 128, 128)
            columns += [dqkv_scr[:, pl.ds(j * width + at, 128)] for j in range(3)]
        put(t + 1, dot(actt_scr[...], jnp.concatenate(columns, axis=1)))
        reduce(t + 1).step(0)
        reduce(t).step(1)

        @pl.when(t >= 1)
        def _():
            reduce(t - 1).step(2)

        @pl.when(t >= 2)
        def _():
            reduce(t - 2).step(3)

        to_x(t + 1).start()

    @pl.loop(0, blocks)
    def _(i):
        rows = pl.ds(pl.multiple_of(i * BLOCK, BLOCK), BLOCK)
        normed, factor = normalize(x_ref[rows, :].astype(F32))
        dn = dot_t(dqkv_scr[rows, :], weight(w_ref, 0, 3 * width))
        ggs[0, 0:1, :] += jnp.sum(dn * normed, axis=0, keepdims=True)
        gt_ref[rows, :] += norm_back(dn * gain_one, normed, factor)

    stores = [loads.start(gt_ref, gt_hbm)]
    gains_copy = links.push(ggs.at[0], rg.at[0], core)
    reduce(3).step(1)
    reduce(2).step(2)
    reduce(1).step(3)
    reduce(0).step(4)
    gains_copy.wait()
    ggs[1] = ggs[0] + rg[0]
    gains_copy = links.push(ggs.at[1], rg.at[1], xpeer)

    def finish(lo, hi):
        @pl.loop(lo, hi)
        def _(i):
            rows = pl.ds(pl.multiple_of(i * BLOCK, BLOCK), BLOCK)
            got = dot(picks(rows), yback[...].reshape(slots, width))
            ct_ref[rows, :] = (h_ref[rows, :] + jax.nn.sigmoid(col_ref[rows, 1:2]) * got).astype(BF16)

    for copy in y_copies:
        copy.wait()
    finish(0, 2)
    reduce(3).step(2)
    reduce(2).step(3)
    reduce(1).step(4)
    gains_copy.wait()
    ggs[2] = ggs[1] + rg[1]
    gains_copy = links.push(ggs.at[2], rg.at[2], ypeer)
    finish(2, blocks)
    stores.append(loads.start(ct_ref, out_hbm))
    reduce(3).step(3)
    reduce(2).step(4)
    gains_copy.wait()
    ggs[3] = ggs[2] + rg[2]
    gain_copies = [links.push(ggs.at[3], rg.at[2 + k], device(across(z, k), y, x, c)) for k in (1, 2, 3)]
    for i in range(4):
        to_x(i).wait()
    lb = loads.start(r2_hbm, nb)
    lb.wait()
    gw_out[...] = nsum[1].astype(F32) + nb[...].astype(F32)
    reduce(3).step(4)
    for copy in gain_copies:
        copy.wait()
    share = width // 32
    mine = ((z * 2 + y) * 2 + x) * 2 + c
    take = (iota((width, 128), 0) == mine * share + iota((width, 128), 1)).astype(F32)
    gg_ref[...] = lax.dot_general(
        ggs[3] + rg[3] + rg[4] + rg[5],
        take,
        (((1,), (0,)), ((), ())),
        precision=lax.Precision.HIGHEST,
        preferred_element_type=F32,
    )[0:2, 0:share]
    for ph in range(4):
        kept = fin[ph, pl.ds(pl.multiple_of(c * 24, 8), 24), :]
        reduce(ph).four().wait()
        for owner, part in ((c, kept), (1 - c, q4[ph])):
            if ph == 0:
                owno_ref[:, pl.ds(pl.multiple_of(owner * half, 128), half)] = part
            else:
                for j in range(3):
                    at = pl.multiple_of(j * width + (2 * (ph - 1) + owner) * 128, 128)
                    ownq_ref[:, pl.ds(at, 128)] = part[:, j * 128 : (j + 1) * 128]
    for copy in stores:
        copy.wait()


def tail(returned, cols, rows, tokens_in, cotangent, hidden, qkv, context, stats, w_blocks, gains, y_rows, gw):
    tokens, width = tokens_in.shape
    slots = returned.shape[0]
    half = width // 2
    any_spec = pl.BlockSpec(memory_space=pl.ANY)
    vmem = pl.BlockSpec(memory_space=pltpu.VMEM)
    return pl.pallas_call(
        tail_kernel,
        out_shape=(
            jax.ShapeDtypeStruct((tokens, width), F32),
            jax.ShapeDtypeStruct((2,) + gw.shape[1:], BF16),
            jax.ShapeDtypeStruct(gw.shape[1:], BF16),
            jax.ShapeDtypeStruct(gw.shape[1:], F32),
            jax.ShapeDtypeStruct((tokens, width), BF16),
            jax.ShapeDtypeStruct((24, 3 * width), F32),
            jax.ShapeDtypeStruct((24, width), F32),
            jax.ShapeDtypeStruct((2, 24), F32),
        ),
        in_specs=[any_spec] * 9 + [vmem] * 4,
        out_specs=(any_spec, any_spec, any_spec, vmem, any_spec, vmem, vmem, vmem),
        scratch_shapes=[
            pltpu.VMEM((slots, width), BF16),
            pltpu.VMEM((tokens, width), BF16),
            pltpu.VMEM((tokens, width), BF16),
            pltpu.VMEM((tokens, width), F32),
            pltpu.VMEM((tokens, 3 * width), BF16),
            pltpu.VMEM((tokens, width), BF16),
            pltpu.VMEM(w_blocks.shape, BF16),
            pltpu.VMEM((tokens, width), F32),
            pltpu.VMEM((tokens, width), BF16),
            pltpu.VMEM((tokens, width), BF16),
            pltpu.VMEM((tokens, 3 * width), BF16),
            pltpu.VMEM((width, tokens), BF16),
            pltpu.VMEM((16, tokens), F32),
            pltpu.VMEM((tokens, 128), F32),
            pltpu.VMEM((tokens, 128), F32),
            pltpu.VMEM((4, 2, 4, 2, 2, 48, half), BF16),
            pltpu.VMEM((4, 4, 2, 2, 48, half), BF16),
            pltpu.VMEM((4, 4, 2, 48, half), BF16),
            pltpu.VMEM((4, 4, 48, half), BF16),
            pltpu.VMEM((4, 3, 48, half), BF16),
            pltpu.VMEM((4, 48, half), F32),
            pltpu.VMEM((4, 24, half), F32),
            pltpu.VMEM((4, 8, width), F32),
            pltpu.VMEM((6, 8, width), F32),
            pltpu.VMEM(gw.shape[1:], BF16),
            pltpu.VMEM(gw.shape[1:], BF16),
            pltpu.VMEM((2,) + gw.shape[1:], BF16),
            pltpu.VMEM(y_rows.shape, BF16),
            pltpu.SemaphoreType.DMA((20,)),
            pltpu.SemaphoreType.DMA((20,)),
            pltpu.SemaphoreType.DMA((28,)),
            pltpu.SemaphoreType.DMA((28,)),
            pltpu.SemaphoreType.DMA((16,)),
        ],
        compiler_params=pltpu.CompilerParams(vmem_limit_bytes=62 << 20, collective_id=2, has_side_effects=True),
        cost_estimate=pl.CostEstimate(flops=80 << 30, bytes_accessed=40 << 20, transcendentals=0),
    )(returned, tokens_in, cotangent, hidden, qkv, context, w_blocks, y_rows, gw, cols, rows, stats, gains)


def flipped(z, y, k):
    hi, lo = z // 2, lax.rem(z, 2)
    zz = lax.rem(hi + k // 4, 2) * 2 + lax.rem(lo + lax.rem(k // 2, 2), 2)
    return zz, lax.rem(y + lax.rem(k, 2), 2)


def swap_kernel(
    act_hbm,
    dy_hbm,
    win_hbm,
    whid_hbm,
    own_in_hbm,
    own_hid_hbm,
    ret_hbm,
    y_hbm,
    gin_hbm,
    ghid_hbm,
    a_ref,
    dy_ref,
    win_ref,
    whid_ref,
    g_ref,
    du_ref,
    da_ref,
    us,
    gs,
    stage,
    near,
    next_x,
    send_sems,
    recv_sems,
    load_sems,
):
    z, y, x, c = place()
    me = z * 2 + y
    me_n = x * 2 + c
    count, cap, width = a_ref.shape
    parts = win_ref.shape[0]
    wide = win_ref.shape[2]
    loads = Loads(load_sems)
    first = [
        loads.start(a, b)
        for a, b in (
            (act_hbm.at[me], a_ref.at[me]),
            (own_in_hbm, win_ref.at[me_n]),
            (own_hid_hbm, whid_ref.at[me_n]),
            (dy_hbm, dy_ref),
        )
    ]
    for i in range(1, parts):
        n = lax.rem(me_n + i, parts)
        first += [loads.start(win_hbm.at[n], win_ref.at[n]), loads.start(whid_hbm.at[n], whid_ref.at[n])]

    def partner(k):
        zz, yy = flipped(z, y, k)
        return zz * 2 + yy, device(zz, yy, x, c)

    def outward(k):
        e, to = partner(k)
        return pltpu.make_async_remote_copy(
            src_ref=act_hbm.at[e],
            dst_ref=a_ref.at[me],
            send_sem=send_sems.at[k],
            recv_sem=recv_sems.at[k],
            device_id=to,
            device_id_type=MESH,
        )

    def homeward(k):
        e, to = partner(k)
        return pltpu.make_async_remote_copy(
            src_ref=da_ref.at[e],
            dst_ref=ret_hbm.at[me],
            send_sem=send_sems.at[8 + k],
            recv_sem=recv_sems.at[8 + k],
            device_id=to,
            device_id_type=MESH,
        )

    core, xpeer = device(z, y, x, 1 - c), device(z, y, 1 - x, c)
    greet([partner(k)[1] for k in range(1, 8)] + [core, xpeer])
    for k in FLIPS:
        outward(k).start()
    for copy in first:
        copy.wait()

    @pl.loop(0, count)
    def _(k):
        @pl.when(k > 0)
        def _():
            outward(k).wait_recv()

        e, _to = partner(k)
        a = a_ref[e]
        dy = dy_ref[e]
        rows = pl.ds(pl.multiple_of(e * cap, cap), cap)

        def enter(j):
            us[j % 2] = dot(a, win_ref[j])
            gs[j % 2] = dot_t(dy, whid_ref[j])

        def bend(j):
            g, slope = gelu_pair(us[j % 2])
            g_ref[rows, j * wide : (j + 1) * wide] = g.astype(BF16)
            du_ref[rows, j * wide : (j + 1) * wide] = (gs[j % 2] * slope).astype(BF16)

        def leave(j):
            return dot_t(du_ref[rows, j * wide : (j + 1) * wide], win_ref[j])

        enter(0)
        total = None
        for j in range(parts):
            if j + 1 < parts:
                enter(j + 1)
            bend(j)
            if j > 0:
                term = leave(j - 1)
                total = term if total is None else total + term
        da_ref[e] = (total + leave(parts - 1)).astype(BF16)

        @pl.when(k > 0)
        def _():
            homeward(k).start()

    own = loads.start(da_ref.at[me], ret_hbm.at[me])

    def put(i, out):
        return pltpu.make_async_copy(stage.at[i], out, load_sems.at[16 + i])

    def third(i, src, dst, to):
        return pltpu.make_async_remote_copy(
            src_ref=src,
            dst_ref=dst,
            send_sem=send_sems.at[16 + i],
            recv_sem=recv_sems.at[16 + i],
            device_id=to,
            device_id_type=MESH,
        )

    acts = a_ref[...].reshape(count * cap, width)

    @pl.loop(0, parts)
    def _(j):
        cols = pl.ds(pl.multiple_of(j * wide, wide), wide)
        win_ref[j] = t_dot(acts, du_ref[:, cols]).astype(BF16)

    to_core = [third(xx, win_ref.at[xx * 2 + 1 - c], near.at[xx], core) for xx in range(2)]
    for copy in to_core:
        copy.start()

    @pl.loop(0, parts // 2)
    def _(jj):
        for i in range(2):
            j = 2 * jj + i
            cols = pl.ds(pl.multiple_of(j * wide, wide), wide)

            @pl.when(jj >= 1)
            def _():
                put(i, ghid_hbm.at[j - 2]).wait()

            stage[i] = t_dot(g_ref[:, cols], dy_ref[...].reshape(count * cap, width)).astype(BF16)
            put(i, ghid_hbm.at[j]).start()

    for copy in to_core:
        copy.wait()
    other = (1 - x) * 2 + c
    win_ref[other] = (win_ref[other].astype(F32) + near[1 - x].astype(F32)).astype(BF16)
    to_x = third(2, win_ref.at[other], next_x, xpeer)
    to_x.start()

    @pl.loop(0, count)
    def _(i):
        rows = pl.ds(pl.multiple_of(i * cap, cap), cap)
        a_ref[i] = dot(g_ref[rows, :], whid_ref[...].reshape(parts * wide, width)).astype(BF16)

    out = loads.start(a_ref, y_hbm)
    for i in range(2):
        put(i, ghid_hbm.at[parts - 2 + i]).wait()
    to_x.wait()
    tiles = []
    for i, tile in enumerate((us.at[0], us.at[1], gs.at[0])):
        rows = pl.ds(i * cap, cap)
        tile[...] = win_ref[me_n, rows].astype(F32) + near[x, rows].astype(F32) + next_x[rows].astype(F32)
        tiles.append(loads.start(tile, gin_hbm.at[rows]))
    for k in range(1, 8):
        outward(k).wait_send()
        homeward(k).wait()
    for copy in tiles + [own, out]:
        copy.wait()


def swap(act_slots, dy_rows, w_in, w_hid, own_in, own_hid):
    count, cap, width = act_slots.shape
    parts, _, wide = w_in.shape
    hidden = parts * wide
    any_spec = pl.BlockSpec(memory_space=pl.ANY)
    return pl.pallas_call(
        swap_kernel,
        out_shape=(
            jax.ShapeDtypeStruct((count, cap, width), BF16),
            jax.ShapeDtypeStruct((count, cap, width), BF16),
            jax.ShapeDtypeStruct((width, wide), F32),
            jax.ShapeDtypeStruct((parts, wide, width), BF16),
        ),
        in_specs=[any_spec] * 6,
        out_specs=(any_spec,) * 4,
        scratch_shapes=[
            pltpu.VMEM((count, cap, width), BF16),
            pltpu.VMEM((count, cap, width), BF16),
            pltpu.VMEM(w_in.shape, BF16),
            pltpu.VMEM(w_hid.shape, BF16),
            pltpu.VMEM((count * cap, hidden), BF16),
            pltpu.VMEM((count * cap, hidden), BF16),
            pltpu.VMEM((count, cap, width), BF16),
            pltpu.VMEM((2, cap, wide), F32),
            pltpu.VMEM((2, cap, wide), F32),
            pltpu.VMEM((2, width, wide), BF16),
            pltpu.VMEM((2, width, wide), BF16),
            pltpu.VMEM((width, wide), BF16),
            pltpu.SemaphoreType.DMA((20,)),
            pltpu.SemaphoreType.DMA((20,)),
            pltpu.SemaphoreType.DMA((18,)),
        ],
        compiler_params=pltpu.CompilerParams(vmem_limit_bytes=62 << 20, collective_id=1, has_side_effects=True),
        cost_estimate=pl.CostEstimate(flops=100 << 30, bytes_accessed=60 << 20, transcendentals=0),
    )(act_slots, dy_rows, w_in, w_hid, own_in, own_hid)


def local(tokens, segments, routes, gate_logit, w_qkv, w_out, norm_gains, w_in, w_hid, cotangent):
    tok_count, width = tokens.shape
    n_expert = lax.axis_size("expert")
    n_narrow = lax.axis_size("narrow")
    capacity = 2 * tok_count // n_expert
    slot_rows = n_expert * capacity
    everyone = ("expert", "narrow")

    if n_expert == 8 and n_narrow == 4:
        listed = jnp.concatenate(
            (
                routes.reshape(1, tok_count).astype(F32),
                gate_logit.reshape(1, tok_count),
                segments.reshape(1, tok_count).astype(F32),
                jnp.zeros((5, tok_count), F32),
            )
        )
        qkv, context, hidden, act_slots, w_blocks, dy_rows, w_in_all, w_hid_all, stats, cols, gains = head(
            tokens, cotangent, w_in[0], w_hid[0], listed, w_qkv, w_out, norm_gains, n_expert, capacity
        )
        da_back, y_rows, gin_own, ghid = swap(act_slots, dy_rows, w_in_all, w_hid_all, w_in[0], w_hid[0])
        grad_tokens, _r1, _r2, ghid_own, block_out, own_qkv, own_out, own_gains = tail(
            da_back.reshape(slot_rows, width),
            cols,
            listed,
            tokens,
            cotangent,
            hidden,
            qkv,
            context,
            stats,
            w_blocks,
            gains,
            y_rows,
            ghid,
        )
        return (
            block_out,
            grad_tokens,
            own_qkv,
            own_out,
            own_gains,
            gin_own[None],
            ghid_own[None],
        )
    gain_cols = jnp.pad(norm_gains.T, ((0, 0), (0, 126)))
    w_all = lax.all_gather(
        jnp.concatenate((w_qkv, w_out, gain_cols), axis=1), everyone, axis=0, tiled=True
    )
    gains = w_all[:, 4 * width : 4 * width + 2].T.astype(F32)
    w_in_all = lax.all_gather(w_in[0], "narrow", axis=0, tiled=False)
    w_hid_all = lax.all_gather(w_hid[0], "narrow", axis=0, tiled=False)

    def exchange(values):
        return lax.all_to_all(
            values.reshape(n_expert, capacity, width), "expert", split_axis=0, concat_axis=0, tiled=True
        ).reshape(slot_rows, width)

    segr = segments.reshape(1, tok_count)
    segc = segments.reshape(tok_count, 1)
    srow, scol, dy_slots = prep(routes, gate_logit, cotangent, n_expert, capacity)
    dy_rows = exchange(dy_slots)
    qkv, context, stats, hidden, act_slots = attend_fwd(tokens, w_all, gains, segr, segc, srow, slot_rows)
    act_rows = exchange(act_slots)
    activated, grad_pre, da_rows = experts(act_rows, dy_rows, w_in_all, w_hid_all)
    da_back = exchange(da_rows)
    hidden_units = activated.shape[1]
    y_rows = dot(activated, w_hid_all.reshape(hidden_units, width)).astype(BF16)
    grad_hid = t_dot(activated, dy_rows).astype(BF16)
    grad_in = lax.dot_general(
        act_rows, grad_pre.reshape(slot_rows, n_narrow, -1), (((0,), (0,)), ((), ())), preferred_element_type=F32
    ).astype(BF16)
    y_back = exchange(y_rows)
    grad_tokens, grad_w, grad_gains = attend_bwd(
        da_back, scol, tokens, cotangent, hidden, qkv, context, stats, w_all, gains, segr, segc
    )
    block_out = block_output(y_back, scol, hidden, gate_logit)
    grad_hid_w = lax.psum_scatter(grad_hid, "narrow", scatter_dimension=0, tiled=True).astype(F32)[None]
    grad_in_w = lax.psum_scatter(grad_in, "narrow", scatter_dimension=1, tiled=True).astype(F32)
    grad_in_w = grad_in_w.reshape(1, width, -1)
    packed = jnp.concatenate((grad_w, jnp.pad(grad_gains[:2].T, ((0, 0), (0, 126)))), axis=1)
    own = lax.psum_scatter(packed, everyone, scatter_dimension=0, tiled=True)
    return (
        block_out,
        grad_tokens,
        own[:, : 3 * width],
        own[:, 3 * width : 4 * width],
        own[:, 4 * width : 4 * width + 2].T,
        grad_in_w,
        grad_hid_w,
    )


def solution(mesh):
    placed = (
        P(("expert", "narrow"), None),
        P(("expert", "narrow"), None),
        P(("expert", "narrow"), None),
        P(("expert", "narrow")),
        P(("expert", "narrow"), None),
        P(("expert", "narrow"), None),
        P(None, ("expert", "narrow")),
        P("expert", None, "narrow"),
        P("expert", "narrow", None),
        P(("expert", "narrow"), None),
    )
    return jax.shard_map(
        local,
        mesh=mesh,
        in_specs=placed,
        out_specs=(
            P(("expert", "narrow"), None),
            P(("expert", "narrow"), None),
            P(("expert", "narrow"), None),
            P(("expert", "narrow"), None),
            P(None, ("expert", "narrow")),
            P("expert", None, "narrow"),
            P("expert", "narrow", None),
        ),
        check_vma=False,
    )
```

```python
import functools

import jax
import jax.numpy as jnp
from jax import lax
from jax.experimental import pallas as pl
from jax.experimental.pallas import tpu as pltpu
from jax.sharding import PartitionSpec as P

HEAD_DIM = 64
SEQ = 1024
BLOCK = 256
LOOKBACK = 2
EPSILON = 1e-05
BIG_NEGATIVE = -1e30
F32 = jnp.float32
BF16 = jnp.bfloat16

TAIL_P = 0.3
TAIL_C = (
    0.11962923306946524,
    0.12075497050525577,
    0.0999071263144056,
    0.12858273368127124,
    -0.053723704944995426,
    0.20639718480180155,
    -0.1572285075725372,
    0.03568089149479804,
)


def dot(a, b):
    return lax.dot_general(a, b, (((1,), (0,)), ((), ())), preferred_element_type=F32)


def dot_t(a, b):
    return lax.dot_general(a, b, (((1,), (1,)), ((), ())), preferred_element_type=F32)


def t_dot(a, b):
    return lax.dot_general(a, b, (((0,), (0,)), ((), ())), preferred_element_type=F32)


def normalize(values):
    centre = jnp.mean(values, axis=-1, keepdims=True)
    shifted = values - centre
    factor = lax.rsqrt(jnp.mean(shifted * shifted, axis=-1, keepdims=True) + EPSILON)
    return shifted * factor, factor


def norm_back(grad_normed, normed, factor):
    return factor * (
        grad_normed
        - jnp.mean(grad_normed, axis=-1, keepdims=True)
        - normed * jnp.mean(grad_normed * normed, axis=-1, keepdims=True)
    )


def gelu_pair(u):
    size = jnp.abs(u)
    t = 1.0 / (1.0 + TAIL_P * size)
    poly = jnp.full_like(t, TAIL_C[-1])
    for c in TAIL_C[-2::-1]:
        poly = poly * t + c
    bell = jnp.exp(-0.5 * (u * u))
    tail = poly * t * bell
    phi = jnp.where(u >= 0, 1.0 - tail, tail)
    return u * phi, phi + u * (bell * 0.3989422804014327)


def iota(shape, dim):
    return lax.broadcasted_iota(jnp.int32, shape, dim)


def prep_kernel(capacity, experts, rrow_ref, rcol_ref, gate_ref, ct_ref, srow_ref, scol_ref, send_ref):
    tokens = ct_ref.shape[0]
    wide = max(8, experts)
    hot = (iota((wide, tokens), 0) == rrow_ref[...]).astype(F32)
    before = (iota((tokens, tokens), 0) < iota((tokens, tokens), 1)).astype(BF16)
    rank = dot(hot.astype(BF16), before)
    base = (iota((wide, tokens), 0) * capacity).astype(F32)
    srow = jnp.sum(hot * (rank + base), axis=0, keepdims=True)
    srow_ref[...] = jnp.broadcast_to(srow, srow_ref.shape)
    hot_c = (iota((tokens, 128), 1) == rcol_ref[...]).astype(F32)
    after = (iota((tokens, tokens), 1) < iota((tokens, tokens), 0)).astype(BF16)
    rank_c = dot(after, hot_c.astype(BF16))
    base_c = (iota((tokens, 128), 1) * capacity).astype(F32)
    scol_ref[...] = jnp.sum(hot_c * (rank_c + base_c), axis=1, keepdims=True)
    gated = (jax.nn.sigmoid(gate_ref[...]) * ct_ref[...].astype(F32)).astype(BF16)
    fill_slots(srow, gated, send_ref)


def fill_slots(srow, values, send_ref):
    rows = send_ref.shape[0]
    tokens = values.shape[0]

    @pl.loop(0, rows // BLOCK)
    def _(i):
        first = i * BLOCK
        ids = (iota((BLOCK, tokens), 0) + first).astype(F32)
        pick = (ids == srow).astype(BF16)
        send_ref[pl.ds(pl.multiple_of(first, BLOCK), BLOCK), :] = dot(pick, values).astype(BF16)


def prep(routes, gate_logit, cotangent, experts, capacity):
    tokens, width = cotangent.shape
    return pl.pallas_call(
        functools.partial(prep_kernel, capacity, experts),
        out_shape=(
            jax.ShapeDtypeStruct((8, tokens), F32),
            jax.ShapeDtypeStruct((tokens, 1), F32),
            jax.ShapeDtypeStruct((experts * capacity, width), BF16),
        ),
        compiler_params=pltpu.CompilerParams(vmem_limit_bytes=56 << 20),
        cost_estimate=pl.CostEstimate(flops=8 << 30, bytes_accessed=8 << 20, transcendentals=0),
    )(routes.reshape(1, tokens), routes, gate_logit.reshape(tokens, 1), cotangent)


def fwd_kernel(
    x_ref, w_ref, gain_ref, segr_ref, segc_ref, srow_ref, qkv_ref, c_ref, stat_ref, h_ref, send_ref, act_scr, bias_scr, col_scr
):
    tokens, width = x_ref.shape
    blocks = tokens // BLOCK
    pairs = width // 128
    gain_one = gain_ref[0:1, :]
    gain_two = gain_ref[1:2, :]

    @pl.loop(0, blocks)
    def _(i):
        rows = pl.ds(pl.multiple_of(i * BLOCK, BLOCK), BLOCK)
        normed, _f = normalize(x_ref[rows, :].astype(F32))
        act = (normed * gain_one).astype(BF16)
        qkv_ref[rows, :] = dot(act, w_ref[:, : 3 * width]).astype(BF16)

    col_scr[...] = jnp.zeros_like(col_scr)
    low = iota((BLOCK, 128), 1) < HEAD_DIM
    for qb in range(blocks):
        kb = max(0, qb - LOOKBACK)
        span = (qb - kb + 1) * BLOCK
        rows = pl.ds(qb * BLOCK, BLOCK)
        keys = pl.ds(kb * BLOCK, span)
        q_pos = iota((BLOCK, span), 0) + qb * BLOCK
        k_pos = iota((BLOCK, span), 1) + kb * BLOCK
        ok = (k_pos <= q_pos) & (segc_ref[rows, :] == segr_ref[0:1, keys])
        bias_scr[:, :span] = jnp.where(ok, 0.0, BIG_NEGATIVE)

        @pl.loop(0, pairs)
        def _(hp):
            at = pl.multiple_of(hp * 128, 128)
            q = qkv_ref[rows, pl.ds(at, 128)] * jnp.asarray(HEAD_DIM**-0.5, BF16)
            k = qkv_ref[keys, pl.ds(width + at, 128)]
            v = qkv_ref[keys, pl.ds(2 * width + at, 128)]
            outs = []
            col = col_scr[rows, :]
            for half in range(2):
                mine = low if half == 0 else ~low
                s = dot_t(jnp.where(mine, q, 0), k) + bias_scr[:, :span]
                top = jnp.max(s, axis=1, keepdims=True)
                raised = jnp.exp(s - top)
                total = jnp.sum(raised, axis=1, keepdims=True)
                outs.append(dot((raised * (1.0 / total)).astype(BF16), v))
                col = jnp.where(iota((BLOCK, 128), 1) == 2 * hp + half, top + jnp.log(total), col)
            col_scr[rows, :] = col
            c_ref[rows, pl.ds(at, 128)] = jnp.where(low, outs[0], outs[1]).astype(BF16)

    stat_ref[...] = col_scr[...].T

    @pl.loop(0, blocks)
    def _(i):
        rows = pl.ds(pl.multiple_of(i * BLOCK, BLOCK), BLOCK)
        hidden = x_ref[rows, :].astype(F32) + dot(c_ref[rows, :], w_ref[:, 3 * width : 4 * width])
        h_ref[rows, :] = hidden
        normed, _f = normalize(hidden)
        act_scr[rows, :] = (normed * gain_two).astype(BF16)

    fill_slots(srow_ref[0:1, :], act_scr[...], send_ref)


def attend_fwd(tokens_in, w_all, gains, segr, segc, srow, slot_rows):
    tokens, width = tokens_in.shape
    return pl.pallas_call(
        fwd_kernel,
        out_shape=(
            jax.ShapeDtypeStruct((tokens, 3 * width), BF16),
            jax.ShapeDtypeStruct((tokens, width), BF16),
            jax.ShapeDtypeStruct((128, tokens), F32),
            jax.ShapeDtypeStruct((tokens, width), F32),
            jax.ShapeDtypeStruct((slot_rows, width), BF16),
        ),
        scratch_shapes=[
            pltpu.VMEM((tokens, width), BF16),
            pltpu.VMEM((BLOCK, (LOOKBACK + 1) * BLOCK), F32),
            pltpu.VMEM((tokens, 128), F32),
        ],
        compiler_params=pltpu.CompilerParams(vmem_limit_bytes=56 << 20),
        cost_estimate=pl.CostEstimate(flops=40 << 30, bytes_accessed=24 << 20, transcendentals=0),
    )(tokens_in, w_all, gains, segr, segc, srow)


def expert_kernel(a_ref, dy_ref, win_ref, whid_ref, g_ref, du_ref, da_ref, acc_scr):
    a = a_ref[...]
    dy = dy_ref[...]
    parts = win_ref.shape[0]
    wide = win_ref.shape[2]
    acc_scr[...] = jnp.zeros_like(acc_scr)

    @pl.loop(0, parts)
    def _(j):
        cols = pl.ds(pl.multiple_of(j * wide, wide), wide)
        u = dot(a, win_ref[j])
        grad = dot_t(dy, whid_ref[j])
        g, slope = gelu_pair(u)
        g_ref[:, cols] = g.astype(BF16)
        du = (grad * slope).astype(BF16)
        du_ref[:, cols] = du
        acc_scr[...] += dot_t(du, win_ref[j])

    da_ref[...] = acc_scr[...].astype(BF16)


def experts(acts, grads, w_in, w_hid):
    rows, width = acts.shape
    parts, _, wide = w_in.shape
    hidden = parts * wide
    row_spec = pl.BlockSpec((BLOCK, width), lambda i: (i, 0))
    wide_spec = pl.BlockSpec((BLOCK, hidden), lambda i: (i, 0))
    return pl.pallas_call(
        expert_kernel,
        grid=(rows // BLOCK,),
        out_shape=(
            jax.ShapeDtypeStruct((rows, hidden), BF16),
            jax.ShapeDtypeStruct((rows, hidden), BF16),
            jax.ShapeDtypeStruct((rows, width), BF16),
        ),
        in_specs=[
            row_spec,
            row_spec,
            pl.BlockSpec(w_in.shape, lambda i: (0, 0, 0), pipeline_mode=pl.Buffered(1)),
            pl.BlockSpec(w_hid.shape, lambda i: (0, 0, 0), pipeline_mode=pl.Buffered(1)),
        ],
        out_specs=(wide_spec, wide_spec, row_spec),
        scratch_shapes=[pltpu.VMEM((BLOCK, width), F32)],
        compiler_params=pltpu.CompilerParams(vmem_limit_bytes=56 << 20),
        cost_estimate=pl.CostEstimate(flops=60 << 30, bytes_accessed=40 << 20, transcendentals=0),
    )(acts, grads, w_in, w_hid)


def out_kernel(ret_ref, scol_ref, h_ref, gate_ref, out_ref):
    tokens, rows = out_ref.shape[0], ret_ref.shape[0]
    pick = (iota((tokens, rows), 1).astype(F32) == scol_ref[...]).astype(BF16)
    y = dot(pick, ret_ref[...])
    out_ref[...] = (h_ref[...] + jax.nn.sigmoid(gate_ref[...]) * y).astype(BF16)


def block_output(returned, scol, hidden, gate_logit):
    rows, width = returned.shape
    tokens = hidden.shape[0]
    tile = pl.BlockSpec((BLOCK, width), lambda i: (i, 0))
    column = pl.BlockSpec((BLOCK, 1), lambda i: (i, 0))
    return pl.pallas_call(
        out_kernel,
        grid=(tokens // BLOCK,),
        out_shape=jax.ShapeDtypeStruct((tokens, width), BF16),
        in_specs=[pl.BlockSpec((rows, width), lambda i: (0, 0)), column, tile, column],
        out_specs=tile,
        compiler_params=pltpu.CompilerParams(vmem_limit_bytes=40 << 20),
        cost_estimate=pl.CostEstimate(flops=4 << 30, bytes_accessed=10 << 20, transcendentals=0),
    )(returned, scol, hidden, gate_logit.reshape(tokens, 1))


def bwd_kernel(
    ret_ref,
    scol_ref,
    x_ref,
    ct_ref,
    h_ref,
    qkv_ref,
    c_ref,
    stat_ref,
    w_ref,
    gain_ref,
    segr_ref,
    segc_ref,
    gt_ref,
    gw_ref,
    gg_ref,
    dc_scr,
    dhb_scr,
    dqkv_scr,
    act_scr,
    d_scr,
    dk_scr,
    dv_scr,
):
    tokens, width = x_ref.shape
    slots = ret_ref.shape[0]
    blocks = tokens // BLOCK
    pairs = width // 128
    gain_one = gain_ref[0:1, :]
    gain_two = gain_ref[1:2, :]
    gg_ref[...] = jnp.zeros_like(gg_ref)
    member = (iota((16, width), 1) // HEAD_DIM == iota((16, width), 0)).astype(F32)

    for i in range(blocks):
        rows = pl.ds(i * BLOCK, BLOCK)
        pick = (iota((BLOCK, slots), 1).astype(F32) == scol_ref[rows, :]).astype(BF16)
        da = dot(pick, ret_ref[...])
        normed, factor = normalize(h_ref[rows, :])
        gg_ref[1:2, :] += jnp.sum(da * normed, axis=0, keepdims=True)
        dh = ct_ref[rows, :].astype(F32) + norm_back(da * gain_two, normed, factor)
        gt_ref[rows, :] = dh
        dhb = dh.astype(BF16)
        dhb_scr[rows, :] = dhb
        dc = dot_t(dhb, w_ref[:, 3 * width : 4 * width]).astype(BF16)
        dc_scr[rows, :] = dc
        d_scr[:, rows] = lax.dot_general(
            member,
            dc.astype(F32) * c_ref[rows, :].astype(F32),
            (((1,), (1,)), ((), ())),
            precision=lax.Precision.HIGHEST,
            preferred_element_type=F32,
        )

    gw_ref[:, 3 * width : 4 * width] = t_dot(c_ref[...], dhb_scr[...])
    low = iota((BLOCK, 128), 1) < HEAD_DIM
    scale = HEAD_DIM**-0.5

    @pl.loop(0, pairs)
    def _(hp):
        at = pl.multiple_of(hp * 128, 128)
        dk_scr[...] = jnp.zeros_like(dk_scr)
        dv_scr[...] = jnp.zeros_like(dv_scr)
        for qb in range(blocks):
            rows = pl.ds(qb * BLOCK, BLOCK)
            q = qkv_ref[rows, pl.ds(at, 128)] * jnp.asarray(scale, BF16)
            dc = dc_scr[rows, pl.ds(at, 128)]
            q_half = [jnp.where(low, q, 0), jnp.where(low, 0, q)]
            dc_half = [jnp.where(low, dc, 0), jnp.where(low, 0, dc)]
            dq = jnp.zeros((BLOCK, 128), F32)
            for kb in range(max(0, qb - LOOKBACK), qb + 1):
                keys = pl.ds(kb * BLOCK, BLOCK)
                k = qkv_ref[keys, pl.ds(width + at, 128)]
                v = qkv_ref[keys, pl.ds(2 * width + at, 128)]
                ok = segc_ref[keys, :] == segr_ref[0:1, rows]
                if kb == qb:
                    ok = ok & (iota((BLOCK, BLOCK), 0) <= iota((BLOCK, BLOCK), 1))
                ps, dss = [], []
                for half in range(2):
                    s = dot_t(k, q_half[half])
                    p = jnp.where(ok, jnp.exp(s - stat_ref[pl.ds(2 * hp + half, 1), rows]), 0.0)
                    dp = dot_t(v, dc_half[half])
                    dss.append((p * (dp - d_scr[pl.ds(2 * hp + half, 1), rows])).astype(BF16))
                    ps.append(p.astype(BF16))
                dv_scr[keys, :] += dot(jnp.concatenate(ps, 1), jnp.concatenate(dc_half, 0))
                dk_scr[keys, :] += dot(jnp.concatenate(dss, 1), jnp.concatenate(q_half, 0))
                dq += jnp.where(low, t_dot(dss[0], k), t_dot(dss[1], k))
            dqkv_scr[rows, pl.ds(at, 128)] = (dq * scale).astype(BF16)
        dqkv_scr[:, pl.ds(width + at, 128)] = dk_scr[...].astype(BF16)
        dqkv_scr[:, pl.ds(2 * width + at, 128)] = dv_scr[...].astype(BF16)

    @pl.loop(0, blocks)
    def _(i):
        rows = pl.ds(pl.multiple_of(i * BLOCK, BLOCK), BLOCK)
        normed, factor = normalize(x_ref[rows, :].astype(F32))
        act_scr[rows, :] = (normed * gain_one).astype(BF16)
        dn = dot_t(dqkv_scr[rows, :], w_ref[:, : 3 * width])
        gg_ref[0:1, :] += jnp.sum(dn * normed, axis=0, keepdims=True)
        gt_ref[rows, :] += norm_back(dn * gain_one, normed, factor)

    gw_ref[:, : 3 * width] = t_dot(act_scr[...], dqkv_scr[...])


def attend_bwd(returned, scol, tokens_in, cotangent, hidden, qkv, context, stats, w_all, gains, segr, segc):
    tokens, width = tokens_in.shape
    return pl.pallas_call(
        bwd_kernel,
        out_shape=(
            jax.ShapeDtypeStruct((tokens, width), F32),
            jax.ShapeDtypeStruct((width, 4 * width), F32),
            jax.ShapeDtypeStruct((8, width), F32),
        ),
        scratch_shapes=[
            pltpu.VMEM((tokens, width), BF16),
            pltpu.VMEM((tokens, width), BF16),
            pltpu.VMEM((tokens, 3 * width), BF16),
            pltpu.VMEM((tokens, width), BF16),
            pltpu.VMEM((16, tokens), F32),
            pltpu.VMEM((tokens, 128), F32),
            pltpu.VMEM((tokens, 128), F32),
        ],
        compiler_params=pltpu.CompilerParams(vmem_limit_bytes=60 << 20),
        cost_estimate=pl.CostEstimate(flops=80 << 30, bytes_accessed=40 << 20, transcendentals=0),
    )(returned, scol, tokens_in, cotangent, hidden, qkv, context, stats, w_all, gains, segr, segc)


MESH = pl.DeviceIdType.MESH


def place():
    e, n = lax.axis_index("expert"), lax.axis_index("narrow")
    return e // 2, lax.rem(e, 2), n // 2, lax.rem(n, 2)


def device(z, y, x, c):
    return (z * 2 + y, x * 2 + c)


def across(z, k):
    hi, lo = z // 2, lax.rem(z, 2)
    hi = 1 - hi if k & 2 else hi
    lo = 1 - lo if k & 1 else lo
    return hi * 2 + lo


class Links:
    def __init__(self, send, recv):
        self.send, self.recv, self.used = send, recv, 0

    def make(self, src, dst, to):
        i = self.used
        self.used += 1
        return pltpu.make_async_remote_copy(
            src_ref=src, dst_ref=dst, send_sem=self.send.at[i], recv_sem=self.recv.at[i], device_id=to, device_id_type=MESH
        )

    def push(self, src, dst, to):
        copy = self.make(src, dst, to)
        copy.start()
        return copy


class Loads:
    def __init__(self, sems):
        self.sems, self.used = sems, 0

    def start(self, src, dst):
        copy = pltpu.make_async_copy(src, dst, self.sems.at[self.used])
        self.used += 1
        copy.start()
        return copy


def greet(peers):
    barrier = pltpu.get_barrier_semaphore()
    for peer in peers:
        pl.semaphore_signal(barrier, inc=1, device_id=peer, device_id_type=MESH)
    pl.semaphore_wait(barrier, len(peers))


FLIPS = (4, 2, 6, 1, 5, 3, 7)


def peers_of(z, y, x, c):
    return [device(across(z, k >> 1), 1 - y if k & 1 else y, x, c) for k in FLIPS]


def weight(ref, lo, hi):
    return ref[:, :, :, :, lo:hi].reshape(-1, hi - lo)


def head_kernel(
    capacity,
    experts,
    x_hbm,
    ct_hbm,
    win_hbm,
    whid_hbm,
    row_ref,
    wqkv_ref,
    wout_ref,
    gshard_ref,
    qkv_hbm,
    c_hbm,
    h_hbm,
    act_hbm,
    w_hbm,
    dyrow_hbm,
    win4_hbm,
    whid4_hbm,
    stat_ref,
    col_ref,
    gain_ref,
    x_ref,
    ct_ref,
    sh,
    st,
    square,
    wq,
    wg,
    qkv_ref,
    c_ref,
    h_ref,
    a_scr,
    act_ref,
    dy_ref,
    bias_scr,
    send_sems,
    recv_sems,
    load_sems,
):
    z, y, x, c = place()
    me_e = z * 2 + y
    me_n = x * 2 + c
    tokens, width = x_ref.shape
    blocks = tokens // BLOCK
    pairs = width // 128
    half = width // 2
    core, xpeer, ypeer = device(z, y, x, 1 - c), device(z, y, 1 - x, c), device(z, 1 - y, x, c)
    links = Links(send_sems, recv_sems)
    loads = Loads(load_sems)
    loading_ct = loads.start(ct_hbm, ct_ref)
    loading_x = loads.start(x_hbm, x_ref)

    square[...] = jnp.zeros_like(square)
    square[0:2, 0 : gshard_ref.shape[1]] = gshard_ref[...].astype(F32)
    gain_cols = square[...].T
    for side in range(2):
        for j in range(4):
            src, at = (wqkv_ref, j * width) if j < 3 else (wout_ref, 0)
            sh[side, :, j * half : (j + 1) * half] = src[:, at + side * half : at + (side + 1) * half].astype(F32)
        sh[side, :, 4 * half :] = gain_cols[0 : gshard_ref.shape[1], :]
    st[c] = sh[c]

    greet(peers_of(z, y, x, c) + [core, xpeer])
    zero = links.push(sh.at[1 - c], st.at[c], core)

    deep = width // 2
    upper, lower = pl.ds(0, deep), pl.ds(deep, deep)

    def hand(src, dst, rows):
        return links.push(src.at[rows], dst.at[me_n, rows], xpeer)

    def onward(dst, rows):
        part = dst.at[(1 - x) * 2 + c, rows]
        return links.push(part, part, core)

    parts = [(hand(win_hbm, win4_hbm, upper), win4_hbm, upper)]

    def cols(j):
        return pl.ds(pl.multiple_of((2 * j + c) * half, 128), half)

    zero.wait()
    rows48 = jnp.concatenate((st[0], st[1]), axis=0)
    for j in range(4):
        wq[z, y, x, :, cols(j)] = rows48[:, j * half : (j + 1) * half].astype(BF16)
    wg[z, y, x] = rows48[:, 4 * half :].astype(BF16)
    ring_z = []
    for piece in range(2):
        group = []
        for k in (1, 2, 3):
            to = device(across(z, k), y, x, c)
            for j in (2 * piece, 2 * piece + 1):
                part = wq.at[z, y, x, :, cols(j)]
                group.append(links.push(part, part, to))
            if piece == 0:
                group.append(links.push(wg.at[z, y, x], wg.at[z, y, x], to))
        ring_z.append(group)

    wide = max(8, experts)
    hot = (iota((wide, tokens), 0).astype(F32) == row_ref[0:1, :]).astype(F32)
    before = (iota((tokens, tokens), 0) < iota((tokens, tokens), 1)).astype(BF16)
    rank = dot(hot.astype(BF16), before)
    base = (iota((wide, tokens), 0) * capacity).astype(F32)
    srow = jnp.sum(hot * (rank + base), axis=0, keepdims=True)

    listed = row_ref[...].T
    hot_c = (iota((tokens, 128), 1).astype(F32) == listed[:, 0:1]).astype(F32)
    after = (iota((tokens, tokens), 1) < iota((tokens, tokens), 0)).astype(BF16)
    rank_c = dot(after, hot_c.astype(BF16))
    base_c = (iota((tokens, 128), 1) * capacity).astype(F32)
    scol = jnp.sum(hot_c * (rank_c + base_c), axis=1, keepdims=True)
    col_ref[...] = jnp.where(iota(listed.shape, 1) == 0, scol, listed)

    def fill(values, out):
        @pl.loop(0, out.shape[0])
        def _(i):
            ids = (iota((capacity, tokens), 0) + i * capacity).astype(F32)
            out[i] = dot((ids == srow).astype(BF16), values).astype(BF16)

    loading_ct.wait()
    fill((jax.nn.sigmoid(listed[:, 1:2]) * ct_ref[...].astype(F32)).astype(BF16), dy_ref)

    ring_2 = []
    for piece in range(2):
        for copy in ring_z[piece]:
            copy.wait()
        ca, cb = cols(2 * piece), cols(2 * piece + 1)
        group = [
            links.push(wq.at[:, y, x, :, ca], wq.at[:, y, x, :, ca], ypeer),
            links.push(wq.at[:, y, x, :, cb], wq.at[:, y, x, :, cb], xpeer),
        ]
        if piece == 0:
            group.append(links.push(wg.at[:, y, x], wg.at[:, y, x], ypeer))
        ring_2.append(group)
    dy_copies = []
    for k in FLIPS:
        zz, yy = across(z, k >> 1), (1 - y if k & 1 else y)
        dy_copies.append(links.push(dy_ref.at[zz * 2 + yy], dyrow_hbm.at[me_e], device(zz, yy, x, c)))
    own_dy = loads.start(dy_ref.at[me_e], dyrow_hbm.at[me_e])
    ring_3 = []
    for piece in range(2):
        for copy in ring_2[piece]:
            copy.wait()
        ca, cb = cols(2 * piece), cols(2 * piece + 1)
        group = [
            links.push(wq.at[:, :, x, :, ca], wq.at[:, :, x, :, ca], xpeer),
            links.push(wq.at[:, y, :, :, cb], wq.at[:, y, :, :, cb], ypeer),
        ]
        if piece == 0:
            group.append(links.push(wg.at[:, :, x], wg.at[:, :, x], xpeer))
        ring_3.append(group)
    for src, dst, rows in ((win_hbm, win4_hbm, lower), (whid_hbm, whid4_hbm, upper), (whid_hbm, whid4_hbm, lower)):
        parts.append((hand(src, dst, rows), dst, rows))
    ring_4 = []
    for piece in range(2):
        for copy in ring_3[piece]:
            copy.wait()
        ring_4.append([links.push(wq.at[:, :, :, :, cols(j)], wq.at[:, :, :, :, cols(j)], core) for j in (2 * piece, 2 * piece + 1)])

    gains = jnp.transpose(wg[...].reshape(width, 128).astype(F32))[0:8, :]
    gain_ref[...] = gains
    gain_one = gains[0:1, :]
    gain_two = gains[1:2, :]
    loading_x.wait()
    for piece in range(2):
        for copy in ring_4[piece]:
            copy.wait()
    storing = [loads.start(wq, w_hbm)]
    core_slices = [links.push(src, dst.at[me_n], core) for src, dst in ((win_hbm, win4_hbm), (whid_hbm, whid4_hbm))]

    def pass_on(i):
        copy, dst, rows = parts[i]
        copy.wait()
        core_slices.append(onward(dst, rows))

    pass_on(0)

    @pl.loop(0, blocks)
    def _(i):
        rows = pl.ds(pl.multiple_of(i * BLOCK, BLOCK), BLOCK)
        normed, _f = normalize(x_ref[rows, :].astype(F32))
        act = (normed * gain_one).astype(BF16)
        qkv_ref[rows, :] = dot(act, weight(wq, 0, 3 * width)).astype(BF16)

    storing.append(loads.start(qkv_ref, qkv_hbm))
    low = iota((BLOCK, 128), 1) < HEAD_DIM
    tiles = [(qb, kb) for qb in range(blocks) for kb in range(max(0, qb - LOOKBACK), qb + 1)]
    for n, (qb, kb) in enumerate(tiles):
        ok = col_ref[pl.ds(kb * BLOCK, BLOCK), 2:3] == row_ref[2:3, pl.ds(qb * BLOCK, BLOCK)]
        if kb == qb:
            ok = ok & (iota((BLOCK, BLOCK), 0) <= iota((BLOCK, BLOCK), 1))
        bias_scr[n] = jnp.where(ok, 0.0, BIG_NEGATIVE)

    @pl.loop(0, pairs)
    def _(hp):
        at = pl.multiple_of(hp * 128, 128)
        for qb in range(blocks):
            mine = [(n, kb) for n, (qq, kb) in enumerate(tiles) if qq == qb]
            rows = pl.ds(qb * BLOCK, BLOCK)
            q = qkv_ref[rows, pl.ds(at, 128)] * jnp.asarray(HEAD_DIM**-0.5, BF16)
            v = qkv_ref[pl.ds(mine[0][1] * BLOCK, len(mine) * BLOCK), pl.ds(2 * width + at, 128)]
            outs = []
            for side in range(2):
                q_half = jnp.where(low, q, 0) if side == 0 else jnp.where(low, 0, q)
                scores = [
                    dot_t(qkv_ref[pl.ds(kb * BLOCK, BLOCK), pl.ds(width + at, 128)], q_half) + bias_scr[n] for n, kb in mine
                ]
                top = functools.reduce(jnp.maximum, [jnp.max(s, axis=0, keepdims=True) for s in scores])
                raised = [jnp.exp(s - top) for s in scores]
                total = functools.reduce(jnp.add, [jnp.sum(r, axis=0, keepdims=True) for r in raised])
                share = 1.0 / total
                weights = jnp.concatenate([(r * share).astype(BF16) for r in raised], axis=0)
                outs.append(t_dot(weights, v))
                stat_ref[pl.ds(2 * hp + side, 1), rows] = top + jnp.log(total)
            c_ref[rows, pl.ds(at, 128)] = jnp.where(low, outs[0], outs[1]).astype(BF16)

    storing.append(loads.start(c_ref, c_hbm))

    @pl.loop(0, blocks)
    def _(i):
        rows = pl.ds(pl.multiple_of(i * BLOCK, BLOCK), BLOCK)
        hidden = x_ref[rows, :].astype(F32) + dot(c_ref[rows, :], weight(wq, 3 * width, 4 * width))
        h_ref[rows, :] = hidden
        normed, _f = normalize(hidden)
        a_scr[rows, :] = (normed * gain_two).astype(BF16)

    storing.append(loads.start(h_ref, h_hbm))
    fill(a_scr[...], act_ref)
    storing.append(loads.start(act_ref, act_hbm))
    for i in range(1, 4):
        pass_on(i)
    for copy in storing + [own_dy] + core_slices + dy_copies:
        copy.wait()


def head(tokens_in, cotangent, w_in, w_hid, listed, w_qkv, w_out, gain_shard, experts, capacity):
    tokens, width = tokens_in.shape
    any_spec = pl.BlockSpec(memory_space=pl.ANY)
    vmem = pl.BlockSpec(memory_space=pltpu.VMEM)
    slots = (experts, capacity, width)
    blocks = (4, 2, 2, 48, 4 * width)
    shard = (2, w_qkv.shape[0], 2 * width + 128)
    return pl.pallas_call(
        functools.partial(head_kernel, capacity, experts),
        out_shape=(
            jax.ShapeDtypeStruct((tokens, 3 * width), BF16),
            jax.ShapeDtypeStruct((tokens, width), BF16),
            jax.ShapeDtypeStruct((tokens, width), F32),
            jax.ShapeDtypeStruct(slots, BF16),
            jax.ShapeDtypeStruct(blocks, BF16),
            jax.ShapeDtypeStruct(slots, BF16),
            jax.ShapeDtypeStruct((4,) + w_in.shape, BF16),
            jax.ShapeDtypeStruct((4,) + w_hid.shape, BF16),
            jax.ShapeDtypeStruct((16, tokens), F32),
            jax.ShapeDtypeStruct((tokens, 8), F32),
            jax.ShapeDtypeStruct((8, width), F32),
        ),
        in_specs=[any_spec] * 4 + [vmem] * 4,
        out_specs=(any_spec,) * 8 + (vmem,) * 3,
        scratch_shapes=[
            pltpu.VMEM((tokens, width), BF16),
            pltpu.VMEM((tokens, width), BF16),
            pltpu.VMEM(shard, F32),
            pltpu.VMEM(shard, F32),
            pltpu.VMEM((128, 128), F32),
            pltpu.VMEM(blocks, BF16),
            pltpu.VMEM((4, 2, 2, 48, 128), BF16),
            pltpu.VMEM((tokens, 3 * width), BF16),
            pltpu.VMEM((tokens, width), BF16),
            pltpu.VMEM((tokens, width), F32),
            pltpu.VMEM((tokens, width), BF16),
            pltpu.VMEM(slots, BF16),
            pltpu.VMEM(slots, BF16),
            pltpu.VMEM((tokens // BLOCK * (LOOKBACK + 1), BLOCK, BLOCK), F32),
            pltpu.SemaphoreType.DMA((48,)),
            pltpu.SemaphoreType.DMA((48,)),
            pltpu.SemaphoreType.DMA((16,)),
        ],
        compiler_params=pltpu.CompilerParams(vmem_limit_bytes=62 << 20, collective_id=0, has_side_effects=True),
        cost_estimate=pl.CostEstimate(flops=60 << 30, bytes_accessed=40 << 20, transcendentals=0),
    )(tokens_in, cotangent, w_in, w_hid, listed, w_qkv, w_out, gain_shard)


class Reduce:
    def __init__(self, spot, ph, gq, rc, r1, r2, r3, fin, r4, send_sems, recv_sems):
        self.z, self.y, self.x, self.c = spot
        self.gq, self.rc, self.r1, self.r2, self.r3, self.fin, self.r4 = (
            gq.at[ph],
            rc.at[ph],
            r1.at[ph],
            r2.at[ph],
            r3.at[ph],
            fin.at[ph],
            r4.at[ph],
        )
        self.base = ph * 7
        self.send, self.recv = send_sems, recv_sems

    def copy(self, i, src, dst, to):
        return pltpu.make_async_remote_copy(
            src_ref=src,
            dst_ref=dst,
            send_sem=self.send.at[self.base + i],
            recv_sem=self.recv.at[self.base + i],
            device_id=to,
            device_id_type=MESH,
        )

    def turn(self, i):
        return i * (1 - self.c) + self.y * self.c, self.x * (1 - self.c) + i * self.c

    def add(self, where, term):
        self.gq[where] = (self.gq[where].astype(F32) + term.astype(F32)).astype(BF16)

    def cores(self):
        z, y, x, c = self.z, self.y, self.x, self.c
        return self.copy(0, self.gq.at[1 - c], self.rc, device(z, y, x, 1 - c))

    def by_core(self, go, first, second):
        @pl.when(self.c == 0)
        def _():
            go(first)

        @pl.when(self.c == 1)
        def _():
            go(second)

    def one(self, go):
        z, y, x, c = self.z, self.y, self.x, self.c
        self.by_core(
            go,
            self.copy(1, self.gq.at[0, :, :, 1 - x], self.r1, device(z, y, 1 - x, c)),
            self.copy(1, self.gq.at[1, :, 1 - y], self.r1, device(z, 1 - y, x, c)),
        )

    def two(self, go):
        z, y, x, c = self.z, self.y, self.x, self.c
        self.by_core(
            go,
            self.copy(2, self.gq.at[0, :, 1 - y, x], self.r2, device(z, 1 - y, x, c)),
            self.copy(2, self.gq.at[1, :, y, 1 - x], self.r2, device(z, y, 1 - x, c)),
        )

    def three(self):
        z, y, x, c = self.z, self.y, self.x, self.c
        return [
            self.copy(2 + k, self.gq.at[c, across(z, k), y, x], self.r3.at[k - 1], device(across(z, k), y, x, c))
            for k in (1, 2, 3)
        ]

    def four(self):
        z, y, x, c = self.z, self.y, self.x, self.c
        rows = pl.ds(pl.multiple_of((1 - c) * 24, 8), 24)
        return self.copy(6, self.fin.at[rows], self.r4, device(z, y, x, 1 - c))

    def step(self, stage):
        z, y, x, c = self.z, self.y, self.x, self.c
        if stage == 0:
            self.cores().start()
        if stage == 1:
            self.cores().wait()

            @pl.loop(0, 4)
            def _(k):
                self.add((c, k), self.rc[k])

            self.one(lambda copy: copy.start())
        if stage == 2:
            self.one(lambda copy: copy.wait())

            @pl.loop(0, 4)
            def _(k):
                for i in range(2):
                    yy, xx = self.turn(i)
                    self.add((c, k, yy, xx), self.r1[k, i])

            self.two(lambda copy: copy.start())
        if stage == 3:
            self.two(lambda copy: copy.wait())

            @pl.loop(0, 4)
            def _(k):
                self.add((c, k, y, x), self.r2[k])

            for copy in self.three():
                copy.start()
        if stage == 4:
            for copy in self.three():
                copy.wait()
            total = self.gq[c, z, y, x].astype(F32)
            for k in range(3):
                total = total + self.r3[k].astype(F32)
            self.fin[...] = total
            self.four().start()


def tail_kernel(
    ret_hbm,
    x_hbm,
    ct_hbm,
    h_hbm,
    qkv_hbm,
    c_hbm,
    w_hbm,
    yrow_hbm,
    gw_hbm,
    col_ref,
    row_ref,
    stat_ref,
    gain_ref,
    gt_hbm,
    gw_out,
    out_hbm,
    ownq_ref,
    owno_ref,
    gg_ref,
    ret_ref,
    x_ref,
    ct_ref,
    h_ref,
    qkv_ref,
    c_ref,
    w_ref,
    gt_ref,
    dc_scr,
    dhb_scr,
    dqkv_scr,
    actt_scr,
    d_scr,
    dk_scr,
    dv_scr,
    gq,
    rc,
    q1,
    q2,
    q3,
    fin,
    q4,
    ggs,
    rg,
    near,
    next_x,
    nsum,
    yback,
    send_sems,
    recv_sems,
    red_send,
    red_recv,
    load_sems,
):
    spot = place()
    z, y, x, c = spot
    me_e = z * 2 + y
    tokens, width = x_ref.shape
    slots, _w = ret_ref.shape
    blocks = tokens // BLOCK
    half = width // 2
    core, xpeer, ypeer = device(z, y, x, 1 - c), device(z, y, 1 - x, c), device(z, 1 - y, x, c)
    far = peers_of(z, y, x, c)
    links = Links(send_sems, recv_sems)
    loads = Loads(load_sems)

    def reduce(ph):
        return Reduce(spot, ph, gq, rc, q1, q2, q3, fin, q4, red_send, red_recv)

    first = [
        loads.start(a, b)
        for a, b in (
            (ret_hbm, ret_ref),
            (h_hbm, h_ref),
            (w_hbm.at[:, :, :, :, pl.ds(3 * width, width)], w_ref.at[:, :, :, :, pl.ds(3 * width, width)]),
            (ct_hbm, ct_ref),
            (c_hbm, c_ref),
        )
    ]
    second = [
        loads.start(a, b)
        for a, b in (
            (gw_hbm.at[(1 - x) * 2 + c], nsum.at[0]),
            (gw_hbm.at[x * 2 + c], nsum.at[1]),
            (x_hbm, x_ref),
            (qkv_hbm, qkv_ref),
            (w_hbm.at[:, :, :, :, pl.ds(0, 3 * width)], w_ref.at[:, :, :, :, pl.ds(0, 3 * width)]),
            (yrow_hbm.at[me_e], yback.at[me_e]),
        )
    ]
    greet(far + [core, xpeer])

    w_copies = [links.push(gw_hbm.at[xx * 2 + 1 - c], near.at[xx], core) for xx in range(2)]
    y_near, y_far = [], []
    for k, to in zip(FLIPS, far):
        (y_far if k >= 4 else y_near).append(links.push(yrow_hbm.at[to[0]], yback.at[me_e], to))

    gain_one = gain_ref[0:1, :]
    gain_two = gain_ref[1:2, :]
    member = (iota((16, 2 * width), 1) % width // HEAD_DIM == iota((16, 2 * width), 0)).astype(BF16)
    for copy in first:
        copy.wait()
    ggs[...] = jnp.zeros_like(ggs)

    def picks(rows):
        return (iota((BLOCK, slots), 1).astype(F32) == col_ref[rows, 0:1]).astype(BF16)

    @pl.loop(0, blocks)
    def _(i):
        rows = pl.ds(pl.multiple_of(i * BLOCK, BLOCK), BLOCK)
        da = dot(picks(rows), ret_ref[...])
        normed, factor = normalize(h_ref[rows, :])
        ggs[0, 1:2, :] += jnp.sum(da * normed, axis=0, keepdims=True)
        dh = ct_ref[rows, :].astype(F32) + norm_back(da * gain_two, normed, factor)
        gt_ref[rows, :] = dh
        dhb = dh.astype(BF16)
        dhb_scr[rows, :] = dhb
        dc = dot_t(dhb, weight(w_ref, 3 * width, 4 * width)).astype(BF16)
        dc_scr[rows, :] = dc
        product = dc.astype(F32) * c_ref[rows, :].astype(F32)
        high = product.astype(BF16)
        rest = (product - high.astype(F32)).astype(BF16)
        d_scr[:, rows] = dot_t(member, jnp.concatenate((high, rest), axis=1))

    def put(ph, value):
        for owner in range(2):
            for chip in range(16):
                gq[ph, owner, chip // 4, chip // 2 % 2, chip % 2] = value[
                    chip * 48 : chip * 48 + 48, owner * half : (owner + 1) * half
                ].astype(BF16)

    put(0, t_dot(c_ref[...], dhb_scr[...]))
    reduce(0).step(0)

    for copy in w_copies:
        copy.wait()

    def to_x(i):
        rows = pl.ds(pl.multiple_of(i * (width // 4), width // 4), width // 4)
        return pltpu.make_async_remote_copy(
            src_ref=nsum.at[0, rows],
            dst_ref=next_x.at[rows],
            send_sem=send_sems.at[16 + i],
            recv_sem=recv_sems.at[16 + i],
            device_id=xpeer,
            device_id_type=MESH,
        )

    for copy in second:
        copy.wait()
    nsum[0] = (nsum[0].astype(F32) + near[1 - x].astype(F32)).astype(BF16)
    to_x(0).start()

    @pl.loop(0, blocks)
    def _(i):
        rows = pl.ds(pl.multiple_of(i * BLOCK, BLOCK), BLOCK)
        normed, _f = normalize(x_ref[rows, :].astype(F32))
        dhb_scr[rows, :] = (normed * gain_one).astype(BF16)

    actt_scr[...] = dhb_scr[...].T
    low = iota((BLOCK, 128), 1) < HEAD_DIM
    scale = HEAD_DIM**-0.5

    @pl.loop(0, 3)
    def _(t):
        @pl.loop(0, 2)
        def _(inner):
            hp = 2 * t + inner
            at = pl.multiple_of(hp * 128, 128)
            dk_scr[...] = jnp.zeros_like(dk_scr)
            dv_scr[...] = jnp.zeros_like(dv_scr)
            for qb in range(blocks):
                rows = pl.ds(qb * BLOCK, BLOCK)
                q = qkv_ref[rows, pl.ds(at, 128)] * jnp.asarray(scale, BF16)
                dc = dc_scr[rows, pl.ds(at, 128)]
                q_half = [jnp.where(low, q, 0), jnp.where(low, 0, q)]
                dc_half = [jnp.where(low, dc, 0), jnp.where(low, 0, dc)]
                dq = jnp.zeros((BLOCK, 128), F32)
                for kb in range(max(0, qb - LOOKBACK), qb + 1):
                    keys = pl.ds(kb * BLOCK, BLOCK)
                    k = qkv_ref[keys, pl.ds(width + at, 128)]
                    v = qkv_ref[keys, pl.ds(2 * width + at, 128)]
                    ok = col_ref[keys, 2:3] == row_ref[2:3, rows]
                    if kb == qb:
                        ok = ok & (iota((BLOCK, BLOCK), 0) <= iota((BLOCK, BLOCK), 1))
                    ps, dss = [], []
                    for side in range(2):
                        s = dot_t(k, q_half[side])
                        p = jnp.where(ok, jnp.exp(s - stat_ref[pl.ds(2 * hp + side, 1), rows]), 0.0)
                        dp = dot_t(v, dc_half[side])
                        dss.append((p * (dp - d_scr[pl.ds(2 * hp + side, 1), rows])).astype(BF16))
                        ps.append(p.astype(BF16))
                    dv_scr[keys, :] += dot(jnp.concatenate(ps, 1), jnp.concatenate(dc_half, 0))
                    dk_scr[keys, :] += dot(jnp.concatenate(dss, 1), jnp.concatenate(q_half, 0))
                    dq += jnp.where(low, t_dot(dss[0], k), t_dot(dss[1], k))
                dqkv_scr[rows, pl.ds(at, 128)] = (dq * scale).astype(BF16)
            dqkv_scr[:, pl.ds(width + at, 128)] = dk_scr[...].astype(BF16)
            dqkv_scr[:, pl.ds(2 * width + at, 128)] = dv_scr[...].astype(BF16)

        columns = []
        for inner in range(2):
            at = pl.multiple_of((2 * t + inner) * 128, 128)
            columns += [dqkv_scr[:, pl.ds(j * width + at, 128)] for j in range(3)]
        put(t + 1, dot(actt_scr[...], jnp.concatenate(columns, axis=1)))
        reduce(t + 1).step(0)
        reduce(t).step(1)

        @pl.when(t >= 1)
        def _():
            reduce(t - 1).step(2)

        @pl.when(t >= 2)
        def _():
            reduce(t - 2).step(3)

        to_x(t + 1).start()

    @pl.loop(0, blocks)
    def _(i):
        rows = pl.ds(pl.multiple_of(i * BLOCK, BLOCK), BLOCK)
        normed, factor = normalize(x_ref[rows, :].astype(F32))
        dn = dot_t(dqkv_scr[rows, :], weight(w_ref, 0, 3 * width))
        ggs[0, 0:1, :] += jnp.sum(dn * normed, axis=0, keepdims=True)
        gt_ref[rows, :] += norm_back(dn * gain_one, normed, factor)

    stores = [loads.start(gt_ref, gt_hbm)]
    gains_copy = links.push(ggs.at[0], rg.at[0], core)
    reduce(3).step(1)
    reduce(2).step(2)
    reduce(1).step(3)
    reduce(0).step(4)
    gains_copy.wait()
    ggs[1] = ggs[0] + rg[0]
    gains_copy = links.push(ggs.at[1], rg.at[1], xpeer)

    def finish(side, last):
        group = slots // 2
        places = yback.shape[0] // 2

        @pl.loop(0, blocks)
        def _(i):
            rows = pl.ds(pl.multiple_of(i * BLOCK, BLOCK), BLOCK)
            pick = ((iota((BLOCK, group), 1) + side * group).astype(F32) == col_ref[rows, 0:1]).astype(BF16)
            got = dot(pick, yback[pl.ds(side * places, places)].reshape(group, width))
            value = h_ref[rows, :] + jax.nn.sigmoid(col_ref[rows, 1:2]) * got
            if last:
                ct_ref[rows, :] = value.astype(BF16)
            else:
                h_ref[rows, :] = value

    reduce(3).step(2)
    reduce(2).step(3)
    reduce(1).step(4)
    gains_copy.wait()
    ggs[2] = ggs[1] + rg[1]
    gains_copy = links.push(ggs.at[2], rg.at[2], ypeer)
    reduce(3).step(3)
    reduce(2).step(4)
    gains_copy.wait()
    ggs[3] = ggs[2] + rg[2]
    gain_copies = [links.push(ggs.at[3], rg.at[2 + k], device(across(z, k), y, x, c)) for k in (1, 2, 3)]
    for copy in y_near:
        copy.wait()
    finish(z // 2, False)
    for i in range(4):
        to_x(i).wait()
    gw_out[...] = nsum[1].astype(F32) + near[x].astype(F32) + next_x[...].astype(F32)
    reduce(3).step(4)
    for copy in gain_copies:
        copy.wait()
    share = width // 32
    mine = ((z * 2 + y) * 2 + x) * 2 + c
    take = (iota((width, 128), 0) == mine * share + iota((width, 128), 1)).astype(F32)
    gg_ref[...] = lax.dot_general(
        ggs[3] + rg[3] + rg[4] + rg[5],
        take,
        (((1,), (0,)), ((), ())),
        precision=lax.Precision.HIGHEST,
        preferred_element_type=F32,
    )[0:2, 0:share]
    for ph in range(4):
        kept = fin[ph, pl.ds(pl.multiple_of(c * 24, 8), 24), :]
        reduce(ph).four().wait()
        for owner, part in ((c, kept), (1 - c, q4[ph])):
            if ph == 0:
                owno_ref[:, pl.ds(pl.multiple_of(owner * half, 128), half)] = part
            else:
                for j in range(3):
                    at = pl.multiple_of(j * width + (2 * (ph - 1) + owner) * 128, 128)
                    ownq_ref[:, pl.ds(at, 128)] = part[:, j * 128 : (j + 1) * 128]
    for copy in y_far:
        copy.wait()
    finish(1 - z // 2, True)
    stores.append(loads.start(ct_ref, out_hbm))
    for copy in stores:
        copy.wait()


def tail(returned, cols, rows, tokens_in, cotangent, hidden, qkv, context, stats, w_blocks, gains, y_rows, gw):
    tokens, width = tokens_in.shape
    slots = returned.shape[0]
    half = width // 2
    any_spec = pl.BlockSpec(memory_space=pl.ANY)
    vmem = pl.BlockSpec(memory_space=pltpu.VMEM)
    return pl.pallas_call(
        tail_kernel,
        out_shape=(
            jax.ShapeDtypeStruct((tokens, width), F32),
            jax.ShapeDtypeStruct(gw.shape[1:], F32),
            jax.ShapeDtypeStruct((tokens, width), BF16),
            jax.ShapeDtypeStruct((24, 3 * width), F32),
            jax.ShapeDtypeStruct((24, width), F32),
            jax.ShapeDtypeStruct((2, 24), F32),
        ),
        in_specs=[any_spec] * 9 + [vmem] * 4,
        out_specs=(any_spec, vmem, any_spec, vmem, vmem, vmem),
        scratch_shapes=[
            pltpu.VMEM((slots, width), BF16),
            pltpu.VMEM((tokens, width), BF16),
            pltpu.VMEM((tokens, width), BF16),
            pltpu.VMEM((tokens, width), F32),
            pltpu.VMEM((tokens, 3 * width), BF16),
            pltpu.VMEM((tokens, width), BF16),
            pltpu.VMEM(w_blocks.shape, BF16),
            pltpu.VMEM((tokens, width), F32),
            pltpu.VMEM((tokens, width), BF16),
            pltpu.VMEM((tokens, width), BF16),
            pltpu.VMEM((tokens, 3 * width), BF16),
            pltpu.VMEM((width, tokens), BF16),
            pltpu.VMEM((16, tokens), F32),
            pltpu.VMEM((tokens, 128), F32),
            pltpu.VMEM((tokens, 128), F32),
            pltpu.VMEM((4, 2, 4, 2, 2, 48, half), BF16),
            pltpu.VMEM((4, 4, 2, 2, 48, half), BF16),
            pltpu.VMEM((4, 4, 2, 48, half), BF16),
            pltpu.VMEM((4, 4, 48, half), BF16),
            pltpu.VMEM((4, 3, 48, half), BF16),
            pltpu.VMEM((4, 48, half), F32),
            pltpu.VMEM((4, 24, half), F32),
            pltpu.VMEM((4, 8, width), F32),
            pltpu.VMEM((6, 8, width), F32),
            pltpu.VMEM((2,) + gw.shape[1:], BF16),
            pltpu.VMEM(gw.shape[1:], BF16),
            pltpu.VMEM((2,) + gw.shape[1:], BF16),
            pltpu.VMEM(y_rows.shape, BF16),
            pltpu.SemaphoreType.DMA((20,)),
            pltpu.SemaphoreType.DMA((20,)),
            pltpu.SemaphoreType.DMA((28,)),
            pltpu.SemaphoreType.DMA((28,)),
            pltpu.SemaphoreType.DMA((16,)),
        ],
        compiler_params=pltpu.CompilerParams(vmem_limit_bytes=62 << 20, collective_id=2, has_side_effects=True),
        cost_estimate=pl.CostEstimate(flops=80 << 30, bytes_accessed=40 << 20, transcendentals=0),
    )(returned, tokens_in, cotangent, hidden, qkv, context, w_blocks, y_rows, gw, cols, rows, stats, gains)


def flipped(z, y, k):
    hi, lo = z // 2, lax.rem(z, 2)
    zz = lax.rem(hi + k // 4, 2) * 2 + lax.rem(lo + lax.rem(k // 2, 2), 2)
    return zz, lax.rem(y + lax.rem(k, 2), 2)


def swap_kernel(
    act_hbm,
    dy_hbm,
    win_hbm,
    whid_hbm,
    own_in_hbm,
    own_hid_hbm,
    ret_hbm,
    y_hbm,
    gin_hbm,
    ghid_hbm,
    a_ref,
    dy_ref,
    win_ref,
    whid_ref,
    g_ref,
    du_ref,
    da_ref,
    us,
    gs,
    stage,
    near,
    next_x,
    send_sems,
    recv_sems,
    load_sems,
):
    z, y, x, c = place()
    me = z * 2 + y
    me_n = x * 2 + c
    count, cap, width = a_ref.shape
    parts = win_ref.shape[0]
    wide = win_ref.shape[2]
    loads = Loads(load_sems)
    first = [
        loads.start(a, b)
        for a, b in (
            (act_hbm.at[me], a_ref.at[me]),
            (own_in_hbm, win_ref.at[me_n]),
            (own_hid_hbm, whid_ref.at[me_n]),
            (dy_hbm, dy_ref),
        )
    ]
    for i in range(1, parts):
        n = lax.rem(me_n + i, parts)
        first += [loads.start(win_hbm.at[n], win_ref.at[n]), loads.start(whid_hbm.at[n], whid_ref.at[n])]

    def partner(k):
        zz, yy = flipped(z, y, k)
        return zz * 2 + yy, device(zz, yy, x, c)

    def outward(k):
        e, to = partner(k)
        return pltpu.make_async_remote_copy(
            src_ref=act_hbm.at[e],
            dst_ref=a_ref.at[me],
            send_sem=send_sems.at[k],
            recv_sem=recv_sems.at[k],
            device_id=to,
            device_id_type=MESH,
        )

    def homeward(k):
        e, to = partner(k)
        return pltpu.make_async_remote_copy(
            src_ref=da_ref.at[e],
            dst_ref=ret_hbm.at[me],
            send_sem=send_sems.at[8 + k],
            recv_sem=recv_sems.at[8 + k],
            device_id=to,
            device_id_type=MESH,
        )

    core, xpeer = device(z, y, x, 1 - c), device(z, y, 1 - x, c)
    greet([partner(k)[1] for k in range(1, 8)] + [core, xpeer])
    for k in FLIPS:
        outward(k).start()
    for copy in first:
        copy.wait()

    @pl.loop(0, count)
    def _(k):
        @pl.when(k > 0)
        def _():
            outward(k).wait_recv()

        e, _to = partner(k)
        a = a_ref[e]
        dy = dy_ref[e]
        rows = pl.ds(pl.multiple_of(e * cap, cap), cap)

        def enter(j):
            us[j % 2] = dot(a, win_ref[j])
            gs[j % 2] = dot_t(dy, whid_ref[j])

        def bend(j):
            g, slope = gelu_pair(us[j % 2])
            g_ref[rows, j * wide : (j + 1) * wide] = g.astype(BF16)
            du_ref[rows, j * wide : (j + 1) * wide] = (gs[j % 2] * slope).astype(BF16)

        def leave(j):
            return dot_t(du_ref[rows, j * wide : (j + 1) * wide], win_ref[j])

        enter(0)
        total = None
        for j in range(parts):
            if j + 1 < parts:
                enter(j + 1)
            bend(j)
            if j > 0:
                term = leave(j - 1)
                total = term if total is None else total + term
        da_ref[e] = (total + leave(parts - 1)).astype(BF16)

        @pl.when(k > 0)
        def _():
            homeward(k).start()

    own = loads.start(da_ref.at[me], ret_hbm.at[me])

    def put(i, out):
        return pltpu.make_async_copy(stage.at[i], out, load_sems.at[16 + i])

    def third(i, src, dst, to):
        return pltpu.make_async_remote_copy(
            src_ref=src,
            dst_ref=dst,
            send_sem=send_sems.at[16 + i],
            recv_sem=recv_sems.at[16 + i],
            device_id=to,
            device_id_type=MESH,
        )

    acts = a_ref[...].reshape(count * cap, width)

    @pl.loop(0, parts)
    def _(j):
        cols = pl.ds(pl.multiple_of(j * wide, wide), wide)
        win_ref[j] = t_dot(acts, du_ref[:, cols]).astype(BF16)

    to_core = [third(xx, win_ref.at[xx * 2 + 1 - c], near.at[xx], core) for xx in range(2)]
    for copy in to_core:
        copy.start()

    @pl.loop(0, parts // 2)
    def _(jj):
        for i in range(2):
            j = 2 * jj + i
            cols = pl.ds(pl.multiple_of(j * wide, wide), wide)

            @pl.when(jj >= 1)
            def _():
                put(i, ghid_hbm.at[j - 2]).wait()

            stage[i] = t_dot(g_ref[:, cols], dy_ref[...].reshape(count * cap, width)).astype(BF16)
            put(i, ghid_hbm.at[j]).start()

    for copy in to_core:
        copy.wait()
    other = (1 - x) * 2 + c
    win_ref[other] = (win_ref[other].astype(F32) + near[1 - x].astype(F32)).astype(BF16)
    to_x = third(2, win_ref.at[other], next_x, xpeer)
    to_x.start()

    @pl.loop(0, count)
    def _(i):
        rows = pl.ds(pl.multiple_of(i * cap, cap), cap)
        a_ref[i] = dot(g_ref[rows, :], whid_ref[...].reshape(parts * wide, width)).astype(BF16)

    out = loads.start(a_ref, y_hbm)
    for i in range(2):
        put(i, ghid_hbm.at[parts - 2 + i]).wait()
    to_x.wait()
    tiles = []
    for i, tile in enumerate((us.at[0], us.at[1], gs.at[0])):
        rows = pl.ds(i * cap, cap)
        tile[...] = win_ref[me_n, rows].astype(F32) + near[x, rows].astype(F32) + next_x[rows].astype(F32)
        tiles.append(loads.start(tile, gin_hbm.at[rows]))
    for k in range(1, 8):
        outward(k).wait_send()
        homeward(k).wait()
    for copy in tiles + [own, out]:
        copy.wait()


def swap(act_slots, dy_rows, w_in, w_hid, own_in, own_hid):
    count, cap, width = act_slots.shape
    parts, _, wide = w_in.shape
    hidden = parts * wide
    any_spec = pl.BlockSpec(memory_space=pl.ANY)
    return pl.pallas_call(
        swap_kernel,
        out_shape=(
            jax.ShapeDtypeStruct((count, cap, width), BF16),
            jax.ShapeDtypeStruct((count, cap, width), BF16),
            jax.ShapeDtypeStruct((width, wide), F32),
            jax.ShapeDtypeStruct((parts, wide, width), BF16),
        ),
        in_specs=[any_spec] * 6,
        out_specs=(any_spec,) * 4,
        scratch_shapes=[
            pltpu.VMEM((count, cap, width), BF16),
            pltpu.VMEM((count, cap, width), BF16),
            pltpu.VMEM(w_in.shape, BF16),
            pltpu.VMEM(w_hid.shape, BF16),
            pltpu.VMEM((count * cap, hidden), BF16),
            pltpu.VMEM((count * cap, hidden), BF16),
            pltpu.VMEM((count, cap, width), BF16),
            pltpu.VMEM((2, cap, wide), F32),
            pltpu.VMEM((2, cap, wide), F32),
            pltpu.VMEM((2, width, wide), BF16),
            pltpu.VMEM((2, width, wide), BF16),
            pltpu.VMEM((width, wide), BF16),
            pltpu.SemaphoreType.DMA((20,)),
            pltpu.SemaphoreType.DMA((20,)),
            pltpu.SemaphoreType.DMA((18,)),
        ],
        compiler_params=pltpu.CompilerParams(vmem_limit_bytes=62 << 20, collective_id=1, has_side_effects=True),
        cost_estimate=pl.CostEstimate(flops=100 << 30, bytes_accessed=60 << 20, transcendentals=0),
    )(act_slots, dy_rows, w_in, w_hid, own_in, own_hid)


def local(tokens, segments, routes, gate_logit, w_qkv, w_out, norm_gains, w_in, w_hid, cotangent):
    tok_count, width = tokens.shape
    n_expert = lax.axis_size("expert")
    n_narrow = lax.axis_size("narrow")
    capacity = 2 * tok_count // n_expert
    slot_rows = n_expert * capacity
    everyone = ("expert", "narrow")

    if n_expert == 8 and n_narrow == 4:
        listed = jnp.concatenate(
            (
                routes.reshape(1, tok_count).astype(F32),
                gate_logit.reshape(1, tok_count),
                segments.reshape(1, tok_count).astype(F32),
                jnp.zeros((5, tok_count), F32),
            )
        )
        qkv, context, hidden, act_slots, w_blocks, dy_rows, w_in_all, w_hid_all, stats, cols, gains = head(
            tokens, cotangent, w_in[0], w_hid[0], listed, w_qkv, w_out, norm_gains, n_expert, capacity
        )
        da_back, y_rows, gin_own, ghid = swap(act_slots, dy_rows, w_in_all, w_hid_all, w_in[0], w_hid[0])
        grad_tokens, ghid_own, block_out, own_qkv, own_out, own_gains = tail(
            da_back.reshape(slot_rows, width),
            cols,
            listed,
            tokens,
            cotangent,
            hidden,
            qkv,
            context,
            stats,
            w_blocks,
            gains,
            y_rows,
            ghid,
        )
        return (
            block_out,
            grad_tokens,
            own_qkv,
            own_out,
            own_gains,
            gin_own[None],
            ghid_own[None],
        )
    gain_cols = jnp.pad(norm_gains.T, ((0, 0), (0, 126)))
    w_all = lax.all_gather(
        jnp.concatenate((w_qkv, w_out, gain_cols), axis=1), everyone, axis=0, tiled=True
    )
    gains = w_all[:, 4 * width : 4 * width + 2].T.astype(F32)
    w_in_all = lax.all_gather(w_in[0], "narrow", axis=0, tiled=False)
    w_hid_all = lax.all_gather(w_hid[0], "narrow", axis=0, tiled=False)

    def exchange(values):
        return lax.all_to_all(
            values.reshape(n_expert, capacity, width), "expert", split_axis=0, concat_axis=0, tiled=True
        ).reshape(slot_rows, width)

    segr = segments.reshape(1, tok_count)
    segc = segments.reshape(tok_count, 1)
    srow, scol, dy_slots = prep(routes, gate_logit, cotangent, n_expert, capacity)
    dy_rows = exchange(dy_slots)
    qkv, context, stats, hidden, act_slots = attend_fwd(tokens, w_all, gains, segr, segc, srow, slot_rows)
    act_rows = exchange(act_slots)
    activated, grad_pre, da_rows = experts(act_rows, dy_rows, w_in_all, w_hid_all)
    da_back = exchange(da_rows)
    hidden_units = activated.shape[1]
    y_rows = dot(activated, w_hid_all.reshape(hidden_units, width)).astype(BF16)
    grad_hid = t_dot(activated, dy_rows).astype(BF16)
    grad_in = lax.dot_general(
        act_rows, grad_pre.reshape(slot_rows, n_narrow, -1), (((0,), (0,)), ((), ())), preferred_element_type=F32
    ).astype(BF16)
    y_back = exchange(y_rows)
    grad_tokens, grad_w, grad_gains = attend_bwd(
        da_back, scol, tokens, cotangent, hidden, qkv, context, stats, w_all, gains, segr, segc
    )
    block_out = block_output(y_back, scol, hidden, gate_logit)
    grad_hid_w = lax.psum_scatter(grad_hid, "narrow", scatter_dimension=0, tiled=True).astype(F32)[None]
    grad_in_w = lax.psum_scatter(grad_in, "narrow", scatter_dimension=1, tiled=True).astype(F32)
    grad_in_w = grad_in_w.reshape(1, width, -1)
    packed = jnp.concatenate((grad_w, jnp.pad(grad_gains[:2].T, ((0, 0), (0, 126)))), axis=1)
    own = lax.psum_scatter(packed, everyone, scatter_dimension=0, tiled=True)
    return (
        block_out,
        grad_tokens,
        own[:, : 3 * width],
        own[:, 3 * width : 4 * width],
        own[:, 4 * width : 4 * width + 2].T,
        grad_in_w,
        grad_hid_w,
    )


def solution(mesh):
    placed = (
        P(("expert", "narrow"), None),
        P(("expert", "narrow"), None),
        P(("expert", "narrow"), None),
        P(("expert", "narrow")),
        P(("expert", "narrow"), None),
        P(("expert", "narrow"), None),
        P(None, ("expert", "narrow")),
        P("expert", None, "narrow"),
        P("expert", "narrow", None),
        P(("expert", "narrow"), None),
    )
    return jax.shard_map(
        local,
        mesh=mesh,
        in_specs=placed,
        out_specs=(
            P(("expert", "narrow"), None),
            P(("expert", "narrow"), None),
            P(("expert", "narrow"), None),
            P(("expert", "narrow"), None),
            P(None, ("expert", "narrow")),
            P("expert", None, "narrow"),
            P("expert", "narrow", None),
        ),
        check_vma=False,
    )
```

```python
import functools

import jax
import jax.numpy as jnp
from jax import lax
from jax.experimental import pallas as pl
from jax.experimental.pallas import tpu as pltpu
from jax.sharding import PartitionSpec as P

HEAD_DIM = 64
SEQ = 1024
BLOCK = 256
LOOKBACK = 2
EPSILON = 1e-05
BIG_NEGATIVE = -1e30
F32 = jnp.float32
BF16 = jnp.bfloat16

TAIL_P = 0.3
TAIL_C = (
    0.11962923306946524,
    0.12075497050525577,
    0.0999071263144056,
    0.12858273368127124,
    -0.053723704944995426,
    0.20639718480180155,
    -0.1572285075725372,
    0.03568089149479804,
)


def dot(a, b):
    return lax.dot_general(a, b, (((1,), (0,)), ((), ())), preferred_element_type=F32)


def dot_t(a, b):
    return lax.dot_general(a, b, (((1,), (1,)), ((), ())), preferred_element_type=F32)


def t_dot(a, b):
    return lax.dot_general(a, b, (((0,), (0,)), ((), ())), preferred_element_type=F32)


def normalize(values):
    centre = jnp.mean(values, axis=-1, keepdims=True)
    shifted = values - centre
    factor = lax.rsqrt(jnp.mean(shifted * shifted, axis=-1, keepdims=True) + EPSILON)
    return shifted * factor, factor


def norm_back(grad_normed, normed, factor):
    return factor * (
        grad_normed
        - jnp.mean(grad_normed, axis=-1, keepdims=True)
        - normed * jnp.mean(grad_normed * normed, axis=-1, keepdims=True)
    )


def gelu_pair(u):
    size = jnp.abs(u)
    t = 1.0 / (1.0 + TAIL_P * size)
    poly = jnp.full_like(t, TAIL_C[-1])
    for c in TAIL_C[-2::-1]:
        poly = poly * t + c
    bell = jnp.exp(-0.5 * (u * u))
    tail = poly * t * bell
    phi = jnp.where(u >= 0, 1.0 - tail, tail)
    return u * phi, phi + u * (bell * 0.3989422804014327)


def iota(shape, dim):
    return lax.broadcasted_iota(jnp.int32, shape, dim)


def prep_kernel(capacity, experts, rrow_ref, rcol_ref, gate_ref, ct_ref, srow_ref, scol_ref, send_ref):
    tokens = ct_ref.shape[0]
    wide = max(8, experts)
    hot = (iota((wide, tokens), 0) == rrow_ref[...]).astype(F32)
    before = (iota((tokens, tokens), 0) < iota((tokens, tokens), 1)).astype(BF16)
    rank = dot(hot.astype(BF16), before)
    base = (iota((wide, tokens), 0) * capacity).astype(F32)
    srow = jnp.sum(hot * (rank + base), axis=0, keepdims=True)
    srow_ref[...] = jnp.broadcast_to(srow, srow_ref.shape)
    hot_c = (iota((tokens, 128), 1) == rcol_ref[...]).astype(F32)
    after = (iota((tokens, tokens), 1) < iota((tokens, tokens), 0)).astype(BF16)
    rank_c = dot(after, hot_c.astype(BF16))
    base_c = (iota((tokens, 128), 1) * capacity).astype(F32)
    scol_ref[...] = jnp.sum(hot_c * (rank_c + base_c), axis=1, keepdims=True)
    gated = (jax.nn.sigmoid(gate_ref[...]) * ct_ref[...].astype(F32)).astype(BF16)
    fill_slots(srow, gated, send_ref)


def fill_slots(srow, values, send_ref):
    rows = send_ref.shape[0]
    tokens = values.shape[0]

    @pl.loop(0, rows // BLOCK)
    def _(i):
        first = i * BLOCK
        ids = (iota((BLOCK, tokens), 0) + first).astype(F32)
        pick = (ids == srow).astype(BF16)
        send_ref[pl.ds(pl.multiple_of(first, BLOCK), BLOCK), :] = dot(pick, values).astype(BF16)


def prep(routes, gate_logit, cotangent, experts, capacity):
    tokens, width = cotangent.shape
    return pl.pallas_call(
        functools.partial(prep_kernel, capacity, experts),
        out_shape=(
            jax.ShapeDtypeStruct((8, tokens), F32),
            jax.ShapeDtypeStruct((tokens, 1), F32),
            jax.ShapeDtypeStruct((experts * capacity, width), BF16),
        ),
        compiler_params=pltpu.CompilerParams(vmem_limit_bytes=56 << 20),
        cost_estimate=pl.CostEstimate(flops=8 << 30, bytes_accessed=8 << 20, transcendentals=0),
    )(routes.reshape(1, tokens), routes, gate_logit.reshape(tokens, 1), cotangent)


def fwd_kernel(
    x_ref, w_ref, gain_ref, segr_ref, segc_ref, srow_ref, qkv_ref, c_ref, stat_ref, h_ref, send_ref, act_scr, bias_scr, col_scr
):
    tokens, width = x_ref.shape
    blocks = tokens // BLOCK
    pairs = width // 128
    gain_one = gain_ref[0:1, :]
    gain_two = gain_ref[1:2, :]

    @pl.loop(0, blocks)
    def _(i):
        rows = pl.ds(pl.multiple_of(i * BLOCK, BLOCK), BLOCK)
        normed, _f = normalize(x_ref[rows, :].astype(F32))
        act = (normed * gain_one).astype(BF16)
        qkv_ref[rows, :] = dot(act, w_ref[:, : 3 * width]).astype(BF16)

    col_scr[...] = jnp.zeros_like(col_scr)
    low = iota((BLOCK, 128), 1) < HEAD_DIM
    for qb in range(blocks):
        kb = max(0, qb - LOOKBACK)
        span = (qb - kb + 1) * BLOCK
        rows = pl.ds(qb * BLOCK, BLOCK)
        keys = pl.ds(kb * BLOCK, span)
        q_pos = iota((BLOCK, span), 0) + qb * BLOCK
        k_pos = iota((BLOCK, span), 1) + kb * BLOCK
        ok = (k_pos <= q_pos) & (segc_ref[rows, :] == segr_ref[0:1, keys])
        bias_scr[:, :span] = jnp.where(ok, 0.0, BIG_NEGATIVE)

        @pl.loop(0, pairs)
        def _(hp):
            at = pl.multiple_of(hp * 128, 128)
            q = qkv_ref[rows, pl.ds(at, 128)] * jnp.asarray(HEAD_DIM**-0.5, BF16)
            k = qkv_ref[keys, pl.ds(width + at, 128)]
            v = qkv_ref[keys, pl.ds(2 * width + at, 128)]
            outs = []
            col = col_scr[rows, :]
            for half in range(2):
                mine = low if half == 0 else ~low
                s = dot_t(jnp.where(mine, q, 0), k) + bias_scr[:, :span]
                top = jnp.max(s, axis=1, keepdims=True)
                raised = jnp.exp(s - top)
                total = jnp.sum(raised, axis=1, keepdims=True)
                outs.append(dot((raised * (1.0 / total)).astype(BF16), v))
                col = jnp.where(iota((BLOCK, 128), 1) == 2 * hp + half, top + jnp.log(total), col)
            col_scr[rows, :] = col
            c_ref[rows, pl.ds(at, 128)] = jnp.where(low, outs[0], outs[1]).astype(BF16)

    stat_ref[...] = col_scr[...].T

    @pl.loop(0, blocks)
    def _(i):
        rows = pl.ds(pl.multiple_of(i * BLOCK, BLOCK), BLOCK)
        hidden = x_ref[rows, :].astype(F32) + dot(c_ref[rows, :], w_ref[:, 3 * width : 4 * width])
        h_ref[rows, :] = hidden
        normed, _f = normalize(hidden)
        act_scr[rows, :] = (normed * gain_two).astype(BF16)

    fill_slots(srow_ref[0:1, :], act_scr[...], send_ref)


def attend_fwd(tokens_in, w_all, gains, segr, segc, srow, slot_rows):
    tokens, width = tokens_in.shape
    return pl.pallas_call(
        fwd_kernel,
        out_shape=(
            jax.ShapeDtypeStruct((tokens, 3 * width), BF16),
            jax.ShapeDtypeStruct((tokens, width), BF16),
            jax.ShapeDtypeStruct((128, tokens), F32),
            jax.ShapeDtypeStruct((tokens, width), F32),
            jax.ShapeDtypeStruct((slot_rows, width), BF16),
        ),
        scratch_shapes=[
            pltpu.VMEM((tokens, width), BF16),
            pltpu.VMEM((BLOCK, (LOOKBACK + 1) * BLOCK), F32),
            pltpu.VMEM((tokens, 128), F32),
        ],
        compiler_params=pltpu.CompilerParams(vmem_limit_bytes=56 << 20),
        cost_estimate=pl.CostEstimate(flops=40 << 30, bytes_accessed=24 << 20, transcendentals=0),
    )(tokens_in, w_all, gains, segr, segc, srow)


def expert_kernel(a_ref, dy_ref, win_ref, whid_ref, g_ref, du_ref, da_ref, acc_scr):
    a = a_ref[...]
    dy = dy_ref[...]
    parts = win_ref.shape[0]
    wide = win_ref.shape[2]
    acc_scr[...] = jnp.zeros_like(acc_scr)

    @pl.loop(0, parts)
    def _(j):
        cols = pl.ds(pl.multiple_of(j * wide, wide), wide)
        u = dot(a, win_ref[j])
        grad = dot_t(dy, whid_ref[j])
        g, slope = gelu_pair(u)
        g_ref[:, cols] = g.astype(BF16)
        du = (grad * slope).astype(BF16)
        du_ref[:, cols] = du
        acc_scr[...] += dot_t(du, win_ref[j])

    da_ref[...] = acc_scr[...].astype(BF16)


def experts(acts, grads, w_in, w_hid):
    rows, width = acts.shape
    parts, _, wide = w_in.shape
    hidden = parts * wide
    row_spec = pl.BlockSpec((BLOCK, width), lambda i: (i, 0))
    wide_spec = pl.BlockSpec((BLOCK, hidden), lambda i: (i, 0))
    return pl.pallas_call(
        expert_kernel,
        grid=(rows // BLOCK,),
        out_shape=(
            jax.ShapeDtypeStruct((rows, hidden), BF16),
            jax.ShapeDtypeStruct((rows, hidden), BF16),
            jax.ShapeDtypeStruct((rows, width), BF16),
        ),
        in_specs=[
            row_spec,
            row_spec,
            pl.BlockSpec(w_in.shape, lambda i: (0, 0, 0), pipeline_mode=pl.Buffered(1)),
            pl.BlockSpec(w_hid.shape, lambda i: (0, 0, 0), pipeline_mode=pl.Buffered(1)),
        ],
        out_specs=(wide_spec, wide_spec, row_spec),
        scratch_shapes=[pltpu.VMEM((BLOCK, width), F32)],
        compiler_params=pltpu.CompilerParams(vmem_limit_bytes=56 << 20),
        cost_estimate=pl.CostEstimate(flops=60 << 30, bytes_accessed=40 << 20, transcendentals=0),
    )(acts, grads, w_in, w_hid)


def out_kernel(ret_ref, scol_ref, h_ref, gate_ref, out_ref):
    tokens, rows = out_ref.shape[0], ret_ref.shape[0]
    pick = (iota((tokens, rows), 1).astype(F32) == scol_ref[...]).astype(BF16)
    y = dot(pick, ret_ref[...])
    out_ref[...] = (h_ref[...] + jax.nn.sigmoid(gate_ref[...]) * y).astype(BF16)


def block_output(returned, scol, hidden, gate_logit):
    rows, width = returned.shape
    tokens = hidden.shape[0]
    tile = pl.BlockSpec((BLOCK, width), lambda i: (i, 0))
    column = pl.BlockSpec((BLOCK, 1), lambda i: (i, 0))
    return pl.pallas_call(
        out_kernel,
        grid=(tokens // BLOCK,),
        out_shape=jax.ShapeDtypeStruct((tokens, width), BF16),
        in_specs=[pl.BlockSpec((rows, width), lambda i: (0, 0)), column, tile, column],
        out_specs=tile,
        compiler_params=pltpu.CompilerParams(vmem_limit_bytes=40 << 20),
        cost_estimate=pl.CostEstimate(flops=4 << 30, bytes_accessed=10 << 20, transcendentals=0),
    )(returned, scol, hidden, gate_logit.reshape(tokens, 1))


def bwd_kernel(
    ret_ref,
    scol_ref,
    x_ref,
    ct_ref,
    h_ref,
    qkv_ref,
    c_ref,
    stat_ref,
    w_ref,
    gain_ref,
    segr_ref,
    segc_ref,
    gt_ref,
    gw_ref,
    gg_ref,
    dc_scr,
    dhb_scr,
    dqkv_scr,
    act_scr,
    d_scr,
    dk_scr,
    dv_scr,
):
    tokens, width = x_ref.shape
    slots = ret_ref.shape[0]
    blocks = tokens // BLOCK
    pairs = width // 128
    gain_one = gain_ref[0:1, :]
    gain_two = gain_ref[1:2, :]
    gg_ref[...] = jnp.zeros_like(gg_ref)
    member = (iota((16, width), 1) // HEAD_DIM == iota((16, width), 0)).astype(F32)

    for i in range(blocks):
        rows = pl.ds(i * BLOCK, BLOCK)
        pick = (iota((BLOCK, slots), 1).astype(F32) == scol_ref[rows, :]).astype(BF16)
        da = dot(pick, ret_ref[...])
        normed, factor = normalize(h_ref[rows, :])
        gg_ref[1:2, :] += jnp.sum(da * normed, axis=0, keepdims=True)
        dh = ct_ref[rows, :].astype(F32) + norm_back(da * gain_two, normed, factor)
        gt_ref[rows, :] = dh
        dhb = dh.astype(BF16)
        dhb_scr[rows, :] = dhb
        dc = dot_t(dhb, w_ref[:, 3 * width : 4 * width]).astype(BF16)
        dc_scr[rows, :] = dc
        d_scr[:, rows] = lax.dot_general(
            member,
            dc.astype(F32) * c_ref[rows, :].astype(F32),
            (((1,), (1,)), ((), ())),
            precision=lax.Precision.HIGHEST,
            preferred_element_type=F32,
        )

    gw_ref[:, 3 * width : 4 * width] = t_dot(c_ref[...], dhb_scr[...])
    low = iota((BLOCK, 128), 1) < HEAD_DIM
    scale = HEAD_DIM**-0.5

    @pl.loop(0, pairs)
    def _(hp):
        at = pl.multiple_of(hp * 128, 128)
        dk_scr[...] = jnp.zeros_like(dk_scr)
        dv_scr[...] = jnp.zeros_like(dv_scr)
        for qb in range(blocks):
            rows = pl.ds(qb * BLOCK, BLOCK)
            q = qkv_ref[rows, pl.ds(at, 128)] * jnp.asarray(scale, BF16)
            dc = dc_scr[rows, pl.ds(at, 128)]
            q_half = [jnp.where(low, q, 0), jnp.where(low, 0, q)]
            dc_half = [jnp.where(low, dc, 0), jnp.where(low, 0, dc)]
            dq = jnp.zeros((BLOCK, 128), F32)
            for kb in range(max(0, qb - LOOKBACK), qb + 1):
                keys = pl.ds(kb * BLOCK, BLOCK)
                k = qkv_ref[keys, pl.ds(width + at, 128)]
                v = qkv_ref[keys, pl.ds(2 * width + at, 128)]
                ok = segc_ref[keys, :] == segr_ref[0:1, rows]
                if kb == qb:
                    ok = ok & (iota((BLOCK, BLOCK), 0) <= iota((BLOCK, BLOCK), 1))
                ps, dss = [], []
                for half in range(2):
                    s = dot_t(k, q_half[half])
                    p = jnp.where(ok, jnp.exp(s - stat_ref[pl.ds(2 * hp + half, 1), rows]), 0.0)
                    dp = dot_t(v, dc_half[half])
                    dss.append((p * (dp - d_scr[pl.ds(2 * hp + half, 1), rows])).astype(BF16))
                    ps.append(p.astype(BF16))
                dv_scr[keys, :] += dot(jnp.concatenate(ps, 1), jnp.concatenate(dc_half, 0))
                dk_scr[keys, :] += dot(jnp.concatenate(dss, 1), jnp.concatenate(q_half, 0))
                dq += jnp.where(low, t_dot(dss[0], k), t_dot(dss[1], k))
            dqkv_scr[rows, pl.ds(at, 128)] = (dq * scale).astype(BF16)
        dqkv_scr[:, pl.ds(width + at, 128)] = dk_scr[...].astype(BF16)
        dqkv_scr[:, pl.ds(2 * width + at, 128)] = dv_scr[...].astype(BF16)

    @pl.loop(0, blocks)
    def _(i):
        rows = pl.ds(pl.multiple_of(i * BLOCK, BLOCK), BLOCK)
        normed, factor = normalize(x_ref[rows, :].astype(F32))
        act_scr[rows, :] = (normed * gain_one).astype(BF16)
        dn = dot_t(dqkv_scr[rows, :], w_ref[:, : 3 * width])
        gg_ref[0:1, :] += jnp.sum(dn * normed, axis=0, keepdims=True)
        gt_ref[rows, :] += norm_back(dn * gain_one, normed, factor)

    gw_ref[:, : 3 * width] = t_dot(act_scr[...], dqkv_scr[...])


def attend_bwd(returned, scol, tokens_in, cotangent, hidden, qkv, context, stats, w_all, gains, segr, segc):
    tokens, width = tokens_in.shape
    return pl.pallas_call(
        bwd_kernel,
        out_shape=(
            jax.ShapeDtypeStruct((tokens, width), F32),
            jax.ShapeDtypeStruct((width, 4 * width), F32),
            jax.ShapeDtypeStruct((8, width), F32),
        ),
        scratch_shapes=[
            pltpu.VMEM((tokens, width), BF16),
            pltpu.VMEM((tokens, width), BF16),
            pltpu.VMEM((tokens, 3 * width), BF16),
            pltpu.VMEM((tokens, width), BF16),
            pltpu.VMEM((16, tokens), F32),
            pltpu.VMEM((tokens, 128), F32),
            pltpu.VMEM((tokens, 128), F32),
        ],
        compiler_params=pltpu.CompilerParams(vmem_limit_bytes=60 << 20),
        cost_estimate=pl.CostEstimate(flops=80 << 30, bytes_accessed=40 << 20, transcendentals=0),
    )(returned, scol, tokens_in, cotangent, hidden, qkv, context, stats, w_all, gains, segr, segc)


MESH = pl.DeviceIdType.MESH


def place():
    e, n = lax.axis_index("expert"), lax.axis_index("narrow")
    return e // 2, lax.rem(e, 2), n // 2, lax.rem(n, 2)


def device(z, y, x, c):
    return (z * 2 + y, x * 2 + c)


def across(z, k):
    hi, lo = z // 2, lax.rem(z, 2)
    hi = 1 - hi if k & 2 else hi
    lo = 1 - lo if k & 1 else lo
    return hi * 2 + lo


class Links:
    def __init__(self, send, recv):
        self.send, self.recv, self.used = send, recv, 0

    def make(self, src, dst, to):
        i = self.used
        self.used += 1
        return pltpu.make_async_remote_copy(
            src_ref=src, dst_ref=dst, send_sem=self.send.at[i], recv_sem=self.recv.at[i], device_id=to, device_id_type=MESH
        )

    def push(self, src, dst, to):
        copy = self.make(src, dst, to)
        copy.start()
        return copy


class Loads:
    def __init__(self, sems):
        self.sems, self.used = sems, 0

    def start(self, src, dst):
        copy = pltpu.make_async_copy(src, dst, self.sems.at[self.used])
        self.used += 1
        copy.start()
        return copy


def greet(peers):
    barrier = pltpu.get_barrier_semaphore()
    for peer in peers:
        pl.semaphore_signal(barrier, inc=1, device_id=peer, device_id_type=MESH)
    pl.semaphore_wait(barrier, len(peers))


FLIPS = (4, 2, 6, 1, 5, 3, 7)


def peers_of(z, y, x, c):
    return [device(across(z, k >> 1), 1 - y if k & 1 else y, x, c) for k in FLIPS]


def weight(ref, lo, hi):
    return ref[:, :, :, :, lo:hi].reshape(-1, hi - lo)


def head_kernel(
    capacity,
    experts,
    x_hbm,
    ct_hbm,
    win_hbm,
    whid_hbm,
    row_ref,
    wqkv_ref,
    wout_ref,
    gshard_ref,
    qkv_hbm,
    c_hbm,
    h_hbm,
    act_hbm,
    w_hbm,
    dyrow_hbm,
    win4_hbm,
    whid4_hbm,
    stat_ref,
    col_ref,
    gain_ref,
    x_ref,
    ct_ref,
    sh,
    st,
    square,
    wq,
    wg,
    qkv_ref,
    c_ref,
    h_ref,
    a_scr,
    act_ref,
    dy_ref,
    bias_scr,
    send_sems,
    recv_sems,
    load_sems,
):
    z, y, x, c = place()
    me_e = z * 2 + y
    me_n = x * 2 + c
    tokens, width = x_ref.shape
    blocks = tokens // BLOCK
    pairs = width // 128
    half = width // 2
    core, xpeer, ypeer = device(z, y, x, 1 - c), device(z, y, 1 - x, c), device(z, 1 - y, x, c)
    links = Links(send_sems, recv_sems)
    loads = Loads(load_sems)
    loading_ct = loads.start(ct_hbm, ct_ref)
    loading_x = loads.start(x_hbm, x_ref)

    square[...] = jnp.zeros_like(square)
    square[0:2, 0 : gshard_ref.shape[1]] = gshard_ref[...].astype(F32)
    gain_cols = square[...].T
    for side in range(2):
        for j in range(4):
            src, at = (wqkv_ref, j * width) if j < 3 else (wout_ref, 0)
            sh[side, :, j * half : (j + 1) * half] = src[:, at + side * half : at + (side + 1) * half].astype(F32)
        sh[side, :, 4 * half :] = gain_cols[0 : gshard_ref.shape[1], :]
    st[c] = sh[c]

    greet(peers_of(z, y, x, c) + [core, xpeer])
    zero = links.push(sh.at[1 - c], st.at[c], core)

    deep = width // 2
    upper, lower = pl.ds(0, deep), pl.ds(deep, deep)

    def hand(src, dst, rows):
        return links.push(src.at[rows], dst.at[me_n, rows], xpeer)

    def onward(dst, rows):
        part = dst.at[(1 - x) * 2 + c, rows]
        return links.push(part, part, core)

    parts = [(hand(win_hbm, win4_hbm, upper), win4_hbm, upper)]

    def cols(j):
        return pl.ds(pl.multiple_of((2 * j + c) * half, 128), half)

    zero.wait()
    rows48 = jnp.concatenate((st[0], st[1]), axis=0)
    for j in range(4):
        wq[z, y, x, :, cols(j)] = rows48[:, j * half : (j + 1) * half].astype(BF16)
    wg[z, y, x] = rows48[:, 4 * half :].astype(BF16)
    ring_z = []
    for piece in range(2):
        group = []
        for k in (1, 2, 3):
            to = device(across(z, k), y, x, c)
            for j in (2 * piece, 2 * piece + 1):
                part = wq.at[z, y, x, :, cols(j)]
                group.append(links.push(part, part, to))
            if piece == 0:
                group.append(links.push(wg.at[z, y, x], wg.at[z, y, x], to))
        ring_z.append(group)

    wide = max(8, experts)
    hot = (iota((wide, tokens), 0).astype(F32) == row_ref[0:1, :]).astype(F32)
    before = (iota((tokens, tokens), 0) < iota((tokens, tokens), 1)).astype(BF16)
    rank = dot(hot.astype(BF16), before)
    base = (iota((wide, tokens), 0) * capacity).astype(F32)
    srow = jnp.sum(hot * (rank + base), axis=0, keepdims=True)

    listed = row_ref[...].T
    hot_c = (iota((tokens, 128), 1).astype(F32) == listed[:, 0:1]).astype(F32)
    after = (iota((tokens, tokens), 1) < iota((tokens, tokens), 0)).astype(BF16)
    rank_c = dot(after, hot_c.astype(BF16))
    base_c = (iota((tokens, 128), 1) * capacity).astype(F32)
    scol = jnp.sum(hot_c * (rank_c + base_c), axis=1, keepdims=True)
    col_ref[...] = jnp.where(iota(listed.shape, 1) == 0, scol, listed)

    def storing_act(i):
        return pltpu.make_async_copy(act_ref.at[i], act_hbm.at[i], load_sems.at[16 + i])

    def fill(values, out, then=None):
        @pl.loop(0, out.shape[0])
        def _(i):
            ids = (iota((capacity, tokens), 0) + i * capacity).astype(F32)
            out[i] = dot((ids == srow).astype(BF16), values).astype(BF16)
            if then is not None:
                then(i).start()

    loading_ct.wait()
    fill((jax.nn.sigmoid(listed[:, 1:2]) * ct_ref[...].astype(F32)).astype(BF16), dy_ref)

    ring_2 = []
    for piece in range(2):
        for copy in ring_z[piece]:
            copy.wait()
        ca, cb = cols(2 * piece), cols(2 * piece + 1)
        group = [
            links.push(wq.at[:, y, x, :, ca], wq.at[:, y, x, :, ca], ypeer),
            links.push(wq.at[:, y, x, :, cb], wq.at[:, y, x, :, cb], xpeer),
        ]
        if piece == 0:
            group.append(links.push(wg.at[:, y, x], wg.at[:, y, x], ypeer))
        ring_2.append(group)
    dy_copies = []
    for k in FLIPS:
        zz, yy = across(z, k >> 1), (1 - y if k & 1 else y)
        dy_copies.append(links.push(dy_ref.at[zz * 2 + yy], dyrow_hbm.at[me_e], device(zz, yy, x, c)))
    own_dy = loads.start(dy_ref.at[me_e], dyrow_hbm.at[me_e])
    ring_3 = []
    for piece in range(2):
        for copy in ring_2[piece]:
            copy.wait()
        ca, cb = cols(2 * piece), cols(2 * piece + 1)
        group = [
            links.push(wq.at[:, :, x, :, ca], wq.at[:, :, x, :, ca], xpeer),
            links.push(wq.at[:, y, :, :, cb], wq.at[:, y, :, :, cb], ypeer),
        ]
        if piece == 0:
            group.append(links.push(wg.at[:, :, x], wg.at[:, :, x], xpeer))
        ring_3.append(group)
    for src, dst, rows in ((win_hbm, win4_hbm, lower), (whid_hbm, whid4_hbm, upper), (whid_hbm, whid4_hbm, lower)):
        parts.append((hand(src, dst, rows), dst, rows))
    ring_4 = []
    for piece in range(2):
        for copy in ring_3[piece]:
            copy.wait()
        ring_4.append([links.push(wq.at[:, :, :, :, cols(j)], wq.at[:, :, :, :, cols(j)], core) for j in (2 * piece, 2 * piece + 1)])

    gains = jnp.transpose(wg[...].reshape(width, 128).astype(F32))[0:8, :]
    gain_ref[...] = gains
    gain_one = gains[0:1, :]
    gain_two = gains[1:2, :]
    loading_x.wait()
    for piece in range(2):
        for copy in ring_4[piece]:
            copy.wait()
    storing = [loads.start(wq, w_hbm)]
    core_slices = [links.push(src, dst.at[me_n], core) for src, dst in ((win_hbm, win4_hbm), (whid_hbm, whid4_hbm))]

    def pass_on(i):
        copy, dst, rows = parts[i]
        copy.wait()
        core_slices.append(onward(dst, rows))

    pass_on(0)

    @pl.loop(0, blocks)
    def _(i):
        rows = pl.ds(pl.multiple_of(i * BLOCK, BLOCK), BLOCK)
        normed, _f = normalize(x_ref[rows, :].astype(F32))
        act = (normed * gain_one).astype(BF16)
        qkv_ref[rows, :] = dot(act, weight(wq, 0, 3 * width)).astype(BF16)

    storing.append(loads.start(qkv_ref, qkv_hbm))
    low = iota((BLOCK, 128), 1) < HEAD_DIM
    tiles = [(qb, kb) for qb in range(blocks) for kb in range(max(0, qb - LOOKBACK), qb + 1)]
    for n, (qb, kb) in enumerate(tiles):
        ok = col_ref[pl.ds(kb * BLOCK, BLOCK), 2:3] == row_ref[2:3, pl.ds(qb * BLOCK, BLOCK)]
        if kb == qb:
            ok = ok & (iota((BLOCK, BLOCK), 0) <= iota((BLOCK, BLOCK), 1))
        bias_scr[n] = jnp.where(ok, 0.0, BIG_NEGATIVE)

    @pl.loop(0, pairs)
    def _(hp):
        at = pl.multiple_of(hp * 128, 128)
        for qb in range(blocks):
            mine = [(n, kb) for n, (qq, kb) in enumerate(tiles) if qq == qb]
            rows = pl.ds(qb * BLOCK, BLOCK)
            q = qkv_ref[rows, pl.ds(at, 128)] * jnp.asarray(HEAD_DIM**-0.5, BF16)
            v = qkv_ref[pl.ds(mine[0][1] * BLOCK, len(mine) * BLOCK), pl.ds(2 * width + at, 128)]
            outs = []
            for side in range(2):
                q_half = jnp.where(low, q, 0) if side == 0 else jnp.where(low, 0, q)
                scores = [
                    dot_t(qkv_ref[pl.ds(kb * BLOCK, BLOCK), pl.ds(width + at, 128)], q_half) + bias_scr[n] for n, kb in mine
                ]
                top = functools.reduce(jnp.maximum, [jnp.max(s, axis=0, keepdims=True) for s in scores])
                raised = [jnp.exp(s - top) for s in scores]
                total = functools.reduce(jnp.add, [jnp.sum(r, axis=0, keepdims=True) for r in raised])
                share = 1.0 / total
                weights = jnp.concatenate([(r * share).astype(BF16) for r in raised], axis=0)
                outs.append(t_dot(weights, v))
                stat_ref[pl.ds(2 * hp + side, 1), rows] = top + jnp.log(total)
            c_ref[rows, pl.ds(at, 128)] = jnp.where(low, outs[0], outs[1]).astype(BF16)

    storing.append(loads.start(c_ref, c_hbm))

    @pl.loop(0, blocks)
    def _(i):
        rows = pl.ds(pl.multiple_of(i * BLOCK, BLOCK), BLOCK)
        hidden = x_ref[rows, :].astype(F32) + dot(c_ref[rows, :], weight(wq, 3 * width, 4 * width))
        h_ref[rows, :] = hidden
        normed, _f = normalize(hidden)
        a_scr[rows, :] = (normed * gain_two).astype(BF16)

    storing.append(loads.start(h_ref, h_hbm))
    fill(a_scr[...], act_ref, storing_act)
    storing += [storing_act(i) for i in range(experts)]
    for i in range(1, 4):
        pass_on(i)
    for copy in storing + [own_dy] + core_slices + dy_copies:
        copy.wait()


def head(tokens_in, cotangent, w_in, w_hid, listed, w_qkv, w_out, gain_shard, experts, capacity):
    tokens, width = tokens_in.shape
    any_spec = pl.BlockSpec(memory_space=pl.ANY)
    vmem = pl.BlockSpec(memory_space=pltpu.VMEM)
    slots = (experts, capacity, width)
    blocks = (4, 2, 2, 48, 4 * width)
    shard = (2, w_qkv.shape[0], 2 * width + 128)
    return pl.pallas_call(
        functools.partial(head_kernel, capacity, experts),
        out_shape=(
            jax.ShapeDtypeStruct((tokens, 3 * width), BF16),
            jax.ShapeDtypeStruct((tokens, width), BF16),
            jax.ShapeDtypeStruct((tokens, width), F32),
            jax.ShapeDtypeStruct(slots, BF16),
            jax.ShapeDtypeStruct(blocks, BF16),
            jax.ShapeDtypeStruct(slots, BF16),
            jax.ShapeDtypeStruct((4,) + w_in.shape, BF16),
            jax.ShapeDtypeStruct((4,) + w_hid.shape, BF16),
            jax.ShapeDtypeStruct((16, tokens), F32),
            jax.ShapeDtypeStruct((tokens, 8), F32),
            jax.ShapeDtypeStruct((8, width), F32),
        ),
        in_specs=[any_spec] * 4 + [vmem] * 4,
        out_specs=(any_spec,) * 8 + (vmem,) * 3,
        scratch_shapes=[
            pltpu.VMEM((tokens, width), BF16),
            pltpu.VMEM((tokens, width), BF16),
            pltpu.VMEM(shard, F32),
            pltpu.VMEM(shard, F32),
            pltpu.VMEM((128, 128), F32),
            pltpu.VMEM(blocks, BF16),
            pltpu.VMEM((4, 2, 2, 48, 128), BF16),
            pltpu.VMEM((tokens, 3 * width), BF16),
            pltpu.VMEM((tokens, width), BF16),
            pltpu.VMEM((tokens, width), F32),
            pltpu.VMEM((tokens, width), BF16),
            pltpu.VMEM(slots, BF16),
            pltpu.VMEM(slots, BF16),
            pltpu.VMEM((tokens // BLOCK * (LOOKBACK + 1), BLOCK, BLOCK), F32),
            pltpu.SemaphoreType.DMA((48,)),
            pltpu.SemaphoreType.DMA((48,)),
            pltpu.SemaphoreType.DMA((16 + experts,)),
        ],
        compiler_params=pltpu.CompilerParams(vmem_limit_bytes=62 << 20, collective_id=0, has_side_effects=True),
        cost_estimate=pl.CostEstimate(flops=60 << 30, bytes_accessed=40 << 20, transcendentals=0),
    )(tokens_in, cotangent, w_in, w_hid, listed, w_qkv, w_out, gain_shard)


class Reduce:
    def __init__(self, spot, ph, gq, rc, r1, r2, r3, fin, r4, send_sems, recv_sems):
        self.z, self.y, self.x, self.c = spot
        self.gq, self.rc, self.r1, self.r2, self.r3, self.fin, self.r4 = (
            gq.at[ph],
            rc.at[ph],
            r1.at[ph],
            r2.at[ph],
            r3.at[ph],
            fin.at[ph],
            r4.at[ph],
        )
        self.base = ph * 7
        self.send, self.recv = send_sems, recv_sems

    def copy(self, i, src, dst, to):
        return pltpu.make_async_remote_copy(
            src_ref=src,
            dst_ref=dst,
            send_sem=self.send.at[self.base + i],
            recv_sem=self.recv.at[self.base + i],
            device_id=to,
            device_id_type=MESH,
        )

    def turn(self, i):
        return i * (1 - self.c) + self.y * self.c, self.x * (1 - self.c) + i * self.c

    def add(self, where, term):
        self.gq[where] = (self.gq[where].astype(F32) + term.astype(F32)).astype(BF16)

    def cores(self):
        z, y, x, c = self.z, self.y, self.x, self.c
        return self.copy(0, self.gq.at[1 - c], self.rc, device(z, y, x, 1 - c))

    def by_core(self, go, first, second):
        @pl.when(self.c == 0)
        def _():
            go(first)

        @pl.when(self.c == 1)
        def _():
            go(second)

    def one(self, go):
        z, y, x, c = self.z, self.y, self.x, self.c
        self.by_core(
            go,
            self.copy(1, self.gq.at[0, :, :, 1 - x], self.r1, device(z, y, 1 - x, c)),
            self.copy(1, self.gq.at[1, :, 1 - y], self.r1, device(z, 1 - y, x, c)),
        )

    def two(self, go):
        z, y, x, c = self.z, self.y, self.x, self.c
        self.by_core(
            go,
            self.copy(2, self.gq.at[0, :, 1 - y, x], self.r2, device(z, 1 - y, x, c)),
            self.copy(2, self.gq.at[1, :, y, 1 - x], self.r2, device(z, y, 1 - x, c)),
        )

    def three(self):
        z, y, x, c = self.z, self.y, self.x, self.c
        return [
            self.copy(2 + k, self.gq.at[c, across(z, k), y, x], self.r3.at[k - 1], device(across(z, k), y, x, c))
            for k in (1, 2, 3)
        ]

    def four(self):
        z, y, x, c = self.z, self.y, self.x, self.c
        rows = pl.ds(pl.multiple_of((1 - c) * 24, 8), 24)
        return self.copy(6, self.fin.at[rows], self.r4, device(z, y, x, 1 - c))

    def step(self, stage):
        z, y, x, c = self.z, self.y, self.x, self.c
        if stage == 0:
            self.cores().start()
        if stage == 1:
            self.cores().wait()

            @pl.loop(0, 4)
            def _(k):
                self.add((c, k), self.rc[k])

            self.one(lambda copy: copy.start())
        if stage == 2:
            self.one(lambda copy: copy.wait())

            @pl.loop(0, 4)
            def _(k):
                for i in range(2):
                    yy, xx = self.turn(i)
                    self.add((c, k, yy, xx), self.r1[k, i])

            self.two(lambda copy: copy.start())
        if stage == 3:
            self.two(lambda copy: copy.wait())

            @pl.loop(0, 4)
            def _(k):
                self.add((c, k, y, x), self.r2[k])

            for copy in self.three():
                copy.start()
        if stage == 4:
            for copy in self.three():
                copy.wait()
            total = self.gq[c, z, y, x].astype(F32)
            for k in range(3):
                total = total + self.r3[k].astype(F32)
            self.fin[...] = total
            self.four().start()


def tail_kernel(
    ret_hbm,
    x_hbm,
    ct_hbm,
    h_hbm,
    qkv_hbm,
    c_hbm,
    w_hbm,
    yrow_hbm,
    gw_hbm,
    col_ref,
    row_ref,
    stat_ref,
    gain_ref,
    gt_hbm,
    gw_out,
    out_hbm,
    ownq_ref,
    owno_ref,
    gg_ref,
    ret_ref,
    x_ref,
    ct_ref,
    h_ref,
    qkv_ref,
    c_ref,
    w_ref,
    gt_ref,
    dc_scr,
    dhb_scr,
    dqkv_scr,
    actt_scr,
    d_scr,
    dk_scr,
    dv_scr,
    gq,
    rc,
    q1,
    q2,
    q3,
    fin,
    q4,
    ggs,
    rg,
    near,
    next_x,
    nsum,
    yback,
    gw_scr,
    send_sems,
    recv_sems,
    red_send,
    red_recv,
    load_sems,
):
    spot = place()
    z, y, x, c = spot
    me_e = z * 2 + y
    tokens, width = x_ref.shape
    slots, _w = ret_ref.shape
    blocks = tokens // BLOCK
    half = width // 2
    core, xpeer, ypeer = device(z, y, x, 1 - c), device(z, y, 1 - x, c), device(z, 1 - y, x, c)
    far = peers_of(z, y, x, c)
    links = Links(send_sems, recv_sems)
    loads = Loads(load_sems)

    def reduce(ph):
        return Reduce(spot, ph, gq, rc, q1, q2, q3, fin, q4, red_send, red_recv)

    first = [
        loads.start(a, b)
        for a, b in (
            (ret_hbm, ret_ref),
            (h_hbm, h_ref),
            (w_hbm.at[:, :, :, :, pl.ds(3 * width, width)], w_ref.at[:, :, :, :, pl.ds(3 * width, width)]),
            (ct_hbm, ct_ref),
            (c_hbm, c_ref),
        )
    ]
    second = [
        loads.start(a, b)
        for a, b in (
            (gw_hbm.at[(1 - x) * 2 + c], nsum.at[0]),
            (gw_hbm.at[x * 2 + c], nsum.at[1]),
            (x_hbm, x_ref),
            (qkv_hbm, qkv_ref),
            (w_hbm.at[:, :, :, :, pl.ds(0, 3 * width)], w_ref.at[:, :, :, :, pl.ds(0, 3 * width)]),
            (yrow_hbm.at[me_e], yback.at[me_e]),
        )
    ]
    greet(far + [core, xpeer])

    w_copies = [links.push(gw_hbm.at[xx * 2 + 1 - c], near.at[xx], core) for xx in range(2)]
    y_near, y_far = [], []
    for k, to in zip(FLIPS, far):
        (y_far if k >= 4 else y_near).append(links.push(yrow_hbm.at[to[0]], yback.at[me_e], to))

    gain_one = gain_ref[0:1, :]
    gain_two = gain_ref[1:2, :]
    member = (iota((16, 2 * width), 1) % width // HEAD_DIM == iota((16, 2 * width), 0)).astype(BF16)
    for copy in first:
        copy.wait()
    ggs[...] = jnp.zeros_like(ggs)

    def picks(rows):
        return (iota((BLOCK, slots), 1).astype(F32) == col_ref[rows, 0:1]).astype(BF16)

    @pl.loop(0, blocks)
    def _(i):
        rows = pl.ds(pl.multiple_of(i * BLOCK, BLOCK), BLOCK)
        da = dot(picks(rows), ret_ref[...])
        normed, factor = normalize(h_ref[rows, :])
        ggs[0, 1:2, :] += jnp.sum(da * normed, axis=0, keepdims=True)
        dh = ct_ref[rows, :].astype(F32) + norm_back(da * gain_two, normed, factor)
        gt_ref[rows, :] = dh
        dhb = dh.astype(BF16)
        dhb_scr[rows, :] = dhb
        dc = dot_t(dhb, weight(w_ref, 3 * width, 4 * width)).astype(BF16)
        dc_scr[rows, :] = dc
        product = dc.astype(F32) * c_ref[rows, :].astype(F32)
        high = product.astype(BF16)
        rest = (product - high.astype(F32)).astype(BF16)
        d_scr[:, rows] = dot_t(member, jnp.concatenate((high, rest), axis=1))

    def put(ph, value):
        for owner in range(2):
            for chip in range(16):
                gq[ph, owner, chip // 4, chip // 2 % 2, chip % 2] = value[
                    chip * 48 : chip * 48 + 48, owner * half : (owner + 1) * half
                ].astype(BF16)

    put(0, t_dot(c_ref[...], dhb_scr[...]))
    reduce(0).step(0)

    for copy in w_copies:
        copy.wait()

    def to_x(i):
        rows = pl.ds(pl.multiple_of(i * (width // 4), width // 4), width // 4)
        return pltpu.make_async_remote_copy(
            src_ref=nsum.at[0, rows],
            dst_ref=next_x.at[rows],
            send_sem=send_sems.at[16 + i],
            recv_sem=recv_sems.at[16 + i],
            device_id=xpeer,
            device_id_type=MESH,
        )

    for copy in second:
        copy.wait()
    nsum[0] = (nsum[0].astype(F32) + near[1 - x].astype(F32)).astype(BF16)
    to_x(0).start()

    @pl.loop(0, blocks)
    def _(i):
        rows = pl.ds(pl.multiple_of(i * BLOCK, BLOCK), BLOCK)
        normed, _f = normalize(x_ref[rows, :].astype(F32))
        dhb_scr[rows, :] = (normed * gain_one).astype(BF16)

    actt_scr[...] = dhb_scr[...].T
    low = iota((BLOCK, 128), 1) < HEAD_DIM
    scale = HEAD_DIM**-0.5

    @pl.loop(0, 3)
    def _(t):
        @pl.loop(0, 2)
        def _(inner):
            hp = 2 * t + inner
            at = pl.multiple_of(hp * 128, 128)
            dk_scr[...] = jnp.zeros_like(dk_scr)
            dv_scr[...] = jnp.zeros_like(dv_scr)
            for qb in range(blocks):
                rows = pl.ds(qb * BLOCK, BLOCK)
                q = qkv_ref[rows, pl.ds(at, 128)] * jnp.asarray(scale, BF16)
                dc = dc_scr[rows, pl.ds(at, 128)]
                q_half = [jnp.where(low, q, 0), jnp.where(low, 0, q)]
                dc_half = [jnp.where(low, dc, 0), jnp.where(low, 0, dc)]
                dq = jnp.zeros((BLOCK, 128), F32)
                for kb in range(max(0, qb - LOOKBACK), qb + 1):
                    keys = pl.ds(kb * BLOCK, BLOCK)
                    k = qkv_ref[keys, pl.ds(width + at, 128)]
                    v = qkv_ref[keys, pl.ds(2 * width + at, 128)]
                    ok = col_ref[keys, 2:3] == row_ref[2:3, rows]
                    if kb == qb:
                        ok = ok & (iota((BLOCK, BLOCK), 0) <= iota((BLOCK, BLOCK), 1))
                    ps, dss = [], []
                    for side in range(2):
                        s = dot_t(k, q_half[side])
                        p = jnp.where(ok, jnp.exp(s - stat_ref[pl.ds(2 * hp + side, 1), rows]), 0.0)
                        dp = dot_t(v, dc_half[side])
                        dss.append((p * (dp - d_scr[pl.ds(2 * hp + side, 1), rows])).astype(BF16))
                        ps.append(p.astype(BF16))
                    dv_scr[keys, :] += dot(jnp.concatenate(ps, 1), jnp.concatenate(dc_half, 0))
                    dk_scr[keys, :] += dot(jnp.concatenate(dss, 1), jnp.concatenate(q_half, 0))
                    dq += jnp.where(low, t_dot(dss[0], k), t_dot(dss[1], k))
                dqkv_scr[rows, pl.ds(at, 128)] = (dq * scale).astype(BF16)
            dqkv_scr[:, pl.ds(width + at, 128)] = dk_scr[...].astype(BF16)
            dqkv_scr[:, pl.ds(2 * width + at, 128)] = dv_scr[...].astype(BF16)

        columns = []
        for inner in range(2):
            at = pl.multiple_of((2 * t + inner) * 128, 128)
            columns += [dqkv_scr[:, pl.ds(j * width + at, 128)] for j in range(3)]
        put(t + 1, dot(actt_scr[...], jnp.concatenate(columns, axis=1)))
        reduce(t + 1).step(0)
        reduce(t).step(1)

        @pl.when(t >= 1)
        def _():
            reduce(t - 1).step(2)

        @pl.when(t >= 2)
        def _():
            reduce(t - 2).step(3)

        to_x(t + 1).start()

    @pl.loop(0, blocks)
    def _(i):
        rows = pl.ds(pl.multiple_of(i * BLOCK, BLOCK), BLOCK)
        normed, factor = normalize(x_ref[rows, :].astype(F32))
        dn = dot_t(dqkv_scr[rows, :], weight(w_ref, 0, 3 * width))
        ggs[0, 0:1, :] += jnp.sum(dn * normed, axis=0, keepdims=True)
        gt_ref[rows, :] += norm_back(dn * gain_one, normed, factor)

    stores = [loads.start(gt_ref, gt_hbm)]
    gains_copy = links.push(ggs.at[0], rg.at[0], core)
    reduce(3).step(1)
    reduce(2).step(2)
    reduce(1).step(3)
    reduce(0).step(4)
    gains_copy.wait()
    ggs[1] = ggs[0] + rg[0]
    gains_copy = links.push(ggs.at[1], rg.at[1], xpeer)

    def finish(side, last):
        group = slots // 2
        places = yback.shape[0] // 2

        @pl.loop(0, blocks)
        def _(i):
            rows = pl.ds(pl.multiple_of(i * BLOCK, BLOCK), BLOCK)
            pick = ((iota((BLOCK, group), 1) + side * group).astype(F32) == col_ref[rows, 0:1]).astype(BF16)
            got = dot(pick, yback[pl.ds(side * places, places)].reshape(group, width))
            value = h_ref[rows, :] + jax.nn.sigmoid(col_ref[rows, 1:2]) * got
            if last:
                ct_ref[rows, :] = value.astype(BF16)
            else:
                h_ref[rows, :] = value

    reduce(3).step(2)
    reduce(2).step(3)
    reduce(1).step(4)
    gains_copy.wait()
    ggs[2] = ggs[1] + rg[1]
    gains_copy = links.push(ggs.at[2], rg.at[2], ypeer)
    reduce(3).step(3)
    reduce(2).step(4)
    gains_copy.wait()
    ggs[3] = ggs[2] + rg[2]
    gain_copies = [links.push(ggs.at[3], rg.at[2 + k], device(across(z, k), y, x, c)) for k in (1, 2, 3)]
    for copy in y_near:
        copy.wait()
    finish(z // 2, False)
    for i in range(4):
        to_x(i).wait()
    gw_scr[...] = nsum[1].astype(F32) + near[x].astype(F32) + next_x[...].astype(F32)
    stores.append(loads.start(gw_scr, gw_out))
    reduce(3).step(4)
    for copy in gain_copies:
        copy.wait()
    share = width // 32
    mine = ((z * 2 + y) * 2 + x) * 2 + c
    take = (iota((width, 128), 0) == mine * share + iota((width, 128), 1)).astype(F32)
    gg_ref[...] = lax.dot_general(
        ggs[3] + rg[3] + rg[4] + rg[5],
        take,
        (((1,), (0,)), ((), ())),
        precision=lax.Precision.HIGHEST,
        preferred_element_type=F32,
    )[0:2, 0:share]
    for ph in range(4):
        kept = fin[ph, pl.ds(pl.multiple_of(c * 24, 8), 24), :]
        reduce(ph).four().wait()
        for owner, part in ((c, kept), (1 - c, q4[ph])):
            if ph == 0:
                owno_ref[:, pl.ds(pl.multiple_of(owner * half, 128), half)] = part
            else:
                for j in range(3):
                    at = pl.multiple_of(j * width + (2 * (ph - 1) + owner) * 128, 128)
                    ownq_ref[:, pl.ds(at, 128)] = part[:, j * 128 : (j + 1) * 128]
    for copy in y_far:
        copy.wait()
    finish(1 - z // 2, True)
    stores.append(loads.start(ct_ref, out_hbm))
    for copy in stores:
        copy.wait()


def tail(returned, cols, rows, tokens_in, cotangent, hidden, qkv, context, stats, w_blocks, gains, y_rows, gw):
    tokens, width = tokens_in.shape
    slots = returned.shape[0]
    half = width // 2
    any_spec = pl.BlockSpec(memory_space=pl.ANY)
    vmem = pl.BlockSpec(memory_space=pltpu.VMEM)
    return pl.pallas_call(
        tail_kernel,
        out_shape=(
            jax.ShapeDtypeStruct((tokens, width), F32),
            jax.ShapeDtypeStruct(gw.shape[1:], F32),
            jax.ShapeDtypeStruct((tokens, width), BF16),
            jax.ShapeDtypeStruct((24, 3 * width), F32),
            jax.ShapeDtypeStruct((24, width), F32),
            jax.ShapeDtypeStruct((2, 24), F32),
        ),
        in_specs=[any_spec] * 9 + [vmem] * 4,
        out_specs=(any_spec, any_spec, any_spec, vmem, vmem, vmem),
        scratch_shapes=[
            pltpu.VMEM((slots, width), BF16),
            pltpu.VMEM((tokens, width), BF16),
            pltpu.VMEM((tokens, width), BF16),
            pltpu.VMEM((tokens, width), F32),
            pltpu.VMEM((tokens, 3 * width), BF16),
            pltpu.VMEM((tokens, width), BF16),
            pltpu.VMEM(w_blocks.shape, BF16),
            pltpu.VMEM((tokens, width), F32),
            pltpu.VMEM((tokens, width), BF16),
            pltpu.VMEM((tokens, width), BF16),
            pltpu.VMEM((tokens, 3 * width), BF16),
            pltpu.VMEM((width, tokens), BF16),
            pltpu.VMEM((16, tokens), F32),
            pltpu.VMEM((tokens, 128), F32),
            pltpu.VMEM((tokens, 128), F32),
            pltpu.VMEM((4, 2, 4, 2, 2, 48, half), BF16),
            pltpu.VMEM((4, 4, 2, 2, 48, half), BF16),
            pltpu.VMEM((4, 4, 2, 48, half), BF16),
            pltpu.VMEM((4, 4, 48, half), BF16),
            pltpu.VMEM((4, 3, 48, half), BF16),
            pltpu.VMEM((4, 48, half), F32),
            pltpu.VMEM((4, 24, half), F32),
            pltpu.VMEM((4, 8, width), F32),
            pltpu.VMEM((6, 8, width), F32),
            pltpu.VMEM((2,) + gw.shape[1:], BF16),
            pltpu.VMEM(gw.shape[1:], BF16),
            pltpu.VMEM((2,) + gw.shape[1:], BF16),
            pltpu.VMEM(y_rows.shape, BF16),
            pltpu.VMEM(gw.shape[1:], F32),
            pltpu.SemaphoreType.DMA((20,)),
            pltpu.SemaphoreType.DMA((20,)),
            pltpu.SemaphoreType.DMA((28,)),
            pltpu.SemaphoreType.DMA((28,)),
            pltpu.SemaphoreType.DMA((16,)),
        ],
        compiler_params=pltpu.CompilerParams(vmem_limit_bytes=62 << 20, collective_id=2, has_side_effects=True),
        cost_estimate=pl.CostEstimate(flops=80 << 30, bytes_accessed=40 << 20, transcendentals=0),
    )(returned, tokens_in, cotangent, hidden, qkv, context, w_blocks, y_rows, gw, cols, rows, stats, gains)


def flipped(z, y, k):
    hi, lo = z // 2, lax.rem(z, 2)
    zz = lax.rem(hi + k // 4, 2) * 2 + lax.rem(lo + lax.rem(k // 2, 2), 2)
    return zz, lax.rem(y + lax.rem(k, 2), 2)


def swap_kernel(
    act_hbm,
    dy_hbm,
    win_hbm,
    whid_hbm,
    own_in_hbm,
    own_hid_hbm,
    ret_hbm,
    y_hbm,
    gin_hbm,
    ghid_hbm,
    a_ref,
    dy_ref,
    win_ref,
    whid_ref,
    g_ref,
    du_ref,
    da_ref,
    us,
    gs,
    stage,
    near,
    next_x,
    send_sems,
    recv_sems,
    load_sems,
):
    z, y, x, c = place()
    me = z * 2 + y
    me_n = x * 2 + c
    count, cap, width = a_ref.shape
    parts = win_ref.shape[0]
    wide = win_ref.shape[2]
    loads = Loads(load_sems)
    first = [
        loads.start(a, b)
        for a, b in (
            (act_hbm.at[me], a_ref.at[me]),
            (own_in_hbm, win_ref.at[me_n]),
            (own_hid_hbm, whid_ref.at[me_n]),
            (dy_hbm, dy_ref),
        )
    ]
    for i in range(1, parts):
        n = lax.rem(me_n + i, parts)
        first += [loads.start(win_hbm.at[n], win_ref.at[n]), loads.start(whid_hbm.at[n], whid_ref.at[n])]

    def partner(k):
        zz, yy = flipped(z, y, k)
        return zz * 2 + yy, device(zz, yy, x, c)

    def outward(k):
        e, to = partner(k)
        return pltpu.make_async_remote_copy(
            src_ref=act_hbm.at[e],
            dst_ref=a_ref.at[me],
            send_sem=send_sems.at[k],
            recv_sem=recv_sems.at[k],
            device_id=to,
            device_id_type=MESH,
        )

    def homeward(k):
        e, to = partner(k)
        return pltpu.make_async_remote_copy(
            src_ref=da_ref.at[e],
            dst_ref=ret_hbm.at[me],
            send_sem=send_sems.at[8 + k],
            recv_sem=recv_sems.at[8 + k],
            device_id=to,
            device_id_type=MESH,
        )

    core, xpeer = device(z, y, x, 1 - c), device(z, y, 1 - x, c)
    greet([partner(k)[1] for k in range(1, 8)] + [core, xpeer])
    for k in FLIPS:
        outward(k).start()
    for copy in first:
        copy.wait()

    @pl.loop(0, count)
    def _(k):
        @pl.when(k > 0)
        def _():
            outward(k).wait_recv()

        e, _to = partner(k)
        a = a_ref[e]
        dy = dy_ref[e]
        rows = pl.ds(pl.multiple_of(e * cap, cap), cap)

        def enter(j):
            us[j % 2] = dot(a, win_ref[j])
            gs[j % 2] = dot_t(dy, whid_ref[j])

        def bend(j):
            g, slope = gelu_pair(us[j % 2])
            g_ref[rows, j * wide : (j + 1) * wide] = g.astype(BF16)
            du_ref[rows, j * wide : (j + 1) * wide] = (gs[j % 2] * slope).astype(BF16)

        def leave(j):
            return dot_t(du_ref[rows, j * wide : (j + 1) * wide], win_ref[j])

        enter(0)
        total = None
        for j in range(parts):
            if j + 1 < parts:
                enter(j + 1)
            bend(j)
            if j > 0:
                term = leave(j - 1)
                total = term if total is None else total + term
        da_ref[e] = (total + leave(parts - 1)).astype(BF16)

        @pl.when(k > 0)
        def _():
            homeward(k).start()

    own = loads.start(da_ref.at[me], ret_hbm.at[me])

    def put(i, out):
        return pltpu.make_async_copy(stage.at[i], out, load_sems.at[16 + i])

    def third(i, src, dst, to):
        return pltpu.make_async_remote_copy(
            src_ref=src,
            dst_ref=dst,
            send_sem=send_sems.at[16 + i],
            recv_sem=recv_sems.at[16 + i],
            device_id=to,
            device_id_type=MESH,
        )

    acts = a_ref[...].reshape(count * cap, width)

    @pl.loop(0, parts)
    def _(j):
        cols = pl.ds(pl.multiple_of(j * wide, wide), wide)
        win_ref[j] = t_dot(acts, du_ref[:, cols]).astype(BF16)

    to_core = [third(xx, win_ref.at[xx * 2 + 1 - c], near.at[xx], core) for xx in range(2)]
    for copy in to_core:
        copy.start()

    @pl.loop(0, parts // 2)
    def _(jj):
        for i in range(2):
            j = 2 * jj + i
            cols = pl.ds(pl.multiple_of(j * wide, wide), wide)

            @pl.when(jj >= 1)
            def _():
                put(i, ghid_hbm.at[j - 2]).wait()

            stage[i] = t_dot(g_ref[:, cols], dy_ref[...].reshape(count * cap, width)).astype(BF16)
            put(i, ghid_hbm.at[j]).start()

    for copy in to_core:
        copy.wait()
    other = (1 - x) * 2 + c
    win_ref[other] = (win_ref[other].astype(F32) + near[1 - x].astype(F32)).astype(BF16)
    to_x = third(2, win_ref.at[other], next_x, xpeer)
    to_x.start()

    @pl.loop(0, count)
    def _(i):
        rows = pl.ds(pl.multiple_of(i * cap, cap), cap)
        a_ref[i] = dot(g_ref[rows, :], whid_ref[...].reshape(parts * wide, width)).astype(BF16)

    out = loads.start(a_ref, y_hbm)
    for i in range(2):
        put(i, ghid_hbm.at[parts - 2 + i]).wait()
    to_x.wait()
    tiles = []
    for i, tile in enumerate((us.at[0], us.at[1], gs.at[0])):
        rows = pl.ds(i * cap, cap)
        tile[...] = win_ref[me_n, rows].astype(F32) + near[x, rows].astype(F32) + next_x[rows].astype(F32)
        tiles.append(loads.start(tile, gin_hbm.at[rows]))
    for k in range(1, 8):
        outward(k).wait_send()
        homeward(k).wait()
    for copy in tiles + [own, out]:
        copy.wait()


def swap(act_slots, dy_rows, w_in, w_hid, own_in, own_hid):
    count, cap, width = act_slots.shape
    parts, _, wide = w_in.shape
    hidden = parts * wide
    any_spec = pl.BlockSpec(memory_space=pl.ANY)
    return pl.pallas_call(
        swap_kernel,
        out_shape=(
            jax.ShapeDtypeStruct((count, cap, width), BF16),
            jax.ShapeDtypeStruct((count, cap, width), BF16),
            jax.ShapeDtypeStruct((width, wide), F32),
            jax.ShapeDtypeStruct((parts, wide, width), BF16),
        ),
        in_specs=[any_spec] * 6,
        out_specs=(any_spec,) * 4,
        scratch_shapes=[
            pltpu.VMEM((count, cap, width), BF16),
            pltpu.VMEM((count, cap, width), BF16),
            pltpu.VMEM(w_in.shape, BF16),
            pltpu.VMEM(w_hid.shape, BF16),
            pltpu.VMEM((count * cap, hidden), BF16),
            pltpu.VMEM((count * cap, hidden), BF16),
            pltpu.VMEM((count, cap, width), BF16),
            pltpu.VMEM((2, cap, wide), F32),
            pltpu.VMEM((2, cap, wide), F32),
            pltpu.VMEM((2, width, wide), BF16),
            pltpu.VMEM((2, width, wide), BF16),
            pltpu.VMEM((width, wide), BF16),
            pltpu.SemaphoreType.DMA((20,)),
            pltpu.SemaphoreType.DMA((20,)),
            pltpu.SemaphoreType.DMA((18,)),
        ],
        compiler_params=pltpu.CompilerParams(vmem_limit_bytes=62 << 20, collective_id=1, has_side_effects=True),
        cost_estimate=pl.CostEstimate(flops=100 << 30, bytes_accessed=60 << 20, transcendentals=0),
    )(act_slots, dy_rows, w_in, w_hid, own_in, own_hid)


def local(tokens, segments, routes, gate_logit, w_qkv, w_out, norm_gains, w_in, w_hid, cotangent):
    tok_count, width = tokens.shape
    n_expert = lax.axis_size("expert")
    n_narrow = lax.axis_size("narrow")
    capacity = 2 * tok_count // n_expert
    slot_rows = n_expert * capacity
    everyone = ("expert", "narrow")

    if n_expert == 8 and n_narrow == 4:
        listed = jnp.concatenate(
            (
                routes.reshape(1, tok_count).astype(F32),
                gate_logit.reshape(1, tok_count),
                segments.reshape(1, tok_count).astype(F32),
                jnp.zeros((5, tok_count), F32),
            )
        )
        qkv, context, hidden, act_slots, w_blocks, dy_rows, w_in_all, w_hid_all, stats, cols, gains = head(
            tokens, cotangent, w_in[0], w_hid[0], listed, w_qkv, w_out, norm_gains, n_expert, capacity
        )
        da_back, y_rows, gin_own, ghid = swap(act_slots, dy_rows, w_in_all, w_hid_all, w_in[0], w_hid[0])
        grad_tokens, ghid_own, block_out, own_qkv, own_out, own_gains = tail(
            da_back.reshape(slot_rows, width),
            cols,
            listed,
            tokens,
            cotangent,
            hidden,
            qkv,
            context,
            stats,
            w_blocks,
            gains,
            y_rows,
            ghid,
        )
        return (
            block_out,
            grad_tokens,
            own_qkv,
            own_out,
            own_gains,
            gin_own[None],
            ghid_own[None],
        )
    gain_cols = jnp.pad(norm_gains.T, ((0, 0), (0, 126)))
    w_all = lax.all_gather(
        jnp.concatenate((w_qkv, w_out, gain_cols), axis=1), everyone, axis=0, tiled=True
    )
    gains = w_all[:, 4 * width : 4 * width + 2].T.astype(F32)
    w_in_all = lax.all_gather(w_in[0], "narrow", axis=0, tiled=False)
    w_hid_all = lax.all_gather(w_hid[0], "narrow", axis=0, tiled=False)

    def exchange(values):
        return lax.all_to_all(
            values.reshape(n_expert, capacity, width), "expert", split_axis=0, concat_axis=0, tiled=True
        ).reshape(slot_rows, width)

    segr = segments.reshape(1, tok_count)
    segc = segments.reshape(tok_count, 1)
    srow, scol, dy_slots = prep(routes, gate_logit, cotangent, n_expert, capacity)
    dy_rows = exchange(dy_slots)
    qkv, context, stats, hidden, act_slots = attend_fwd(tokens, w_all, gains, segr, segc, srow, slot_rows)
    act_rows = exchange(act_slots)
    activated, grad_pre, da_rows = experts(act_rows, dy_rows, w_in_all, w_hid_all)
    da_back = exchange(da_rows)
    hidden_units = activated.shape[1]
    y_rows = dot(activated, w_hid_all.reshape(hidden_units, width)).astype(BF16)
    grad_hid = t_dot(activated, dy_rows).astype(BF16)
    grad_in = lax.dot_general(
        act_rows, grad_pre.reshape(slot_rows, n_narrow, -1), (((0,), (0,)), ((), ())), preferred_element_type=F32
    ).astype(BF16)
    y_back = exchange(y_rows)
    grad_tokens, grad_w, grad_gains = attend_bwd(
        da_back, scol, tokens, cotangent, hidden, qkv, context, stats, w_all, gains, segr, segc
    )
    block_out = block_output(y_back, scol, hidden, gate_logit)
    grad_hid_w = lax.psum_scatter(grad_hid, "narrow", scatter_dimension=0, tiled=True).astype(F32)[None]
    grad_in_w = lax.psum_scatter(grad_in, "narrow", scatter_dimension=1, tiled=True).astype(F32)
    grad_in_w = grad_in_w.reshape(1, width, -1)
    packed = jnp.concatenate((grad_w, jnp.pad(grad_gains[:2].T, ((0, 0), (0, 126)))), axis=1)
    own = lax.psum_scatter(packed, everyone, scatter_dimension=0, tiled=True)
    return (
        block_out,
        grad_tokens,
        own[:, : 3 * width],
        own[:, 3 * width : 4 * width],
        own[:, 4 * width : 4 * width + 2].T,
        grad_in_w,
        grad_hid_w,
    )


def solution(mesh):
    placed = (
        P(("expert", "narrow"), None),
        P(("expert", "narrow"), None),
        P(("expert", "narrow"), None),
        P(("expert", "narrow")),
        P(("expert", "narrow"), None),
        P(("expert", "narrow"), None),
        P(None, ("expert", "narrow")),
        P("expert", None, "narrow"),
        P("expert", "narrow", None),
        P(("expert", "narrow"), None),
    )
    return jax.shard_map(
        local,
        mesh=mesh,
        in_specs=placed,
        out_specs=(
            P(("expert", "narrow"), None),
            P(("expert", "narrow"), None),
            P(("expert", "narrow"), None),
            P(("expert", "narrow"), None),
            P(None, ("expert", "narrow")),
            P("expert", None, "narrow"),
            P("expert", "narrow", None),
        ),
        check_vma=False,
    )
```

```python
import functools

import jax
import jax.numpy as jnp
from jax import lax
from jax.experimental import pallas as pl
from jax.experimental.pallas import tpu as pltpu
from jax.sharding import PartitionSpec as P

HEAD_DIM = 64
SEQ = 1024
BLOCK = 256
LOOKBACK = 2
EPSILON = 1e-05
BIG_NEGATIVE = -1e30
F32 = jnp.float32
BF16 = jnp.bfloat16

TAIL_P = 0.3
TAIL_C = (
    0.11962923306946524,
    0.12075497050525577,
    0.0999071263144056,
    0.12858273368127124,
    -0.053723704944995426,
    0.20639718480180155,
    -0.1572285075725372,
    0.03568089149479804,
)


def dot(a, b):
    return lax.dot_general(a, b, (((1,), (0,)), ((), ())), preferred_element_type=F32)


def dot_t(a, b):
    return lax.dot_general(a, b, (((1,), (1,)), ((), ())), preferred_element_type=F32)


def t_dot(a, b):
    return lax.dot_general(a, b, (((0,), (0,)), ((), ())), preferred_element_type=F32)


def normalize(values):
    centre = jnp.mean(values, axis=-1, keepdims=True)
    shifted = values - centre
    factor = lax.rsqrt(jnp.mean(shifted * shifted, axis=-1, keepdims=True) + EPSILON)
    return shifted * factor, factor


def norm_back(grad_normed, normed, factor):
    return factor * (
        grad_normed
        - jnp.mean(grad_normed, axis=-1, keepdims=True)
        - normed * jnp.mean(grad_normed * normed, axis=-1, keepdims=True)
    )


def gelu_pair(u):
    size = jnp.abs(u)
    t = 1.0 / (1.0 + TAIL_P * size)
    poly = jnp.full_like(t, TAIL_C[-1])
    for c in TAIL_C[-2::-1]:
        poly = poly * t + c
    bell = jnp.exp(-0.5 * (u * u))
    tail = poly * t * bell
    phi = jnp.where(u >= 0, 1.0 - tail, tail)
    return u * phi, phi + u * (bell * 0.3989422804014327)


def iota(shape, dim):
    return lax.broadcasted_iota(jnp.int32, shape, dim)


def prep_kernel(capacity, experts, rrow_ref, rcol_ref, gate_ref, ct_ref, srow_ref, scol_ref, send_ref):
    tokens = ct_ref.shape[0]
    wide = max(8, experts)
    hot = (iota((wide, tokens), 0) == rrow_ref[...]).astype(F32)
    before = (iota((tokens, tokens), 0) < iota((tokens, tokens), 1)).astype(BF16)
    rank = dot(hot.astype(BF16), before)
    base = (iota((wide, tokens), 0) * capacity).astype(F32)
    srow = jnp.sum(hot * (rank + base), axis=0, keepdims=True)
    srow_ref[...] = jnp.broadcast_to(srow, srow_ref.shape)
    hot_c = (iota((tokens, 128), 1) == rcol_ref[...]).astype(F32)
    after = (iota((tokens, tokens), 1) < iota((tokens, tokens), 0)).astype(BF16)
    rank_c = dot(after, hot_c.astype(BF16))
    base_c = (iota((tokens, 128), 1) * capacity).astype(F32)
    scol_ref[...] = jnp.sum(hot_c * (rank_c + base_c), axis=1, keepdims=True)
    gated = (jax.nn.sigmoid(gate_ref[...]) * ct_ref[...].astype(F32)).astype(BF16)
    fill_slots(srow, gated, send_ref)


def fill_slots(srow, values, send_ref):
    rows = send_ref.shape[0]
    tokens = values.shape[0]

    @pl.loop(0, rows // BLOCK)
    def _(i):
        first = i * BLOCK
        ids = (iota((BLOCK, tokens), 0) + first).astype(F32)
        pick = (ids == srow).astype(BF16)
        send_ref[pl.ds(pl.multiple_of(first, BLOCK), BLOCK), :] = dot(pick, values).astype(BF16)


def prep(routes, gate_logit, cotangent, experts, capacity):
    tokens, width = cotangent.shape
    return pl.pallas_call(
        functools.partial(prep_kernel, capacity, experts),
        out_shape=(
            jax.ShapeDtypeStruct((8, tokens), F32),
            jax.ShapeDtypeStruct((tokens, 1), F32),
            jax.ShapeDtypeStruct((experts * capacity, width), BF16),
        ),
        compiler_params=pltpu.CompilerParams(vmem_limit_bytes=56 << 20),
        cost_estimate=pl.CostEstimate(flops=8 << 30, bytes_accessed=8 << 20, transcendentals=0),
    )(routes.reshape(1, tokens), routes, gate_logit.reshape(tokens, 1), cotangent)


def fwd_kernel(
    x_ref, w_ref, gain_ref, segr_ref, segc_ref, srow_ref, qkv_ref, c_ref, stat_ref, h_ref, send_ref, act_scr, bias_scr, col_scr
):
    tokens, width = x_ref.shape
    blocks = tokens // BLOCK
    pairs = width // 128
    gain_one = gain_ref[0:1, :]
    gain_two = gain_ref[1:2, :]

    @pl.loop(0, blocks)
    def _(i):
        rows = pl.ds(pl.multiple_of(i * BLOCK, BLOCK), BLOCK)
        normed, _f = normalize(x_ref[rows, :].astype(F32))
        act = (normed * gain_one).astype(BF16)
        qkv_ref[rows, :] = dot(act, w_ref[:, : 3 * width]).astype(BF16)

    col_scr[...] = jnp.zeros_like(col_scr)
    low = iota((BLOCK, 128), 1) < HEAD_DIM
    for qb in range(blocks):
        kb = max(0, qb - LOOKBACK)
        span = (qb - kb + 1) * BLOCK
        rows = pl.ds(qb * BLOCK, BLOCK)
        keys = pl.ds(kb * BLOCK, span)
        q_pos = iota((BLOCK, span), 0) + qb * BLOCK
        k_pos = iota((BLOCK, span), 1) + kb * BLOCK
        ok = (k_pos <= q_pos) & (segc_ref[rows, :] == segr_ref[0:1, keys])
        bias_scr[:, :span] = jnp.where(ok, 0.0, BIG_NEGATIVE)

        @pl.loop(0, pairs)
        def _(hp):
            at = pl.multiple_of(hp * 128, 128)
            q = qkv_ref[rows, pl.ds(at, 128)] * jnp.asarray(HEAD_DIM**-0.5, BF16)
            k = qkv_ref[keys, pl.ds(width + at, 128)]
            v = qkv_ref[keys, pl.ds(2 * width + at, 128)]
            outs = []
            col = col_scr[rows, :]
            for half in range(2):
                mine = low if half == 0 else ~low
                s = dot_t(jnp.where(mine, q, 0), k) + bias_scr[:, :span]
                top = jnp.max(s, axis=1, keepdims=True)
                raised = jnp.exp(s - top)
                total = jnp.sum(raised, axis=1, keepdims=True)
                outs.append(dot((raised * (1.0 / total)).astype(BF16), v))
                col = jnp.where(iota((BLOCK, 128), 1) == 2 * hp + half, top + jnp.log(total), col)
            col_scr[rows, :] = col
            c_ref[rows, pl.ds(at, 128)] = jnp.where(low, outs[0], outs[1]).astype(BF16)

    stat_ref[...] = col_scr[...].T

    @pl.loop(0, blocks)
    def _(i):
        rows = pl.ds(pl.multiple_of(i * BLOCK, BLOCK), BLOCK)
        hidden = x_ref[rows, :].astype(F32) + dot(c_ref[rows, :], w_ref[:, 3 * width : 4 * width])
        h_ref[rows, :] = hidden
        normed, _f = normalize(hidden)
        act_scr[rows, :] = (normed * gain_two).astype(BF16)

    fill_slots(srow_ref[0:1, :], act_scr[...], send_ref)


def attend_fwd(tokens_in, w_all, gains, segr, segc, srow, slot_rows):
    tokens, width = tokens_in.shape
    return pl.pallas_call(
        fwd_kernel,
        out_shape=(
            jax.ShapeDtypeStruct((tokens, 3 * width), BF16),
            jax.ShapeDtypeStruct((tokens, width), BF16),
            jax.ShapeDtypeStruct((128, tokens), F32),
            jax.ShapeDtypeStruct((tokens, width), F32),
            jax.ShapeDtypeStruct((slot_rows, width), BF16),
        ),
        scratch_shapes=[
            pltpu.VMEM((tokens, width), BF16),
            pltpu.VMEM((BLOCK, (LOOKBACK + 1) * BLOCK), F32),
            pltpu.VMEM((tokens, 128), F32),
        ],
        compiler_params=pltpu.CompilerParams(vmem_limit_bytes=56 << 20),
        cost_estimate=pl.CostEstimate(flops=40 << 30, bytes_accessed=24 << 20, transcendentals=0),
    )(tokens_in, w_all, gains, segr, segc, srow)


def expert_kernel(a_ref, dy_ref, win_ref, whid_ref, g_ref, du_ref, da_ref, acc_scr):
    a = a_ref[...]
    dy = dy_ref[...]
    parts = win_ref.shape[0]
    wide = win_ref.shape[2]
    acc_scr[...] = jnp.zeros_like(acc_scr)

    @pl.loop(0, parts)
    def _(j):
        cols = pl.ds(pl.multiple_of(j * wide, wide), wide)
        u = dot(a, win_ref[j])
        grad = dot_t(dy, whid_ref[j])
        g, slope = gelu_pair(u)
        g_ref[:, cols] = g.astype(BF16)
        du = (grad * slope).astype(BF16)
        du_ref[:, cols] = du
        acc_scr[...] += dot_t(du, win_ref[j])

    da_ref[...] = acc_scr[...].astype(BF16)


def experts(acts, grads, w_in, w_hid):
    rows, width = acts.shape
    parts, _, wide = w_in.shape
    hidden = parts * wide
    row_spec = pl.BlockSpec((BLOCK, width), lambda i: (i, 0))
    wide_spec = pl.BlockSpec((BLOCK, hidden), lambda i: (i, 0))
    return pl.pallas_call(
        expert_kernel,
        grid=(rows // BLOCK,),
        out_shape=(
            jax.ShapeDtypeStruct((rows, hidden), BF16),
            jax.ShapeDtypeStruct((rows, hidden), BF16),
            jax.ShapeDtypeStruct((rows, width), BF16),
        ),
        in_specs=[
            row_spec,
            row_spec,
            pl.BlockSpec(w_in.shape, lambda i: (0, 0, 0), pipeline_mode=pl.Buffered(1)),
            pl.BlockSpec(w_hid.shape, lambda i: (0, 0, 0), pipeline_mode=pl.Buffered(1)),
        ],
        out_specs=(wide_spec, wide_spec, row_spec),
        scratch_shapes=[pltpu.VMEM((BLOCK, width), F32)],
        compiler_params=pltpu.CompilerParams(vmem_limit_bytes=56 << 20),
        cost_estimate=pl.CostEstimate(flops=60 << 30, bytes_accessed=40 << 20, transcendentals=0),
    )(acts, grads, w_in, w_hid)


def out_kernel(ret_ref, scol_ref, h_ref, gate_ref, out_ref):
    tokens, rows = out_ref.shape[0], ret_ref.shape[0]
    pick = (iota((tokens, rows), 1).astype(F32) == scol_ref[...]).astype(BF16)
    y = dot(pick, ret_ref[...])
    out_ref[...] = (h_ref[...] + jax.nn.sigmoid(gate_ref[...]) * y).astype(BF16)


def block_output(returned, scol, hidden, gate_logit):
    rows, width = returned.shape
    tokens = hidden.shape[0]
    tile = pl.BlockSpec((BLOCK, width), lambda i: (i, 0))
    column = pl.BlockSpec((BLOCK, 1), lambda i: (i, 0))
    return pl.pallas_call(
        out_kernel,
        grid=(tokens // BLOCK,),
        out_shape=jax.ShapeDtypeStruct((tokens, width), BF16),
        in_specs=[pl.BlockSpec((rows, width), lambda i: (0, 0)), column, tile, column],
        out_specs=tile,
        compiler_params=pltpu.CompilerParams(vmem_limit_bytes=40 << 20),
        cost_estimate=pl.CostEstimate(flops=4 << 30, bytes_accessed=10 << 20, transcendentals=0),
    )(returned, scol, hidden, gate_logit.reshape(tokens, 1))


def bwd_kernel(
    ret_ref,
    scol_ref,
    x_ref,
    ct_ref,
    h_ref,
    qkv_ref,
    c_ref,
    stat_ref,
    w_ref,
    gain_ref,
    segr_ref,
    segc_ref,
    gt_ref,
    gw_ref,
    gg_ref,
    dc_scr,
    dhb_scr,
    dqkv_scr,
    act_scr,
    d_scr,
    dk_scr,
    dv_scr,
):
    tokens, width = x_ref.shape
    slots = ret_ref.shape[0]
    blocks = tokens // BLOCK
    pairs = width // 128
    gain_one = gain_ref[0:1, :]
    gain_two = gain_ref[1:2, :]
    gg_ref[...] = jnp.zeros_like(gg_ref)
    member = (iota((16, width), 1) // HEAD_DIM == iota((16, width), 0)).astype(F32)

    for i in range(blocks):
        rows = pl.ds(i * BLOCK, BLOCK)
        pick = (iota((BLOCK, slots), 1).astype(F32) == scol_ref[rows, :]).astype(BF16)
        da = dot(pick, ret_ref[...])
        normed, factor = normalize(h_ref[rows, :])
        gg_ref[1:2, :] += jnp.sum(da * normed, axis=0, keepdims=True)
        dh = ct_ref[rows, :].astype(F32) + norm_back(da * gain_two, normed, factor)
        gt_ref[rows, :] = dh
        dhb = dh.astype(BF16)
        dhb_scr[rows, :] = dhb
        dc = dot_t(dhb, w_ref[:, 3 * width : 4 * width]).astype(BF16)
        dc_scr[rows, :] = dc
        d_scr[:, rows] = lax.dot_general(
            member,
            dc.astype(F32) * c_ref[rows, :].astype(F32),
            (((1,), (1,)), ((), ())),
            precision=lax.Precision.HIGHEST,
            preferred_element_type=F32,
        )

    gw_ref[:, 3 * width : 4 * width] = t_dot(c_ref[...], dhb_scr[...])
    low = iota((BLOCK, 128), 1) < HEAD_DIM
    scale = HEAD_DIM**-0.5

    @pl.loop(0, pairs)
    def _(hp):
        at = pl.multiple_of(hp * 128, 128)
        dk_scr[...] = jnp.zeros_like(dk_scr)
        dv_scr[...] = jnp.zeros_like(dv_scr)
        for qb in range(blocks):
            rows = pl.ds(qb * BLOCK, BLOCK)
            q = qkv_ref[rows, pl.ds(at, 128)] * jnp.asarray(scale, BF16)
            dc = dc_scr[rows, pl.ds(at, 128)]
            q_half = [jnp.where(low, q, 0), jnp.where(low, 0, q)]
            dc_half = [jnp.where(low, dc, 0), jnp.where(low, 0, dc)]
            dq = jnp.zeros((BLOCK, 128), F32)
            for kb in range(max(0, qb - LOOKBACK), qb + 1):
                keys = pl.ds(kb * BLOCK, BLOCK)
                k = qkv_ref[keys, pl.ds(width + at, 128)]
                v = qkv_ref[keys, pl.ds(2 * width + at, 128)]
                ok = segc_ref[keys, :] == segr_ref[0:1, rows]
                if kb == qb:
                    ok = ok & (iota((BLOCK, BLOCK), 0) <= iota((BLOCK, BLOCK), 1))
                ps, dss = [], []
                for half in range(2):
                    s = dot_t(k, q_half[half])
                    p = jnp.where(ok, jnp.exp(s - stat_ref[pl.ds(2 * hp + half, 1), rows]), 0.0)
                    dp = dot_t(v, dc_half[half])
                    dss.append((p * (dp - d_scr[pl.ds(2 * hp + half, 1), rows])).astype(BF16))
                    ps.append(p.astype(BF16))
                dv_scr[keys, :] += dot(jnp.concatenate(ps, 1), jnp.concatenate(dc_half, 0))
                dk_scr[keys, :] += dot(jnp.concatenate(dss, 1), jnp.concatenate(q_half, 0))
                dq += jnp.where(low, t_dot(dss[0], k), t_dot(dss[1], k))
            dqkv_scr[rows, pl.ds(at, 128)] = (dq * scale).astype(BF16)
        dqkv_scr[:, pl.ds(width + at, 128)] = dk_scr[...].astype(BF16)
        dqkv_scr[:, pl.ds(2 * width + at, 128)] = dv_scr[...].astype(BF16)

    @pl.loop(0, blocks)
    def _(i):
        rows = pl.ds(pl.multiple_of(i * BLOCK, BLOCK), BLOCK)
        normed, factor = normalize(x_ref[rows, :].astype(F32))
        act_scr[rows, :] = (normed * gain_one).astype(BF16)
        dn = dot_t(dqkv_scr[rows, :], w_ref[:, : 3 * width])
        gg_ref[0:1, :] += jnp.sum(dn * normed, axis=0, keepdims=True)
        gt_ref[rows, :] += norm_back(dn * gain_one, normed, factor)

    gw_ref[:, : 3 * width] = t_dot(act_scr[...], dqkv_scr[...])


def attend_bwd(returned, scol, tokens_in, cotangent, hidden, qkv, context, stats, w_all, gains, segr, segc):
    tokens, width = tokens_in.shape
    return pl.pallas_call(
        bwd_kernel,
        out_shape=(
            jax.ShapeDtypeStruct((tokens, width), F32),
            jax.ShapeDtypeStruct((width, 4 * width), F32),
            jax.ShapeDtypeStruct((8, width), F32),
        ),
        scratch_shapes=[
            pltpu.VMEM((tokens, width), BF16),
            pltpu.VMEM((tokens, width), BF16),
            pltpu.VMEM((tokens, 3 * width), BF16),
            pltpu.VMEM((tokens, width), BF16),
            pltpu.VMEM((16, tokens), F32),
            pltpu.VMEM((tokens, 128), F32),
            pltpu.VMEM((tokens, 128), F32),
        ],
        compiler_params=pltpu.CompilerParams(vmem_limit_bytes=60 << 20),
        cost_estimate=pl.CostEstimate(flops=80 << 30, bytes_accessed=40 << 20, transcendentals=0),
    )(returned, scol, tokens_in, cotangent, hidden, qkv, context, stats, w_all, gains, segr, segc)


MESH = pl.DeviceIdType.MESH


def place():
    e, n = lax.axis_index("expert"), lax.axis_index("narrow")
    return e // 2, lax.rem(e, 2), n // 2, lax.rem(n, 2)


def device(z, y, x, c):
    return (z * 2 + y, x * 2 + c)


def across(z, k):
    hi, lo = z // 2, lax.rem(z, 2)
    hi = 1 - hi if k & 2 else hi
    lo = 1 - lo if k & 1 else lo
    return hi * 2 + lo


class Links:
    def __init__(self, send, recv):
        self.send, self.recv, self.used = send, recv, 0

    def make(self, src, dst, to):
        i = self.used
        self.used += 1
        return pltpu.make_async_remote_copy(
            src_ref=src, dst_ref=dst, send_sem=self.send.at[i], recv_sem=self.recv.at[i], device_id=to, device_id_type=MESH
        )

    def push(self, src, dst, to):
        copy = self.make(src, dst, to)
        copy.start()
        return copy


class Loads:
    def __init__(self, sems):
        self.sems, self.used = sems, 0

    def start(self, src, dst):
        copy = pltpu.make_async_copy(src, dst, self.sems.at[self.used])
        self.used += 1
        copy.start()
        return copy


def greet(peers):
    barrier = pltpu.get_barrier_semaphore()
    for peer in peers:
        pl.semaphore_signal(barrier, inc=1, device_id=peer, device_id_type=MESH)
    pl.semaphore_wait(barrier, len(peers))


FLIPS = (4, 2, 6, 1, 5, 3, 7)


def peers_of(z, y, x, c):
    return [device(across(z, k >> 1), 1 - y if k & 1 else y, x, c) for k in FLIPS]


def weight(ref, lo, hi):
    return ref[:, :, :, :, lo:hi].reshape(-1, hi - lo)


def head_kernel(
    capacity,
    experts,
    x_hbm,
    ct_hbm,
    win_hbm,
    whid_hbm,
    row_ref,
    wqkv_ref,
    wout_ref,
    gshard_ref,
    qkv_hbm,
    c_hbm,
    h_hbm,
    act_hbm,
    w_hbm,
    dyrow_hbm,
    win4_hbm,
    whid4_hbm,
    stat_ref,
    col_ref,
    gain_ref,
    x_ref,
    ct_ref,
    sh,
    st,
    square,
    wq,
    wg,
    qkv_ref,
    c_ref,
    h_ref,
    a_scr,
    act_ref,
    dy_ref,
    bias_scr,
    send_sems,
    recv_sems,
    load_sems,
):
    z, y, x, c = place()
    me_e = z * 2 + y
    me_n = x * 2 + c
    tokens, width = x_ref.shape
    blocks = tokens // BLOCK
    pairs = width // 128
    half = width // 2
    core, xpeer, ypeer = device(z, y, x, 1 - c), device(z, y, 1 - x, c), device(z, 1 - y, x, c)
    links = Links(send_sems, recv_sems)
    loads = Loads(load_sems)
    loading_ct = loads.start(ct_hbm, ct_ref)
    loading_x = loads.start(x_hbm, x_ref)

    square[...] = jnp.zeros_like(square)
    square[0:2, 0 : gshard_ref.shape[1]] = gshard_ref[...].astype(F32)
    gain_cols = square[...].T
    for side in range(2):
        for j in range(4):
            src, at = (wqkv_ref, j * width) if j < 3 else (wout_ref, 0)
            sh[side, :, j * half : (j + 1) * half] = src[:, at + side * half : at + (side + 1) * half].astype(F32)
        sh[side, :, 4 * half :] = gain_cols[0 : gshard_ref.shape[1], :]
    st[c] = sh[c]

    greet(peers_of(z, y, x, c) + [core, xpeer])
    zero = links.push(sh.at[1 - c], st.at[c], core)

    deep = width // 2
    upper, lower = pl.ds(0, deep), pl.ds(deep, deep)

    def hand(src, dst, rows):
        return links.push(src.at[rows], dst.at[me_n, rows], xpeer)

    def onward(dst, rows):
        part = dst.at[(1 - x) * 2 + c, rows]
        return links.push(part, part, core)

    parts = [(hand(win_hbm, win4_hbm, upper), win4_hbm, upper)]

    def cols(j):
        return pl.ds(pl.multiple_of((2 * j + c) * half, 128), half)

    zero.wait()
    rows48 = jnp.concatenate((st[0], st[1]), axis=0)
    for j in range(4):
        wq[z, y, x, :, cols(j)] = rows48[:, j * half : (j + 1) * half].astype(BF16)
    wg[z, y, x] = rows48[:, 4 * half :].astype(BF16)
    ring_z = []
    for piece in range(2):
        group = []
        for k in (1, 2, 3):
            to = device(across(z, k), y, x, c)
            for j in (2 * piece, 2 * piece + 1):
                part = wq.at[z, y, x, :, cols(j)]
                group.append(links.push(part, part, to))
            if piece == 0:
                group.append(links.push(wg.at[z, y, x], wg.at[z, y, x], to))
        ring_z.append(group)

    wide = max(8, experts)
    hot = (iota((wide, tokens), 0).astype(F32) == row_ref[0:1, :]).astype(F32)
    before = (iota((tokens, tokens), 0) < iota((tokens, tokens), 1)).astype(BF16)
    rank = dot(hot.astype(BF16), before)
    base = (iota((wide, tokens), 0) * capacity).astype(F32)
    srow = jnp.sum(hot * (rank + base), axis=0, keepdims=True)

    listed = row_ref[...].T
    hot_c = (iota((tokens, 128), 1).astype(F32) == listed[:, 0:1]).astype(F32)
    after = (iota((tokens, tokens), 1) < iota((tokens, tokens), 0)).astype(BF16)
    rank_c = dot(after, hot_c.astype(BF16))
    base_c = (iota((tokens, 128), 1) * capacity).astype(F32)
    scol = jnp.sum(hot_c * (rank_c + base_c), axis=1, keepdims=True)
    col_ref[...] = jnp.where(iota(listed.shape, 1) == 0, scol, listed)

    def fill(values, out):
        @pl.loop(0, out.shape[0])
        def _(i):
            ids = (iota((capacity, tokens), 0) + i * capacity).astype(F32)
            out[i] = dot((ids == srow).astype(BF16), values).astype(BF16)

    loading_ct.wait()
    fill((jax.nn.sigmoid(listed[:, 1:2]) * ct_ref[...].astype(F32)).astype(BF16), dy_ref)

    ring_2 = []
    for piece in range(2):
        for copy in ring_z[piece]:
            copy.wait()
        ca, cb = cols(2 * piece), cols(2 * piece + 1)
        group = [
            links.push(wq.at[:, y, x, :, ca], wq.at[:, y, x, :, ca], ypeer),
            links.push(wq.at[:, y, x, :, cb], wq.at[:, y, x, :, cb], xpeer),
        ]
        if piece == 0:
            group.append(links.push(wg.at[:, y, x], wg.at[:, y, x], ypeer))
        ring_2.append(group)
    dy_copies = []
    for k in FLIPS:
        zz, yy = across(z, k >> 1), (1 - y if k & 1 else y)
        dy_copies.append(links.push(dy_ref.at[zz * 2 + yy], dyrow_hbm.at[me_e], device(zz, yy, x, c)))
    own_dy = loads.start(dy_ref.at[me_e], dyrow_hbm.at[me_e])
    ring_3 = []
    for piece in range(2):
        for copy in ring_2[piece]:
            copy.wait()
        ca, cb = cols(2 * piece), cols(2 * piece + 1)
        group = [
            links.push(wq.at[:, :, x, :, ca], wq.at[:, :, x, :, ca], xpeer),
            links.push(wq.at[:, y, :, :, cb], wq.at[:, y, :, :, cb], ypeer),
        ]
        if piece == 0:
            group.append(links.push(wg.at[:, :, x], wg.at[:, :, x], xpeer))
        ring_3.append(group)
    for src, dst, rows in ((win_hbm, win4_hbm, lower), (whid_hbm, whid4_hbm, upper), (whid_hbm, whid4_hbm, lower)):
        parts.append((hand(src, dst, rows), dst, rows))
    ring_4 = []
    for piece in range(2):
        for copy in ring_3[piece]:
            copy.wait()
        ring_4.append([links.push(wq.at[:, :, :, :, cols(j)], wq.at[:, :, :, :, cols(j)], core) for j in (2 * piece, 2 * piece + 1)])

    gains = jnp.transpose(wg[...].reshape(width, 128).astype(F32))[0:8, :]
    gain_ref[...] = gains
    gain_one = gains[0:1, :]
    gain_two = gains[1:2, :]
    loading_x.wait()
    for piece in range(2):
        for copy in ring_4[piece]:
            copy.wait()
    storing = [loads.start(wq, w_hbm)]
    core_slices = [links.push(src, dst.at[me_n], core) for src, dst in ((win_hbm, win4_hbm), (whid_hbm, whid4_hbm))]

    def pass_on(i):
        copy, dst, rows = parts[i]
        copy.wait()
        core_slices.append(onward(dst, rows))

    pass_on(0)

    @pl.loop(0, blocks)
    def _(i):
        rows = pl.ds(pl.multiple_of(i * BLOCK, BLOCK), BLOCK)
        normed, _f = normalize(x_ref[rows, :].astype(F32))
        act = (normed * gain_one).astype(BF16)
        qkv_ref[rows, :] = dot(act, weight(wq, 0, 3 * width)).astype(BF16)

    storing.append(loads.start(qkv_ref, qkv_hbm))
    low = iota((BLOCK, 128), 1) < HEAD_DIM
    tiles = [(qb, kb) for qb in range(blocks) for kb in range(max(0, qb - LOOKBACK), qb + 1)]
    for n, (qb, kb) in enumerate(tiles):
        ok = col_ref[pl.ds(kb * BLOCK, BLOCK), 2:3] == row_ref[2:3, pl.ds(qb * BLOCK, BLOCK)]
        if kb == qb:
            ok = ok & (iota((BLOCK, BLOCK), 0) <= iota((BLOCK, BLOCK), 1))
        bias_scr[n] = jnp.where(ok, 0.0, BIG_NEGATIVE)

    @pl.loop(0, pairs)
    def _(hp):
        at = pl.multiple_of(hp * 128, 128)
        for qb in range(blocks):
            mine = [(n, kb) for n, (qq, kb) in enumerate(tiles) if qq == qb]
            rows = pl.ds(qb * BLOCK, BLOCK)
            q = qkv_ref[rows, pl.ds(at, 128)] * jnp.asarray(HEAD_DIM**-0.5, BF16)
            v = qkv_ref[pl.ds(mine[0][1] * BLOCK, len(mine) * BLOCK), pl.ds(2 * width + at, 128)]
            outs = []
            for side in range(2):
                q_half = jnp.where(low, q, 0) if side == 0 else jnp.where(low, 0, q)
                scores = [
                    dot_t(qkv_ref[pl.ds(kb * BLOCK, BLOCK), pl.ds(width + at, 128)], q_half) + bias_scr[n] for n, kb in mine
                ]
                top = functools.reduce(jnp.maximum, [jnp.max(s, axis=0, keepdims=True) for s in scores])
                raised = [jnp.exp(s - top) for s in scores]
                total = functools.reduce(jnp.add, [jnp.sum(r, axis=0, keepdims=True) for r in raised])
                share = 1.0 / total
                weights = jnp.concatenate([(r * share).astype(BF16) for r in raised], axis=0)
                outs.append(t_dot(weights, v))
                stat_ref[pl.ds(2 * hp + side, 1), rows] = top + jnp.log(total)
            c_ref[rows, pl.ds(at, 128)] = jnp.where(low, outs[0], outs[1]).astype(BF16)

    storing.append(loads.start(c_ref, c_hbm))

    @pl.loop(0, blocks)
    def _(i):
        rows = pl.ds(pl.multiple_of(i * BLOCK, BLOCK), BLOCK)
        hidden = x_ref[rows, :].astype(F32) + dot(c_ref[rows, :], weight(wq, 3 * width, 4 * width))
        h_ref[rows, :] = hidden
        normed, _f = normalize(hidden)
        a_scr[rows, :] = (normed * gain_two).astype(BF16)

    storing.append(loads.start(h_ref, h_hbm))
    fill(a_scr[...], act_ref)
    storing.append(loads.start(act_ref, act_hbm))
    for i in range(1, 4):
        pass_on(i)
    for copy in storing + [own_dy] + core_slices + dy_copies:
        copy.wait()


def head(tokens_in, cotangent, w_in, w_hid, listed, w_qkv, w_out, gain_shard, experts, capacity):
    tokens, width = tokens_in.shape
    any_spec = pl.BlockSpec(memory_space=pl.ANY)
    vmem = pl.BlockSpec(memory_space=pltpu.VMEM)
    slots = (experts, capacity, width)
    blocks = (4, 2, 2, 48, 4 * width)
    shard = (2, w_qkv.shape[0], 2 * width + 128)
    return pl.pallas_call(
        functools.partial(head_kernel, capacity, experts),
        out_shape=(
            jax.ShapeDtypeStruct((tokens, 3 * width), BF16),
            jax.ShapeDtypeStruct((tokens, width), BF16),
            jax.ShapeDtypeStruct((tokens, width), F32),
            jax.ShapeDtypeStruct(slots, BF16),
            jax.ShapeDtypeStruct(blocks, BF16),
            jax.ShapeDtypeStruct(slots, BF16),
            jax.ShapeDtypeStruct((4,) + w_in.shape, BF16),
            jax.ShapeDtypeStruct((4,) + w_hid.shape, BF16),
            jax.ShapeDtypeStruct((16, tokens), F32),
            jax.ShapeDtypeStruct((tokens, 8), F32),
            jax.ShapeDtypeStruct((8, width), F32),
        ),
        in_specs=[any_spec] * 4 + [vmem] * 4,
        out_specs=(any_spec,) * 8 + (vmem,) * 3,
        scratch_shapes=[
            pltpu.VMEM((tokens, width), BF16),
            pltpu.VMEM((tokens, width), BF16),
            pltpu.VMEM(shard, F32),
            pltpu.VMEM(shard, F32),
            pltpu.VMEM((128, 128), F32),
            pltpu.VMEM(blocks, BF16),
            pltpu.VMEM((4, 2, 2, 48, 128), BF16),
            pltpu.VMEM((tokens, 3 * width), BF16),
            pltpu.VMEM((tokens, width), BF16),
            pltpu.VMEM((tokens, width), F32),
            pltpu.VMEM((tokens, width), BF16),
            pltpu.VMEM(slots, BF16),
            pltpu.VMEM(slots, BF16),
            pltpu.VMEM((tokens // BLOCK * (LOOKBACK + 1), BLOCK, BLOCK), F32),
            pltpu.SemaphoreType.DMA((48,)),
            pltpu.SemaphoreType.DMA((48,)),
            pltpu.SemaphoreType.DMA((16,)),
        ],
        compiler_params=pltpu.CompilerParams(vmem_limit_bytes=62 << 20, collective_id=0, has_side_effects=True),
        cost_estimate=pl.CostEstimate(flops=60 << 30, bytes_accessed=40 << 20, transcendentals=0),
    )(tokens_in, cotangent, w_in, w_hid, listed, w_qkv, w_out, gain_shard)


class Reduce:
    def __init__(self, spot, ph, gq, rc, r1, r2, r3, fin, r4, send_sems, recv_sems):
        self.z, self.y, self.x, self.c = spot
        self.gq, self.rc, self.r1, self.r2, self.r3, self.fin, self.r4 = (
            gq.at[ph],
            rc.at[ph],
            r1.at[ph],
            r2.at[ph],
            r3.at[ph],
            fin.at[ph],
            r4.at[ph],
        )
        self.base = ph * 7
        self.send, self.recv = send_sems, recv_sems

    def copy(self, i, src, dst, to):
        return pltpu.make_async_remote_copy(
            src_ref=src,
            dst_ref=dst,
            send_sem=self.send.at[self.base + i],
            recv_sem=self.recv.at[self.base + i],
            device_id=to,
            device_id_type=MESH,
        )

    def turn(self, i):
        return i * (1 - self.c) + self.y * self.c, self.x * (1 - self.c) + i * self.c

    def add(self, where, term):
        self.gq[where] = (self.gq[where].astype(F32) + term.astype(F32)).astype(BF16)

    def cores(self):
        z, y, x, c = self.z, self.y, self.x, self.c
        return self.copy(0, self.gq.at[1 - c], self.rc, device(z, y, x, 1 - c))

    def by_core(self, go, first, second):
        @pl.when(self.c == 0)
        def _():
            go(first)

        @pl.when(self.c == 1)
        def _():
            go(second)

    def one(self, go):
        z, y, x, c = self.z, self.y, self.x, self.c
        self.by_core(
            go,
            self.copy(1, self.gq.at[0, :, :, 1 - x], self.r1, device(z, y, 1 - x, c)),
            self.copy(1, self.gq.at[1, :, 1 - y], self.r1, device(z, 1 - y, x, c)),
        )

    def two(self, go):
        z, y, x, c = self.z, self.y, self.x, self.c
        self.by_core(
            go,
            self.copy(2, self.gq.at[0, :, 1 - y, x], self.r2, device(z, 1 - y, x, c)),
            self.copy(2, self.gq.at[1, :, y, 1 - x], self.r2, device(z, y, 1 - x, c)),
        )

    def three(self):
        z, y, x, c = self.z, self.y, self.x, self.c
        return [
            self.copy(2 + k, self.gq.at[c, across(z, k), y, x], self.r3.at[k - 1], device(across(z, k), y, x, c))
            for k in (1, 2, 3)
        ]

    def four(self):
        z, y, x, c = self.z, self.y, self.x, self.c
        rows = pl.ds(pl.multiple_of((1 - c) * 24, 8), 24)
        return self.copy(6, self.fin.at[rows], self.r4, device(z, y, x, 1 - c))

    def step(self, stage):
        z, y, x, c = self.z, self.y, self.x, self.c
        if stage == 0:
            self.cores().start()
        if stage == 1:
            self.cores().wait()

            @pl.loop(0, 4)
            def _(k):
                self.add((c, k), self.rc[k])

            self.one(lambda copy: copy.start())
        if stage == 2:
            self.one(lambda copy: copy.wait())

            @pl.loop(0, 4)
            def _(k):
                for i in range(2):
                    yy, xx = self.turn(i)
                    self.add((c, k, yy, xx), self.r1[k, i])

            self.two(lambda copy: copy.start())
        if stage == 3:
            self.two(lambda copy: copy.wait())

            @pl.loop(0, 4)
            def _(k):
                self.add((c, k, y, x), self.r2[k])

            for copy in self.three():
                copy.start()
        if stage == 4:
            for copy in self.three():
                copy.wait()
            total = self.gq[c, z, y, x].astype(F32)
            for k in range(3):
                total = total + self.r3[k].astype(F32)
            self.fin[...] = total
            self.four().start()


def tail_kernel(
    ret_hbm,
    x_hbm,
    ct_hbm,
    h_hbm,
    qkv_hbm,
    c_hbm,
    w_hbm,
    yrow_hbm,
    gw_hbm,
    col_ref,
    row_ref,
    stat_ref,
    gain_ref,
    gt_hbm,
    gw_out,
    out_hbm,
    ownq_ref,
    owno_ref,
    gg_ref,
    ret_ref,
    x_ref,
    ct_ref,
    h_ref,
    qkv_ref,
    c_ref,
    w_ref,
    gt_ref,
    dc_scr,
    dhb_scr,
    dqkv_scr,
    actt_scr,
    d_scr,
    dk_scr,
    dv_scr,
    gq,
    rc,
    q1,
    q2,
    q3,
    fin,
    q4,
    ggs,
    rg,
    near,
    next_x,
    nsum,
    yback,
    send_sems,
    recv_sems,
    red_send,
    red_recv,
    load_sems,
):
    spot = place()
    z, y, x, c = spot
    me_e = z * 2 + y
    tokens, width = x_ref.shape
    slots, _w = ret_ref.shape
    blocks = tokens // BLOCK
    half = width // 2
    core, xpeer, ypeer = device(z, y, x, 1 - c), device(z, y, 1 - x, c), device(z, 1 - y, x, c)
    far = peers_of(z, y, x, c)
    links = Links(send_sems, recv_sems)
    loads = Loads(load_sems)

    def reduce(ph):
        return Reduce(spot, ph, gq, rc, q1, q2, q3, fin, q4, red_send, red_recv)

    first = [
        loads.start(a, b)
        for a, b in (
            (ret_hbm, ret_ref),
            (h_hbm, h_ref),
            (w_hbm.at[:, :, :, :, pl.ds(3 * width, width)], w_ref.at[:, :, :, :, pl.ds(3 * width, width)]),
            (ct_hbm, ct_ref),
            (c_hbm, c_ref),
        )
    ]
    second = [
        loads.start(a, b)
        for a, b in (
            (gw_hbm.at[(1 - x) * 2 + c], nsum.at[0]),
            (gw_hbm.at[x * 2 + c], nsum.at[1]),
            (x_hbm, x_ref),
            (qkv_hbm, qkv_ref),
            (w_hbm.at[:, :, :, :, pl.ds(0, 3 * width)], w_ref.at[:, :, :, :, pl.ds(0, 3 * width)]),
            (yrow_hbm.at[me_e], yback.at[me_e]),
        )
    ]
    greet(far + [core, xpeer])

    w_copies = [links.push(gw_hbm.at[xx * 2 + 1 - c], near.at[xx], core) for xx in range(2)]
    y_near, y_far = [], []
    for k, to in zip(FLIPS, far):
        (y_far if k >= 4 else y_near).append(links.push(yrow_hbm.at[to[0]], yback.at[me_e], to))

    gain_one = gain_ref[0:1, :]
    gain_two = gain_ref[1:2, :]
    member = (iota((16, 2 * width), 1) % width // HEAD_DIM == iota((16, 2 * width), 0)).astype(BF16)
    for copy in first:
        copy.wait()
    ggs[...] = jnp.zeros_like(ggs)

    def picks(rows):
        return (iota((BLOCK, slots), 1).astype(F32) == col_ref[rows, 0:1]).astype(BF16)

    @pl.loop(0, blocks)
    def _(i):
        rows = pl.ds(pl.multiple_of(i * BLOCK, BLOCK), BLOCK)
        da = dot(picks(rows), ret_ref[...])
        normed, factor = normalize(h_ref[rows, :])
        ggs[0, 1:2, :] += jnp.sum(da * normed, axis=0, keepdims=True)
        dh = ct_ref[rows, :].astype(F32) + norm_back(da * gain_two, normed, factor)
        gt_ref[rows, :] = dh
        dhb = dh.astype(BF16)
        dhb_scr[rows, :] = dhb
        dc = dot_t(dhb, weight(w_ref, 3 * width, 4 * width)).astype(BF16)
        dc_scr[rows, :] = dc
        product = dc.astype(F32) * c_ref[rows, :].astype(F32)
        high = product.astype(BF16)
        rest = (product - high.astype(F32)).astype(BF16)
        d_scr[:, rows] = dot_t(member, jnp.concatenate((high, rest), axis=1))

    def put(ph, value):
        for owner in range(2):
            for chip in range(16):
                gq[ph, owner, chip // 4, chip // 2 % 2, chip % 2] = value[
                    chip * 48 : chip * 48 + 48, owner * half : (owner + 1) * half
                ].astype(BF16)

    put(0, t_dot(c_ref[...], dhb_scr[...]))
    reduce(0).step(0)

    for copy in w_copies:
        copy.wait()

    def to_x(i):
        rows = pl.ds(pl.multiple_of(i * (width // 4), width // 4), width // 4)
        return pltpu.make_async_remote_copy(
            src_ref=nsum.at[0, rows],
            dst_ref=next_x.at[rows],
            send_sem=send_sems.at[16 + i],
            recv_sem=recv_sems.at[16 + i],
            device_id=xpeer,
            device_id_type=MESH,
        )

    for copy in second:
        copy.wait()
    nsum[0] = (nsum[0].astype(F32) + near[1 - x].astype(F32)).astype(BF16)
    to_x(0).start()

    @pl.loop(0, blocks)
    def _(i):
        rows = pl.ds(pl.multiple_of(i * BLOCK, BLOCK), BLOCK)
        normed, _f = normalize(x_ref[rows, :].astype(F32))
        dhb_scr[rows, :] = (normed * gain_one).astype(BF16)

    actt_scr[...] = dhb_scr[...].T
    low = iota((BLOCK, 128), 1) < HEAD_DIM
    scale = HEAD_DIM**-0.5

    @pl.loop(0, 3)
    def _(t):
        @pl.loop(0, 2)
        def _(inner):
            hp = 2 * t + inner
            at = pl.multiple_of(hp * 128, 128)
            dk_scr[...] = jnp.zeros_like(dk_scr)
            dv_scr[...] = jnp.zeros_like(dv_scr)
            for qb in range(blocks):
                rows = pl.ds(qb * BLOCK, BLOCK)
                q = qkv_ref[rows, pl.ds(at, 128)] * jnp.asarray(scale, BF16)
                dc = dc_scr[rows, pl.ds(at, 128)]
                q_half = [jnp.where(low, q, 0), jnp.where(low, 0, q)]
                dc_half = [jnp.where(low, dc, 0), jnp.where(low, 0, dc)]
                dq = jnp.zeros((BLOCK, 128), F32)
                for kb in range(max(0, qb - LOOKBACK), qb + 1):
                    keys = pl.ds(kb * BLOCK, BLOCK)
                    k = qkv_ref[keys, pl.ds(width + at, 128)]
                    v = qkv_ref[keys, pl.ds(2 * width + at, 128)]
                    ok = col_ref[keys, 2:3] == row_ref[2:3, rows]
                    if kb == qb:
                        ok = ok & (iota((BLOCK, BLOCK), 0) <= iota((BLOCK, BLOCK), 1))
                    ps, dss = [], []
                    for side in range(2):
                        s = dot_t(k, q_half[side])
                        p = jnp.where(ok, jnp.exp(s - stat_ref[pl.ds(2 * hp + side, 1), rows]), 0.0)
                        dp = dot_t(v, dc_half[side])
                        dss.append((p * (dp - d_scr[pl.ds(2 * hp + side, 1), rows])).astype(BF16))
                        ps.append(p.astype(BF16))
                    dv_scr[keys, :] += dot(jnp.concatenate(ps, 1), jnp.concatenate(dc_half, 0))
                    dk_scr[keys, :] += dot(jnp.concatenate(dss, 1), jnp.concatenate(q_half, 0))
                    dq += jnp.where(low, t_dot(dss[0], k), t_dot(dss[1], k))
                dqkv_scr[rows, pl.ds(at, 128)] = (dq * scale).astype(BF16)
            dqkv_scr[:, pl.ds(width + at, 128)] = dk_scr[...].astype(BF16)
            dqkv_scr[:, pl.ds(2 * width + at, 128)] = dv_scr[...].astype(BF16)

        columns = []
        for inner in range(2):
            at = pl.multiple_of((2 * t + inner) * 128, 128)
            columns += [dqkv_scr[:, pl.ds(j * width + at, 128)] for j in range(3)]
        put(t + 1, dot(actt_scr[...], jnp.concatenate(columns, axis=1)))
        reduce(t + 1).step(0)
        reduce(t).step(1)

        @pl.when(t >= 1)
        def _():
            reduce(t - 1).step(2)

        @pl.when(t >= 2)
        def _():
            reduce(t - 2).step(3)

        to_x(t + 1).start()

    @pl.loop(0, blocks)
    def _(i):
        rows = pl.ds(pl.multiple_of(i * BLOCK, BLOCK), BLOCK)
        normed, factor = normalize(x_ref[rows, :].astype(F32))
        dn = dot_t(dqkv_scr[rows, :], weight(w_ref, 0, 3 * width))
        ggs[0, 0:1, :] += jnp.sum(dn * normed, axis=0, keepdims=True)
        gt_ref[rows, :] += norm_back(dn * gain_one, normed, factor)

    stores = [loads.start(gt_ref, gt_hbm)]
    gains_copy = links.push(ggs.at[0], rg.at[0], core)
    reduce(3).step(1)
    reduce(2).step(2)
    reduce(1).step(3)
    reduce(0).step(4)
    gains_copy.wait()
    ggs[1] = ggs[0] + rg[0]
    gains_copy = links.push(ggs.at[1], rg.at[1], xpeer)

    def finish(side, last):
        group = slots // 2
        places = yback.shape[0] // 2

        @pl.loop(0, blocks)
        def _(i):
            rows = pl.ds(pl.multiple_of(i * BLOCK, BLOCK), BLOCK)
            pick = ((iota((BLOCK, group), 1) + side * group).astype(F32) == col_ref[rows, 0:1]).astype(BF16)
            got = dot(pick, yback[pl.ds(side * places, places)].reshape(group, width))
            value = h_ref[rows, :] + jax.nn.sigmoid(col_ref[rows, 1:2]) * got
            if last:
                ct_ref[rows, :] = value.astype(BF16)
            else:
                h_ref[rows, :] = value

    reduce(3).step(2)
    reduce(2).step(3)
    reduce(1).step(4)
    gains_copy.wait()
    ggs[2] = ggs[1] + rg[1]
    gains_copy = links.push(ggs.at[2], rg.at[2], ypeer)
    reduce(3).step(3)
    reduce(2).step(4)
    gains_copy.wait()
    ggs[3] = ggs[2] + rg[2]
    gain_copies = [links.push(ggs.at[3], rg.at[2 + k], device(across(z, k), y, x, c)) for k in (1, 2, 3)]
    for copy in y_near:
        copy.wait()
    finish(z // 2, False)
    for i in range(4):
        to_x(i).wait()
    gw_out[...] = nsum[1].astype(F32) + near[x].astype(F32) + next_x[...].astype(F32)
    reduce(3).step(4)
    for copy in gain_copies:
        copy.wait()
    share = width // 32
    mine = ((z * 2 + y) * 2 + x) * 2 + c
    take = (iota((width, 128), 0) == mine * share + iota((width, 128), 1)).astype(F32)
    gg_ref[...] = lax.dot_general(
        ggs[3] + rg[3] + rg[4] + rg[5],
        take,
        (((1,), (0,)), ((), ())),
        precision=lax.Precision.HIGHEST,
        preferred_element_type=F32,
    )[0:2, 0:share]
    for ph in range(4):
        kept = fin[ph, pl.ds(pl.multiple_of(c * 24, 8), 24), :]
        reduce(ph).four().wait()
        for owner, part in ((c, kept), (1 - c, q4[ph])):
            if ph == 0:
                owno_ref[:, pl.ds(pl.multiple_of(owner * half, 128), half)] = part
            else:
                for j in range(3):
                    at = pl.multiple_of(j * width + (2 * (ph - 1) + owner) * 128, 128)
                    ownq_ref[:, pl.ds(at, 128)] = part[:, j * 128 : (j + 1) * 128]
    for copy in y_far:
        copy.wait()
    finish(1 - z // 2, True)
    stores.append(loads.start(ct_ref, out_hbm))
    for copy in stores:
        copy.wait()


def tail(returned, cols, rows, tokens_in, cotangent, hidden, qkv, context, stats, w_blocks, gains, y_rows, gw):
    tokens, width = tokens_in.shape
    slots = returned.shape[0]
    half = width // 2
    any_spec = pl.BlockSpec(memory_space=pl.ANY)
    vmem = pl.BlockSpec(memory_space=pltpu.VMEM)
    return pl.pallas_call(
        tail_kernel,
        out_shape=(
            jax.ShapeDtypeStruct((tokens, width), F32),
            jax.ShapeDtypeStruct(gw.shape[1:], F32),
            jax.ShapeDtypeStruct((tokens, width), BF16),
            jax.ShapeDtypeStruct((24, 3 * width), F32),
            jax.ShapeDtypeStruct((24, width), F32),
            jax.ShapeDtypeStruct((2, 24), F32),
        ),
        in_specs=[any_spec] * 9 + [vmem] * 4,
        out_specs=(any_spec, vmem, any_spec, vmem, vmem, vmem),
        scratch_shapes=[
            pltpu.VMEM((slots, width), BF16),
            pltpu.VMEM((tokens, width), BF16),
            pltpu.VMEM((tokens, width), BF16),
            pltpu.VMEM((tokens, width), F32),
            pltpu.VMEM((tokens, 3 * width), BF16),
            pltpu.VMEM((tokens, width), BF16),
            pltpu.VMEM(w_blocks.shape, BF16),
            pltpu.VMEM((tokens, width), F32),
            pltpu.VMEM((tokens, width), BF16),
            pltpu.VMEM((tokens, width), BF16),
            pltpu.VMEM((tokens, 3 * width), BF16),
            pltpu.VMEM((width, tokens), BF16),
            pltpu.VMEM((16, tokens), F32),
            pltpu.VMEM((tokens, 128), F32),
            pltpu.VMEM((tokens, 128), F32),
            pltpu.VMEM((4, 2, 4, 2, 2, 48, half), BF16),
            pltpu.VMEM((4, 4, 2, 2, 48, half), BF16),
            pltpu.VMEM((4, 4, 2, 48, half), BF16),
            pltpu.VMEM((4, 4, 48, half), BF16),
            pltpu.VMEM((4, 3, 48, half), BF16),
            pltpu.VMEM((4, 48, half), F32),
            pltpu.VMEM((4, 24, half), F32),
            pltpu.VMEM((4, 8, width), F32),
            pltpu.VMEM((6, 8, width), F32),
            pltpu.VMEM((2,) + gw.shape[1:], BF16),
            pltpu.VMEM(gw.shape[1:], BF16),
            pltpu.VMEM((2,) + gw.shape[1:], BF16),
            pltpu.VMEM(y_rows.shape, BF16),
            pltpu.SemaphoreType.DMA((20,)),
            pltpu.SemaphoreType.DMA((20,)),
            pltpu.SemaphoreType.DMA((28,)),
            pltpu.SemaphoreType.DMA((28,)),
            pltpu.SemaphoreType.DMA((16,)),
        ],
        compiler_params=pltpu.CompilerParams(vmem_limit_bytes=62 << 20, collective_id=2, has_side_effects=True),
        cost_estimate=pl.CostEstimate(flops=80 << 30, bytes_accessed=40 << 20, transcendentals=0),
    )(returned, tokens_in, cotangent, hidden, qkv, context, w_blocks, y_rows, gw, cols, rows, stats, gains)


def flipped(z, y, k):
    hi, lo = z // 2, lax.rem(z, 2)
    zz = lax.rem(hi + k // 4, 2) * 2 + lax.rem(lo + lax.rem(k // 2, 2), 2)
    return zz, lax.rem(y + lax.rem(k, 2), 2)


def swap_kernel(
    act_hbm,
    dy_hbm,
    win_hbm,
    whid_hbm,
    own_in_hbm,
    own_hid_hbm,
    ret_hbm,
    y_hbm,
    gin_hbm,
    ghid_hbm,
    a_ref,
    dy_ref,
    win_ref,
    whid_ref,
    g_ref,
    du_ref,
    da_ref,
    us,
    gs,
    stage,
    near,
    next_x,
    send_sems,
    recv_sems,
    load_sems,
):
    z, y, x, c = place()
    me = z * 2 + y
    me_n = x * 2 + c
    count, cap, width = a_ref.shape
    parts = win_ref.shape[0]
    wide = win_ref.shape[2]
    loads = Loads(load_sems)
    first = [
        loads.start(a, b)
        for a, b in (
            (act_hbm.at[me], a_ref.at[me]),
            (own_in_hbm, win_ref.at[me_n]),
            (own_hid_hbm, whid_ref.at[me_n]),
            (dy_hbm, dy_ref),
        )
    ]
    for i in range(1, parts):
        n = lax.rem(me_n + i, parts)
        first += [loads.start(win_hbm.at[n], win_ref.at[n]), loads.start(whid_hbm.at[n], whid_ref.at[n])]

    def partner(k):
        zz, yy = flipped(z, y, k)
        return zz * 2 + yy, device(zz, yy, x, c)

    def outward(k):
        e, to = partner(k)
        return pltpu.make_async_remote_copy(
            src_ref=act_hbm.at[e],
            dst_ref=a_ref.at[me],
            send_sem=send_sems.at[k],
            recv_sem=recv_sems.at[k],
            device_id=to,
            device_id_type=MESH,
        )

    def homeward(k):
        e, to = partner(k)
        return pltpu.make_async_remote_copy(
            src_ref=da_ref.at[e],
            dst_ref=ret_hbm.at[me],
            send_sem=send_sems.at[8 + k],
            recv_sem=recv_sems.at[8 + k],
            device_id=to,
            device_id_type=MESH,
        )

    core, xpeer = device(z, y, x, 1 - c), device(z, y, 1 - x, c)
    greet([partner(k)[1] for k in range(1, 8)] + [core, xpeer])
    for k in FLIPS:
        outward(k).start()
    for copy in first:
        copy.wait()

    @pl.loop(0, count)
    def _(turn):
        k = lax.rem(turn, 2) * 4 + lax.rem(turn // 2, 2) * 2 + turn // 4

        @pl.when(k > 0)
        def _():
            outward(k).wait_recv()

        e, _to = partner(k)
        a = a_ref[e]
        dy = dy_ref[e]
        rows = pl.ds(pl.multiple_of(e * cap, cap), cap)

        def enter(j):
            us[j % 2] = dot(a, win_ref[j])
            gs[j % 2] = dot_t(dy, whid_ref[j])

        def bend(j):
            g, slope = gelu_pair(us[j % 2])
            g_ref[rows, j * wide : (j + 1) * wide] = g.astype(BF16)
            du_ref[rows, j * wide : (j + 1) * wide] = (gs[j % 2] * slope).astype(BF16)

        def leave(j):
            return dot_t(du_ref[rows, j * wide : (j + 1) * wide], win_ref[j])

        enter(0)
        total = None
        for j in range(parts):
            if j + 1 < parts:
                enter(j + 1)
            bend(j)
            if j > 0:
                term = leave(j - 1)
                total = term if total is None else total + term
        da_ref[e] = (total + leave(parts - 1)).astype(BF16)

        @pl.when(k > 0)
        def _():
            homeward(k).start()

    own = loads.start(da_ref.at[me], ret_hbm.at[me])

    def put(i, out):
        return pltpu.make_async_copy(stage.at[i], out, load_sems.at[16 + i])

    def third(i, src, dst, to):
        return pltpu.make_async_remote_copy(
            src_ref=src,
            dst_ref=dst,
            send_sem=send_sems.at[16 + i],
            recv_sem=recv_sems.at[16 + i],
            device_id=to,
            device_id_type=MESH,
        )

    acts = a_ref[...].reshape(count * cap, width)

    @pl.loop(0, parts)
    def _(j):
        cols = pl.ds(pl.multiple_of(j * wide, wide), wide)
        win_ref[j] = t_dot(acts, du_ref[:, cols]).astype(BF16)

    to_core = [third(xx, win_ref.at[xx * 2 + 1 - c], near.at[xx], core) for xx in range(2)]
    for copy in to_core:
        copy.start()

    @pl.loop(0, parts // 2)
    def _(jj):
        for i in range(2):
            j = 2 * jj + i
            cols = pl.ds(pl.multiple_of(j * wide, wide), wide)

            @pl.when(jj >= 1)
            def _():
                put(i, ghid_hbm.at[j - 2]).wait()

            stage[i] = t_dot(g_ref[:, cols], dy_ref[...].reshape(count * cap, width)).astype(BF16)
            put(i, ghid_hbm.at[j]).start()

    for copy in to_core:
        copy.wait()
    other = (1 - x) * 2 + c
    win_ref[other] = (win_ref[other].astype(F32) + near[1 - x].astype(F32)).astype(BF16)
    to_x = third(2, win_ref.at[other], next_x, xpeer)
    to_x.start()

    @pl.loop(0, count)
    def _(i):
        rows = pl.ds(pl.multiple_of(i * cap, cap), cap)
        a_ref[i] = dot(g_ref[rows, :], whid_ref[...].reshape(parts * wide, width)).astype(BF16)

    out = loads.start(a_ref, y_hbm)
    for i in range(2):
        put(i, ghid_hbm.at[parts - 2 + i]).wait()
    to_x.wait()
    tiles = []
    for i, tile in enumerate((us.at[0], us.at[1], gs.at[0])):
        rows = pl.ds(i * cap, cap)
        tile[...] = win_ref[me_n, rows].astype(F32) + near[x, rows].astype(F32) + next_x[rows].astype(F32)
        tiles.append(loads.start(tile, gin_hbm.at[rows]))
    for k in range(1, 8):
        outward(k).wait_send()
        homeward(k).wait()
    for copy in tiles + [own, out]:
        copy.wait()


def swap(act_slots, dy_rows, w_in, w_hid, own_in, own_hid):
    count, cap, width = act_slots.shape
    parts, _, wide = w_in.shape
    hidden = parts * wide
    any_spec = pl.BlockSpec(memory_space=pl.ANY)
    return pl.pallas_call(
        swap_kernel,
        out_shape=(
            jax.ShapeDtypeStruct((count, cap, width), BF16),
            jax.ShapeDtypeStruct((count, cap, width), BF16),
            jax.ShapeDtypeStruct((width, wide), F32),
            jax.ShapeDtypeStruct((parts, wide, width), BF16),
        ),
        in_specs=[any_spec] * 6,
        out_specs=(any_spec,) * 4,
        scratch_shapes=[
            pltpu.VMEM((count, cap, width), BF16),
            pltpu.VMEM((count, cap, width), BF16),
            pltpu.VMEM(w_in.shape, BF16),
            pltpu.VMEM(w_hid.shape, BF16),
            pltpu.VMEM((count * cap, hidden), BF16),
            pltpu.VMEM((count * cap, hidden), BF16),
            pltpu.VMEM((count, cap, width), BF16),
            pltpu.VMEM((2, cap, wide), F32),
            pltpu.VMEM((2, cap, wide), F32),
            pltpu.VMEM((2, width, wide), BF16),
            pltpu.VMEM((2, width, wide), BF16),
            pltpu.VMEM((width, wide), BF16),
            pltpu.SemaphoreType.DMA((20,)),
            pltpu.SemaphoreType.DMA((20,)),
            pltpu.SemaphoreType.DMA((18,)),
        ],
        compiler_params=pltpu.CompilerParams(vmem_limit_bytes=62 << 20, collective_id=1, has_side_effects=True),
        cost_estimate=pl.CostEstimate(flops=100 << 30, bytes_accessed=60 << 20, transcendentals=0),
    )(act_slots, dy_rows, w_in, w_hid, own_in, own_hid)


def local(tokens, segments, routes, gate_logit, w_qkv, w_out, norm_gains, w_in, w_hid, cotangent):
    tok_count, width = tokens.shape
    n_expert = lax.axis_size("expert")
    n_narrow = lax.axis_size("narrow")
    capacity = 2 * tok_count // n_expert
    slot_rows = n_expert * capacity
    everyone = ("expert", "narrow")

    if n_expert == 8 and n_narrow == 4:
        listed = jnp.concatenate(
            (
                routes.reshape(1, tok_count).astype(F32),
                gate_logit.reshape(1, tok_count),
                segments.reshape(1, tok_count).astype(F32),
                jnp.zeros((5, tok_count), F32),
            )
        )
        qkv, context, hidden, act_slots, w_blocks, dy_rows, w_in_all, w_hid_all, stats, cols, gains = head(
            tokens, cotangent, w_in[0], w_hid[0], listed, w_qkv, w_out, norm_gains, n_expert, capacity
        )
        da_back, y_rows, gin_own, ghid = swap(act_slots, dy_rows, w_in_all, w_hid_all, w_in[0], w_hid[0])
        grad_tokens, ghid_own, block_out, own_qkv, own_out, own_gains = tail(
            da_back.reshape(slot_rows, width),
            cols,
            listed,
            tokens,
            cotangent,
            hidden,
            qkv,
            context,
            stats,
            w_blocks,
            gains,
            y_rows,
            ghid,
        )
        return (
            block_out,
            grad_tokens,
            own_qkv,
            own_out,
            own_gains,
            gin_own[None],
            ghid_own[None],
        )
    gain_cols = jnp.pad(norm_gains.T, ((0, 0), (0, 126)))
    w_all = lax.all_gather(
        jnp.concatenate((w_qkv, w_out, gain_cols), axis=1), everyone, axis=0, tiled=True
    )
    gains = w_all[:, 4 * width : 4 * width + 2].T.astype(F32)
    w_in_all = lax.all_gather(w_in[0], "narrow", axis=0, tiled=False)
    w_hid_all = lax.all_gather(w_hid[0], "narrow", axis=0, tiled=False)

    def exchange(values):
        return lax.all_to_all(
            values.reshape(n_expert, capacity, width), "expert", split_axis=0, concat_axis=0, tiled=True
        ).reshape(slot_rows, width)

    segr = segments.reshape(1, tok_count)
    segc = segments.reshape(tok_count, 1)
    srow, scol, dy_slots = prep(routes, gate_logit, cotangent, n_expert, capacity)
    dy_rows = exchange(dy_slots)
    qkv, context, stats, hidden, act_slots = attend_fwd(tokens, w_all, gains, segr, segc, srow, slot_rows)
    act_rows = exchange(act_slots)
    activated, grad_pre, da_rows = experts(act_rows, dy_rows, w_in_all, w_hid_all)
    da_back = exchange(da_rows)
    hidden_units = activated.shape[1]
    y_rows = dot(activated, w_hid_all.reshape(hidden_units, width)).astype(BF16)
    grad_hid = t_dot(activated, dy_rows).astype(BF16)
    grad_in = lax.dot_general(
        act_rows, grad_pre.reshape(slot_rows, n_narrow, -1), (((0,), (0,)), ((), ())), preferred_element_type=F32
    ).astype(BF16)
    y_back = exchange(y_rows)
    grad_tokens, grad_w, grad_gains = attend_bwd(
        da_back, scol, tokens, cotangent, hidden, qkv, context, stats, w_all, gains, segr, segc
    )
    block_out = block_output(y_back, scol, hidden, gate_logit)
    grad_hid_w = lax.psum_scatter(grad_hid, "narrow", scatter_dimension=0, tiled=True).astype(F32)[None]
    grad_in_w = lax.psum_scatter(grad_in, "narrow", scatter_dimension=1, tiled=True).astype(F32)
    grad_in_w = grad_in_w.reshape(1, width, -1)
    packed = jnp.concatenate((grad_w, jnp.pad(grad_gains[:2].T, ((0, 0), (0, 126)))), axis=1)
    own = lax.psum_scatter(packed, everyone, scatter_dimension=0, tiled=True)
    return (
        block_out,
        grad_tokens,
        own[:, : 3 * width],
        own[:, 3 * width : 4 * width],
        own[:, 4 * width : 4 * width + 2].T,
        grad_in_w,
        grad_hid_w,
    )


def solution(mesh):
    placed = (
        P(("expert", "narrow"), None),
        P(("expert", "narrow"), None),
        P(("expert", "narrow"), None),
        P(("expert", "narrow")),
        P(("expert", "narrow"), None),
        P(("expert", "narrow"), None),
        P(None, ("expert", "narrow")),
        P("expert", None, "narrow"),
        P("expert", "narrow", None),
        P(("expert", "narrow"), None),
    )
    return jax.shard_map(
        local,
        mesh=mesh,
        in_specs=placed,
        out_specs=(
            P(("expert", "narrow"), None),
            P(("expert", "narrow"), None),
            P(("expert", "narrow"), None),
            P(("expert", "narrow"), None),
            P(None, ("expert", "narrow")),
            P("expert", None, "narrow"),
            P("expert", "narrow", None),
        ),
        check_vma=False,
    )
```
